32 devices in a mesh: edge: 8 (over y, x, core), feat: 4 (over z).
Axes of the slice: x: 2, y: 2, z: 4, core: 2. Of those that a mesh axis runs over, the one named last changes fastest.
Arguments:
- node_latents: bfloat16 [4, 4096, 256], P('feat', 'edge'), may hold values from -6 to 6
- edge_latents: bfloat16 [4, 32768, 256], P('feat', 'edge'), may hold values from -6 to 6
- senders: int32 [32768], P('edge'), may hold values from 0 to 4095, as said below
- receivers: int32 [32768], P('edge'), may hold values from 0 to 4095, as said below
- regions: int32 [32768], P('edge'), may hold values from 0 to 23
- forced: int32 [4096], P('edge'), may hold values 0 or 1
- params: float32 [1824, 256], P('feat'), may hold values from -1.5 to 1.5, as said below
- first_moment: float32 [1824, 256], P('feat'), may hold values from -0.34 to 0.34
- second_moment: float32 [1824, 256], P('feat'), may hold values from 0.004 to 0.22
- averaged: float32 [1824, 256], P('feat'), may hold values from -1.7 to 1.7
- step: int32 [1], replicated, may hold values from 1 to 20
- cotangent: float32 [4, 4096, 256], P('feat', 'edge'), may hold values from -6 to 6
Outputs:
- new_latents: float32 [4, 4096, 256], P('feat', 'edge')
- grad_latents: float32 [4, 4096, 256], P('feat', 'edge')
- grad_edges: bfloat16 [4, 32768, 256], P('feat', 'edge')
- new_first: float32 [1824, 256], P('feat')
- new_second: float32 [1824, 256], P('feat')
- new_params: float32 [1824, 256], P('feat')
- new_average: float32 [1824, 256], P('feat')
- grad_norm: float32 [1], replicated
- vector_grads: float32 [8, 256], replicated
The draws below stay inside these ranges and needn't reach their ends.
Inputs may be any that keep to these rules, and one draw needn't show every extreme that they name: `senders`: nodes are numbered so that node block b is nodes b * 512 to (b + 1) * 512 - 1. Edge k lies in edge block e = k // 4096; its sender lies in node block e - 1, e or e + 1, taken cyclically over the 4096 nodes. `receivers`: the receiver of edge k lies in node block e - 1, e or e + 1 of its edge block e = k // 4096, taken cyclically. `params`: parameters scaled by fan-in; gains near one.
All inputs are finite; a program needn't handle non-finite values. No bound on the sum of `forced` on one device may be relied on, other than what follows from the above.
Results may differ from the reference program's by a relative error of at most 0.0039.
The reference program's roundings to bfloat16 on the way count: a program that leaves them out, or rounds other values in their place, can miss the bound.
Values may be sent and summed in bfloat16 or wider, within the bound.
No kernel may reach another device: no remote copies, remote signals or barrier semaphores. Data moves between devices by JAX's collectives and lax.ppermute only.
A program may use at most 128 MiB of HBM per device.

```python
import math
import jax
import jax.numpy as jnp
import numpy as np
from jax import lax

L = 256
REGIONS = 24
NODE_DEV = 512
EDGE_DEV = 4096
SAMPLES = 4
NODES = 4096
EDGES = 32768


def base_values(key, shape):
    return jax.random.truncated_normal(key, -3.0, 3.0, shape, jnp.float32)


def row_index():
    return jnp.arange(7 * L + 8 + REGIONS)[:, None]


def parameter_values(key):
    total = 7 * L + 8 + REGIONS
    row = row_index()
    base = base_values(key, (total, L))
    scale = jnp.where(row < 3 * L, 1.0 / math.sqrt(3 * L), jnp.where(row < 4 * L, 1.0 / math.sqrt(L), jnp.where(row < 6 * L, 1.0 / math.sqrt(2 * L), 1.0 / math.sqrt(L))))
    vector_row = row - 7 * L
    gains = (vector_row == 2) | (vector_row == 6)
    vector_values = jnp.where(gains, 1.0 + 0.1 * base, 0.1 * base)
    values = jnp.where(row < 7 * L, scale * base, jnp.where(row < 7 * L + 8, vector_values, 0.5 * base))
    return values.astype(jnp.float32)


def gradient_scale():
    row = row_index()
    scale = jnp.where(row < 3 * L, 0.8, jnp.where(row < 4 * L, 1.0, jnp.where(row < 5 * L, 0.3, jnp.where(row < 6 * L, 1.0, jnp.where(row < 7 * L, 0.33, jnp.where(row < 7 * L + 8, 0.5, 0.3))))))
    return scale.astype(jnp.float32)


def neighbour_nodes(key):
    blocks = NODES // NODE_DEV
    device = jnp.arange(EDGES, dtype=jnp.int32) // EDGE_DEV
    offset = jax.random.randint(jax.random.fold_in(key, 0), (EDGES,), -1, 2, dtype=jnp.int32)
    within = jax.random.randint(jax.random.fold_in(key, 1), (EDGES,), 0, NODE_DEV, dtype=jnp.int32)
    return (jnp.mod(device + offset, blocks) * NODE_DEV + within).astype(jnp.int32)


def draw_senders(key, part):
    return neighbour_nodes(jax.random.fold_in(key, 11))


def draw_receivers(key, part):
    return neighbour_nodes(jax.random.fold_in(key, 12))


def draw_params(key, part):
    return parameter_values(jax.random.fold_in(key, 1))


def draw_averaged(key, part):
    noise = base_values(jax.random.fold_in(key, 2), (7 * L + 8 + REGIONS, L))
    return (parameter_values(jax.random.fold_in(key, 1)) + 0.05 * noise).astype(jnp.float32)


def draw_first_moment(key, part):
    base = base_values(jax.random.fold_in(key, 3), (7 * L + 8 + REGIONS, L))
    return (0.111 * gradient_scale() * base).astype(jnp.float32)


def draw_second_moment(key, part):
    shape = (7 * L + 8 + REGIONS, L)
    factor = jnp.exp(jax.random.uniform(jax.random.fold_in(key, 4), shape, jnp.float32, math.log(0.5), math.log(2.0)))
    scale = gradient_scale()
    return (0.105 * scale * scale * factor).astype(jnp.float32)


def plant(entries, stream_key, least, top_value):
    longest = entries.shape.index(max(entries.shape))
    spots = []
    for shift in (0, 1):
        where = [jax.random.randint(jax.random.fold_in(stream_key, axis), (), 0, length) for axis, length in enumerate(entries.shape)]
        where[longest] = (where[longest] + shift) % entries.shape[longest]
        spots.append(tuple(where))
    return entries.at[spots[0]].set(least).at[spots[1]].set(top_value)


def block_levels(stream_key, dims, cuts, low, high):
    def one(dim, shards_of):
        steps = jax.random.uniform(jax.random.fold_in(jax.random.fold_in(stream_key, 6), dim), (shards_of,), jnp.float32, low / len(cuts), high / len(cuts))
        return jnp.repeat(jnp.exp(steps), dims[dim] // shards_of).reshape((-1,) + (1,) * (len(dims) - dim - 1))

    loudness = one(*cuts[0])
    for cut in cuts[1:]:
        loudness = loudness * one(*cut)
    return loudness


def cumulative_ranks(count, slope):
    weights = [(1 << 20) // math.isqrt(standing ** slope) + 1 for standing in range(1, count + 1)]
    deviation = 1 + sum(weights) // (1 << 30)
    return np.cumsum(np.array([max(1, weight // deviation) for weight in weights]))


def skewed_ids(own_key, dims, count, skew):
    table = cumulative_ranks(count, skew)
    pick = jax.random.randint(jax.random.fold_in(own_key, 1), dims, 0, int(table[count - 1]))
    grade = jnp.searchsorted(jnp.asarray(table, jnp.int32), pick, side="right")
    return jax.random.permutation(jax.random.fold_in(own_key, 2), count)[grade].astype(jnp.int32)


def gaussian(key, dims, scale, reach, cuts=(), kind=jnp.bfloat16):
    drawn = scale * jax.random.normal(key, dims, jnp.float32)
    if cuts:
        drawn = drawn * block_levels(key, dims, cuts, -0.22, 0.18)
    return jnp.clip(drawn, -reach, reach).astype(kind)


def setup_inputs(seed: int = 0) -> dict:
    arg_keys = jax.random.split(jax.random.key(seed), 13)
    node_latents = gaussian(arg_keys[0], (SAMPLES, NODES, L), 1.0, 6.0, ((0, 4), (1, 8)))
    edge_latents = gaussian(arg_keys[1], (SAMPLES, EDGES, L), 1.0, 6.0, ((0, 4), (1, 8)))
    senders = draw_senders(jax.random.fold_in(arg_keys[12], 71), 0)
    receivers = draw_receivers(jax.random.fold_in(arg_keys[12], 71), 0)
    regions = plant(skewed_ids(arg_keys[4], (EDGES,), REGIONS, 2), jax.random.fold_in(arg_keys[4], 3), 0, REGIONS - 1).astype(jnp.int32)
    forced = plant((jax.random.randint(arg_keys[5], (NODES,), 0, 8) < 1).astype(jnp.int32), jax.random.fold_in(arg_keys[5], 1), 0, 1)
    params = draw_params(jax.random.fold_in(arg_keys[12], 71), 0)
    first_moment = draw_first_moment(jax.random.fold_in(arg_keys[12], 71), 0)
    second_moment = draw_second_moment(jax.random.fold_in(arg_keys[12], 71), 0)
    averaged = draw_averaged(jax.random.fold_in(arg_keys[12], 71), 0)
    step = jax.random.randint(arg_keys[10], (1,), 1, 21).astype(jnp.int32)
    cotangent = gaussian(arg_keys[11], (SAMPLES, NODES, L), 1.0, 6.0, ((0, 4), (1, 8)), jnp.float32)
    return {"node_latents": node_latents, "edge_latents": edge_latents, "senders": senders, "receivers": receivers, "regions": regions, "forced": forced, "params": params, "first_moment": first_moment, "second_moment": second_moment, "averaged": averaged, "step": step, "cotangent": cotangent}


@jax.custom_vjp
def low(v):
    return lax.optimization_barrier(v.astype(jnp.bfloat16)).astype(jnp.float32)

@jax.custom_vjp
def low_back(v):
    return v

def low_keep(v):
    return (low(v), None)

def low_pass(kept, grad):
    return (grad,)

def back_keep(v):
    return (v, None)

def back_low(kept, grad):
    return (low(grad),)
low.defvjp(low_keep, low_pass)
low_back.defvjp(back_keep, back_low)
NORM_EPS = 1e-05
MAX_NORM = 512.0
RATE = 0.05
BETA_ONE = 0.9
BETA_TWO = 0.95
ADAM_EPS = 1e-08
WEIGHT_DECAY = 0.1
AVERAGE_DECAY = 0.999

def matmul(left, right):
    return jnp.dot(left, right, precision=lax.Precision.HIGHEST, preferred_element_type=jnp.float32)

def layer_norm(values, gain, shift):
    center = values - lax.optimization_barrier(jnp.mean(values, axis=-1, keepdims=True))
    spread = lax.optimization_barrier(jnp.mean(center * center, axis=-1, keepdims=True))
    return center * lax.rsqrt(spread + NORM_EPS) * gain + shift

def sample_forward(weights, latents, edges, senders, receivers, regions, keep):
    width = latents.shape[1]
    first = weights[0:3 * width]
    second = weights[3 * width:4 * width]
    node_first = weights[4 * width:6 * width]
    node_second = weights[6 * width:7 * width]
    vectors = weights[7 * width:7 * width + 8]
    table = weights[7 * width + 8:]
    blocks = edges.shape[0] // EDGE_DEV

    def edge_block(pieces):
        edge_rows, send_rows, recv_rows, region_rows = pieces
        pre = matmul(latents[send_rows], first[0:width]) + matmul(latents[recv_rows], first[width:2 * width])
        pre = pre + matmul(edge_rows, first[2 * width:3 * width]) + vectors[0] + table[region_rows]
        pre = low_back(pre)
        hidden = low(jax.nn.silu(pre))
        inner = low_back(matmul(hidden, second) + vectors[1])
        return layer_norm(inner, vectors[2], vectors[3])
    messages = lax.map(jax.checkpoint(edge_block), (edges.reshape(blocks, EDGE_DEV, width), senders.reshape(blocks, EDGE_DEV), receivers.reshape(blocks, EDGE_DEV), regions.reshape(blocks, EDGE_DEV)))
    messages = messages.reshape(-1, width)
    gathered = jax.ops.segment_sum(messages, receivers, num_segments=latents.shape[0])
    gathered = low(low_back(gathered))
    pre_node = low_back(matmul(latents, node_first[0:width]) + matmul(gathered, node_first[width:2 * width]) + vectors[4])
    hidden_node = low(jax.nn.silu(pre_node))
    inner_node = low_back(matmul(hidden_node, node_second) + vectors[5])
    update = layer_norm(inner_node, vectors[6], vectors[7])
    return latents + keep * update

def reference(node_latents, edge_latents, senders, receivers, regions, forced, params, first_moment, second_moment, averaged, step, cotangent):
    keep = (1 - forced).astype(jnp.float32)[:, None]
    width = params.shape[1]

    def one_sample(total, inputs):
        latents, edges, upstream = inputs

        def forward(weights, lat, edg):
            return sample_forward(low(weights), lat, edg, senders, receivers, regions, keep)
        result, pullback = jax.vjp(forward, params, latents.astype(jnp.float32), edges.astype(jnp.float32))
        grad_weights, grad_nodes, grad_edge = pullback(upstream.astype(jnp.float32))
        return (total + grad_weights, (result, grad_nodes, grad_edge.astype(jnp.bfloat16)))
    total, (outputs, grad_nodes, grad_edges) = lax.scan(one_sample, jnp.zeros_like(params), (node_latents, edge_latents, cotangent))
    grad_norm = jnp.sqrt(jnp.sum(total * total))
    factor = jnp.minimum(1.0, MAX_NORM / (grad_norm + 1e-06))
    clipped = total * factor
    vector_grads = clipped[7 * width:7 * width + 8]
    new_first = BETA_ONE * first_moment + (1.0 - BETA_ONE) * clipped
    new_second = BETA_TWO * second_moment + (1.0 - BETA_TWO) * clipped * clipped
    count = step[0].astype(jnp.float32)
    first_hat = new_first / (1.0 - jnp.power(BETA_ONE, count))
    second_hat = new_second / (1.0 - jnp.power(BETA_TWO, count))
    new_params = params - RATE * (first_hat / (jnp.sqrt(second_hat) + ADAM_EPS) + WEIGHT_DECAY * params)
    decay_now = jnp.minimum(AVERAGE_DECAY, (1.0 + count) / (10.0 + count))
    new_average = decay_now * averaged + (1.0 - decay_now) * new_params
    return (outputs, grad_nodes, grad_edges, new_first, new_second, new_params, new_average, grad_norm.reshape(1), vector_grads)
```

```python
import functools

import jax
import jax.numpy as jnp
from jax import lax
from jax.experimental import pallas as pl
from jax.experimental.pallas import tpu as pltpu
from jax.sharding import PartitionSpec as P

NORM_EPS = 1e-05
MAX_NORM = 512.0
RATE = 0.05
BETA_ONE = 0.9
BETA_TWO = 0.95
ADAM_EPS = 1e-08
WEIGHT_DECAY = 0.1
AVERAGE_DECAY = 0.999

LANES = 128
TILE = 1024
B16 = jnp.bfloat16
F32 = jnp.float32
I32 = jnp.int32
PARAMS = pltpu.CompilerParams(vmem_limit_bytes=56 * 1024 * 1024)


def dot(left, right):
    return jnp.dot(left, right, preferred_element_type=F32)


def dot_rows(left, right):
    return lax.dot_general(left, right, (((0,), (0,)), ((), ())), preferred_element_type=F32)


def dot_back(left, right):
    return lax.dot_general(left, right, (((1,), (1,)), ((), ())), preferred_element_type=F32)


def split(values):
    high = values.astype(B16)
    return high, (values - high.astype(F32)).astype(B16)


def whole(shape):
    return pl.BlockSpec(shape, lambda i: (0,) * len(shape))


def tiled(rows, cols):
    return pl.BlockSpec((rows, cols), lambda i: (i, 0))


def column(row):
    return jnp.broadcast_to(row, (LANES, LANES)).T


def chosen_columns(index_ref, tile, rows, first, last):
    lane = lax.broadcasted_iota(I32, (LANES, LANES), 1)
    groups = []
    for g in range(rows // LANES):
        col = column(index_ref[pl.ds(tile * (rows // LANES) + g, 1), :])
        groups.append(
            jnp.concatenate(
                [jnp.where(col == lane + base, 1.0, 0.0).astype(B16) for base in range(first, last, LANES)],
                axis=1,
            )
        )
    return jnp.concatenate(groups, axis=0)


def chosen_rows(index_row, first, count):
    node = lax.broadcasted_iota(I32, (count, index_row.shape[1]), 0) + first
    return jnp.where(index_row == node, 1.0, 0.0).astype(B16)


def gather_kernel(send_ref, recv_ref, own_ref, pair_ref, off_ref, hs_ref, hr_ref):
    tile = pl.program_id(0)
    rows = hs_ref.shape[0]
    nodes = own_ref.shape[0]
    for index_ref, out_ref in ((send_ref, hs_ref), (recv_ref, hr_ref)):
        total = None
        for slot, table in enumerate((own_ref, pair_ref, off_ref)):
            part = dot(chosen_columns(index_ref, tile, rows, slot * nodes, (slot + 1) * nodes), table[...])
            total = part if total is None else total + part
        out_ref[...] = total.astype(B16)


def gather_latents(send, recv, own, pair, off):
    nodes, width = own.shape
    edges = send.size
    out = jax.ShapeDtypeStruct((edges, width), B16)
    index = whole((edges // LANES, LANES))
    return pl.pallas_call(
        gather_kernel,
        grid=(edges // TILE,),
        in_specs=[index, index] + [whole((nodes, width))] * 3,
        out_specs=[tiled(TILE, width)] * 2,
        out_shape=[out, out],
        compiler_params=PARAMS,
        name="gather_latents",
        cost_estimate=pl.CostEstimate(
            flops=2 * 2 * edges * 3 * nodes * width, transcendentals=0, bytes_accessed=edges * width * 4
        ),
    )(send.reshape(-1, LANES), recv.reshape(-1, LANES), own, pair, off)


def edge_forward_kernel(
    region_ref, recv_row_ref, hs_ref, hr_ref, x_ref, w_ref, table_ref, vec_ref,
    hidden_ref, slope_ref, unit_ref, inverse_ref, high_ref, low_ref, pair_ref, off_ref,
):
    step = pl.program_id(0)
    rows = x_ref.shape[0]
    width = x_ref.shape[1]
    nodes = pair_ref.shape[0]
    steps = pl.num_programs(0)

    @pl.when(step < steps - 1)
    def _():
        pre = dot(hs_ref[...], w_ref[0:width, :])
        pre = pre + dot(hr_ref[...], w_ref[width : 2 * width, :])
        pre = pre + dot(x_ref[...], w_ref[2 * width : 3 * width, :])
        pre = pre + dot(chosen_columns(region_ref, step, rows, 0, LANES), table_ref[...])
        pre = pre + vec_ref[0:1, :]
        sigma = 1.0 / (1.0 + jnp.exp(-pre))
        hidden = (pre * sigma).astype(B16)
        hidden_ref[...] = hidden
        slope_ref[...] = sigma * (1.0 + pre * (1.0 - sigma))
        inner = dot(hidden, w_ref[3 * width : 4 * width, :]) + vec_ref[1:2, :]
        center = inner - jnp.mean(inner, axis=-1, keepdims=True)
        inverse = lax.rsqrt(jnp.mean(center * center, axis=-1, keepdims=True) + NORM_EPS)
        unit = center * inverse
        unit_ref[...] = unit
        inverse_ref[...] = jnp.broadcast_to(inverse, (rows, LANES))
        high, low = split(unit * vec_ref[2:3, :] + vec_ref[3:4, :])
        base = pl.multiple_of(step * rows, rows)
        high_ref[pl.ds(base, rows), :] = high
        low_ref[pl.ds(base, rows), :] = low

    @pl.when(step == steps - 1)
    def _():
        for slot, out_ref in ((1, pair_ref), (2, off_ref)):
            onehot = chosen_rows(recv_row_ref[...], slot * nodes, nodes)
            total = dot(onehot, high_ref[...]) + dot(onehot, low_ref[...])
            out_ref[...] = total.astype(out_ref.dtype)


def edge_forward(regions, recv, hs, hr, edges, weights, table, vectors, nodes, wire):
    count, width = edges.shape
    steps = count // TILE
    last = steps - 1
    tile = pl.BlockSpec((TILE, width), lambda i: (jnp.minimum(i, last), 0))
    thin = pl.BlockSpec((TILE, LANES), lambda i: (jnp.minimum(i, last), 0))
    return pl.pallas_call(
        edge_forward_kernel,
        grid=(steps + 1,),
        in_specs=[
            whole((count // LANES, LANES)), whole((1, count)), tile, tile, tile,
            whole(weights.shape), whole(table.shape), whole(vectors.shape),
        ],
        out_specs=[tile, tile, tile, thin, whole((count, width)), whole((count, width)), whole((nodes, width)), whole((nodes, width))],
        out_shape=[
            jax.ShapeDtypeStruct((count, width), B16),
            jax.ShapeDtypeStruct((count, width), F32),
            jax.ShapeDtypeStruct((count, width), F32),
            jax.ShapeDtypeStruct((count, LANES), F32),
            jax.ShapeDtypeStruct((count, width), B16),
            jax.ShapeDtypeStruct((count, width), B16),
            jax.ShapeDtypeStruct((nodes, width), wire),
            jax.ShapeDtypeStruct((nodes, width), wire),
        ],
        compiler_params=PARAMS,
        name="edge_forward",
        cost_estimate=pl.CostEstimate(
            flops=2 * count * width * (5 * width + 4 * nodes), transcendentals=2 * count * width,
            bytes_accessed=count * width * 20,
        ),
    )(regions.reshape(-1, LANES), recv.reshape(1, -1), hs, hr, edges, weights, table, vectors)


def own_sum_kernel(recv_row_ref, high_ref, low_ref, out_ref):
    onehot = chosen_rows(recv_row_ref[...], 0, out_ref.shape[0])
    total = dot(onehot, high_ref[...]) + dot(onehot, low_ref[...])

    @pl.when(pl.program_id(0) == 0)
    def _():
        out_ref[...] = total

    @pl.when(pl.program_id(0) > 0)
    def _():
        out_ref[...] += total


def own_sum(recv, high, low, nodes):
    count, width = high.shape
    return pl.pallas_call(
        own_sum_kernel,
        grid=(count // TILE,),
        in_specs=[pl.BlockSpec((1, TILE), lambda i: (0, i)), tiled(TILE, width), tiled(TILE, width)],
        out_specs=whole((nodes, width)),
        out_shape=jax.ShapeDtypeStruct((nodes, width), F32),
        compiler_params=PARAMS,
        name="own_sum",
        cost_estimate=pl.CostEstimate(
            flops=4 * count * width * nodes, transcendentals=0, bytes_accessed=count * width * 4
        ),
    )(recv.reshape(1, -1), high, low)


def node_kernel(
    h_ref, own_ref, pair_ref, off_ref, w_ref, vec_ref, keep_ref, up_ref,
    new_ref, d_agg_ref, agg_ref, hidden_ref, d_inner_ref, d_pre_ref, sums_ref,
):
    width = h_ref.shape[1]
    agg = (own_ref[...] + pair_ref[...].astype(F32) + off_ref[...].astype(F32)).astype(B16)
    agg_ref[...] = agg
    h = h_ref[...]
    latent, aggregate = w_ref[4 * width : 5 * width, :], w_ref[5 * width : 6 * width, :]
    second = w_ref[6 * width : 7 * width, :]
    pre = dot(h, latent) + dot(agg, aggregate) + vec_ref[4:5, :]
    sigma = 1.0 / (1.0 + jnp.exp(-pre))
    hidden = (pre * sigma).astype(B16)
    hidden_ref[...] = hidden
    inner = dot(hidden, second) + vec_ref[5:6, :]
    center = inner - jnp.mean(inner, axis=-1, keepdims=True)
    inverse = lax.rsqrt(jnp.mean(center * center, axis=-1, keepdims=True) + NORM_EPS)
    unit = center * inverse
    keep = keep_ref[...].astype(F32)
    new_ref[...] = h.astype(F32) + keep * (unit * vec_ref[6:7, :] + vec_ref[7:8, :])
    d_update = keep * up_ref[...]
    scaled = d_update * vec_ref[6:7, :]
    d_inner = inverse * (
        scaled
        - jnp.mean(scaled, axis=-1, keepdims=True)
        - unit * jnp.mean(scaled * unit, axis=-1, keepdims=True)
    )
    d_inner = d_inner.astype(B16)
    d_inner_ref[...] = d_inner
    slope = sigma * (1.0 + pre * (1.0 - sigma))
    d_pre = (dot_back(d_inner, second) * slope).astype(B16)
    d_pre_ref[...] = d_pre
    d_agg_ref[...] = dot_back(d_pre, aggregate).astype(B16)
    sums_ref[...] = jnp.concatenate(
        [
            jnp.sum(d_pre.astype(F32), axis=0, keepdims=True),
            jnp.sum(d_inner.astype(F32), axis=0, keepdims=True),
            jnp.sum(d_update * unit, axis=0, keepdims=True),
            jnp.sum(d_update, axis=0, keepdims=True),
        ],
        axis=0,
    )


def node_update(h, own, pair, off, weights, vectors, keep, upstream):
    nodes, width = h.shape
    full = jax.ShapeDtypeStruct((nodes, width), F32)
    half = jax.ShapeDtypeStruct((nodes, width), B16)
    return pl.pallas_call(
        node_kernel,
        out_shape=[full, half, half, half, half, half, jax.ShapeDtypeStruct((4, width), F32)],
        compiler_params=PARAMS,
        name="node_update",
        cost_estimate=pl.CostEstimate(
            flops=2 * nodes * width * width * 5, transcendentals=2 * nodes * width, bytes_accessed=nodes * width * 20
        ),
    )(h, own, pair, off, weights, vectors, keep, upstream)


def node_grads_kernel(h_ref, agg_ref, hidden_ref, d_inner_ref, d_pre_ref, w_ref, up_ref, grad_ref, back_ref):
    width = h_ref.shape[1]
    d_pre = d_pre_ref[...]
    grad_ref[0:width, :] = dot_rows(h_ref[...], d_pre)
    grad_ref[width : 2 * width, :] = dot_rows(agg_ref[...], d_pre)
    grad_ref[2 * width : 3 * width, :] = dot_rows(hidden_ref[...], d_inner_ref[...])
    back_ref[...] = up_ref[...] + dot_back(d_pre, w_ref[4 * width : 5 * width, :])


def node_grads(h, agg, hidden, d_inner, d_pre, weights, upstream):
    nodes, width = h.shape
    return pl.pallas_call(
        node_grads_kernel,
        out_shape=[jax.ShapeDtypeStruct((3 * width, width), F32), jax.ShapeDtypeStruct((nodes, width), F32)],
        compiler_params=PARAMS,
        name="node_grads",
        cost_estimate=pl.CostEstimate(
            flops=2 * nodes * width * width * 4, transcendentals=0, bytes_accessed=nodes * width * 18
        ),
    )(h, agg, hidden, d_inner, d_pre, weights, upstream)


def edge_backward_kernel(
    core_ref, recv_ref, send_row_ref, recv_row_ref, region_row_ref, own_ref, pair_ref, off_ref,
    h_own_ref, h_pair_ref, h_off_ref, x_ref, hidden_ref, slope_ref, unit_ref, inverse_ref, w_ref, vec_ref,
    node_grad_ref, node_sum_ref,
    grad_x_ref, kept_ref, sent_ref, part_own_ref, part_pair_ref, part_off_ref,
    d_pre_ref, second_ref, third_ref, vec_acc_ref,
):
    step = pl.program_id(0)
    steps = pl.num_programs(0)
    rows, width = x_ref.shape
    nodes = own_ref.shape[0]
    regions = third_ref.shape[0] - width

    @pl.when(step == 0)
    def _():
        second_ref[...] = jnp.zeros_like(second_ref)
        third_ref[...] = jnp.zeros_like(third_ref)
        vec_acc_ref[...] = jnp.zeros_like(vec_acc_ref)

    @pl.when(step < steps - 1)
    def _():
        d_message = None
        for slot, table in enumerate((own_ref, pair_ref, off_ref)):
            part = dot(chosen_columns(recv_ref, step, rows, slot * nodes, (slot + 1) * nodes), table[...])
            d_message = part if d_message is None else d_message + part
        unit = unit_ref[...]
        gained = d_message * unit
        scaled = d_message * vec_ref[2:3, :]
        inverse = inverse_ref[:, 0:1]
        d_inner = inverse * (
            scaled
            - jnp.mean(scaled, axis=-1, keepdims=True)
            - unit * jnp.mean(scaled * unit, axis=-1, keepdims=True)
        )
        vec_acc_ref[0:8, :] += jnp.sum(gained.reshape(rows // 8, 8, width), axis=0)
        vec_acc_ref[8:16, :] += jnp.sum(d_message.reshape(rows // 8, 8, width), axis=0)
        d_inner = d_inner.astype(B16)
        second_ref[0:width, :] += dot_rows(hidden_ref[...], d_inner)
        second_ref[width : width + 16, :] += dot(jnp.ones((16, rows), B16), d_inner)
        d_pre = (dot_back(d_inner, w_ref[3 * width : 4 * width, :]) * slope_ref[...]).astype(B16)
        base = pl.multiple_of(step * rows, rows)
        d_pre_ref[pl.ds(base, rows), :] = d_pre
        third_ref[0:width, :] += dot_rows(x_ref[...], d_pre)
        region_row = region_row_ref[:, pl.ds(base, rows)]
        third_ref[width : width + regions, :] += dot(chosen_rows(region_row, 0, regions), d_pre)
        grad_x_ref[...] = dot_back(d_pre, w_ref[2 * width : 3 * width, :]).astype(B16)

    @pl.when(step == steps - 1)
    def _():
        table_rows = node_grad_ref.shape[0] + 4 * width
        sender, receiver = w_ref[0:width, :], w_ref[width : 2 * width, :]
        first_send = first_recv = None
        d_pre = d_pre_ref[...]
        for slot, (h_ref, out_ref) in enumerate(
            ((h_own_ref, part_own_ref), (h_pair_ref, part_pair_ref), (h_off_ref, part_off_ref))
        ):
            h = h_ref[...]
            s_high, s_low = split(dot(chosen_rows(send_row_ref[...], slot * nodes, nodes), d_pre))
            r_high, r_low = split(dot(chosen_rows(recv_row_ref[...], slot * nodes, nodes), d_pre))
            part = dot_back(s_high, sender) + dot_back(s_low, sender)
            part = part + dot_back(r_high, receiver) + dot_back(r_low, receiver)
            out_ref[...] = part.astype(out_ref.dtype)
            grad_send = dot_rows(h, s_high) + dot_rows(h, s_low)
            grad_recv = dot_rows(h, r_high) + dot_rows(h, r_low)
            first_send = grad_send if first_send is None else first_send + grad_send
            first_recv = grad_recv if first_recv is None else first_recv + grad_recv
        table_grad = third_ref[width : width + regions, :]
        vector_rows = jnp.concatenate(
            [
                jnp.sum(table_grad, axis=0, keepdims=True),
                second_ref[width : width + 1, :],
                jnp.sum(vec_acc_ref[0:8, :], axis=0, keepdims=True),
                jnp.sum(vec_acc_ref[8:16, :], axis=0, keepdims=True),
                node_sum_ref[...],
            ],
            axis=0,
        )
        pieces = (
            (0, first_send),
            (width, first_recv),
            (2 * width, third_ref[0:width, :]),
            (3 * width, second_ref[0:width, :]),
            (4 * width, node_grad_ref[...]),
            (table_rows, vector_rows),
            (table_rows + 8, table_grad),
        )
        odd = core_ref[0] == 1
        for start, piece in pieces:
            left, right = piece[:, 0:LANES], piece[:, LANES:]
            kept_ref[start : start + piece.shape[0], :] = jnp.where(odd, right, left)
            sent_ref[start : start + piece.shape[0], :] = jnp.where(odd, left, right)


def edge_backward(
    core, recv, send, regions, near_back, near, edges, hidden, slope, unit, inverse, weights, vectors,
    node_grad, node_sum, region_count,
):
    count, width = edges.shape
    nodes = near[0].shape[0]
    steps = count // TILE
    last = steps - 1
    tile = pl.BlockSpec((TILE, width), lambda i: (jnp.minimum(i, last), 0))
    thin = pl.BlockSpec((TILE, LANES), lambda i: (jnp.minimum(i, last), 0))
    node = whole((nodes, width))
    grad_rows = weights.shape[0]
    row = whole((1, count))
    half = whole((grad_rows, LANES))
    return pl.pallas_call(
        edge_backward_kernel,
        grid=(steps + 1,),
        in_specs=[
            pl.BlockSpec(memory_space=pltpu.SMEM), whole((count // LANES, LANES)), row, row, row,
            node, node, node, node, node, node, tile, tile, tile, tile, thin,
            whole(weights.shape), whole(vectors.shape), whole(node_grad.shape), whole(node_sum.shape),
        ],
        out_specs=[tile, half, half, node, node, node],
        out_shape=[
            jax.ShapeDtypeStruct((count, width), B16),
            jax.ShapeDtypeStruct((grad_rows, LANES), F32),
            jax.ShapeDtypeStruct((grad_rows, LANES), F32),
            jax.ShapeDtypeStruct((nodes, width), F32),
            jax.ShapeDtypeStruct((nodes, width), B16),
            jax.ShapeDtypeStruct((nodes, width), B16),
        ],
        scratch_shapes=[
            pltpu.VMEM((count, width), B16),
            pltpu.VMEM((width + 16, width), F32),
            pltpu.VMEM((width + region_count, width), F32),
            pltpu.VMEM((16, width), F32),
        ],
        compiler_params=PARAMS,
        name="edge_backward",
        cost_estimate=pl.CostEstimate(
            flops=2 * count * width * (5 * width + 9 * nodes), transcendentals=0, bytes_accessed=count * width * 16
        ),
    )(
        core, recv.reshape(-1, LANES), send.reshape(1, -1), recv.reshape(1, -1), regions.reshape(1, -1),
        *near_back, *near, edges, hidden, slope, unit, inverse, weights, vectors, node_grad, node_sum,
    )


def flipped(value, axis, bit):
    return lax.ppermute(value, axis, [(i, i ^ bit) for i in range(lax.axis_size(axis))])


def across(value, axis):
    count = lax.axis_size(axis)
    return lax.ppermute(value, axis, [(i, (i + 1 if i % 2 else i - 1) % count) for i in range(count)])


def neighbours(value):
    off = across(value, "edge")
    return flipped(value, "edge", 1), off


def on_device(
    node_latents, edge_latents, senders, receivers, regions, forced, params, first_moment, second_moment,
    averaged, step, cotangent,
):
    latents = node_latents[0]
    edges = edge_latents[0]
    upstream = cotangent[0]
    nodes, width = latents.shape
    share = params.shape[0]
    e, f = lax.axis_index("edge"), lax.axis_index("feat")
    blocks, feats = lax.axis_size("edge"), lax.axis_size("feat")
    core = e % 2
    total = share * feats
    vector_row = 7 * width
    region_count = total - vector_row - 8

    pair, off = neighbours(latents)

    mine = lax.dynamic_slice_in_dim(params, core * LANES, LANES, 1).astype(B16)
    shares = jnp.stack([mine] + [flipped(mine, "feat", k) for k in range(1, feats)])
    mine = jnp.concatenate([lax.dynamic_index_in_dim(shares, k ^ f, 0, keepdims=False) for k in range(feats)])
    other = flipped(mine, "edge", 1)
    odd = core == 1
    weights = jnp.concatenate([jnp.where(odd, other, mine), jnp.where(odd, mine, other)], axis=1)
    vectors = weights[vector_row : vector_row + 8].astype(F32)
    table = jnp.pad(weights[vector_row + 8 :], ((0, LANES - region_count), (0, 0)))

    def local(index):
        block = index // nodes
        slot = jnp.where(block == e, 0, jnp.where(block == e + 1 - 2 * core, 1, 2))
        return slot * nodes + index % nodes

    send, recv = local(senders), local(receivers)

    hs, hr = gather_latents(send, recv, latents, pair, off)
    hidden, slope, unit, inverse, high, low, to_pair, to_off = edge_forward(
        regions, recv, hs, hr, edges, weights, table, vectors, nodes, F32
    )
    from_off = across(to_off, "edge")
    from_pair = flipped(to_pair, "edge", 1)
    own = own_sum(recv, high, low, nodes)

    keep = (1 - forced)[:, None]
    new_latents, d_agg, agg, node_hidden, d_inner, d_pre, node_sum = node_update(
        latents, own, from_pair, from_off, weights, vectors, keep, upstream
    )
    back_pair, back_off = neighbours(d_agg)
    node_grad, back = node_grads(latents, agg, node_hidden, d_inner, d_pre, weights, upstream)

    grad_edges, kept, sent, part_own, part_pair, part_off = edge_backward(
        core.reshape(1), recv, send, regions, (d_agg, back_pair, back_off), (latents, pair, off),
        edges, hidden, slope, unit, inverse, weights, vectors, node_grad, node_sum, region_count,
    )

    grad = kept + flipped(sent, "edge", 1)
    low_rows = vector_row % share

    def packed(values):
        top, rest = split(values)
        return jnp.concatenate([top, rest[..., low_rows : low_rows + 8, :]], axis=-2)

    def unpacked(values):
        values = values.astype(F32)
        rest = jnp.pad(values[..., share:, :], ((0, 0),) * (values.ndim - 2) + ((low_rows, share - low_rows - 8), (0, 0)))
        return values[..., :share, :] + rest

    part = grad.reshape(feats, share, LANES)
    bit = 1
    while bit < feats:
        part = part.reshape(-1, 2, share, LANES)
        here = (f // bit) % 2
        keep_part = lax.dynamic_index_in_dim(part, here, 1, keepdims=False)
        send_part = lax.dynamic_index_in_dim(part, 1 - here, 1, keepdims=False)
        part = keep_part + unpacked(flipped(packed(send_part), "feat", bit))
        bit *= 2
    part = part.reshape(share, LANES)

    grads_off = across(part_off, "edge").astype(F32)
    grads_pair = flipped(part_pair, "edge", 1).astype(F32)
    grad_latents = back + part_own + grads_pair + grads_off

    bit = 2
    while bit < blocks:
        wire = packed(part)
        part = unpacked(wire) + unpacked(flipped(wire, "edge", bit))
        bit *= 2

    owner = vector_row // share
    rows = jnp.where(f == owner, part[low_rows : low_rows + 8], 0.0)
    squares = jnp.broadcast_to(jnp.sum(part * part), (8, LANES))
    stats = jnp.concatenate([rows, squares], axis=0)
    bit = 1
    while bit < feats:
        stats = stats + flipped(stats, "feat", bit)
        bit *= 2
    both = flipped(jnp.concatenate([part, stats], axis=0), "edge", 1)
    there, stats_there = both[:share], both[share:]
    grad_norm = jnp.sqrt(stats[8, 0] + stats_there[8, 0])

    def joined(here_half, there_half):
        return jnp.concatenate(
            [jnp.where(odd, there_half, here_half), jnp.where(odd, here_half, there_half)], axis=1
        )

    factor = jnp.minimum(1.0, MAX_NORM / (grad_norm + 1e-06))
    clipped = joined(part, there) * factor
    vector_grads = joined(stats[:8], stats_there[:8]) * factor
    new_first = BETA_ONE * first_moment + (1.0 - BETA_ONE) * clipped
    new_second = BETA_TWO * second_moment + (1.0 - BETA_TWO) * clipped * clipped
    count_steps = step[0].astype(F32)
    first_hat = new_first / (1.0 - jnp.power(BETA_ONE, count_steps))
    second_hat = new_second / (1.0 - jnp.power(BETA_TWO, count_steps))
    new_params = params - RATE * (first_hat / (jnp.sqrt(second_hat) + ADAM_EPS) + WEIGHT_DECAY * params)
    decay_now = jnp.minimum(AVERAGE_DECAY, (1.0 + count_steps) / (10.0 + count_steps))
    new_average = decay_now * averaged + (1.0 - decay_now) * new_params
    return (
        new_latents[None],
        grad_latents[None],
        grad_edges[None],
        new_first,
        new_second,
        new_params,
        new_average,
        grad_norm.reshape(1),
        vector_grads,
    )


def solution(mesh):
    nodes, rows = P("feat", "edge", None), P("feat", None)
    return jax.shard_map(
        on_device,
        mesh=mesh,
        in_specs=(nodes, nodes, P("edge"), P("edge"), P("edge"), P("edge"), rows, rows, rows, rows, P(), nodes),
        out_specs=(nodes, nodes, nodes, rows, rows, rows, rows, P(), P()),
        check_vma=False,
    )
```

```python
import functools

import jax
import jax.numpy as jnp
from jax import lax
from jax.experimental import pallas as pl
from jax.experimental.pallas import tpu as pltpu
from jax.sharding import PartitionSpec as P

NORM_EPS = 1e-05
MAX_NORM = 512.0
RATE = 0.05
BETA_ONE = 0.9
BETA_TWO = 0.95
ADAM_EPS = 1e-08
WEIGHT_DECAY = 0.1
AVERAGE_DECAY = 0.999

LANES = 128
TILE = 1024
B16 = jnp.bfloat16
F32 = jnp.float32
I32 = jnp.int32
PARAMS = pltpu.CompilerParams(vmem_limit_bytes=20 * 1024 * 1024)


def dot(left, right):
    return jnp.dot(left, right, preferred_element_type=F32)


def dot_rows(left, right):
    return lax.dot_general(left, right, (((0,), (0,)), ((), ())), preferred_element_type=F32)


def dot_back(left, right):
    return lax.dot_general(left, right, (((1,), (1,)), ((), ())), preferred_element_type=F32)


def split(values):
    high = values.astype(B16)
    return high, (values - high.astype(F32)).astype(B16)


def whole(shape):
    return pl.BlockSpec(shape, lambda i: (0,) * len(shape))


def tiled(rows, cols):
    return pl.BlockSpec((rows, cols), lambda i: (i, 0))


def column(row):
    return jnp.broadcast_to(row, (LANES, LANES)).T


def chosen_columns(index_ref, tile, rows, first, last):
    lane = lax.broadcasted_iota(I32, (LANES, LANES), 1)
    groups = []
    for g in range(rows // LANES):
        col = column(index_ref[pl.ds(tile * (rows // LANES) + g, 1), :])
        groups.append(
            jnp.concatenate(
                [jnp.where(col == lane + base, 1.0, 0.0).astype(B16) for base in range(first, last, LANES)],
                axis=1,
            )
        )
    return jnp.concatenate(groups, axis=0)


def chosen_rows(index_row, first, count):
    node = lax.broadcasted_iota(I32, (count, index_row.shape[1]), 0) + first
    return jnp.where(index_row == node, 1.0, 0.0).astype(B16)


def gather_near_kernel(index_ref, own_ref, pair_ref, out_ref):
    tile = pl.program_id(0)
    rows = out_ref.shape[0]
    nodes = own_ref.shape[0]
    total = dot(chosen_columns(index_ref, tile, rows, 0, nodes), own_ref[...])
    total = total + dot(chosen_columns(index_ref, tile, rows, nodes, 2 * nodes), pair_ref[...])
    out_ref[...] = total.astype(B16)


def gather_near(index, own, pair):
    nodes, width = own.shape
    edges = index.size
    return pl.pallas_call(
        gather_near_kernel,
        grid=(edges // TILE,),
        in_specs=[whole((edges // LANES, LANES))] + [whole((nodes, width))] * 2,
        out_specs=tiled(TILE, width),
        out_shape=jax.ShapeDtypeStruct((edges, width), B16),
        compiler_params=PARAMS,
        name="gather_near",
        cost_estimate=pl.CostEstimate(
            flops=2 * edges * 2 * nodes * width, transcendentals=0, bytes_accessed=edges * width * 2
        ),
    )(index.reshape(-1, LANES), own, pair)


def gather_off_kernel(index_ref, off_ref, near_ref, out_ref):
    tile = pl.program_id(0)
    rows = out_ref.shape[0]
    nodes = off_ref.shape[0]
    total = dot(chosen_columns(index_ref, tile, rows, 2 * nodes, 3 * nodes), off_ref[...])
    out_ref[...] = (total + near_ref[...].astype(F32)).astype(B16)


def gather_off(index, off, near):
    nodes, width = off.shape
    edges = index.size
    return pl.pallas_call(
        gather_off_kernel,
        grid=(edges // TILE,),
        in_specs=[whole((edges // LANES, LANES)), whole((nodes, width)), tiled(TILE, width)],
        out_specs=tiled(TILE, width),
        out_shape=jax.ShapeDtypeStruct((edges, width), B16),
        compiler_params=PARAMS,
        name="gather_off",
        cost_estimate=pl.CostEstimate(
            flops=2 * edges * nodes * width, transcendentals=0, bytes_accessed=edges * width * 4
        ),
    )(index.reshape(-1, LANES), off, near)


def edge_forward_kernel(
    place_ref, region_ref, recv_row_ref, hs_ref, hr_ref, x_ref, *refs,
):
    pieces, refs = refs[:-9], refs[-9:]
    w_ref, hidden_ref, slope_ref, unit_ref, inverse_ref, high_ref, low_ref, halo_ref, wide_ref = refs
    step = pl.program_id(0)
    rows = x_ref.shape[0]
    width = x_ref.shape[1]
    nodes = halo_ref.shape[0]
    steps = pl.num_programs(0)
    vector_row = 7 * width
    regions = w_ref.shape[0] - vector_row - 8

    @pl.when(step == 0)
    def _():
        odd = place_ref[0] == 1
        shares = len(pieces) // 2
        share = pieces[0].shape[0]
        for k in range(shares):
            mine, other = pieces[k][...].astype(F32), pieces[shares + k][...].astype(F32)
            base = pl.multiple_of(place_ref[2 + k] * share, 8)
            wide_ref[pl.ds(base, share), 0:LANES] = jnp.where(odd, other, mine)
            wide_ref[pl.ds(base, share), LANES : 2 * LANES] = jnp.where(odd, mine, other)
        w_ref[...] = wide_ref[...].astype(B16)

    @pl.when(step < steps - 1)
    def _():
        vec = wide_ref[vector_row : vector_row + 8, :]
        table = jnp.concatenate(
            [wide_ref[vector_row + 8 :, :], jnp.zeros((LANES - regions, width), F32)], axis=0
        ).astype(B16)
        pre = dot(hs_ref[...], w_ref[0:width, :])
        pre = pre + dot(hr_ref[...], w_ref[width : 2 * width, :])
        pre = pre + dot(x_ref[...], w_ref[2 * width : 3 * width, :])
        pre = pre + dot(chosen_columns(region_ref, step, rows, 0, LANES), table)
        pre = pre + vec[0:1, :]
        sigma = 1.0 / (1.0 + jnp.exp(-pre))
        hidden = (pre * sigma).astype(B16)
        hidden_ref[...] = hidden
        slope_ref[...] = sigma * (1.0 + pre * (1.0 - sigma))
        inner = dot(hidden, w_ref[3 * width : 4 * width, :]) + vec[1:2, :]
        center = inner - jnp.mean(inner, axis=-1, keepdims=True)
        inverse = lax.rsqrt(jnp.mean(center * center, axis=-1, keepdims=True) + NORM_EPS)
        unit = center * inverse
        unit_ref[...] = unit
        inverse_ref[...] = jnp.broadcast_to(inverse, (rows, LANES))
        high, low = split(unit * vec[2:3, :] + vec[3:4, :])
        base = pl.multiple_of(step * rows, rows)
        high_ref[pl.ds(base, rows), :] = high
        low_ref[pl.ds(base, rows), :] = low

    @pl.when(step == steps - 1)
    def _():
        onehot = chosen_rows(recv_row_ref[...], 2 * nodes, nodes)
        halo_ref[...] = dot(onehot, high_ref[...]) + dot(onehot, low_ref[...])


def edge_forward(place, regions, recv, hs, hr, edges, pieces, total, nodes):
    count, width = edges.shape
    steps = count // TILE
    last = steps - 1
    tile = pl.BlockSpec((TILE, width), lambda i: (jnp.minimum(i, last), 0))
    thin = pl.BlockSpec((TILE, LANES), lambda i: (jnp.minimum(i, last), 0))
    return pl.pallas_call(
        edge_forward_kernel,
        grid=(steps + 1,),
        in_specs=[
            pl.BlockSpec(memory_space=pltpu.SMEM), whole((count // LANES, LANES)), whole((1, count)), tile, tile, tile,
            *[whole(piece.shape) for piece in pieces],
        ],
        out_specs=[
            whole((total, width)), tile, tile, tile, thin, whole((count, width)), whole((count, width)),
            whole((nodes, width)),
        ],
        out_shape=[
            jax.ShapeDtypeStruct((total, width), B16),
            jax.ShapeDtypeStruct((count, width), B16),
            jax.ShapeDtypeStruct((count, width), F32),
            jax.ShapeDtypeStruct((count, width), F32),
            jax.ShapeDtypeStruct((count, LANES), F32),
            jax.ShapeDtypeStruct((count, width), B16),
            jax.ShapeDtypeStruct((count, width), B16),
            jax.ShapeDtypeStruct((nodes, width), F32),
        ],
        scratch_shapes=[pltpu.VMEM((total, width), F32)],
        compiler_params=PARAMS,
        name="edge_forward",
        cost_estimate=pl.CostEstimate(
            flops=2 * count * width * (5 * width + 2 * nodes), transcendentals=2 * count * width,
            bytes_accessed=count * width * 20,
        ),
    )(place, regions.reshape(-1, LANES), recv.reshape(1, -1), hs, hr, edges, *pieces)


def near_sum_kernel(recv_row_ref, high_ref, low_ref, pair_ref, own_ref):
    nodes = own_ref.shape[0]
    for first, out_ref in ((nodes, pair_ref), (0, own_ref)):
        onehot = chosen_rows(recv_row_ref[...], first, nodes)
        out_ref[...] = dot(onehot, high_ref[...]) + dot(onehot, low_ref[...])


def near_sum(recv, high, low, nodes):
    count, width = high.shape
    out = jax.ShapeDtypeStruct((nodes, width), F32)
    return pl.pallas_call(
        near_sum_kernel,
        out_shape=[out, out],
        compiler_params=PARAMS,
        name="near_sum",
        cost_estimate=pl.CostEstimate(
            flops=8 * count * width * nodes, transcendentals=0, bytes_accessed=count * width * 4
        ),
    )(recv.reshape(1, -1), high, low)


def vectors_of(w_ref, width):
    return w_ref[7 * width : 7 * width + 8, :].astype(F32)


def node_kernel(
    h_ref, agg_ref, w_ref, forced_ref, up_ref,
    new_ref, d_agg_ref, hidden_ref, d_inner_ref, d_pre_ref, sums_ref,
):
    width = h_ref.shape[1]
    vec = vectors_of(w_ref, width)
    agg = agg_ref[...]
    h = h_ref[...]
    latent, aggregate = w_ref[4 * width : 5 * width, :], w_ref[5 * width : 6 * width, :]
    second = w_ref[6 * width : 7 * width, :]
    pre = dot(h, latent) + dot(agg, aggregate) + vec[4:5, :]
    sigma = 1.0 / (1.0 + jnp.exp(-pre))
    hidden = (pre * sigma).astype(B16)
    hidden_ref[...] = hidden
    inner = dot(hidden, second) + vec[5:6, :]
    center = inner - jnp.mean(inner, axis=-1, keepdims=True)
    inverse = lax.rsqrt(jnp.mean(center * center, axis=-1, keepdims=True) + NORM_EPS)
    unit = center * inverse
    keep = [column(forced_ref[g : g + 1, :]) for g in range(forced_ref.shape[0])]
    keep = 1.0 - jnp.concatenate(keep, axis=0).astype(F32)
    keep = jnp.concatenate([keep] * (width // LANES), axis=1)
    new_ref[...] = h.astype(F32) + keep * (unit * vec[6:7, :] + vec[7:8, :])
    d_update = keep * up_ref[...]
    scaled = d_update * vec[6:7, :]
    d_inner = inverse * (
        scaled
        - jnp.mean(scaled, axis=-1, keepdims=True)
        - unit * jnp.mean(scaled * unit, axis=-1, keepdims=True)
    )
    d_inner = d_inner.astype(B16)
    d_inner_ref[...] = d_inner
    slope = sigma * (1.0 + pre * (1.0 - sigma))
    d_pre = (dot_back(d_inner, second) * slope).astype(B16)
    d_pre_ref[...] = d_pre
    d_agg_ref[...] = dot_back(d_pre, aggregate).astype(B16)
    sums_ref[...] = jnp.concatenate(
        [
            jnp.sum(d_pre.astype(F32), axis=0, keepdims=True),
            jnp.sum(d_inner.astype(F32), axis=0, keepdims=True),
            jnp.sum(d_update * unit, axis=0, keepdims=True),
            jnp.sum(d_update, axis=0, keepdims=True),
        ],
        axis=0,
    )


def node_update(h, agg, weights, forced, upstream):
    nodes, width = h.shape
    full = jax.ShapeDtypeStruct((nodes, width), F32)
    half = jax.ShapeDtypeStruct((nodes, width), B16)
    return pl.pallas_call(
        node_kernel,
        out_shape=[full, half, half, half, half, jax.ShapeDtypeStruct((4, width), F32)],
        compiler_params=PARAMS,
        name="node_update",
        cost_estimate=pl.CostEstimate(
            flops=2 * nodes * width * width * 5, transcendentals=2 * nodes * width, bytes_accessed=nodes * width * 20
        ),
    )(h, agg, weights, forced.reshape(-1, LANES), upstream)


def node_grads_kernel(h_ref, agg_ref, hidden_ref, d_inner_ref, d_pre_ref, w_ref, up_ref, grad_ref, back_ref):
    width = h_ref.shape[1]
    d_pre = d_pre_ref[...]
    grad_ref[0:width, :] = dot_rows(h_ref[...], d_pre)
    grad_ref[width : 2 * width, :] = dot_rows(agg_ref[...], d_pre)
    grad_ref[2 * width : 3 * width, :] = dot_rows(hidden_ref[...], d_inner_ref[...])
    back_ref[...] = up_ref[...] + dot_back(d_pre, w_ref[4 * width : 5 * width, :])


def node_grads(h, agg, hidden, d_inner, d_pre, weights, upstream):
    nodes, width = h.shape
    return pl.pallas_call(
        node_grads_kernel,
        out_shape=[jax.ShapeDtypeStruct((3 * width, width), F32), jax.ShapeDtypeStruct((nodes, width), F32)],
        compiler_params=PARAMS,
        name="node_grads",
        cost_estimate=pl.CostEstimate(
            flops=2 * nodes * width * width * 4, transcendentals=0, bytes_accessed=nodes * width * 18
        ),
    )(h, agg, hidden, d_inner, d_pre, weights, upstream)


def edge_backward_kernel(
    place_ref, recv_ref, region_row_ref, off_ref, near_ref, hs_ref, hr_ref, x_ref, hidden_ref, slope_ref, unit_ref,
    inverse_ref, w_ref, node_grad_ref, node_sum_ref,
    d_pre_ref, kept_ref, sent_ref,
    first_ref, second_ref, table_ref, vec_acc_ref,
):
    step = pl.program_id(0)
    steps = pl.num_programs(0)
    rows, width = x_ref.shape
    nodes = off_ref.shape[0]
    regions = table_ref.shape[0]
    vec = vectors_of(w_ref, width)

    @pl.when(step == 0)
    def _():
        first_ref[...] = jnp.zeros_like(first_ref)
        second_ref[...] = jnp.zeros_like(second_ref)
        table_ref[...] = jnp.zeros_like(table_ref)
        vec_acc_ref[...] = jnp.zeros_like(vec_acc_ref)

    d_message = dot(chosen_columns(recv_ref, step, rows, 2 * nodes, 3 * nodes), off_ref[...])
    d_message = d_message + near_ref[...].astype(F32)
    unit = unit_ref[...]
    scaled = d_message * vec[2:3, :]
    inverse = inverse_ref[:, 0:1]
    d_inner = inverse * (
        scaled
        - jnp.mean(scaled, axis=-1, keepdims=True)
        - unit * jnp.mean(scaled * unit, axis=-1, keepdims=True)
    )
    vec_acc_ref[0:8, :] += jnp.sum((d_message * unit).reshape(rows // 8, 8, width), axis=0)
    vec_acc_ref[8:16, :] += jnp.sum(d_message.reshape(rows // 8, 8, width), axis=0)
    d_inner = d_inner.astype(B16)
    second_ref[0:width, :] += dot_rows(hidden_ref[...], d_inner)
    second_ref[width : width + 16, :] += dot(jnp.ones((16, rows), B16), d_inner)
    d_pre = (dot_back(d_inner, w_ref[3 * width : 4 * width, :]) * slope_ref[...]).astype(B16)
    d_pre_ref[...] = d_pre
    first_ref[0:width, :] += dot_rows(hs_ref[...], d_pre)
    first_ref[width : 2 * width, :] += dot_rows(hr_ref[...], d_pre)
    first_ref[2 * width : 3 * width, :] += dot_rows(x_ref[...], d_pre)
    base = pl.multiple_of(step * rows, rows)
    region_row = region_row_ref[:, pl.ds(base, rows)]
    table_ref[...] += dot(chosen_rows(region_row, 0, regions), d_pre)

    @pl.when(step == steps - 1)
    def _():
        table_rows = node_grad_ref.shape[0] + 4 * width
        table_grad = table_ref[...]
        vector_rows = jnp.concatenate(
            [
                jnp.sum(table_grad, axis=0, keepdims=True),
                second_ref[width : width + 1, :],
                jnp.sum(vec_acc_ref[0:8, :], axis=0, keepdims=True),
                jnp.sum(vec_acc_ref[8:16, :], axis=0, keepdims=True),
                node_sum_ref[...],
            ],
            axis=0,
        )
        pieces = (
            (0, first_ref[...]),
            (3 * width, second_ref[0:width, :]),
            (4 * width, node_grad_ref[...]),
            (table_rows, vector_rows),
            (table_rows + 8, table_grad),
        )
        odd = place_ref[0] == 1
        for start, piece in pieces:
            left, right = piece[:, 0:LANES], piece[:, LANES:]
            kept_ref[start : start + piece.shape[0], :] = jnp.where(odd, right, left)
            sent_ref[start : start + piece.shape[0], :] = jnp.where(odd, left, right)


def edge_backward(
    place, recv, regions, off, near, hs, hr, edges, hidden, slope, unit, inverse, weights, node_grad, node_sum,
    region_count,
):
    count, width = edges.shape
    tile = tiled(TILE, width)
    grad_rows = weights.shape[0]
    half = whole((grad_rows, LANES))
    return pl.pallas_call(
        edge_backward_kernel,
        grid=(count // TILE,),
        in_specs=[
            pl.BlockSpec(memory_space=pltpu.SMEM), whole((count // LANES, LANES)), whole((1, count)),
            whole(off.shape), tile, tile, tile, tile, tile, tile, tile, tiled(TILE, LANES),
            whole(weights.shape), whole(node_grad.shape), whole(node_sum.shape),
        ],
        out_specs=[tile, half, half],
        out_shape=[
            jax.ShapeDtypeStruct((count, width), B16),
            jax.ShapeDtypeStruct((grad_rows, LANES), F32),
            jax.ShapeDtypeStruct((grad_rows, LANES), F32),
        ],
        scratch_shapes=[
            pltpu.VMEM((3 * width, width), F32),
            pltpu.VMEM((width + 16, width), F32),
            pltpu.VMEM((region_count, width), F32),
            pltpu.VMEM((16, width), F32),
        ],
        compiler_params=PARAMS,
        name="edge_backward",
        cost_estimate=pl.CostEstimate(
            flops=2 * count * width * (6 * width + off.shape[0]), transcendentals=0, bytes_accessed=count * width * 20
        ),
    )(
        place, recv.reshape(-1, LANES), regions.reshape(1, -1), off, near, hs, hr, edges, hidden, slope, unit, inverse,
        weights, node_grad, node_sum,
    )


def node_part_kernel(index_row_ref, d_pre_ref, w_ref, out_ref, *, first):
    width = d_pre_ref.shape[1]
    weight = w_ref[first : first + width, :]
    count = out_ref.shape[0]
    base = pl.program_id(0) * count
    high, low = split(dot(chosen_rows(index_row_ref[...], base, count), d_pre_ref[...]))
    out_ref[...] = dot_back(high, weight) + dot_back(low, weight)


def node_part(index, d_pre, weights, first, nodes):
    count, width = d_pre.shape
    return pl.pallas_call(
        functools.partial(node_part_kernel, first=first),
        grid=(3,),
        in_specs=[whole((1, count)), whole((count, width)), whole(weights.shape)],
        out_specs=tiled(nodes, width),
        out_shape=jax.ShapeDtypeStruct((3 * nodes, width), F32),
        compiler_params=PARAMS,
        name="node_part",
        cost_estimate=pl.CostEstimate(
            flops=6 * count * width * nodes, transcendentals=0, bytes_accessed=count * width * 2
        ),
    )(index.reshape(1, -1), d_pre, weights)


def edge_grads_kernel(d_pre_ref, w_ref, out_ref):
    width = d_pre_ref.shape[1]
    out_ref[...] = dot_back(d_pre_ref[...], w_ref[2 * width : 3 * width, :]).astype(B16)


def edge_grads(d_pre, weights):
    count, width = d_pre.shape
    return pl.pallas_call(
        edge_grads_kernel,
        grid=(count // TILE,),
        in_specs=[tiled(TILE, width), whole(weights.shape)],
        out_specs=tiled(TILE, width),
        out_shape=jax.ShapeDtypeStruct((count, width), B16),
        compiler_params=PARAMS,
        name="edge_grads",
        cost_estimate=pl.CostEstimate(
            flops=2 * count * width * width, transcendentals=0, bytes_accessed=count * width * 4
        ),
    )(d_pre, weights)


def finish_kernel(place_ref, mine_ref, other_ref, out_ref, *, first):
    share = out_ref.shape[0] - 16
    rest = slice(share, share + 8)
    rows = slice(first, first + 8)
    part = mine_ref[0:share, :].astype(F32) + other_ref[0:share, :].astype(F32)
    exact = part[rows, :] + (mine_ref[rest, :].astype(F32) + other_ref[rest, :].astype(F32))
    out_ref[0:share, :] = part
    out_ref[rows, :] = exact
    part = out_ref[0:share, :]
    out_ref[share : share + 8, :] = jnp.where(place_ref[1] == 1, exact, 0.0)
    squares = jnp.sum(jnp.sum(part * part, axis=0, keepdims=True), axis=1, keepdims=True)
    out_ref[share + 8 : share + 16, :] = jnp.broadcast_to(squares, (8, LANES))


def finish(place, mine, other, share, first):
    return pl.pallas_call(
        functools.partial(finish_kernel, first=first),
        in_specs=[pl.BlockSpec(memory_space=pltpu.SMEM)] + [pl.BlockSpec(memory_space=pltpu.VMEM)] * 2,
        out_shape=jax.ShapeDtypeStruct((share + 16, LANES), F32),
        compiler_params=PARAMS,
        name="finish",
    )(place, mine, other)


def adam_kernel(
    place_ref, step_ref, stats_ref, more_ref, mine_ref, other_ref, params_ref, first_ref, second_ref, averaged_ref,
    new_first_ref, new_second_ref, new_params_ref, new_average_ref, norm_ref, vector_ref,
):
    share = params_ref.shape[0]
    odd = place_ref[0] == 1
    stats = stats_ref[...] + more_ref[...]
    norm = jnp.sqrt(stats[8:9, 0:1] + stats[24:25, 0:1])
    norm_ref[...] = norm
    factor = jnp.minimum(1.0, MAX_NORM / (norm + 1e-06))
    count = jnp.full((1, 1), step_ref[0], F32)
    first_scale = 1.0 - jnp.exp(count * jnp.log(jnp.full((1, 1), BETA_ONE, F32)))
    second_scale = 1.0 - jnp.exp(count * jnp.log(jnp.full((1, 1), BETA_TWO, F32)))
    decay = jnp.minimum(AVERAGE_DECAY, (1.0 + count) / (10.0 + count))
    for half in range(2):
        swap = odd if half == 0 else jnp.logical_not(odd)
        lanes = slice(half * LANES, (half + 1) * LANES)
        vector_ref[:, lanes] = jnp.where(swap, stats[16:24, :], stats[0:8, :]) * factor
        clipped = jnp.where(swap, other_ref[0:share, :], mine_ref[0:share, :]) * factor
        params = params_ref[:, lanes]
        new_first = BETA_ONE * first_ref[:, lanes] + (1.0 - BETA_ONE) * clipped
        new_second = BETA_TWO * second_ref[:, lanes] + (1.0 - BETA_TWO) * clipped * clipped
        new_first_ref[:, lanes] = new_first
        new_second_ref[:, lanes] = new_second
        first_hat = new_first / first_scale
        second_hat = new_second / second_scale
        new_params = params - RATE * (first_hat / (jnp.sqrt(second_hat) + ADAM_EPS) + WEIGHT_DECAY * params)
        new_params_ref[:, lanes] = new_params
        new_average_ref[:, lanes] = decay * averaged_ref[:, lanes] + (1.0 - decay) * new_params


def adam(place, step, stats, more, mine, other, params, first_moment, second_moment, averaged):
    rows = jax.ShapeDtypeStruct(params.shape, F32)
    smem, vmem = pl.BlockSpec(memory_space=pltpu.SMEM), pl.BlockSpec(memory_space=pltpu.VMEM)
    return pl.pallas_call(
        adam_kernel,
        in_specs=[smem, smem] + [vmem] * 8,
        out_shape=[rows, rows, rows, rows, jax.ShapeDtypeStruct((1, 1), F32), jax.ShapeDtypeStruct((8, params.shape[1]), F32)],
        compiler_params=PARAMS,
        name="adam",
        cost_estimate=pl.CostEstimate(
            flops=20 * params.size, transcendentals=2 * params.size, bytes_accessed=params.size * 32
        ),
    )(place, step, stats, more, mine, other, params, first_moment, second_moment, averaged)


def flipped(value, axis, bit):
    return lax.ppermute(value, axis, [(i, i ^ bit) for i in range(lax.axis_size(axis))])


def across(value, axis):
    count = lax.axis_size(axis)
    return lax.ppermute(value, axis, [(i, (i + 1 if i % 2 else i - 1) % count) for i in range(count)])


def neighbours(value):
    off = across(value, "edge")
    return flipped(value, "edge", 1), off


def on_device(
    node_latents, edge_latents, senders, receivers, regions, forced, params, first_moment, second_moment,
    averaged, step, cotangent,
):
    latents = node_latents[0]
    edges = edge_latents[0]
    upstream = cotangent[0]
    nodes, width = latents.shape
    share = params.shape[0]
    e, f = lax.axis_index("edge"), lax.axis_index("feat")
    blocks, feats = lax.axis_size("edge"), lax.axis_size("feat")
    core = e % 2
    total = share * feats
    vector_row = 7 * width
    region_count = total - vector_row - 8

    pair, off = neighbours(latents)

    mine = lax.dynamic_slice_in_dim(params, core * LANES, LANES, 1).astype(B16)
    fetched = [mine] + [flipped(mine, "feat", k) for k in range(1, feats)]
    owner = (f == vector_row // share).astype(I32)
    place = jnp.stack([core, owner] + [f ^ k for k in range(feats)])

    def local(index):
        block = index // nodes
        slot = jnp.where(block == e, 0, jnp.where(block == e + 1 - 2 * core, 1, 2))
        return slot * nodes + index % nodes

    send, recv = local(senders), local(receivers)

    near_send = gather_near(send, latents, pair)
    near_recv = gather_near(recv, latents, pair)
    fetched = lax.optimization_barrier((near_recv, *fetched))[1:]
    pieces = [*fetched, *(flipped(piece, "edge", 1) for piece in fetched)]
    hs = gather_off(send, off, near_send)
    hr = gather_off(recv, off, near_recv)
    weights, hidden, slope, unit, inverse, high, low, to_off = edge_forward(
        place, regions, recv, hs, hr, edges, pieces, total, nodes
    )
    from_off = across(to_off, "edge")
    to_pair, own = near_sum(recv, high, low, nodes)
    from_pair = flipped(to_pair, "edge", 1)
    agg = (own + from_pair + from_off).astype(B16)

    new_latents, d_agg, node_hidden, d_inner, d_pre, node_sum = node_update(
        latents, agg, weights, forced, upstream
    )
    back_pair, back_off = neighbours(d_agg)
    node_grad, back = node_grads(latents, agg, node_hidden, d_inner, d_pre, weights, upstream)
    near = gather_near(recv, d_agg, back_pair)

    d_pre, kept, sent = edge_backward(
        place, recv, regions, back_off, near, hs, hr, edges, hidden, slope, unit, inverse, weights, node_grad, node_sum,
        region_count,
    )
    grad_edges = edge_grads(d_pre, weights)
    node_grads_send = node_part(send, d_pre, weights, 0, nodes)
    node_grads_recv = node_part(recv, d_pre, weights, width, nodes)
    part_own = node_grads_send[:nodes] + node_grads_recv[:nodes]
    part_halo = (node_grads_send[nodes:] + node_grads_recv[nodes:]).astype(B16)

    grad = kept + flipped(sent, "edge", 1)
    low_rows = vector_row % share

    def packed(values):
        top, rest = split(values)
        return jnp.concatenate([top, rest[..., low_rows : low_rows + 8, :]], axis=-2)

    def unpacked(values):
        values = values.astype(F32)
        rest = jnp.pad(values[..., share:, :], ((0, 0),) * (values.ndim - 2) + ((low_rows, share - low_rows - 8), (0, 0)))
        return values[..., :share, :] + rest

    part = grad.reshape(feats, share, LANES)
    bit = 1
    while bit < feats:
        part = part.reshape(-1, 2, share, LANES)
        here = (f // bit) % 2
        keep_part = lax.dynamic_index_in_dim(part, here, 1, keepdims=False)
        send_part = lax.dynamic_index_in_dim(part, 1 - here, 1, keepdims=False)
        part = keep_part + unpacked(flipped(packed(send_part), "feat", bit))
        bit *= 2
    part = part.reshape(share, LANES)

    grads_off = across(part_halo[nodes:], "edge").astype(F32)
    grads_pair = flipped(part_halo[:nodes], "edge", 1).astype(F32)
    grad_latents = back + part_own + grads_pair + grads_off

    wire = packed(part)
    bit = 2
    while 2 * bit < blocks:
        wire = packed(unpacked(wire) + unpacked(flipped(wire, "edge", bit)))
        bit *= 2
    mine = finish(place, wire, flipped(wire, "edge", bit), share, low_rows)
    other = flipped(mine, "edge", 1)
    stats = jnp.concatenate([mine[share:], other[share:]], axis=0)
    bit = 1
    while 2 * bit < feats:
        stats = stats + flipped(stats, "feat", bit)
        bit *= 2
    more = flipped(stats, "feat", bit)
    new_first, new_second, new_params, new_average, grad_norm, vector_grads = adam(
        place, step, stats, more, mine, other, params, first_moment, second_moment, averaged
    )
    return (
        new_latents[None],
        grad_latents[None],
        grad_edges[None],
        new_first,
        new_second,
        new_params,
        new_average,
        grad_norm.reshape(1),
        vector_grads,
    )


def solution(mesh):
    nodes, rows = P("feat", "edge", None), P("feat", None)
    return jax.shard_map(
        on_device,
        mesh=mesh,
        in_specs=(nodes, nodes, P("edge"), P("edge"), P("edge"), P("edge"), rows, rows, rows, rows, P(), nodes),
        out_specs=(nodes, nodes, nodes, rows, rows, rows, rows, P(), P()),
        check_vma=False,
    )
```

```python
import functools

import jax
import jax.numpy as jnp
from jax import lax
from jax.experimental import pallas as pl
from jax.experimental.pallas import tpu as pltpu
from jax.sharding import PartitionSpec as P

NORM_EPS = 1e-05
MAX_NORM = 512.0
RATE = 0.05
BETA_ONE = 0.9
BETA_TWO = 0.95
ADAM_EPS = 1e-08
WEIGHT_DECAY = 0.1
AVERAGE_DECAY = 0.999

LANES = 128
TINY = 1e-20
STEPS = 22
LOG_TWO = 0.6931471805599453
TILE = 2048
B16 = jnp.bfloat16
F32 = jnp.float32
I32 = jnp.int32
I16 = jnp.int16
PARAMS = pltpu.CompilerParams(vmem_limit_bytes=20 * 1024 * 1024)


def dot(left, right):
    return jnp.dot(left, right, preferred_element_type=F32)


def dot_rows(left, right):
    return lax.dot_general(left, right, (((0,), (0,)), ((), ())), preferred_element_type=F32)


def dot_back(left, right):
    return lax.dot_general(left, right, (((1,), (1,)), ((), ())), preferred_element_type=F32)


def vectors_of(w_ref, width):
    return w_ref[7 * width : 7 * width + 8, :].astype(F32)


def split(values):
    high = values.astype(B16)
    return high, (values - high.astype(F32)).astype(B16)


def whole(shape):
    return pl.BlockSpec(shape, lambda i: (0,) * len(shape))


def tiled(rows, cols):
    return pl.BlockSpec((rows, cols), lambda i: (i, 0))


def column(row):
    return jnp.broadcast_to(row, (LANES, LANES)).T


def chosen_columns(index_ref, tile, rows, first, last):
    lane = lax.broadcasted_iota(I32, (LANES, LANES), 1)
    groups = []
    for g in range(rows // LANES):
        col = column(index_ref[pl.ds(tile * (rows // LANES) + g, 1), :])
        groups.append(
            jnp.concatenate(
                [jnp.where(col == lane + base, 1.0, 0.0).astype(B16) for base in range(first, last, LANES)],
                axis=1,
            )
        )
    return jnp.concatenate(groups, axis=0)


def chosen_rows(index_row, first, count):
    node = lax.broadcasted_iota(I32, (count, index_row.shape[1]), 0) + first
    return jnp.where(index_row == node, 1.0, 0.0).astype(B16)


def prologue_kernel(
    params_hbm, send_hbm, recv_hbm, latents_hbm, half_ref, place_ref, send_ref, recv_ref, latents_ref,
    wide_ref, in_ref, sem, *, nodes, shares, owner,
):
    e, f = lax.axis_index("edge"), lax.axis_index("feat")
    core = e % 2
    lanes = pl.ds(pl.multiple_of(core * LANES, LANES), LANES)
    copies = [
        pltpu.make_async_copy(params_hbm.at[:, lanes], wide_ref, sem.at[0]),
        pltpu.make_async_copy(send_hbm, in_ref.at[0], sem.at[1]),
        pltpu.make_async_copy(recv_hbm, in_ref.at[1], sem.at[2]),
        pltpu.make_async_copy(latents_hbm, latents_ref, sem.at[3]),
    ]
    for copy in copies:
        copy.start()
    place_ref[0] = core
    place_ref[1] = e
    place_ref[2] = f
    place_ref[3] = jnp.where(f == owner, 1, 0)
    for k in range(shares):
        place_ref[4 + k] = jnp.bitwise_xor(f, k)
    for i, out_ref in ((0, send_ref), (1, recv_ref)):
        copies[1 + i].wait()
        index = in_ref[i]
        block = lax.div(index, nodes)
        slot = jnp.where(block == e, 0, jnp.where(block == e + 1 - 2 * core, 1, 2))
        out_ref[...] = (slot - block) * nodes + index
    copies[0].wait()
    half_ref[...] = wide_ref[...].astype(B16)
    copies[3].wait()


def prologue(params, senders, receivers, latents, shares, owner):
    shape = (senders.size // LANES, LANES)
    out = jax.ShapeDtypeStruct(shape, I32)
    vmem, hbm = pl.BlockSpec(memory_space=pltpu.VMEM), pl.BlockSpec(memory_space=pltpu.HBM)
    half, place, send, recv, own = pl.pallas_call(
        functools.partial(prologue_kernel, nodes=latents.shape[0], shares=shares, owner=owner),
        in_specs=[hbm] * 4,
        out_specs=[vmem, pl.BlockSpec(memory_space=pltpu.SMEM), vmem, vmem, vmem],
        out_shape=[
            jax.ShapeDtypeStruct((params.shape[0], LANES), B16), jax.ShapeDtypeStruct((4 + shares,), I32), out, out,
            jax.ShapeDtypeStruct(latents.shape, latents.dtype),
        ],
        scratch_shapes=[
            pltpu.VMEM((params.shape[0], LANES), F32), pltpu.VMEM((2, *shape), I32), pltpu.SemaphoreType.DMA((4,)),
        ],
        compiler_params=PARAMS,
        name="prologue",
    )(params, senders.reshape(shape), receivers.reshape(shape), latents)
    return half, place, send.reshape(-1), recv.reshape(-1), own


def gather_near_kernel(index_ref, own_ref, pair_ref, out_ref):
    tile = pl.program_id(0)
    rows = out_ref.shape[0]
    nodes = own_ref.shape[0]
    total = dot(chosen_columns(index_ref, tile, rows, 0, nodes), own_ref[...])
    total = total + dot(chosen_columns(index_ref, tile, rows, nodes, 2 * nodes), pair_ref[...])
    out_ref[...] = total.astype(B16)


def gather_near(index, own, pair):
    nodes, width = own.shape
    edges = index.size
    return pl.pallas_call(
        gather_near_kernel,
        grid=(1,),
        in_specs=[whole((edges // LANES, LANES))] + [whole((nodes, width))] * 2,
        out_specs=tiled(edges, width),
        out_shape=jax.ShapeDtypeStruct((edges, width), B16),
        compiler_params=PARAMS,
        name="gather_near",
        cost_estimate=pl.CostEstimate(
            flops=2 * edges * 2 * nodes * width, transcendentals=0, bytes_accessed=edges * width * 2
        ),
    )(index.reshape(-1, LANES), own, pair)


def gather_off_kernel(index_ref, off_ref, near_ref, out_ref):
    tile = pl.program_id(0)
    rows = out_ref.shape[0]
    nodes = off_ref.shape[0]
    total = dot(chosen_columns(index_ref, tile, rows, 2 * nodes, 3 * nodes), off_ref[...])
    out_ref[...] = (total + near_ref[...].astype(F32)).astype(B16)


def gather_off(index, off, near):
    nodes, width = off.shape
    edges = index.size
    return pl.pallas_call(
        gather_off_kernel,
        grid=(1,),
        in_specs=[whole((edges // LANES, LANES)), whole((nodes, width)), tiled(edges, width)],
        out_specs=tiled(edges, width),
        out_shape=jax.ShapeDtypeStruct((edges, width), B16),
        compiler_params=PARAMS,
        name="gather_off",
        cost_estimate=pl.CostEstimate(
            flops=2 * edges * nodes * width, transcendentals=0, bytes_accessed=edges * width * 4
        ),
    )(index.reshape(-1, LANES), off, near)


def before_silu(region_ref, tile, hs_ref, hr_ref, x_ref, w_ref):
    rows, width = x_ref.shape
    vector_row = 7 * width
    regions = w_ref.shape[0] - vector_row - 8
    table = jnp.concatenate(
        [w_ref[vector_row + 8 :, :].astype(F32), jnp.zeros((LANES - regions, width), F32)], axis=0
    ).astype(B16)
    pre = dot(hs_ref[...], w_ref[0:width, :])
    pre = pre + dot(hr_ref[...], w_ref[width : 2 * width, :])
    pre = pre + dot(x_ref[...], w_ref[2 * width : 3 * width, :])
    pre = pre + dot(chosen_columns(region_ref, tile, rows, 0, LANES), table)
    return pre + vectors_of(w_ref, width)[0:1, :]


def normalized(hidden, w_ref, vec):
    width = hidden.shape[1]
    inner = dot(hidden, w_ref[3 * width : 4 * width, :]) + vec[1:2, :]
    center = inner - jnp.mean(inner, axis=-1, keepdims=True)
    inverse = lax.rsqrt(jnp.mean(center * center, axis=-1, keepdims=True) + NORM_EPS)
    return center * inverse, inverse


def power_of_two(exponents):
    return jnp.exp(exponents * LOG_TWO)


def encoded(values):
    rows, width = values.shape
    half = width // 2
    largest = jnp.maximum(jnp.max(jnp.abs(values), axis=-1, keepdims=True), TINY)
    exponents = jnp.ceil(jnp.log(largest) * (1.0 / LOG_TWO))
    codes = jnp.round(values * power_of_two(STEPS - exponents)).astype(I32)
    upper = lax.shift_right_arithmetic(codes, 8)
    lower = jnp.bitwise_and(codes, 255)
    words = lax.shift_left(lower[:, :half], 8) + lower[:, half:] - 32768
    marks = [
        jnp.broadcast_to(exponents[g * LANES : (g + 1) * LANES, :], (LANES, LANES)).T[0:1, :]
        for g in range(rows // LANES)
    ]
    marks = jnp.concatenate([*marks, jnp.zeros((16 - len(marks), LANES), F32)], axis=0).astype(I32)
    marks = jnp.concatenate([marks, jnp.zeros((16, width + half - LANES), I32)], axis=1)
    return jnp.concatenate([jnp.concatenate([upper, words], axis=1), marks], axis=0).astype(I16)


def decoded(wire):
    rows, width = wire.shape[0] - 16, wire.shape[1] * 2 // 3
    half = width // 2
    wire = wire.astype(I32)
    words = wire[:rows, width:] + 32768
    lower = jnp.concatenate([lax.shift_right_arithmetic(words, 8), jnp.bitwise_and(words, 255)], axis=1)
    codes = (wire[:rows, :width] * 256 + lower).astype(F32)
    exponents = wire[rows:, :LANES].astype(F32)
    scale = [power_of_two(column(exponents[g : g + 1, :]) - STEPS) for g in range(rows // LANES)]
    return codes * jnp.concatenate([jnp.concatenate(scale, axis=0)] * (width // LANES), axis=1)


def edge_forward_kernel(
    place_ref, region_ref, recv_row_ref, hs_ref, hr_ref, x_ref, *refs,
):
    pieces, refs = refs[:-5], refs[-5:]
    w_ref, high_ref, low_ref, halo_ref, wide_ref = refs
    step = pl.program_id(0)
    rows = x_ref.shape[0]
    width = x_ref.shape[1]
    nodes = halo_ref.shape[0] - 16
    steps = pl.num_programs(0)

    @pl.when(step == 0)
    def _():
        odd = place_ref[0] == 1
        shares = len(pieces) // 2
        share = pieces[0].shape[0]
        for k in range(shares):
            mine, other = pieces[k][...].astype(F32), pieces[shares + k][...].astype(F32)
            base = pl.multiple_of(place_ref[4 + k] * share, 8)
            wide_ref[pl.ds(base, share), 0:LANES] = jnp.where(odd, other, mine)
            wide_ref[pl.ds(base, share), LANES : 2 * LANES] = jnp.where(odd, mine, other)
        w_ref[...] = wide_ref[...].astype(B16)

    vec = vectors_of(w_ref, width)
    pre = before_silu(region_ref, step, hs_ref, hr_ref, x_ref, w_ref)
    hidden = (pre / (1.0 + jnp.exp(-pre))).astype(B16)
    unit, _ = normalized(hidden, w_ref, vec)
    high, low = split(unit * vec[2:3, :] + vec[3:4, :])
    base = pl.multiple_of(step * rows, rows)
    high_ref[pl.ds(base, rows), :] = high
    low_ref[pl.ds(base, rows), :] = low

    @pl.when(step == steps - 1)
    def _():
        onehot = chosen_rows(recv_row_ref[...], 2 * nodes, nodes)
        halo_ref[...] = encoded(dot(onehot, high_ref[...]) + dot(onehot, low_ref[...]))


def edge_forward(place, regions, recv, hs, hr, edges, pieces, total, nodes):
    count, width = edges.shape
    tile = tiled(TILE, width)
    return pl.pallas_call(
        edge_forward_kernel,
        grid=(count // TILE,),
        in_specs=[
            pl.BlockSpec(memory_space=pltpu.SMEM), whole((count // LANES, LANES)), whole((1, count)), tile, tile, tile,
            *[whole(piece.shape) for piece in pieces],
        ],
        out_specs=[
            whole((total, width)), whole((count, width)), whole((count, width)),
            whole((nodes + 16, width + width // 2)),
        ],
        out_shape=[
            jax.ShapeDtypeStruct((total, width), B16),
            jax.ShapeDtypeStruct((count, width), B16),
            jax.ShapeDtypeStruct((count, width), B16),
            jax.ShapeDtypeStruct((nodes + 16, width + width // 2), I16),
        ],
        scratch_shapes=[pltpu.VMEM((total, width), F32)],
        compiler_params=PARAMS,
        name="edge_forward",
        cost_estimate=pl.CostEstimate(
            flops=2 * count * width * (5 * width + 2 * nodes), transcendentals=2 * count * width,
            bytes_accessed=count * width * 10,
        ),
    )(place, regions.reshape(-1, LANES), recv.reshape(1, -1), hs, hr, edges, *pieces)


def edge_slope_kernel(region_ref, hs_ref, hr_ref, x_ref, w_ref, hidden_ref, slope_ref):
    pre = before_silu(region_ref, pl.program_id(0), hs_ref, hr_ref, x_ref, w_ref)
    sigma = 1.0 / (1.0 + jnp.exp(-pre))
    hidden_ref[...] = (pre / (1.0 + jnp.exp(-pre))).astype(B16)
    slope_ref[...] = sigma * (1.0 + pre * (1.0 - sigma))


def edge_slope(regions, hs, hr, edges, weights):
    count, width = edges.shape
    tile = tiled(TILE, width)
    return pl.pallas_call(
        edge_slope_kernel,
        grid=(count // TILE,),
        in_specs=[whole((count // LANES, LANES)), tile, tile, tile, whole(weights.shape)],
        out_specs=[tile, tile],
        out_shape=[jax.ShapeDtypeStruct((count, width), B16), jax.ShapeDtypeStruct((count, width), F32)],
        compiler_params=PARAMS,
        name="edge_slope",
        cost_estimate=pl.CostEstimate(
            flops=2 * count * width * 4 * width, transcendentals=2 * count * width, bytes_accessed=count * width * 12
        ),
    )(regions.reshape(-1, LANES), hs, hr, edges, weights)


def edge_unit_kernel(hidden_ref, w_ref, unit_ref, inverse_ref):
    unit, inverse = normalized(hidden_ref[...], w_ref, vectors_of(w_ref, hidden_ref.shape[1]))
    unit_ref[...] = unit
    inverse_ref[...] = jnp.broadcast_to(inverse, inverse_ref.shape)


def edge_unit(hidden, weights):
    count, width = hidden.shape
    tile = tiled(TILE, width)
    return pl.pallas_call(
        edge_unit_kernel,
        grid=(count // TILE,),
        in_specs=[tile, whole(weights.shape)],
        out_specs=[tile, tiled(TILE, LANES)],
        out_shape=[jax.ShapeDtypeStruct((count, width), F32), jax.ShapeDtypeStruct((count, LANES), F32)],
        compiler_params=PARAMS,
        name="edge_unit",
        cost_estimate=pl.CostEstimate(
            flops=2 * count * width * width, transcendentals=count, bytes_accessed=count * width * 8
        ),
    )(hidden, weights)


def near_sum_kernel(recv_row_ref, high_ref, low_ref, pair_ref, more_ref, own_ref):
    nodes = own_ref.shape[0]
    half = nodes // 2
    for first, out_ref in ((nodes, pair_ref), (nodes + half, more_ref), (0, own_ref)):
        onehot = chosen_rows(recv_row_ref[...], first, out_ref.shape[0])
        out_ref[...] = dot(onehot, high_ref[...]) + dot(onehot, low_ref[...])


def near_sum(recv, high, low, nodes):
    count, width = high.shape
    half = jax.ShapeDtypeStruct((nodes // 2, width), F32)
    return pl.pallas_call(
        near_sum_kernel,
        out_shape=[half, half, jax.ShapeDtypeStruct((nodes, width), F32)],
        compiler_params=PARAMS,
        name="near_sum",
        cost_estimate=pl.CostEstimate(
            flops=8 * count * width * nodes, transcendentals=0, bytes_accessed=count * width * 4
        ),
    )(recv.reshape(1, -1), high, low)


def kept_nodes(forced_ref, width):
    keep = [column(forced_ref[g : g + 1, :]) for g in range(forced_ref.shape[0])]
    keep = 1.0 - jnp.concatenate(keep, axis=0).astype(F32)
    return jnp.concatenate([keep] * (width // LANES), axis=1)


def node_kernel(
    h_ref, own_ref, pair_ref, more_ref, off_ref, w_ref, forced_ref, up_ref,
    d_agg_ref, agg_ref, hidden_ref, d_inner_ref, d_pre_ref, unit_ref,
):
    width = h_ref.shape[1]
    pair = jnp.concatenate([pair_ref[...], more_ref[...]], axis=0)
    agg_ref[...] = (own_ref[...] + pair + decoded(off_ref[...])).astype(B16)
    vec = vectors_of(w_ref, width)
    latent, aggregate = w_ref[4 * width : 5 * width, :], w_ref[5 * width : 6 * width, :]
    second = w_ref[6 * width : 7 * width, :]
    pre = dot(h_ref[...], latent) + dot(agg_ref[...], aggregate) + vec[4:5, :]
    sigma = 1.0 / (1.0 + jnp.exp(-pre))
    hidden = (pre / (1.0 + jnp.exp(-pre))).astype(B16)
    hidden_ref[...] = hidden
    inner = dot(hidden, second) + vec[5:6, :]
    center = inner - jnp.mean(inner, axis=-1, keepdims=True)
    inverse = lax.rsqrt(jnp.mean(center * center, axis=-1, keepdims=True) + NORM_EPS)
    unit = center * inverse
    unit_ref[...] = unit
    scaled = kept_nodes(forced_ref, width) * up_ref[...] * vec[6:7, :]
    d_inner = inverse * (
        scaled
        - jnp.mean(scaled, axis=-1, keepdims=True)
        - unit * jnp.mean(scaled * unit, axis=-1, keepdims=True)
    )
    d_inner = d_inner.astype(B16)
    d_inner_ref[...] = d_inner
    slope = sigma * (1.0 + pre * (1.0 - sigma))
    d_pre = (dot_back(d_inner, second) * slope).astype(B16)
    d_pre_ref[...] = d_pre
    d_agg_ref[...] = dot_back(d_pre, aggregate).astype(B16)


def node_update(h, own, pair, more, off, weights, forced, upstream):
    nodes, width = h.shape
    half = jax.ShapeDtypeStruct((nodes, width), B16)
    return pl.pallas_call(
        node_kernel,
        out_shape=[half, half, half, half, half, jax.ShapeDtypeStruct((nodes, width), F32)],
        compiler_params=PARAMS,
        name="node_update",
        cost_estimate=pl.CostEstimate(
            flops=2 * nodes * width * width * 5, transcendentals=2 * nodes * width, bytes_accessed=nodes * width * 20
        ),
    )(h, own, pair, more, off, weights, forced.reshape(-1, LANES), upstream)


def node_grads_kernel(
    h_ref, agg_ref, hidden_ref, d_inner_ref, d_pre_ref, unit_ref, w_ref, forced_ref, up_ref,
    new_ref, grad_ref, sums_ref, back_ref,
):
    width = h_ref.shape[1]
    vec = vectors_of(w_ref, width)
    keep = kept_nodes(forced_ref, width)
    unit, upstream = unit_ref[...], up_ref[...]
    new_ref[...] = h_ref[...].astype(F32) + keep * (unit * vec[6:7, :] + vec[7:8, :])
    d_pre, d_inner, d_update = d_pre_ref[...], d_inner_ref[...], keep * upstream
    grad_ref[0:width, :] = dot_rows(h_ref[...], d_pre)
    grad_ref[width : 2 * width, :] = dot_rows(agg_ref[...], d_pre)
    grad_ref[2 * width : 3 * width, :] = dot_rows(hidden_ref[...], d_inner)
    back_ref[...] = upstream + dot_back(d_pre, w_ref[4 * width : 5 * width, :])
    sums_ref[...] = jnp.concatenate(
        [
            jnp.sum(d_pre.astype(F32), axis=0, keepdims=True),
            jnp.sum(d_inner.astype(F32), axis=0, keepdims=True),
            jnp.sum(d_update * unit, axis=0, keepdims=True),
            jnp.sum(d_update, axis=0, keepdims=True),
        ],
        axis=0,
    )


def node_grads(h, agg, hidden, d_inner, d_pre, unit, weights, forced, upstream):
    nodes, width = h.shape
    full = jax.ShapeDtypeStruct((nodes, width), F32)
    return pl.pallas_call(
        node_grads_kernel,
        out_shape=[full, jax.ShapeDtypeStruct((3 * width, width), F32), jax.ShapeDtypeStruct((4, width), F32), full],
        compiler_params=PARAMS,
        name="node_grads",
        cost_estimate=pl.CostEstimate(
            flops=2 * nodes * width * width * 4, transcendentals=0, bytes_accessed=nodes * width * 18
        ),
    )(h, agg, hidden, d_inner, d_pre, unit, weights, forced.reshape(-1, LANES), upstream)


def edge_backward_kernel(
    place_ref, recv_ref, region_row_ref, off_ref, near_ref, hs_ref, hr_ref, x_ref, hidden_ref, slope_ref, unit_ref,
    inverse_ref, w_ref, node_grad_ref, node_sum_ref,
    d_pre_ref, kept_ref, sent_ref,
    d_inner_ref, vec_acc_ref,
):
    step = pl.program_id(0)
    steps = pl.num_programs(0)
    rows = slope_ref.shape[0]
    width = x_ref.shape[1]
    nodes = off_ref.shape[0]
    regions = w_ref.shape[0] - 7 * width - 8
    vec = vectors_of(w_ref, width)

    @pl.when(step == 0)
    def _():
        vec_acc_ref[...] = jnp.zeros_like(vec_acc_ref)

    d_message = dot(chosen_columns(recv_ref, step, rows, 2 * nodes, 3 * nodes), off_ref[...])
    d_message = d_message + near_ref[...].astype(F32)
    unit = unit_ref[...]
    scaled = d_message * vec[2:3, :]
    inverse = inverse_ref[:, 0:1]
    d_inner = inverse * (
        scaled
        - jnp.mean(scaled, axis=-1, keepdims=True)
        - unit * jnp.mean(scaled * unit, axis=-1, keepdims=True)
    )
    vec_acc_ref[0:8, :] += jnp.sum((d_message * unit).reshape(rows // 8, 8, width), axis=0)
    vec_acc_ref[8:16, :] += jnp.sum(d_message.reshape(rows // 8, 8, width), axis=0)
    d_inner = d_inner.astype(B16)
    d_pre = (dot_back(d_inner, w_ref[3 * width : 4 * width, :]) * slope_ref[...]).astype(B16)
    base = pl.multiple_of(step * rows, rows)
    d_inner_ref[pl.ds(base, rows), :] = d_inner
    d_pre_ref[pl.ds(base, rows), :] = d_pre

    @pl.when(step == steps - 1)
    def _():
        odd = place_ref[0] == 1

        def put(start, piece):
            left, right = piece[:, 0:LANES], piece[:, LANES:]
            kept_ref[start : start + piece.shape[0], :] = jnp.where(odd, right, left)
            sent_ref[start : start + piece.shape[0], :] = jnp.where(odd, left, right)

        table_rows = node_grad_ref.shape[0] + 4 * width
        d_inner, d_pre = d_inner_ref[...], d_pre_ref[...]
        second_sum = dot(jnp.ones((16, d_inner.shape[0]), B16), d_inner)[0:1, :]
        table_grad = dot(chosen_rows(region_row_ref[...], 0, regions), d_pre)
        put(3 * width, dot_rows(hidden_ref[...], d_inner))
        put(0, dot_rows(hs_ref[...], d_pre))
        put(width, dot_rows(hr_ref[...], d_pre))
        put(2 * width, dot_rows(x_ref[...], d_pre))
        put(4 * width, node_grad_ref[...])
        vector_rows = jnp.concatenate(
            [
                jnp.sum(table_grad, axis=0, keepdims=True),
                second_sum,
                jnp.sum(vec_acc_ref[0:8, :], axis=0, keepdims=True),
                jnp.sum(vec_acc_ref[8:16, :], axis=0, keepdims=True),
                node_sum_ref[...],
            ],
            axis=0,
        )
        put(table_rows, vector_rows)
        put(table_rows + 8, table_grad)


def edge_backward(
    place, recv, regions, off, near, hs, hr, edges, hidden, slope, unit, inverse, weights, node_grad, node_sum,
):
    count, width = edges.shape
    tile, full = tiled(TILE, width), whole((count, width))
    grad_rows = weights.shape[0]
    half = whole((grad_rows, LANES))
    return pl.pallas_call(
        edge_backward_kernel,
        grid=(count // TILE,),
        in_specs=[
            pl.BlockSpec(memory_space=pltpu.SMEM), whole((count // LANES, LANES)), whole((1, count)),
            whole(off.shape), tile, full, full, full, full, tile, tile, tiled(TILE, LANES),
            whole(weights.shape), whole(node_grad.shape), whole(node_sum.shape),
        ],
        out_specs=[full, half, half],
        out_shape=[
            jax.ShapeDtypeStruct((count, width), B16),
            jax.ShapeDtypeStruct((grad_rows, LANES), F32),
            jax.ShapeDtypeStruct((grad_rows, LANES), F32),
        ],
        scratch_shapes=[pltpu.VMEM((count, width), B16), pltpu.VMEM((16, width), F32)],
        compiler_params=PARAMS,
        name="edge_backward",
        cost_estimate=pl.CostEstimate(
            flops=2 * count * width * (6 * width + off.shape[0]), transcendentals=0, bytes_accessed=count * width * 20
        ),
    )(
        place, recv.reshape(-1, LANES), regions.reshape(1, -1), off, near, hs, hr, edges, hidden, slope, unit, inverse,
        weights, node_grad, node_sum,
    )


def node_part_of(index_row_ref, d_pre_ref, weight, slot, nodes):
    high, low = split(dot(chosen_rows(index_row_ref[...], slot * nodes, nodes), d_pre_ref[...]))
    return dot_back(high, weight) + dot_back(low, weight)


def sender_part_kernel(index_row_ref, d_pre_ref, w_ref, out_ref):
    nodes, width = out_ref.shape
    out_ref[...] = node_part_of(index_row_ref, d_pre_ref, w_ref[0:width, :], pl.program_id(0), nodes)


def sender_part(index, d_pre, weights, nodes):
    count, width = d_pre.shape
    return pl.pallas_call(
        sender_part_kernel,
        grid=(3,),
        in_specs=[whole((1, count)), whole((count, width)), whole(weights.shape)],
        out_specs=tiled(nodes, width),
        out_shape=jax.ShapeDtypeStruct((3 * nodes, width), F32),
        compiler_params=PARAMS,
        name="sender_part",
        cost_estimate=pl.CostEstimate(
            flops=6 * count * width * nodes, transcendentals=0, bytes_accessed=count * width * 2
        ),
    )(index.reshape(1, -1), d_pre, weights)


def receiver_part_kernel(index_row_ref, d_pre_ref, w_ref, part_ref, back_ref, own_ref, pair_ref, off_ref):
    nodes, width = back_ref.shape
    slot = pl.program_id(0)
    part = node_part_of(index_row_ref, d_pre_ref, w_ref[width : 2 * width, :], slot, nodes) + part_ref[...]

    @pl.when(slot == 0)
    def _():
        own_ref[...] = part + back_ref[...]

    @pl.when(slot == 1)
    def _():
        pair_ref[...] = part.astype(B16)

    @pl.when(slot == 2)
    def _():
        off_ref[...] = part.astype(B16)


def receiver_part(index, d_pre, weights, part, back):
    count, width = d_pre.shape
    nodes = back.shape[0]
    half = jax.ShapeDtypeStruct(back.shape, B16)
    return pl.pallas_call(
        receiver_part_kernel,
        grid=(3,),
        in_specs=[
            whole((1, count)), whole((count, width)), whole(weights.shape), tiled(nodes, width), whole(back.shape),
        ],
        out_specs=[whole(back.shape)] * 3,
        out_shape=[jax.ShapeDtypeStruct(back.shape, F32), half, half],
        compiler_params=PARAMS,
        name="receiver_part",
        cost_estimate=pl.CostEstimate(
            flops=6 * count * width * nodes, transcendentals=0, bytes_accessed=count * width * 2
        ),
    )(index.reshape(1, -1), d_pre, weights, part, back)


def edge_grads_kernel(d_pre_ref, w_ref, out_ref):
    width = d_pre_ref.shape[1]
    out_ref[...] = dot_back(d_pre_ref[...], w_ref[2 * width : 3 * width, :]).astype(B16)


def edge_grads(d_pre, weights):
    count, width = d_pre.shape
    return pl.pallas_call(
        edge_grads_kernel,
        grid=(count // TILE,),
        in_specs=[tiled(TILE, width), whole(weights.shape)],
        out_specs=tiled(TILE, width),
        out_shape=jax.ShapeDtypeStruct((count, width), B16),
        compiler_params=PARAMS,
        name="edge_grads",
        cost_estimate=pl.CostEstimate(
            flops=2 * count * width * width, transcendentals=0, bytes_accessed=count * width * 4
        ),
    )(d_pre, weights)


def packed(values, first):
    rows = values[first : first + 8, :]
    return jnp.concatenate([values, rows - rows.astype(B16).astype(F32)], axis=0).astype(B16)


def unpacked(wire, first):
    values = wire.astype(F32)
    share = values.shape[0] - 8
    exact = values[first : first + 8, :] + values[share:, :]
    return jnp.concatenate([values[:first, :], exact, values[first + 8 : share, :]], axis=0)


def halve_kernel(place_ref, mine_ref, other_ref, kept_ref, sent_ref, *, share, first, bit, coded):
    here = (place_ref[2] // bit) % 2
    size = share + 8 if coded else share
    for j in range(kept_ref.shape[0] // share):
        for side, out_ref in ((here, kept_ref), (1 - here, sent_ref)):
            index = 2 * j + side
            other = other_ref[pl.ds(pl.multiple_of(index * size, 8), size), :]
            total = mine_ref[pl.ds(pl.multiple_of(index * share, 8), share), :] + (
                unpacked(other, first) if coded else other
            )
            if out_ref is kept_ref:
                out_ref[j * share : (j + 1) * share, :] = total
            else:
                out_ref[j * (share + 8) : (j + 1) * (share + 8), :] = packed(total, first)


def halve(place, mine, other, share, first, bit, coded):
    count = mine.shape[0] // share // 2
    vmem = pl.BlockSpec(memory_space=pltpu.VMEM)
    return pl.pallas_call(
        functools.partial(halve_kernel, share=share, first=first, bit=bit, coded=coded),
        in_specs=[pl.BlockSpec(memory_space=pltpu.SMEM), vmem, vmem],
        out_shape=[
            jax.ShapeDtypeStruct((count * share, LANES), F32),
            jax.ShapeDtypeStruct((count * (share + 8), LANES), B16),
        ],
        compiler_params=PARAMS,
        name="halve",
    )(place, mine, other)


def add_kernel(mine_ref, other_ref, out_ref, *, first):
    mine = mine_ref[...] if mine_ref.dtype == F32 else unpacked(mine_ref[...], first)
    out_ref[...] = packed(mine + unpacked(other_ref[...], first), first)


def add(mine, other, first):
    return pl.pallas_call(
        functools.partial(add_kernel, first=first),
        out_shape=jax.ShapeDtypeStruct(other.shape, B16),
        compiler_params=PARAMS,
        name="add",
    )(mine, other)


def finish_kernel(place_ref, mine_ref, other_ref, out_ref, *, first):
    share = out_ref.shape[0] - 16
    part = unpacked(mine_ref[...], first) + unpacked(other_ref[...], first)
    out_ref[0:share, :] = part
    out_ref[share : share + 8, :] = jnp.where(place_ref[3] == 1, part[first : first + 8, :], 0.0)
    squares = jnp.sum(jnp.sum(part * part, axis=0, keepdims=True), axis=1, keepdims=True)
    out_ref[share + 8 : share + 16, :] = jnp.broadcast_to(squares, (8, LANES))


def finish(place, mine, other, share, first):
    return pl.pallas_call(
        functools.partial(finish_kernel, first=first),
        in_specs=[pl.BlockSpec(memory_space=pltpu.SMEM)] + [pl.BlockSpec(memory_space=pltpu.VMEM)] * 2,
        out_shape=jax.ShapeDtypeStruct((share + 16, LANES), F32),
        compiler_params=PARAMS,
        name="finish",
    )(place, mine, other)


def adam_kernel(
    place_ref, step_ref, stats_ref, more_ref, mine_ref, other_ref, params_ref, first_ref, second_ref, averaged_ref,
    own_ref, pair_ref, off_ref,
    new_first_hbm, new_second_hbm, new_params_hbm, new_average_hbm, norm_ref, vector_ref, latents_hbm,
    new_first_ref, new_second_ref, new_params_ref, new_average_ref, latents_ref, sem,
):
    share = params_ref.shape[0]
    odd = place_ref[0] == 1
    latents_ref[...] = own_ref[...] + pair_ref[...].astype(F32) + off_ref[...].astype(F32)
    copies = [pltpu.make_async_copy(latents_ref, latents_hbm, sem.at[0])]
    copies[0].start()
    stats = stats_ref[...] + more_ref[...]
    norm = jnp.sqrt(stats[8:9, 0:1] + stats[24:25, 0:1])
    norm_ref[...] = norm
    factor = jnp.minimum(1.0, MAX_NORM / (norm + 1e-06))
    count = jnp.full((1, 1), step_ref[0], F32)
    first_scale = 1.0 - jnp.exp(count * jnp.log(jnp.full((1, 1), BETA_ONE, F32)))
    second_scale = 1.0 - jnp.exp(count * jnp.log(jnp.full((1, 1), BETA_TWO, F32)))
    decay = jnp.minimum(AVERAGE_DECAY, (1.0 + count) / (10.0 + count))
    vector_ref[:, 0:LANES] = jnp.where(odd, stats[16:24, :], stats[0:8, :]) * factor
    vector_ref[:, LANES : 2 * LANES] = jnp.where(odd, stats[0:8, :], stats[16:24, :]) * factor
    chunk = share // 3 if share % 24 == 0 else share
    for i in range(share // chunk):
        rows = slice(i * chunk, (i + 1) * chunk)
        mine, other = mine_ref[rows, :], other_ref[rows, :]
        both = jnp.concatenate([jnp.where(odd, other, mine), jnp.where(odd, mine, other)], axis=1)
        clipped = both * factor
        params = params_ref[rows, :]
        new_first = BETA_ONE * first_ref[rows, :] + (1.0 - BETA_ONE) * clipped
        new_second = BETA_TWO * second_ref[rows, :] + (1.0 - BETA_TWO) * clipped * clipped
        first_hat = new_first / first_scale
        second_hat = new_second / second_scale
        new_params = params - RATE * (first_hat / (jnp.sqrt(second_hat) + ADAM_EPS) + WEIGHT_DECAY * params)
        new_first_ref[rows, :] = new_first
        new_second_ref[rows, :] = new_second
        new_params_ref[rows, :] = new_params
        new_average_ref[rows, :] = decay * averaged_ref[rows, :] + (1.0 - decay) * new_params
        for k, (src, dst) in enumerate(
            (
                (new_first_ref, new_first_hbm), (new_second_ref, new_second_hbm), (new_params_ref, new_params_hbm),
                (new_average_ref, new_average_hbm),
            )
        ):
            copies.append(pltpu.make_async_copy(src.at[rows, :], dst.at[rows, :], sem.at[1 + 4 * i + k]))
            copies[-1].start()
    for copy in copies:
        copy.wait()


def adam(place, step, stats, more, mine, other, params, first_moment, second_moment, averaged, own, pair, off):
    rows = jax.ShapeDtypeStruct(params.shape, F32)
    smem, vmem, hbm = (pl.BlockSpec(memory_space=m) for m in (pltpu.SMEM, pltpu.VMEM, pltpu.HBM))
    return pl.pallas_call(
        adam_kernel,
        in_specs=[smem, smem] + [vmem] * 11,
        out_specs=[hbm] * 4 + [vmem] * 2 + [hbm],
        out_shape=[
            rows, rows, rows, rows, jax.ShapeDtypeStruct((1, 1), F32), jax.ShapeDtypeStruct((8, params.shape[1]), F32),
            jax.ShapeDtypeStruct(own.shape, F32),
        ],
        scratch_shapes=[pltpu.VMEM(params.shape, F32)] * 4
        + [pltpu.VMEM(own.shape, F32), pltpu.SemaphoreType.DMA((13,))],
        compiler_params=PARAMS,
        name="adam",
        cost_estimate=pl.CostEstimate(
            flops=20 * params.size, transcendentals=2 * params.size, bytes_accessed=params.size * 32
        ),
    )(place, step, stats, more, mine, other, params, first_moment, second_moment, averaged, own, pair, off)


def flipped(value, axis, bit):
    return lax.ppermute(value, axis, [(i, i ^ bit) for i in range(lax.axis_size(axis))])


def across(value, axis):
    count = lax.axis_size(axis)
    return lax.ppermute(value, axis, [(i, (i + 1 if i % 2 else i - 1) % count) for i in range(count)])


def neighbours(value):
    off = across(value, "edge")
    return flipped(value, "edge", 1), off


def on_device(
    node_latents, edge_latents, senders, receivers, regions, forced, params, first_moment, second_moment,
    averaged, step, cotangent,
):
    latents = node_latents[0]
    edges = edge_latents[0]
    upstream = cotangent[0]
    nodes, width = latents.shape
    share = params.shape[0]
    blocks, feats = lax.axis_size("edge"), lax.axis_size("feat")
    total = share * feats
    vector_row = 7 * width

    pair, off = neighbours(latents)

    mine, place, send, recv, latents = prologue(params, senders, receivers, latents, feats, vector_row // share)
    fetched = [mine] + [flipped(mine, "feat", k) for k in range(1, feats)]

    near_send = gather_near(send, latents, pair)
    near_recv = gather_near(recv, latents, pair)
    fetched = lax.optimization_barrier((near_send, near_recv, *fetched))[2:]
    pieces = [*fetched, *(flipped(piece, "edge", 1) for piece in fetched)]
    hs = gather_off(send, off, near_send)
    hr = gather_off(recv, off, near_recv)
    weights, high, low, to_off = edge_forward(place, regions, recv, hs, hr, edges, pieces, total, nodes)
    from_off = across(to_off, "edge")
    to_pair, more, own = near_sum(recv, high, low, nodes)
    from_pair, more = flipped(to_pair, "edge", 1), flipped(more, "edge", 1)
    hidden, slope = edge_slope(regions, hs, hr, edges, weights)
    own, hidden, slope = lax.optimization_barrier((own, hidden, slope))
    d_agg, agg, node_hidden, d_inner, d_pre, node_unit = node_update(
        latents, own, from_pair, more, from_off, weights, forced, upstream
    )
    back_pair, back_off = neighbours(d_agg)
    new_latents, node_grad, node_sum, back = node_grads(
        latents, agg, node_hidden, d_inner, d_pre, node_unit, weights, forced, upstream
    )
    near = gather_near(recv, d_agg, back_pair)
    unit, inverse = edge_unit(lax.optimization_barrier((hidden, d_agg))[0], weights)

    d_pre, kept, sent = edge_backward(
        place, recv, regions, back_off, near, hs, hr, edges, hidden, slope, unit, inverse, weights, node_grad, node_sum,
    )

    low_rows = vector_row % share
    part, other, coded, bit = kept, flipped(sent, "edge", 1), False, 1
    send_part = sender_part(send, d_pre, weights, nodes)
    while bit < feats:
        part, wire = halve(place, part, other, share, low_rows, bit, coded)
        if bit == 2:
            wire, send_part = lax.optimization_barrier((wire, send_part))
        other = flipped(wire, "feat", bit)
        coded, bit = True, 2 * bit
    wire = add(part, other, low_rows)
    part_own, part_pair, part_off = receiver_part(recv, d_pre, weights, send_part, back)
    wire, part_own, part_pair, part_off = lax.optimization_barrier((wire, part_own, part_pair, part_off))
    bit = 2
    while 2 * bit < blocks:
        wire = add(wire, flipped(wire, "edge", bit), low_rows)
        bit *= 2
    grad_edges = edge_grads(d_pre, weights)
    wire, part_pair, part_off, grad_edges = lax.optimization_barrier((wire, part_pair, part_off, grad_edges))
    mine = finish(place, wire, flipped(wire, "edge", bit), share, low_rows)
    grads_off = across(part_off, "edge")
    grads_pair = flipped(part_pair, "edge", 1)

    other = flipped(mine, "edge", 1)
    stats = jnp.concatenate([mine[share:], other[share:]], axis=0)
    bit = 1
    while 2 * bit < feats:
        stats = stats + flipped(stats, "feat", bit)
        bit *= 2
    more = flipped(stats, "feat", bit)
    new_first, new_second, new_params, new_average, grad_norm, vector_grads, grad_latents = adam(
        place, step, stats, more, mine, other, params, first_moment, second_moment, averaged,
        part_own, grads_pair, grads_off,
    )
    return (
        new_latents[None],
        grad_latents[None],
        grad_edges[None],
        new_first,
        new_second,
        new_params,
        new_average,
        grad_norm.reshape(1),
        vector_grads,
    )


def solution(mesh):
    nodes, rows = P("feat", "edge", None), P("feat", None)
    return jax.shard_map(
        on_device,
        mesh=mesh,
        in_specs=(nodes, nodes, P("edge"), P("edge"), P("edge"), P("edge"), rows, rows, rows, rows, P(), nodes),
        out_specs=(nodes, nodes, nodes, rows, rows, rows, rows, P(), P()),
        check_vma=False,
    )
```

```python
import functools

import jax
import jax.numpy as jnp
from jax import lax
from jax.experimental import pallas as pl
from jax.experimental.pallas import tpu as pltpu
from jax.sharding import PartitionSpec as P

NORM_EPS = 1e-05
MAX_NORM = 512.0
RATE = 0.05
BETA_ONE = 0.9
BETA_TWO = 0.95
ADAM_EPS = 1e-08
WEIGHT_DECAY = 0.1
AVERAGE_DECAY = 0.999

LANES = 128
TINY = 1e-20
STEPS = 22
LOG_TWO = 0.6931471805599453
TILE = 2048
B16 = jnp.bfloat16
F32 = jnp.float32
I32 = jnp.int32
I16 = jnp.int16
PARAMS = pltpu.CompilerParams(vmem_limit_bytes=20 * 1024 * 1024)


def dot(left, right):
    return jnp.dot(left, right, preferred_element_type=F32)


def dot_rows(left, right):
    return lax.dot_general(left, right, (((0,), (0,)), ((), ())), preferred_element_type=F32)


def dot_back(left, right):
    return lax.dot_general(left, right, (((1,), (1,)), ((), ())), preferred_element_type=F32)


def vectors_of(w_ref, width):
    return w_ref[7 * width : 7 * width + 8, :].astype(F32)


def split(values):
    high = values.astype(B16)
    return high, (values - high.astype(F32)).astype(B16)


def whole(shape):
    return pl.BlockSpec(shape, lambda i: (0,) * len(shape))


def tiled(rows, cols):
    return pl.BlockSpec((rows, cols), lambda i: (i, 0))


def column(row):
    return jnp.broadcast_to(row, (LANES, LANES)).T


def chosen_columns(index_ref, tile, rows, first, last):
    lane = lax.broadcasted_iota(I32, (LANES, LANES), 1)
    groups = []
    for g in range(rows // LANES):
        col = column(index_ref[pl.ds(tile * (rows // LANES) + g, 1), :])
        groups.append(
            jnp.concatenate(
                [jnp.where(col == lane + base, 1.0, 0.0).astype(B16) for base in range(first, last, LANES)],
                axis=1,
            )
        )
    return jnp.concatenate(groups, axis=0)


def chosen_rows(index_row, first, count):
    node = lax.broadcasted_iota(I32, (count, index_row.shape[1]), 0) + first
    return jnp.where(index_row == node, 1.0, 0.0).astype(B16)


def prologue_kernel(
    params_hbm, send_hbm, recv_hbm, latents_hbm, half_ref, place_ref, send_ref, recv_ref, latents_ref,
    wide_ref, in_ref, sem, *, nodes, shares, owner,
):
    e, f = lax.axis_index("edge"), lax.axis_index("feat")
    core = e % 2
    lanes = pl.ds(pl.multiple_of(core * LANES, LANES), LANES)
    copies = [
        pltpu.make_async_copy(params_hbm.at[:, lanes], wide_ref, sem.at[0]),
        pltpu.make_async_copy(send_hbm, in_ref.at[0], sem.at[1]),
        pltpu.make_async_copy(recv_hbm, in_ref.at[1], sem.at[2]),
        pltpu.make_async_copy(latents_hbm, latents_ref, sem.at[3]),
    ]
    for copy in copies:
        copy.start()
    place_ref[0] = core
    place_ref[1] = e
    place_ref[2] = f
    place_ref[3] = jnp.where(f == owner, 1, 0)
    for k in range(shares):
        place_ref[4 + k] = jnp.bitwise_xor(f, k)
    for i, out_ref in ((0, send_ref), (1, recv_ref)):
        copies[1 + i].wait()
        index = in_ref[i]
        block = lax.div(index, nodes)
        slot = jnp.where(block == e, 0, jnp.where(block == e + 1 - 2 * core, 1, 2))
        out_ref[...] = (slot - block) * nodes + index
    copies[0].wait()
    half_ref[...] = wide_ref[...].astype(B16)
    copies[3].wait()


def prologue(params, senders, receivers, latents, shares, owner):
    shape = (senders.size // LANES, LANES)
    out = jax.ShapeDtypeStruct(shape, I32)
    vmem, hbm = pl.BlockSpec(memory_space=pltpu.VMEM), pl.BlockSpec(memory_space=pltpu.HBM)
    half, place, send, recv, own = pl.pallas_call(
        functools.partial(prologue_kernel, nodes=latents.shape[0], shares=shares, owner=owner),
        in_specs=[hbm] * 4,
        out_specs=[vmem, pl.BlockSpec(memory_space=pltpu.SMEM), vmem, vmem, vmem],
        out_shape=[
            jax.ShapeDtypeStruct((params.shape[0], LANES), B16), jax.ShapeDtypeStruct((4 + shares,), I32), out, out,
            jax.ShapeDtypeStruct(latents.shape, latents.dtype),
        ],
        scratch_shapes=[
            pltpu.VMEM((params.shape[0], LANES), F32), pltpu.VMEM((2, *shape), I32), pltpu.SemaphoreType.DMA((4,)),
        ],
        compiler_params=PARAMS,
        name="prologue",
    )(*(pltpu.with_memory_space_constraint(a, pltpu.HBM) for a in (params, senders.reshape(shape), receivers.reshape(shape), latents)))
    return half, place, send.reshape(-1), recv.reshape(-1), own


def gather_near_kernel(index_ref, own_ref, pair_ref, out_ref):
    tile = pl.program_id(0)
    rows = out_ref.shape[0]
    nodes = own_ref.shape[0]
    total = dot(chosen_columns(index_ref, tile, rows, 0, nodes), own_ref[...])
    total = total + dot(chosen_columns(index_ref, tile, rows, nodes, 2 * nodes), pair_ref[...])
    out_ref[...] = total.astype(B16)


def gather_near(index, own, pair):
    nodes, width = own.shape
    edges = index.size
    return pl.pallas_call(
        gather_near_kernel,
        grid=(1,),
        in_specs=[whole((edges // LANES, LANES))] + [whole((nodes, width))] * 2,
        out_specs=tiled(edges, width),
        out_shape=jax.ShapeDtypeStruct((edges, width), B16),
        compiler_params=PARAMS,
        name="gather_near",
        cost_estimate=pl.CostEstimate(
            flops=2 * edges * 2 * nodes * width, transcendentals=0, bytes_accessed=edges * width * 2
        ),
    )(index.reshape(-1, LANES), own, pair)


def gather_off_kernel(index_ref, off_ref, near_ref, out_ref):
    tile = pl.program_id(0)
    rows = out_ref.shape[0]
    nodes = off_ref.shape[0]
    total = dot(chosen_columns(index_ref, tile, rows, 2 * nodes, 3 * nodes), off_ref[...])
    out_ref[...] = (total + near_ref[...].astype(F32)).astype(B16)


def gather_off(index, off, near):
    nodes, width = off.shape
    edges = index.size
    return pl.pallas_call(
        gather_off_kernel,
        grid=(1,),
        in_specs=[whole((edges // LANES, LANES)), whole((nodes, width)), tiled(edges, width)],
        out_specs=tiled(edges, width),
        out_shape=jax.ShapeDtypeStruct((edges, width), B16),
        compiler_params=PARAMS,
        name="gather_off",
        cost_estimate=pl.CostEstimate(
            flops=2 * edges * nodes * width, transcendentals=0, bytes_accessed=edges * width * 4
        ),
    )(index.reshape(-1, LANES), off, near)


def before_silu(region_ref, tile, hs_ref, hr_ref, x_ref, w_ref):
    rows, width = x_ref.shape
    vector_row = 7 * width
    regions = w_ref.shape[0] - vector_row - 8
    table = jnp.concatenate(
        [w_ref[vector_row + 8 :, :].astype(F32), jnp.zeros((LANES - regions, width), F32)], axis=0
    ).astype(B16)
    pre = dot(hs_ref[...], w_ref[0:width, :])
    pre = pre + dot(hr_ref[...], w_ref[width : 2 * width, :])
    pre = pre + dot(x_ref[...], w_ref[2 * width : 3 * width, :])
    pre = pre + dot(chosen_columns(region_ref, tile, rows, 0, LANES), table)
    return pre + vectors_of(w_ref, width)[0:1, :]


def normalized(hidden, w_ref, vec):
    width = hidden.shape[1]
    inner = dot(hidden, w_ref[3 * width : 4 * width, :]) + vec[1:2, :]
    center = inner - jnp.mean(inner, axis=-1, keepdims=True)
    inverse = lax.rsqrt(jnp.mean(center * center, axis=-1, keepdims=True) + NORM_EPS)
    return center * inverse, inverse


def power_of_two(exponents):
    return jnp.exp(exponents * LOG_TWO)


def encoded(values):
    rows, width = values.shape
    half = width // 2
    largest = jnp.maximum(jnp.max(jnp.abs(values), axis=-1, keepdims=True), TINY)
    exponents = jnp.ceil(jnp.log(largest) * (1.0 / LOG_TWO))
    codes = jnp.round(values * power_of_two(STEPS - exponents)).astype(I32)
    upper = lax.shift_right_arithmetic(codes, 8)
    lower = jnp.bitwise_and(codes, 255)
    words = lax.shift_left(lower[:, :half], 8) + lower[:, half:] - 32768
    marks = [
        jnp.broadcast_to(exponents[g * LANES : (g + 1) * LANES, :], (LANES, LANES)).T[0:1, :]
        for g in range(rows // LANES)
    ]
    marks = jnp.concatenate([*marks, jnp.zeros((16 - len(marks), LANES), F32)], axis=0).astype(I32)
    marks = jnp.concatenate([marks, jnp.zeros((16, width + half - LANES), I32)], axis=1)
    return jnp.concatenate([jnp.concatenate([upper, words], axis=1), marks], axis=0).astype(I16)


def decoded(wire):
    rows, width = wire.shape[0] - 16, wire.shape[1] * 2 // 3
    half = width // 2
    wire = wire.astype(I32)
    words = wire[:rows, width:] + 32768
    lower = jnp.concatenate([lax.shift_right_arithmetic(words, 8), jnp.bitwise_and(words, 255)], axis=1)
    codes = (wire[:rows, :width] * 256 + lower).astype(F32)
    exponents = wire[rows:, :LANES].astype(F32)
    scale = [power_of_two(column(exponents[g : g + 1, :]) - STEPS) for g in range(rows // LANES)]
    return codes * jnp.concatenate([jnp.concatenate(scale, axis=0)] * (width // LANES), axis=1)


def edge_forward_kernel(
    place_ref, region_ref, recv_row_ref, hs_ref, hr_ref, x_ref, *refs,
):
    pieces, refs = refs[:-5], refs[-5:]
    w_ref, high_ref, low_ref, halo_ref, wide_ref = refs
    step = pl.program_id(0)
    rows = x_ref.shape[0]
    width = x_ref.shape[1]
    nodes = halo_ref.shape[0] - 16
    steps = pl.num_programs(0)

    @pl.when(step == 0)
    def _():
        odd = place_ref[0] == 1
        share = pieces[0].shape[0]
        for k in range(w_ref.shape[0] // share):
            rows = slice((k - 1) * share, k * share)
            mine, other = (pieces[i][...] if k == 0 else pieces[i + 1][rows, :] for i in (0, 2))
            mine, other = mine.astype(F32), other.astype(F32)
            base = pl.multiple_of(place_ref[4 + k] * share, 8)
            wide_ref[pl.ds(base, share), 0:LANES] = jnp.where(odd, other, mine)
            wide_ref[pl.ds(base, share), LANES : 2 * LANES] = jnp.where(odd, mine, other)
        w_ref[...] = wide_ref[...].astype(B16)

    vec = vectors_of(w_ref, width)
    pre = before_silu(region_ref, step, hs_ref, hr_ref, x_ref, w_ref)
    hidden = (pre / (1.0 + jnp.exp(-pre))).astype(B16)
    unit, _ = normalized(hidden, w_ref, vec)
    high, low = split(unit * vec[2:3, :] + vec[3:4, :])
    base = pl.multiple_of(step * rows, rows)
    high_ref[pl.ds(base, rows), :] = high
    low_ref[pl.ds(base, rows), :] = low

    @pl.when(step == steps - 1)
    def _():
        onehot = chosen_rows(recv_row_ref[...], 2 * nodes, nodes)
        halo_ref[...] = encoded(dot(onehot, high_ref[...]) + dot(onehot, low_ref[...]))


def edge_forward(place, regions, recv, hs, hr, edges, pieces, total, nodes):
    count, width = edges.shape
    tile = tiled(TILE, width)
    return pl.pallas_call(
        edge_forward_kernel,
        grid=(count // TILE,),
        in_specs=[
            pl.BlockSpec(memory_space=pltpu.SMEM), whole((count // LANES, LANES)), whole((1, count)), tile, tile, tile,
            *[whole(piece.shape) for piece in pieces],
        ],
        out_specs=[
            whole((total, width)), whole((count, width)), whole((count, width)),
            whole((nodes + 16, width + width // 2)),
        ],
        out_shape=[
            jax.ShapeDtypeStruct((total, width), B16),
            jax.ShapeDtypeStruct((count, width), B16),
            jax.ShapeDtypeStruct((count, width), B16),
            jax.ShapeDtypeStruct((nodes + 16, width + width // 2), I16),
        ],
        scratch_shapes=[pltpu.VMEM((total, width), F32)],
        compiler_params=PARAMS,
        name="edge_forward",
        cost_estimate=pl.CostEstimate(
            flops=2 * count * width * (5 * width + 2 * nodes), transcendentals=2 * count * width,
            bytes_accessed=count * width * 10,
        ),
    )(place, regions.reshape(-1, LANES), recv.reshape(1, -1), hs, hr, edges, *pieces)


def edge_slope_kernel(region_ref, hs_ref, hr_ref, x_ref, w_ref, hidden_ref, slope_ref):
    pre = before_silu(region_ref, pl.program_id(0), hs_ref, hr_ref, x_ref, w_ref)
    sigma = 1.0 / (1.0 + jnp.exp(-pre))
    hidden_ref[...] = (pre / (1.0 + jnp.exp(-pre))).astype(B16)
    slope_ref[...] = sigma * (1.0 + pre * (1.0 - sigma))


def edge_slope(regions, hs, hr, edges, weights):
    count, width = edges.shape
    tile = tiled(TILE, width)
    return pl.pallas_call(
        edge_slope_kernel,
        grid=(count // TILE,),
        in_specs=[whole((count // LANES, LANES)), tile, tile, tile, whole(weights.shape)],
        out_specs=[tile, tile],
        out_shape=[jax.ShapeDtypeStruct((count, width), B16), jax.ShapeDtypeStruct((count, width), F32)],
        compiler_params=PARAMS,
        name="edge_slope",
        cost_estimate=pl.CostEstimate(
            flops=2 * count * width * 4 * width, transcendentals=2 * count * width, bytes_accessed=count * width * 12
        ),
    )(regions.reshape(-1, LANES), hs, hr, edges, weights)


def edge_unit_kernel(hidden_ref, w_ref, unit_ref, inverse_ref):
    unit, inverse = normalized(hidden_ref[...], w_ref, vectors_of(w_ref, hidden_ref.shape[1]))
    unit_ref[...] = unit
    inverse_ref[...] = jnp.broadcast_to(inverse, inverse_ref.shape)


def edge_unit(hidden, weights):
    count, width = hidden.shape
    tile = tiled(TILE, width)
    return pl.pallas_call(
        edge_unit_kernel,
        grid=(count // TILE,),
        in_specs=[tile, whole(weights.shape)],
        out_specs=[tile, tiled(TILE, LANES)],
        out_shape=[jax.ShapeDtypeStruct((count, width), F32), jax.ShapeDtypeStruct((count, LANES), F32)],
        compiler_params=PARAMS,
        name="edge_unit",
        cost_estimate=pl.CostEstimate(
            flops=2 * count * width * width, transcendentals=count, bytes_accessed=count * width * 8
        ),
    )(hidden, weights)


def near_sum_kernel(recv_row_ref, high_ref, low_ref, pair_ref, more_ref, own_ref):
    nodes = own_ref.shape[0]
    half = nodes // 2
    for first, out_ref in ((nodes, pair_ref), (nodes + half, more_ref), (0, own_ref)):
        onehot = chosen_rows(recv_row_ref[...], first, out_ref.shape[0])
        out_ref[...] = dot(onehot, high_ref[...]) + dot(onehot, low_ref[...])


def near_sum(recv, high, low, nodes):
    count, width = high.shape
    half = jax.ShapeDtypeStruct((nodes // 2, width), F32)
    return pl.pallas_call(
        near_sum_kernel,
        out_shape=[half, half, jax.ShapeDtypeStruct((nodes, width), F32)],
        compiler_params=PARAMS,
        name="near_sum",
        cost_estimate=pl.CostEstimate(
            flops=8 * count * width * nodes, transcendentals=0, bytes_accessed=count * width * 4
        ),
    )(recv.reshape(1, -1), high, low)


def kept_nodes(forced_ref, width):
    keep = [column(forced_ref[g : g + 1, :]) for g in range(forced_ref.shape[0])]
    keep = 1.0 - jnp.concatenate(keep, axis=0).astype(F32)
    return jnp.concatenate([keep] * (width // LANES), axis=1)


def node_kernel(
    h_ref, own_ref, pair_ref, more_ref, off_ref, w_ref, forced_ref, up_ref,
    d_agg_ref, agg_ref, hidden_ref, d_inner_ref, d_pre_ref, unit_ref,
):
    width = h_ref.shape[1]
    pair = jnp.concatenate([pair_ref[...], more_ref[...]], axis=0)
    agg_ref[...] = (own_ref[...] + pair + decoded(off_ref[...])).astype(B16)
    vec = vectors_of(w_ref, width)
    latent, aggregate = w_ref[4 * width : 5 * width, :], w_ref[5 * width : 6 * width, :]
    second = w_ref[6 * width : 7 * width, :]
    pre = dot(h_ref[...], latent) + dot(agg_ref[...], aggregate) + vec[4:5, :]
    sigma = 1.0 / (1.0 + jnp.exp(-pre))
    hidden = (pre / (1.0 + jnp.exp(-pre))).astype(B16)
    hidden_ref[...] = hidden
    inner = dot(hidden, second) + vec[5:6, :]
    center = inner - jnp.mean(inner, axis=-1, keepdims=True)
    inverse = lax.rsqrt(jnp.mean(center * center, axis=-1, keepdims=True) + NORM_EPS)
    unit = center * inverse
    unit_ref[...] = unit
    scaled = kept_nodes(forced_ref, width) * up_ref[...] * vec[6:7, :]
    d_inner = inverse * (
        scaled
        - jnp.mean(scaled, axis=-1, keepdims=True)
        - unit * jnp.mean(scaled * unit, axis=-1, keepdims=True)
    )
    d_inner = d_inner.astype(B16)
    d_inner_ref[...] = d_inner
    slope = sigma * (1.0 + pre * (1.0 - sigma))
    d_pre = (dot_back(d_inner, second) * slope).astype(B16)
    d_pre_ref[...] = d_pre
    d_agg_ref[...] = dot_back(d_pre, aggregate).astype(B16)


def node_update(h, own, pair, more, off, weights, forced, upstream):
    nodes, width = h.shape
    half = jax.ShapeDtypeStruct((nodes, width), B16)
    return pl.pallas_call(
        node_kernel,
        out_shape=[half, half, half, half, half, jax.ShapeDtypeStruct((nodes, width), F32)],
        compiler_params=PARAMS,
        name="node_update",
        cost_estimate=pl.CostEstimate(
            flops=2 * nodes * width * width * 5, transcendentals=2 * nodes * width, bytes_accessed=nodes * width * 20
        ),
    )(h, own, pair, more, off, weights, forced.reshape(-1, LANES), upstream)


def node_grads_kernel(
    h_ref, agg_ref, hidden_ref, d_inner_ref, d_pre_ref, unit_ref, w_ref, forced_ref, up_ref,
    new_ref, grad_ref, sums_ref, back_ref,
):
    width = h_ref.shape[1]
    vec = vectors_of(w_ref, width)
    keep = kept_nodes(forced_ref, width)
    unit, upstream = unit_ref[...], up_ref[...]
    new_ref[...] = h_ref[...].astype(F32) + keep * (unit * vec[6:7, :] + vec[7:8, :])
    d_pre, d_inner, d_update = d_pre_ref[...], d_inner_ref[...], keep * upstream
    grad_ref[0:width, :] = dot_rows(h_ref[...], d_pre)
    grad_ref[width : 2 * width, :] = dot_rows(agg_ref[...], d_pre)
    grad_ref[2 * width : 3 * width, :] = dot_rows(hidden_ref[...], d_inner)
    back_ref[...] = upstream + dot_back(d_pre, w_ref[4 * width : 5 * width, :])
    sums_ref[...] = jnp.concatenate(
        [
            jnp.sum(d_pre.astype(F32), axis=0, keepdims=True),
            jnp.sum(d_inner.astype(F32), axis=0, keepdims=True),
            jnp.sum(d_update * unit, axis=0, keepdims=True),
            jnp.sum(d_update, axis=0, keepdims=True),
        ],
        axis=0,
    )


def node_grads(h, agg, hidden, d_inner, d_pre, unit, weights, forced, upstream):
    nodes, width = h.shape
    full = jax.ShapeDtypeStruct((nodes, width), F32)
    return pl.pallas_call(
        node_grads_kernel,
        out_shape=[full, jax.ShapeDtypeStruct((3 * width, width), F32), jax.ShapeDtypeStruct((4, width), F32), full],
        compiler_params=PARAMS,
        name="node_grads",
        cost_estimate=pl.CostEstimate(
            flops=2 * nodes * width * width * 4, transcendentals=0, bytes_accessed=nodes * width * 18
        ),
    )(h, agg, hidden, d_inner, d_pre, unit, weights, forced.reshape(-1, LANES), upstream)


def edge_backward_kernel(
    place_ref, recv_ref, region_row_ref, off_ref, near_ref, hs_ref, hr_ref, x_ref, hidden_ref, slope_ref, unit_ref,
    inverse_ref, w_ref, node_grad_ref, node_sum_ref,
    d_pre_ref, kept_ref, sent_ref,
    d_inner_ref, vec_acc_ref,
):
    step = pl.program_id(0)
    steps = pl.num_programs(0)
    rows = slope_ref.shape[0]
    width = x_ref.shape[1]
    nodes = off_ref.shape[0]
    regions = w_ref.shape[0] - 7 * width - 8
    vec = vectors_of(w_ref, width)

    @pl.when(step == 0)
    def _():
        vec_acc_ref[...] = jnp.zeros_like(vec_acc_ref)

    d_message = dot(chosen_columns(recv_ref, step, rows, 2 * nodes, 3 * nodes), off_ref[...])
    d_message = d_message + near_ref[...].astype(F32)
    unit = unit_ref[...]
    scaled = d_message * vec[2:3, :]
    inverse = inverse_ref[:, 0:1]
    d_inner = inverse * (
        scaled
        - jnp.mean(scaled, axis=-1, keepdims=True)
        - unit * jnp.mean(scaled * unit, axis=-1, keepdims=True)
    )
    vec_acc_ref[0:8, :] += jnp.sum((d_message * unit).reshape(rows // 8, 8, width), axis=0)
    vec_acc_ref[8:16, :] += jnp.sum(d_message.reshape(rows // 8, 8, width), axis=0)
    d_inner = d_inner.astype(B16)
    d_pre = (dot_back(d_inner, w_ref[3 * width : 4 * width, :]) * slope_ref[...]).astype(B16)
    base = pl.multiple_of(step * rows, rows)
    d_inner_ref[pl.ds(base, rows), :] = d_inner
    d_pre_ref[pl.ds(base, rows), :] = d_pre

    @pl.when(step == steps - 1)
    def _():
        odd = place_ref[0] == 1

        def put(start, piece):
            left, right = piece[:, 0:LANES], piece[:, LANES:]
            kept_ref[start : start + piece.shape[0], :] = jnp.where(odd, right, left)
            sent_ref[start : start + piece.shape[0], :] = jnp.where(odd, left, right)

        table_rows = node_grad_ref.shape[0] + 4 * width
        d_inner, d_pre = d_inner_ref[...], d_pre_ref[...]
        second_sum = dot(jnp.ones((16, d_inner.shape[0]), B16), d_inner)[0:1, :]
        table_grad = dot(chosen_rows(region_row_ref[...], 0, regions), d_pre)
        put(3 * width, dot_rows(hidden_ref[...], d_inner))
        put(0, dot_rows(hs_ref[...], d_pre))
        put(width, dot_rows(hr_ref[...], d_pre))
        put(2 * width, dot_rows(x_ref[...], d_pre))
        put(4 * width, node_grad_ref[...])
        vector_rows = jnp.concatenate(
            [
                jnp.sum(table_grad, axis=0, keepdims=True),
                second_sum,
                jnp.sum(vec_acc_ref[0:8, :], axis=0, keepdims=True),
                jnp.sum(vec_acc_ref[8:16, :], axis=0, keepdims=True),
                node_sum_ref[...],
            ],
            axis=0,
        )
        put(table_rows, vector_rows)
        put(table_rows + 8, table_grad)


def edge_backward(
    place, recv, regions, off, near, hs, hr, edges, hidden, slope, unit, inverse, weights, node_grad, node_sum,
):
    count, width = edges.shape
    tile, full = tiled(TILE, width), whole((count, width))
    grad_rows = weights.shape[0]
    half = whole((grad_rows, LANES))
    return pl.pallas_call(
        edge_backward_kernel,
        grid=(count // TILE,),
        in_specs=[
            pl.BlockSpec(memory_space=pltpu.SMEM), whole((count // LANES, LANES)), whole((1, count)),
            whole(off.shape), tile, full, full, full, full, tile, tile, tiled(TILE, LANES),
            whole(weights.shape), whole(node_grad.shape), whole(node_sum.shape),
        ],
        out_specs=[full, half, half],
        out_shape=[
            jax.ShapeDtypeStruct((count, width), B16),
            jax.ShapeDtypeStruct((grad_rows, LANES), F32),
            jax.ShapeDtypeStruct((grad_rows, LANES), F32),
        ],
        scratch_shapes=[pltpu.VMEM((count, width), B16), pltpu.VMEM((16, width), F32)],
        compiler_params=PARAMS,
        name="edge_backward",
        cost_estimate=pl.CostEstimate(
            flops=2 * count * width * (6 * width + off.shape[0]), transcendentals=0, bytes_accessed=count * width * 20
        ),
    )(
        place, recv.reshape(-1, LANES), regions.reshape(1, -1), off, near, hs, hr, edges, hidden, slope, unit, inverse,
        weights, node_grad, node_sum,
    )


def node_part_of(index_row_ref, d_pre_ref, weight, slot, nodes):
    high, low = split(dot(chosen_rows(index_row_ref[...], slot * nodes, nodes), d_pre_ref[...]))
    return dot_back(high, weight) + dot_back(low, weight)


def sender_part_kernel(index_row_ref, d_pre_ref, w_ref, out_ref):
    nodes, width = out_ref.shape
    out_ref[...] = node_part_of(index_row_ref, d_pre_ref, w_ref[0:width, :], pl.program_id(0), nodes)


def sender_part(index, d_pre, weights, nodes):
    count, width = d_pre.shape
    return pl.pallas_call(
        sender_part_kernel,
        grid=(3,),
        in_specs=[whole((1, count)), whole((count, width)), whole(weights.shape)],
        out_specs=tiled(nodes, width),
        out_shape=jax.ShapeDtypeStruct((3 * nodes, width), F32),
        compiler_params=PARAMS,
        name="sender_part",
        cost_estimate=pl.CostEstimate(
            flops=6 * count * width * nodes, transcendentals=0, bytes_accessed=count * width * 2
        ),
    )(index.reshape(1, -1), d_pre, weights)


def receiver_part_kernel(index_row_ref, d_pre_ref, w_ref, part_ref, back_ref, own_ref, pair_ref, off_ref):
    nodes, width = back_ref.shape
    slot = pl.program_id(0)
    part = node_part_of(index_row_ref, d_pre_ref, w_ref[width : 2 * width, :], slot, nodes) + part_ref[...]

    @pl.when(slot == 0)
    def _():
        own_ref[...] = part + back_ref[...]

    @pl.when(slot == 1)
    def _():
        pair_ref[...] = part.astype(B16)

    @pl.when(slot == 2)
    def _():
        off_ref[...] = part.astype(B16)


def receiver_part(index, d_pre, weights, part, back):
    count, width = d_pre.shape
    nodes = back.shape[0]
    half = jax.ShapeDtypeStruct(back.shape, B16)
    return pl.pallas_call(
        receiver_part_kernel,
        grid=(3,),
        in_specs=[
            whole((1, count)), whole((count, width)), whole(weights.shape), tiled(nodes, width), whole(back.shape),
        ],
        out_specs=[whole(back.shape)] * 3,
        out_shape=[jax.ShapeDtypeStruct(back.shape, F32), half, half],
        compiler_params=PARAMS,
        name="receiver_part",
        cost_estimate=pl.CostEstimate(
            flops=6 * count * width * nodes, transcendentals=0, bytes_accessed=count * width * 2
        ),
    )(index.reshape(1, -1), d_pre, weights, part, back)


def edge_grads_kernel(d_pre_ref, w_ref, out_ref):
    width = d_pre_ref.shape[1]
    out_ref[...] = dot_back(d_pre_ref[...], w_ref[2 * width : 3 * width, :]).astype(B16)


def edge_grads(d_pre, weights):
    count, width = d_pre.shape
    return pl.pallas_call(
        edge_grads_kernel,
        grid=(count // TILE,),
        in_specs=[tiled(TILE, width), whole(weights.shape)],
        out_specs=tiled(TILE, width),
        out_shape=jax.ShapeDtypeStruct((count, width), B16),
        compiler_params=PARAMS,
        name="edge_grads",
        cost_estimate=pl.CostEstimate(
            flops=2 * count * width * width, transcendentals=0, bytes_accessed=count * width * 4
        ),
    )(d_pre, weights)


def packed(values, first):
    rows = values[first : first + 8, :]
    return jnp.concatenate([values, rows - rows.astype(B16).astype(F32)], axis=0).astype(B16)


def unpacked(wire, first):
    values = wire.astype(F32)
    share = values.shape[0] - 8
    exact = values[first : first + 8, :] + values[share:, :]
    return jnp.concatenate([values[:first, :], exact, values[first + 8 : share, :]], axis=0)


def parted_kernel(place_ref, mine_ref, other_ref, kept_ref, *sent_refs, share, first):
    for k, out_ref in enumerate((kept_ref, *sent_refs)):
        rows = pl.ds(pl.multiple_of(place_ref[4 + k] * share, 8), share)
        total = mine_ref[rows, :] + other_ref[rows, :]
        out_ref[...] = packed(total, first) if k else total


def parted(place, mine, other, share, first):
    vmem = pl.BlockSpec(memory_space=pltpu.VMEM)
    sent = jax.ShapeDtypeStruct((share + 8, LANES), B16)
    return pl.pallas_call(
        functools.partial(parted_kernel, share=share, first=first),
        in_specs=[pl.BlockSpec(memory_space=pltpu.SMEM), vmem, vmem],
        out_shape=[jax.ShapeDtypeStruct((share, LANES), F32)] + [sent] * (mine.shape[0] // share - 1),
        compiler_params=PARAMS,
        name="parted",
    )(place, mine, other)


def gathered_kernel(mine_ref, *refs, first):
    total = mine_ref[...]
    for ref in refs[:-1]:
        total = total + unpacked(ref[...], first)
    refs[-1][...] = packed(total, first)


def gathered(mine, others, first):
    return pl.pallas_call(
        functools.partial(gathered_kernel, first=first),
        out_shape=jax.ShapeDtypeStruct(others[0].shape, B16),
        compiler_params=PARAMS,
        name="gathered",
    )(mine, *others)


def add_kernel(mine_ref, other_ref, out_ref, *, first):
    out_ref[...] = packed(unpacked(mine_ref[...], first) + unpacked(other_ref[...], first), first)


def add(mine, other, first):
    return pl.pallas_call(
        functools.partial(add_kernel, first=first),
        out_shape=jax.ShapeDtypeStruct(other.shape, B16),
        compiler_params=PARAMS,
        name="add",
    )(mine, other)


def finish_kernel(place_ref, mine_ref, other_ref, out_ref, *, first):
    share = out_ref.shape[0] - 16
    part = unpacked(mine_ref[...], first) + unpacked(other_ref[...], first)
    out_ref[0:share, :] = part
    out_ref[share : share + 8, :] = jnp.where(place_ref[3] == 1, part[first : first + 8, :], 0.0)
    squares = jnp.sum(jnp.sum(part * part, axis=0, keepdims=True), axis=1, keepdims=True)
    out_ref[share + 8 : share + 16, :] = jnp.broadcast_to(squares, (8, LANES))


def finish(place, mine, other, share, first):
    return pl.pallas_call(
        functools.partial(finish_kernel, first=first),
        in_specs=[pl.BlockSpec(memory_space=pltpu.SMEM)] + [pl.BlockSpec(memory_space=pltpu.VMEM)] * 2,
        out_shape=jax.ShapeDtypeStruct((share + 16, LANES), F32),
        compiler_params=PARAMS,
        name="finish",
    )(place, mine, other)


def adam_kernel(
    place_ref, step_ref, stats_ref, more_ref, mine_ref, other_ref, params_ref, first_ref, second_ref, averaged_ref,
    own_ref, pair_ref, off_ref,
    new_first_hbm, new_second_hbm, new_params_hbm, new_average_hbm, norm_ref, vector_ref, latents_hbm,
    new_first_ref, new_second_ref, new_params_ref, new_average_ref, latents_ref, sem,
):
    share = params_ref.shape[0]
    odd = place_ref[0] == 1
    latents_ref[...] = own_ref[...] + pair_ref[...].astype(F32) + off_ref[...].astype(F32)
    copies = [pltpu.make_async_copy(latents_ref, latents_hbm, sem.at[0])]
    copies[0].start()
    stats = stats_ref[...] + more_ref[...]
    norm = jnp.sqrt(stats[8:9, 0:1] + stats[24:25, 0:1])
    norm_ref[...] = norm
    factor = jnp.minimum(1.0, MAX_NORM / (norm + 1e-06))
    count = jnp.full((1, 1), step_ref[0], F32)
    first_scale = 1.0 - jnp.exp(count * jnp.log(jnp.full((1, 1), BETA_ONE, F32)))
    second_scale = 1.0 - jnp.exp(count * jnp.log(jnp.full((1, 1), BETA_TWO, F32)))
    decay = jnp.minimum(AVERAGE_DECAY, (1.0 + count) / (10.0 + count))
    vector_ref[:, 0:LANES] = jnp.where(odd, stats[16:24, :], stats[0:8, :]) * factor
    vector_ref[:, LANES : 2 * LANES] = jnp.where(odd, stats[0:8, :], stats[16:24, :]) * factor
    chunk = share // 3 if share % 24 == 0 else share
    for i in range(share // chunk):
        rows = slice(i * chunk, (i + 1) * chunk)
        mine, other = mine_ref[rows, :], other_ref[rows, :]
        both = jnp.concatenate([jnp.where(odd, other, mine), jnp.where(odd, mine, other)], axis=1)
        clipped = both * factor
        params = params_ref[rows, :]
        new_first = BETA_ONE * first_ref[rows, :] + (1.0 - BETA_ONE) * clipped
        new_second = BETA_TWO * second_ref[rows, :] + (1.0 - BETA_TWO) * clipped * clipped
        first_hat = new_first / first_scale
        second_hat = new_second / second_scale
        new_params = params - RATE * (first_hat / (jnp.sqrt(second_hat) + ADAM_EPS) + WEIGHT_DECAY * params)
        new_first_ref[rows, :] = new_first
        new_second_ref[rows, :] = new_second
        new_params_ref[rows, :] = new_params
        new_average_ref[rows, :] = decay * averaged_ref[rows, :] + (1.0 - decay) * new_params
        for k, (src, dst) in enumerate(
            (
                (new_first_ref, new_first_hbm), (new_second_ref, new_second_hbm), (new_params_ref, new_params_hbm),
                (new_average_ref, new_average_hbm),
            )
        ):
            copies.append(pltpu.make_async_copy(src.at[rows, :], dst.at[rows, :], sem.at[1 + 4 * i + k]))
            copies[-1].start()
    for copy in copies:
        copy.wait()


def adam(place, step, stats, more, mine, other, params, first_moment, second_moment, averaged, own, pair, off):
    rows = jax.ShapeDtypeStruct(params.shape, F32)
    smem, vmem, hbm = (pl.BlockSpec(memory_space=m) for m in (pltpu.SMEM, pltpu.VMEM, pltpu.HBM))
    return pl.pallas_call(
        adam_kernel,
        in_specs=[smem, smem] + [vmem] * 11,
        out_specs=[hbm] * 4 + [vmem] * 2 + [hbm],
        out_shape=[
            rows, rows, rows, rows, jax.ShapeDtypeStruct((1, 1), F32), jax.ShapeDtypeStruct((8, params.shape[1]), F32),
            jax.ShapeDtypeStruct(own.shape, F32),
        ],
        scratch_shapes=[pltpu.VMEM(params.shape, F32)] * 4
        + [pltpu.VMEM(own.shape, F32), pltpu.SemaphoreType.DMA((13,))],
        compiler_params=PARAMS,
        name="adam",
        cost_estimate=pl.CostEstimate(
            flops=20 * params.size, transcendentals=2 * params.size, bytes_accessed=params.size * 32
        ),
    )(place, step, stats, more, mine, other, params, first_moment, second_moment, averaged, own, pair, off)


def flipped(value, axis, bit):
    return lax.ppermute(value, axis, [(i, i ^ bit) for i in range(lax.axis_size(axis))])


def across(value, axis):
    count = lax.axis_size(axis)
    return lax.ppermute(value, axis, [(i, (i + 1 if i % 2 else i - 1) % count) for i in range(count)])


def neighbours(value):
    off = across(value, "edge")
    return flipped(value, "edge", 1), off


def on_device(
    node_latents, edge_latents, senders, receivers, regions, forced, params, first_moment, second_moment,
    averaged, step, cotangent,
):
    latents = node_latents[0]
    edges = edge_latents[0]
    upstream = cotangent[0]
    nodes, width = latents.shape
    share = params.shape[0]
    blocks, feats = lax.axis_size("edge"), lax.axis_size("feat")
    total = share * feats
    vector_row = 7 * width

    pair, off = neighbours(latents)

    mine, place, send, recv, latents = prologue(params, senders, receivers, latents, feats, vector_row // share)
    fetched = [mine] + [flipped(mine, "feat", k) for k in range(1, feats)]

    near_send = gather_near(send, latents, pair)
    near_recv = gather_near(recv, latents, pair)
    others = jnp.concatenate(lax.optimization_barrier((near_send, near_recv, *fetched[1:]))[2:])
    pieces = [fetched[0], others, flipped(fetched[0], "edge", 1), flipped(others, "edge", 1)]
    hs = gather_off(send, off, near_send)
    hr = gather_off(recv, off, near_recv)
    weights, high, low, to_off = edge_forward(place, regions, recv, hs, hr, edges, pieces, total, nodes)
    from_off = across(to_off, "edge")
    to_pair, more, own = near_sum(recv, high, low, nodes)
    from_pair, more = flipped(to_pair, "edge", 1), flipped(more, "edge", 1)
    hidden, slope = edge_slope(regions, hs, hr, edges, weights)
    own, hidden, slope = lax.optimization_barrier((own, hidden, slope))
    d_agg, agg, node_hidden, d_inner, d_pre, node_unit = node_update(
        latents, own, from_pair, more, from_off, weights, forced, upstream
    )
    back_pair, back_off = neighbours(d_agg)
    new_latents, node_grad, node_sum, back = node_grads(
        latents, agg, node_hidden, d_inner, d_pre, node_unit, weights, forced, upstream
    )
    near = gather_near(recv, d_agg, back_pair)
    unit, inverse = edge_unit(lax.optimization_barrier((hidden, d_agg))[0], weights)

    d_pre, kept, sent = edge_backward(
        place, recv, regions, back_off, near, hs, hr, edges, hidden, slope, unit, inverse, weights, node_grad, node_sum,
    )

    low_rows = vector_row % share
    part, *sent = parted(place, kept, flipped(sent, "edge", 1), share, low_rows)
    came = [flipped(wire, "feat", k + 1) for k, wire in enumerate(sent)]
    d_pre, part = lax.optimization_barrier((d_pre, part))
    send_part = sender_part(send, d_pre, weights, nodes)
    part_own, part_pair, part_off = receiver_part(recv, d_pre, weights, send_part, back)
    part, part_own, part_pair, part_off = lax.optimization_barrier((part, part_own, part_pair, part_off))
    wire = gathered(part, came, low_rows)
    bit = 2
    while 2 * bit < blocks:
        wire = add(wire, flipped(wire, "edge", bit), low_rows)
        bit *= 2
    grad_edges = edge_grads(d_pre, weights)
    wire, part_pair, part_off, grad_edges = lax.optimization_barrier((wire, part_pair, part_off, grad_edges))
    mine = finish(place, wire, flipped(wire, "edge", bit), share, low_rows)
    grads_off = across(part_off, "edge")
    grads_pair = flipped(part_pair, "edge", 1)

    other = flipped(mine, "edge", 1)
    stats = jnp.concatenate([mine[share:], other[share:]], axis=0)
    bit = 1
    while 2 * bit < feats:
        stats = stats + flipped(stats, "feat", bit)
        bit *= 2
    more = flipped(stats, "feat", bit)
    new_first, new_second, new_params, new_average, grad_norm, vector_grads, grad_latents = adam(
        place, step, stats, more, mine, other, params, first_moment, second_moment, averaged,
        part_own, grads_pair, grads_off,
    )
    return (
        new_latents[None],
        grad_latents[None],
        grad_edges[None],
        new_first,
        new_second,
        new_params,
        new_average,
        grad_norm.reshape(1),
        vector_grads,
    )


def solution(mesh):
    nodes, rows = P("feat", "edge", None), P("feat", None)
    return jax.shard_map(
        on_device,
        mesh=mesh,
        in_specs=(nodes, nodes, P("edge"), P("edge"), P("edge"), P("edge"), rows, rows, rows, rows, P(), nodes),
        out_specs=(nodes, nodes, nodes, rows, rows, rows, rows, P(), P()),
        check_vma=False,
    )
```

```python
import functools

import jax
import jax.numpy as jnp
from jax import lax
from jax.experimental import pallas as pl
from jax.experimental.pallas import tpu as pltpu
from jax.sharding import PartitionSpec as P

NORM_EPS = 1e-05
MAX_NORM = 512.0
RATE = 0.05
BETA_ONE = 0.9
BETA_TWO = 0.95
ADAM_EPS = 1e-08
WEIGHT_DECAY = 0.1
AVERAGE_DECAY = 0.999

LANES = 128
TINY = 1e-20
STEPS = 18
LOG_TWO = 0.6931471805599453
TILE = 2048
B16 = jnp.bfloat16
F32 = jnp.float32
I32 = jnp.int32
I16 = jnp.int16
PARAMS = pltpu.CompilerParams(vmem_limit_bytes=20 * 1024 * 1024)


def dot(left, right):
    return jnp.dot(left, right, preferred_element_type=F32)


def dot_rows(left, right):
    return lax.dot_general(left, right, (((0,), (0,)), ((), ())), preferred_element_type=F32)


def dot_back(left, right):
    return lax.dot_general(left, right, (((1,), (1,)), ((), ())), preferred_element_type=F32)


def vectors_of(w_ref, width):
    return w_ref[7 * width : 7 * width + 8, :].astype(F32)


def split(values):
    high = values.astype(B16)
    return high, (values - high.astype(F32)).astype(B16)


def whole(shape):
    return pl.BlockSpec(shape, lambda i: (0,) * len(shape))


def tiled(rows, cols):
    return pl.BlockSpec((rows, cols), lambda i: (i, 0))


def column(row):
    return jnp.broadcast_to(row, (LANES, LANES)).T


def chosen_columns(index_ref, tile, rows, first, last):
    lane = lax.broadcasted_iota(I32, (LANES, LANES), 1)
    groups = []
    for g in range(rows // LANES):
        col = column(index_ref[pl.ds(tile * (rows // LANES) + g, 1), :])
        groups.append(
            jnp.concatenate(
                [jnp.where(col == lane + base, 1.0, 0.0).astype(B16) for base in range(first, last, LANES)],
                axis=1,
            )
        )
    return jnp.concatenate(groups, axis=0)


def chosen_rows(index_row, first, count):
    node = lax.broadcasted_iota(I32, (count, index_row.shape[1]), 0) + first
    return jnp.where(index_row == node, 1.0, 0.0).astype(B16)


def core_of(e):
    return e % 2


def odd_core():
    return core_of(lax.axis_index("edge")) == 1


def prologue_kernel(
    params_hbm, send_hbm, recv_hbm, latents_hbm, half_ref, send_ref, recv_ref, latents_ref, wide_ref, in_ref, sem,
    *, nodes,
):
    copies = [
        pltpu.make_async_copy(params_hbm, wide_ref, sem.at[0]),
        pltpu.make_async_copy(send_hbm, in_ref.at[0], sem.at[1]),
        pltpu.make_async_copy(recv_hbm, in_ref.at[1], sem.at[2]),
        pltpu.make_async_copy(latents_hbm, latents_ref, sem.at[3]),
    ]
    for copy in copies:
        copy.start()
    e = lax.axis_index("edge")
    core = core_of(e)
    for i, out_ref in ((0, send_ref), (1, recv_ref)):
        copies[1 + i].wait()
        index = in_ref[i]
        block = lax.div(index, nodes)
        slot = jnp.where(block == e, 0, jnp.where(block == e + 1 - 2 * core, 1, 2))
        out_ref[...] = (slot - block) * nodes + index
    copies[0].wait()
    half_ref[...] = jnp.where(core == 1, wide_ref[:, LANES : 2 * LANES], wide_ref[:, 0:LANES]).astype(B16)
    copies[3].wait()


def prologue(params, senders, receivers, latents):
    shape = (senders.size // LANES, LANES)
    out = jax.ShapeDtypeStruct(shape, I32)
    vmem, hbm = pl.BlockSpec(memory_space=pltpu.VMEM), pl.BlockSpec(memory_space=pltpu.HBM)
    operands = (params, senders.reshape(shape), receivers.reshape(shape), latents)
    half, send, recv, own = pl.pallas_call(
        functools.partial(prologue_kernel, nodes=latents.shape[0]),
        in_specs=[hbm] * 4,
        out_specs=[vmem] * 4,
        out_shape=[
            jax.ShapeDtypeStruct((params.shape[0], LANES), B16), out, out,
            jax.ShapeDtypeStruct(latents.shape, latents.dtype),
        ],
        scratch_shapes=[
            pltpu.VMEM(params.shape, F32), pltpu.VMEM((2, *shape), I32), pltpu.SemaphoreType.DMA((4,)),
        ],
        compiler_params=PARAMS,
        name="prologue",
    )(*(pltpu.with_memory_space_constraint(a, pltpu.HBM) for a in operands))
    return half, send.reshape(-1), recv.reshape(-1), own


def gather_near_kernel(index_ref, own_ref, pair_ref, out_ref):
    tile = pl.program_id(0)
    rows = out_ref.shape[0]
    nodes = own_ref.shape[0]
    total = dot(chosen_columns(index_ref, tile, rows, 0, nodes), own_ref[...])
    total = total + dot(chosen_columns(index_ref, tile, rows, nodes, 2 * nodes), pair_ref[...])
    out_ref[...] = total.astype(B16)


def gather_near(index, own, pair):
    nodes, width = own.shape
    edges = index.size
    return pl.pallas_call(
        gather_near_kernel,
        grid=(1,),
        in_specs=[whole((edges // LANES, LANES))] + [whole((nodes, width))] * 2,
        out_specs=tiled(edges, width),
        out_shape=jax.ShapeDtypeStruct((edges, width), B16),
        compiler_params=PARAMS,
        name="gather_near",
        cost_estimate=pl.CostEstimate(
            flops=2 * edges * 2 * nodes * width, transcendentals=0, bytes_accessed=edges * width * 2
        ),
    )(index.reshape(-1, LANES), own, pair)


def gather_off_kernel(index_ref, off_ref, near_ref, out_ref):
    tile = pl.program_id(0)
    rows = out_ref.shape[0]
    nodes = off_ref.shape[0]
    total = dot(chosen_columns(index_ref, tile, rows, 2 * nodes, 3 * nodes), off_ref[...])
    out_ref[...] = (total + near_ref[...].astype(F32)).astype(B16)


def gather_off(index, off, near):
    nodes, width = off.shape
    edges = index.size
    return pl.pallas_call(
        gather_off_kernel,
        grid=(1,),
        in_specs=[whole((edges // LANES, LANES)), whole((nodes, width)), tiled(edges, width)],
        out_specs=tiled(edges, width),
        out_shape=jax.ShapeDtypeStruct((edges, width), B16),
        compiler_params=PARAMS,
        name="gather_off",
        cost_estimate=pl.CostEstimate(
            flops=2 * edges * nodes * width, transcendentals=0, bytes_accessed=edges * width * 4
        ),
    )(index.reshape(-1, LANES), off, near)


def before_silu(region_ref, tile, hs_ref, hr_ref, x_ref, w_ref):
    rows, width = x_ref.shape
    vector_row = 7 * width
    regions = w_ref.shape[0] - vector_row - 8
    table = jnp.concatenate(
        [w_ref[vector_row + 8 :, :].astype(F32), jnp.zeros((LANES - regions, width), F32)], axis=0
    ).astype(B16)
    pre = dot(hs_ref[...], w_ref[0:width, :])
    pre = pre + dot(hr_ref[...], w_ref[width : 2 * width, :])
    pre = pre + dot(x_ref[...], w_ref[2 * width : 3 * width, :])
    pre = pre + dot(chosen_columns(region_ref, tile, rows, 0, LANES), table)
    return pre + vectors_of(w_ref, width)[0:1, :]


def normalized(hidden, w_ref, vec):
    width = hidden.shape[1]
    inner = dot(hidden, w_ref[3 * width : 4 * width, :]) + vec[1:2, :]
    center = inner - jnp.mean(inner, axis=-1, keepdims=True)
    inverse = lax.rsqrt(jnp.mean(center * center, axis=-1, keepdims=True) + NORM_EPS)
    return center * inverse, inverse


def power_of_two(exponents):
    return jnp.exp(exponents * LOG_TWO)


def encoded(values):
    rows, width = values.shape
    quarter = rows // 4
    largest = jnp.maximum(jnp.max(jnp.abs(values), axis=-1, keepdims=True), TINY)
    exponents = jnp.ceil(jnp.log(largest) * (1.0 / LOG_TWO))
    codes = jnp.round(values * power_of_two(STEPS - exponents)).astype(I32)
    upper = lax.shift_right_arithmetic(codes, 4)
    words = jnp.full((quarter, width), -32768, I32)
    for i in range(4):
        words = words + lax.shift_left(jnp.bitwise_and(codes[i * quarter : (i + 1) * quarter, :], 15), 4 * i)
    marks = [
        jnp.broadcast_to(exponents[g * LANES : (g + 1) * LANES, :], (LANES, LANES)).T[0:1, :]
        for g in range(rows // LANES)
    ]
    marks = jnp.concatenate([*marks, jnp.zeros((16 - len(marks), LANES), F32)], axis=0).astype(I32)
    marks = jnp.concatenate([marks, jnp.zeros((16, width - LANES), I32)], axis=1)
    return jnp.concatenate([upper, words, marks], axis=0).astype(I16)


def decoded(wire):
    width = wire.shape[1]
    quarter = (wire.shape[0] - 16) // 5
    rows = 4 * quarter
    wire = wire.astype(I32)
    words = wire[rows : rows + quarter, :] + 32768
    lower = jnp.concatenate([jnp.bitwise_and(lax.shift_right_arithmetic(words, 4 * i), 15) for i in range(4)], axis=0)
    codes = (wire[:rows, :] * 16 + lower).astype(F32)
    exponents = wire[rows + quarter :, :LANES].astype(F32)
    scale = [power_of_two(column(exponents[g : g + 1, :]) - STEPS) for g in range(rows // LANES)]
    return codes * jnp.concatenate([jnp.concatenate(scale, axis=0)] * (width // LANES), axis=1)


def edge_forward_kernel(
    region_ref, recv_row_ref, hs_ref, hr_ref, x_ref, *refs,
):
    pieces, refs = refs[:-5], refs[-5:]
    w_ref, high_ref, low_ref, halo_ref, wide_ref = refs
    step = pl.program_id(0)
    rows = x_ref.shape[0]
    width = x_ref.shape[1]
    nodes = (halo_ref.shape[0] - 16) // 5 * 4
    steps = pl.num_programs(0)

    @pl.when(step == 0)
    def _():
        odd, f = odd_core(), lax.axis_index("feat")
        share = pieces[0].shape[0]
        for k in range(w_ref.shape[0] // share):
            rows = slice((k - 1) * share, k * share)
            mine, other = (pieces[i][...] if k == 0 else pieces[i + 1][rows, :] for i in (0, 2))
            mine, other = mine.astype(F32), other.astype(F32)
            base = pl.multiple_of(jnp.bitwise_xor(f, k) * share, 8)
            wide_ref[pl.ds(base, share), 0:LANES] = jnp.where(odd, other, mine)
            wide_ref[pl.ds(base, share), LANES : 2 * LANES] = jnp.where(odd, mine, other)
        w_ref[...] = wide_ref[...].astype(B16)

    vec = vectors_of(w_ref, width)
    pre = before_silu(region_ref, step, hs_ref, hr_ref, x_ref, w_ref)
    hidden = (pre / (1.0 + jnp.exp(-pre))).astype(B16)
    unit, _ = normalized(hidden, w_ref, vec)
    high, low = split(unit * vec[2:3, :] + vec[3:4, :])
    base = pl.multiple_of(step * rows, rows)
    high_ref[pl.ds(base, rows), :] = high
    low_ref[pl.ds(base, rows), :] = low

    @pl.when(step == steps - 1)
    def _():
        onehot = chosen_rows(recv_row_ref[...], 2 * nodes, nodes)
        halo_ref[...] = encoded(dot(onehot, high_ref[...]) + dot(onehot, low_ref[...]))


def edge_forward(regions, recv, hs, hr, edges, pieces, total, nodes):
    count, width = edges.shape
    tile = tiled(TILE, width)
    return pl.pallas_call(
        edge_forward_kernel,
        grid=(count // TILE,),
        in_specs=[
            whole((count // LANES, LANES)), whole((1, count)), tile, tile, tile,
            *[whole(piece.shape) for piece in pieces],
        ],
        out_specs=[
            whole((total, width)), whole((count, width)), whole((count, width)),
            whole((nodes + nodes // 4 + 16, width)),
        ],
        out_shape=[
            jax.ShapeDtypeStruct((total, width), B16),
            jax.ShapeDtypeStruct((count, width), B16),
            jax.ShapeDtypeStruct((count, width), B16),
            jax.ShapeDtypeStruct((nodes + nodes // 4 + 16, width), I16),
        ],
        scratch_shapes=[pltpu.VMEM((total, width), F32)],
        compiler_params=PARAMS,
        name="edge_forward",
        cost_estimate=pl.CostEstimate(
            flops=2 * count * width * (5 * width + 2 * nodes), transcendentals=2 * count * width,
            bytes_accessed=count * width * 10,
        ),
    )(regions.reshape(-1, LANES), recv.reshape(1, -1), hs, hr, edges, *pieces)


def edge_slope_kernel(region_ref, hs_ref, hr_ref, x_ref, w_ref, hidden_ref, slope_ref):
    pre = before_silu(region_ref, pl.program_id(0), hs_ref, hr_ref, x_ref, w_ref)
    sigma = 1.0 / (1.0 + jnp.exp(-pre))
    hidden_ref[...] = (pre / (1.0 + jnp.exp(-pre))).astype(B16)
    slope_ref[...] = sigma * (1.0 + pre * (1.0 - sigma))


def edge_slope(regions, hs, hr, edges, weights):
    count, width = edges.shape
    tile = tiled(TILE, width)
    return pl.pallas_call(
        edge_slope_kernel,
        grid=(count // TILE,),
        in_specs=[whole((count // LANES, LANES)), tile, tile, tile, whole(weights.shape)],
        out_specs=[tile, tile],
        out_shape=[jax.ShapeDtypeStruct((count, width), B16), jax.ShapeDtypeStruct((count, width), F32)],
        compiler_params=PARAMS,
        name="edge_slope",
        cost_estimate=pl.CostEstimate(
            flops=2 * count * width * 4 * width, transcendentals=2 * count * width, bytes_accessed=count * width * 12
        ),
    )(regions.reshape(-1, LANES), hs, hr, edges, weights)


def edge_unit_kernel(hidden_ref, w_ref, unit_ref, inverse_ref):
    unit, inverse = normalized(hidden_ref[...], w_ref, vectors_of(w_ref, hidden_ref.shape[1]))
    unit_ref[...] = unit
    inverse_ref[...] = jnp.broadcast_to(inverse, inverse_ref.shape)


def edge_unit(hidden, weights):
    count, width = hidden.shape
    tile = tiled(TILE, width)
    return pl.pallas_call(
        edge_unit_kernel,
        grid=(count // TILE,),
        in_specs=[tile, whole(weights.shape)],
        out_specs=[tile, tiled(TILE, LANES)],
        out_shape=[jax.ShapeDtypeStruct((count, width), F32), jax.ShapeDtypeStruct((count, LANES), F32)],
        compiler_params=PARAMS,
        name="edge_unit",
        cost_estimate=pl.CostEstimate(
            flops=2 * count * width * width, transcendentals=count, bytes_accessed=count * width * 8
        ),
    )(hidden, weights)


def near_sum_kernel(recv_row_ref, high_ref, low_ref, pair_ref, more_ref, own_ref):
    nodes = own_ref.shape[0]
    half = nodes // 2
    for first, out_ref in ((nodes, pair_ref), (nodes + half, more_ref), (0, own_ref)):
        onehot = chosen_rows(recv_row_ref[...], first, out_ref.shape[0])
        out_ref[...] = dot(onehot, high_ref[...]) + dot(onehot, low_ref[...])


def near_sum(recv, high, low, nodes):
    count, width = high.shape
    half = jax.ShapeDtypeStruct((nodes // 2, width), F32)
    return pl.pallas_call(
        near_sum_kernel,
        out_shape=[half, half, jax.ShapeDtypeStruct((nodes, width), F32)],
        compiler_params=PARAMS,
        name="near_sum",
        cost_estimate=pl.CostEstimate(
            flops=8 * count * width * nodes, transcendentals=0, bytes_accessed=count * width * 4
        ),
    )(recv.reshape(1, -1), high, low)


def kept_nodes(forced_ref, width):
    keep = [column(forced_ref[g : g + 1, :]) for g in range(forced_ref.shape[0])]
    keep = 1.0 - jnp.concatenate(keep, axis=0).astype(F32)
    return jnp.concatenate([keep] * (width // LANES), axis=1)


def node_kernel(
    h_ref, own_ref, pair_ref, more_ref, off_ref, w_ref, forced_ref, up_ref,
    d_agg_ref, agg_ref, hidden_ref, d_inner_ref, d_pre_ref, unit_ref,
):
    width = h_ref.shape[1]
    pair = jnp.concatenate([pair_ref[...], more_ref[...]], axis=0)
    agg_ref[...] = (own_ref[...] + pair + decoded(off_ref[...])).astype(B16)
    vec = vectors_of(w_ref, width)
    latent, aggregate = w_ref[4 * width : 5 * width, :], w_ref[5 * width : 6 * width, :]
    second = w_ref[6 * width : 7 * width, :]
    pre = dot(h_ref[...], latent) + dot(agg_ref[...], aggregate) + vec[4:5, :]
    sigma = 1.0 / (1.0 + jnp.exp(-pre))
    hidden = (pre / (1.0 + jnp.exp(-pre))).astype(B16)
    hidden_ref[...] = hidden
    inner = dot(hidden, second) + vec[5:6, :]
    center = inner - jnp.mean(inner, axis=-1, keepdims=True)
    inverse = lax.rsqrt(jnp.mean(center * center, axis=-1, keepdims=True) + NORM_EPS)
    unit = center * inverse
    unit_ref[...] = unit
    scaled = kept_nodes(forced_ref, width) * up_ref[...] * vec[6:7, :]
    d_inner = inverse * (
        scaled
        - jnp.mean(scaled, axis=-1, keepdims=True)
        - unit * jnp.mean(scaled * unit, axis=-1, keepdims=True)
    )
    d_inner = d_inner.astype(B16)
    d_inner_ref[...] = d_inner
    slope = sigma * (1.0 + pre * (1.0 - sigma))
    d_pre = (dot_back(d_inner, second) * slope).astype(B16)
    d_pre_ref[...] = d_pre
    d_agg_ref[...] = dot_back(d_pre, aggregate).astype(B16)


def node_update(h, own, pair, more, off, weights, forced, upstream):
    nodes, width = h.shape
    half = jax.ShapeDtypeStruct((nodes, width), B16)
    return pl.pallas_call(
        node_kernel,
        out_shape=[half, half, half, half, half, jax.ShapeDtypeStruct((nodes, width), F32)],
        compiler_params=PARAMS,
        name="node_update",
        cost_estimate=pl.CostEstimate(
            flops=2 * nodes * width * width * 5, transcendentals=2 * nodes * width, bytes_accessed=nodes * width * 20
        ),
    )(h, own, pair, more, off, weights, forced.reshape(-1, LANES), upstream)


def node_grads_kernel(
    h_ref, agg_ref, hidden_ref, d_inner_ref, d_pre_ref, unit_ref, w_ref, forced_ref, up_ref,
    new_ref, grad_ref, sums_ref, back_ref,
):
    width = h_ref.shape[1]
    vec = vectors_of(w_ref, width)
    keep = kept_nodes(forced_ref, width)
    unit, upstream = unit_ref[...], up_ref[...]
    new_ref[...] = h_ref[...].astype(F32) + keep * (unit * vec[6:7, :] + vec[7:8, :])
    d_pre, d_inner, d_update = d_pre_ref[...], d_inner_ref[...], keep * upstream
    grad_ref[0:width, :] = dot_rows(h_ref[...], d_pre)
    grad_ref[width : 2 * width, :] = dot_rows(agg_ref[...], d_pre)
    grad_ref[2 * width : 3 * width, :] = dot_rows(hidden_ref[...], d_inner)
    back_ref[...] = upstream + dot_back(d_pre, w_ref[4 * width : 5 * width, :])
    sums_ref[...] = jnp.concatenate(
        [
            jnp.sum(d_pre.astype(F32), axis=0, keepdims=True),
            jnp.sum(d_inner.astype(F32), axis=0, keepdims=True),
            jnp.sum(d_update * unit, axis=0, keepdims=True),
            jnp.sum(d_update, axis=0, keepdims=True),
        ],
        axis=0,
    )


def node_grads(h, agg, hidden, d_inner, d_pre, unit, weights, forced, upstream):
    nodes, width = h.shape
    full = jax.ShapeDtypeStruct((nodes, width), F32)
    return pl.pallas_call(
        node_grads_kernel,
        out_shape=[full, jax.ShapeDtypeStruct((3 * width, width), F32), jax.ShapeDtypeStruct((4, width), F32), full],
        compiler_params=PARAMS,
        name="node_grads",
        cost_estimate=pl.CostEstimate(
            flops=2 * nodes * width * width * 4, transcendentals=0, bytes_accessed=nodes * width * 18
        ),
    )(h, agg, hidden, d_inner, d_pre, unit, weights, forced.reshape(-1, LANES), upstream)


def edge_backward_kernel(
    recv_ref, region_row_ref, off_ref, near_ref, hs_ref, hr_ref, x_ref, hidden_ref, slope_ref, unit_ref,
    inverse_ref, w_ref, node_grad_ref, node_sum_ref,
    d_pre_ref, kept_ref, sent_ref,
    d_inner_ref, vec_acc_ref,
):
    step = pl.program_id(0)
    steps = pl.num_programs(0)
    rows = slope_ref.shape[0]
    width = x_ref.shape[1]
    nodes = off_ref.shape[0]
    regions = w_ref.shape[0] - 7 * width - 8
    vec = vectors_of(w_ref, width)

    @pl.when(step == 0)
    def _():
        vec_acc_ref[...] = jnp.zeros_like(vec_acc_ref)

    d_message = dot(chosen_columns(recv_ref, step, rows, 2 * nodes, 3 * nodes), off_ref[...])
    d_message = d_message + near_ref[...].astype(F32)
    unit = unit_ref[...]
    scaled = d_message * vec[2:3, :]
    inverse = inverse_ref[:, 0:1]
    d_inner = inverse * (
        scaled
        - jnp.mean(scaled, axis=-1, keepdims=True)
        - unit * jnp.mean(scaled * unit, axis=-1, keepdims=True)
    )
    vec_acc_ref[0:8, :] += jnp.sum((d_message * unit).reshape(rows // 8, 8, width), axis=0)
    vec_acc_ref[8:16, :] += jnp.sum(d_message.reshape(rows // 8, 8, width), axis=0)
    d_inner = d_inner.astype(B16)
    d_pre = (dot_back(d_inner, w_ref[3 * width : 4 * width, :]) * slope_ref[...]).astype(B16)
    base = pl.multiple_of(step * rows, rows)
    d_inner_ref[pl.ds(base, rows), :] = d_inner
    d_pre_ref[pl.ds(base, rows), :] = d_pre

    @pl.when(step == steps - 1)
    def _():
        odd = odd_core()

        def put(start, piece):
            left, right = piece[:, 0:LANES], piece[:, LANES:]
            kept_ref[start : start + piece.shape[0], :] = jnp.where(odd, right, left)
            sent_ref[start : start + piece.shape[0], :] = jnp.where(odd, left, right)

        table_rows = node_grad_ref.shape[0] + 4 * width
        d_inner, d_pre = d_inner_ref[...], d_pre_ref[...]
        second_sum = dot(jnp.ones((16, d_inner.shape[0]), B16), d_inner)[0:1, :]
        table_grad = dot(chosen_rows(region_row_ref[...], 0, regions), d_pre)
        put(3 * width, dot_rows(hidden_ref[...], d_inner))
        put(0, dot_rows(hs_ref[...], d_pre))
        put(width, dot_rows(hr_ref[...], d_pre))
        put(2 * width, dot_rows(x_ref[...], d_pre))
        put(4 * width, node_grad_ref[...])
        vector_rows = jnp.concatenate(
            [
                jnp.sum(table_grad, axis=0, keepdims=True),
                second_sum,
                jnp.sum(vec_acc_ref[0:8, :], axis=0, keepdims=True),
                jnp.sum(vec_acc_ref[8:16, :], axis=0, keepdims=True),
                node_sum_ref[...],
            ],
            axis=0,
        )
        put(table_rows, vector_rows)
        put(table_rows + 8, table_grad)


def edge_backward(
    recv, regions, off, near, hs, hr, edges, hidden, slope, unit, inverse, weights, node_grad, node_sum,
):
    count, width = edges.shape
    tile, full = tiled(TILE, width), whole((count, width))
    grad_rows = weights.shape[0]
    half = whole((grad_rows, LANES))
    return pl.pallas_call(
        edge_backward_kernel,
        grid=(count // TILE,),
        in_specs=[
            whole((count // LANES, LANES)), whole((1, count)),
            whole(off.shape), tile, full, full, full, full, tile, tile, tiled(TILE, LANES),
            whole(weights.shape), whole(node_grad.shape), whole(node_sum.shape),
        ],
        out_specs=[full, half, half],
        out_shape=[
            jax.ShapeDtypeStruct((count, width), B16),
            jax.ShapeDtypeStruct((grad_rows, LANES), F32),
            jax.ShapeDtypeStruct((grad_rows, LANES), F32),
        ],
        scratch_shapes=[pltpu.VMEM((count, width), B16), pltpu.VMEM((16, width), F32)],
        compiler_params=PARAMS,
        name="edge_backward",
        cost_estimate=pl.CostEstimate(
            flops=2 * count * width * (6 * width + off.shape[0]), transcendentals=0, bytes_accessed=count * width * 20
        ),
    )(
        recv.reshape(-1, LANES), regions.reshape(1, -1), off, near, hs, hr, edges, hidden, slope, unit, inverse,
        weights, node_grad, node_sum,
    )


def node_part_of(index_row_ref, d_pre_ref, weight, slot, nodes):
    high, low = split(dot(chosen_rows(index_row_ref[...], slot * nodes, nodes), d_pre_ref[...]))
    return dot_back(high, weight) + dot_back(low, weight)


def sender_part_kernel(index_row_ref, d_pre_ref, w_ref, out_ref):
    nodes, width = out_ref.shape
    out_ref[...] = node_part_of(index_row_ref, d_pre_ref, w_ref[0:width, :], pl.program_id(0), nodes)


def sender_part(index, d_pre, weights, nodes):
    count, width = d_pre.shape
    return pl.pallas_call(
        sender_part_kernel,
        grid=(3,),
        in_specs=[whole((1, count)), whole((count, width)), whole(weights.shape)],
        out_specs=tiled(nodes, width),
        out_shape=jax.ShapeDtypeStruct((3 * nodes, width), F32),
        compiler_params=PARAMS,
        name="sender_part",
        cost_estimate=pl.CostEstimate(
            flops=6 * count * width * nodes, transcendentals=0, bytes_accessed=count * width * 2
        ),
    )(index.reshape(1, -1), d_pre, weights)


def receiver_part_kernel(index_row_ref, d_pre_ref, w_ref, part_ref, back_ref, own_ref, pair_ref, off_ref):
    nodes, width = back_ref.shape
    slot = pl.program_id(0)
    part = node_part_of(index_row_ref, d_pre_ref, w_ref[width : 2 * width, :], slot, nodes) + part_ref[...]

    @pl.when(slot == 0)
    def _():
        own_ref[...] = part + back_ref[...]

    @pl.when(slot == 1)
    def _():
        pair_ref[...] = part.astype(B16)

    @pl.when(slot == 2)
    def _():
        off_ref[...] = part.astype(B16)


def receiver_part(index, d_pre, weights, part, back):
    count, width = d_pre.shape
    nodes = back.shape[0]
    half = jax.ShapeDtypeStruct(back.shape, B16)
    return pl.pallas_call(
        receiver_part_kernel,
        grid=(3,),
        in_specs=[
            whole((1, count)), whole((count, width)), whole(weights.shape), tiled(nodes, width), whole(back.shape),
        ],
        out_specs=[whole(back.shape)] * 3,
        out_shape=[jax.ShapeDtypeStruct(back.shape, F32), half, half],
        compiler_params=PARAMS,
        name="receiver_part",
        cost_estimate=pl.CostEstimate(
            flops=6 * count * width * nodes, transcendentals=0, bytes_accessed=count * width * 2
        ),
    )(index.reshape(1, -1), d_pre, weights, part, back)


def edge_grads_kernel(d_pre_ref, w_ref, out_ref):
    width = d_pre_ref.shape[1]
    out_ref[...] = dot_back(d_pre_ref[...], w_ref[2 * width : 3 * width, :]).astype(B16)


def edge_grads(d_pre, weights):
    count, width = d_pre.shape
    return pl.pallas_call(
        edge_grads_kernel,
        grid=(count // TILE,),
        in_specs=[tiled(TILE, width), whole(weights.shape)],
        out_specs=tiled(TILE, width),
        out_shape=jax.ShapeDtypeStruct((count, width), B16),
        compiler_params=PARAMS,
        name="edge_grads",
        cost_estimate=pl.CostEstimate(
            flops=2 * count * width * width, transcendentals=0, bytes_accessed=count * width * 4
        ),
    )(d_pre, weights)


def packed(values, first):
    rows = values[first : first + 8, :]
    return jnp.concatenate([values, rows - rows.astype(B16).astype(F32)], axis=0).astype(B16)


def unpacked(wire, first):
    values = wire.astype(F32)
    share = values.shape[0] - 8
    exact = values[first : first + 8, :] + values[share:, :]
    return jnp.concatenate([values[:first, :], exact, values[first + 8 : share, :]], axis=0)


def parted_kernel(mine_ref, other_ref, kept_ref, *sent_refs, share, first):
    for k, out_ref in enumerate((kept_ref, *sent_refs)):
        rows = pl.ds(pl.multiple_of(jnp.bitwise_xor(lax.axis_index("feat"), k) * share, 8), share)
        total = mine_ref[rows, :] + other_ref[rows, :]
        out_ref[...] = packed(total, first) if k else total


def parted(mine, other, share, first):
    sent = jax.ShapeDtypeStruct((share + 8, LANES), B16)
    return pl.pallas_call(
        functools.partial(parted_kernel, share=share, first=first),
        out_shape=[jax.ShapeDtypeStruct((share, LANES), F32)] + [sent] * (mine.shape[0] // share - 1),
        compiler_params=PARAMS,
        name="parted",
    )(mine, other)


def gathered_kernel(mine_ref, *refs, first):
    total = mine_ref[...]
    for ref in refs[:-1]:
        total = total + unpacked(ref[...], first)
    refs[-1][...] = packed(total, first)


def gathered(mine, others, first):
    return pl.pallas_call(
        functools.partial(gathered_kernel, first=first),
        out_shape=jax.ShapeDtypeStruct(others[0].shape, B16),
        compiler_params=PARAMS,
        name="gathered",
    )(mine, *others)


def add_kernel(mine_ref, other_ref, out_ref, *, first):
    out_ref[...] = packed(unpacked(mine_ref[...], first) + unpacked(other_ref[...], first), first)


def add(mine, other, first):
    return pl.pallas_call(
        functools.partial(add_kernel, first=first),
        out_shape=jax.ShapeDtypeStruct(other.shape, B16),
        compiler_params=PARAMS,
        name="add",
    )(mine, other)


def finish_kernel(mine_ref, other_ref, out_ref, *, first, owner):
    share = out_ref.shape[0] - 16
    part = unpacked(mine_ref[...], first) + unpacked(other_ref[...], first)
    out_ref[0:share, :] = part
    out_ref[share : share + 8, :] = jnp.where(lax.axis_index("feat") == owner, part[first : first + 8, :], 0.0)
    squares = jnp.sum(jnp.sum(part * part, axis=0, keepdims=True), axis=1, keepdims=True)
    out_ref[share + 8 : share + 16, :] = jnp.broadcast_to(squares, (8, LANES))


def finish(mine, other, share, first, owner):
    return pl.pallas_call(
        functools.partial(finish_kernel, first=first, owner=owner),
        out_shape=jax.ShapeDtypeStruct((share + 16, LANES), F32),
        compiler_params=PARAMS,
        name="finish",
    )(mine, other)


def adam_kernel(
    step_ref, stats_ref, more_ref, mine_ref, other_ref, params_ref, first_ref, second_ref, averaged_ref,
    own_ref, pair_ref, off_ref,
    new_first_hbm, new_second_hbm, new_params_hbm, new_average_hbm, norm_ref, vector_ref, latents_hbm,
    new_first_ref, new_second_ref, new_params_ref, new_average_ref, latents_ref, sem,
):
    share = params_ref.shape[0]
    odd = odd_core()
    latents_ref[...] = own_ref[...] + pair_ref[...].astype(F32) + off_ref[...].astype(F32)
    copies = [pltpu.make_async_copy(latents_ref, latents_hbm, sem.at[0])]
    copies[0].start()
    stats = stats_ref[...] + more_ref[...]
    norm = jnp.sqrt(stats[8:9, 0:1] + stats[24:25, 0:1])
    norm_ref[...] = norm
    factor = jnp.minimum(1.0, MAX_NORM / (norm + 1e-06))
    count = step_ref[0:1, 0:1]
    first_scale = 1.0 - jnp.exp(count * jnp.log(jnp.full((1, 1), BETA_ONE, F32)))
    second_scale = 1.0 - jnp.exp(count * jnp.log(jnp.full((1, 1), BETA_TWO, F32)))
    decay = jnp.minimum(AVERAGE_DECAY, (1.0 + count) / (10.0 + count))
    vector_ref[:, 0:LANES] = jnp.where(odd, stats[16:24, :], stats[0:8, :]) * factor
    vector_ref[:, LANES : 2 * LANES] = jnp.where(odd, stats[0:8, :], stats[16:24, :]) * factor
    chunk = share // 3 if share % 24 == 0 else share
    for i in range(share // chunk):
        rows = slice(i * chunk, (i + 1) * chunk)
        mine, other = mine_ref[rows, :], other_ref[rows, :]
        both = jnp.concatenate([jnp.where(odd, other, mine), jnp.where(odd, mine, other)], axis=1)
        clipped = both * factor
        params = params_ref[rows, :]
        new_first = BETA_ONE * first_ref[rows, :] + (1.0 - BETA_ONE) * clipped
        new_second = BETA_TWO * second_ref[rows, :] + (1.0 - BETA_TWO) * clipped * clipped
        first_hat = new_first / first_scale
        second_hat = new_second / second_scale
        new_params = params - RATE * (first_hat / (jnp.sqrt(second_hat) + ADAM_EPS) + WEIGHT_DECAY * params)
        new_first_ref[rows, :] = new_first
        new_second_ref[rows, :] = new_second
        new_params_ref[rows, :] = new_params
        new_average_ref[rows, :] = decay * averaged_ref[rows, :] + (1.0 - decay) * new_params
        for k, (src, dst) in enumerate(
            (
                (new_first_ref, new_first_hbm), (new_second_ref, new_second_hbm), (new_params_ref, new_params_hbm),
                (new_average_ref, new_average_hbm),
            )
        ):
            copies.append(pltpu.make_async_copy(src.at[rows, :], dst.at[rows, :], sem.at[1 + 4 * i + k]))
            copies[-1].start()
    for copy in copies:
        copy.wait()


def adam(step, stats, more, mine, other, params, first_moment, second_moment, averaged, own, pair, off):
    rows = jax.ShapeDtypeStruct(params.shape, F32)
    vmem, hbm = (pl.BlockSpec(memory_space=m) for m in (pltpu.VMEM, pltpu.HBM))
    return pl.pallas_call(
        adam_kernel,
        in_specs=[vmem] * 12,
        out_specs=[hbm] * 4 + [vmem] * 2 + [hbm],
        out_shape=[
            rows, rows, rows, rows, jax.ShapeDtypeStruct((1, 1), F32), jax.ShapeDtypeStruct((8, params.shape[1]), F32),
            jax.ShapeDtypeStruct(own.shape, F32),
        ],
        scratch_shapes=[pltpu.VMEM(params.shape, F32)] * 4
        + [pltpu.VMEM(own.shape, F32), pltpu.SemaphoreType.DMA((13,))],
        compiler_params=PARAMS,
        name="adam",
        cost_estimate=pl.CostEstimate(
            flops=20 * params.size, transcendentals=2 * params.size, bytes_accessed=params.size * 32
        ),
    )(jnp.broadcast_to(step.astype(F32), (8, LANES)), stats, more, mine, other, params, first_moment, second_moment, averaged, own, pair, off)


def flipped(value, axis, bit):
    return lax.ppermute(value, axis, [(i, i ^ bit) for i in range(lax.axis_size(axis))])


def across(value, axis):
    count = lax.axis_size(axis)
    return lax.ppermute(value, axis, [(i, (i + 1 if i % 2 else i - 1) % count) for i in range(count)])


def neighbours(value):
    off = across(value, "edge")
    return flipped(value, "edge", 1), off


def on_device(
    node_latents, edge_latents, senders, receivers, regions, forced, params, first_moment, second_moment,
    averaged, step, cotangent,
):
    latents = node_latents[0]
    edges = edge_latents[0]
    upstream = cotangent[0]
    nodes, width = latents.shape
    share = params.shape[0]
    blocks, feats = lax.axis_size("edge"), lax.axis_size("feat")
    total = share * feats
    vector_row = 7 * width

    pair, off = neighbours(latents)

    mine, send, recv, latents = prologue(params, senders, receivers, latents)
    fetched = [mine] + [flipped(mine, "feat", k) for k in range(1, feats)]

    near_send = gather_near(send, latents, pair)
    near_recv = gather_near(recv, latents, pair)
    others = jnp.concatenate(lax.optimization_barrier((near_send, near_recv, *fetched[1:]))[2:])
    pieces = [fetched[0], others, flipped(fetched[0], "edge", 1), flipped(others, "edge", 1)]
    hs = gather_off(send, off, near_send)
    hr = gather_off(recv, off, near_recv)
    weights, high, low, to_off = edge_forward(regions, recv, hs, hr, edges, pieces, total, nodes)
    from_off = across(to_off, "edge")
    to_pair, more, own = near_sum(recv, high, low, nodes)
    from_pair, more = flipped(to_pair, "edge", 1), flipped(more, "edge", 1)
    hidden, slope = edge_slope(regions, hs, hr, edges, weights)
    own, hidden, slope = lax.optimization_barrier((own, hidden, slope))
    d_agg, agg, node_hidden, d_inner, d_pre, node_unit = node_update(
        latents, own, from_pair, more, from_off, weights, forced, upstream
    )
    back_pair, back_off = neighbours(d_agg)
    new_latents, node_grad, node_sum, back = node_grads(
        latents, agg, node_hidden, d_inner, d_pre, node_unit, weights, forced, upstream
    )
    near = gather_near(recv, d_agg, back_pair)
    unit, inverse = edge_unit(lax.optimization_barrier((hidden, d_agg))[0], weights)

    d_pre, kept, sent = edge_backward(
        recv, regions, back_off, near, hs, hr, edges, hidden, slope, unit, inverse, weights, node_grad, node_sum,
    )

    low_rows = vector_row % share
    part, *sent = parted(kept, flipped(sent, "edge", 1), share, low_rows)
    came = [flipped(wire, "feat", k + 1) for k, wire in enumerate(sent)]
    d_pre, part = lax.optimization_barrier((d_pre, part))
    send_part = sender_part(send, d_pre, weights, nodes)
    part_own, part_pair, part_off = receiver_part(recv, d_pre, weights, send_part, back)
    part, part_own, part_pair, part_off = lax.optimization_barrier((part, part_own, part_pair, part_off))
    wire = gathered(part, came, low_rows)
    bit = 2
    while 2 * bit < blocks:
        wire = add(wire, flipped(wire, "edge", bit), low_rows)
        bit *= 2
    grad_edges = edge_grads(d_pre, weights)
    wire, part_pair, part_off, grad_edges = lax.optimization_barrier((wire, part_pair, part_off, grad_edges))
    mine = finish(wire, flipped(wire, "edge", bit), share, low_rows, vector_row // share)
    grads_off = across(part_off, "edge")
    grads_pair = flipped(part_pair, "edge", 1)

    other = flipped(mine, "edge", 1)
    stats = jnp.concatenate([mine[share:], other[share:]], axis=0)
    bit = 1
    while 2 * bit < feats:
        stats = stats + flipped(stats, "feat", bit)
        bit *= 2
    more = flipped(stats, "feat", bit)
    new_first, new_second, new_params, new_average, grad_norm, vector_grads, grad_latents = adam(
        step, stats, more, mine, other, params, first_moment, second_moment, averaged,
        part_own, grads_pair, grads_off,
    )
    return (
        new_latents[None],
        grad_latents[None],
        grad_edges[None],
        new_first,
        new_second,
        new_params,
        new_average,
        grad_norm.reshape(1),
        vector_grads,
    )


def solution(mesh):
    nodes, rows = P("feat", "edge", None), P("feat", None)
    return jax.shard_map(
        on_device,
        mesh=mesh,
        in_specs=(nodes, nodes, P("edge"), P("edge"), P("edge"), P("edge"), rows, rows, rows, rows, P(), nodes),
        out_specs=(nodes, nodes, nodes, rows, rows, rows, rows, P(), P()),
        check_vma=False,
    )
```

```python
import functools

import jax
import jax.numpy as jnp
from jax import lax
from jax.experimental import pallas as pl
from jax.experimental.pallas import tpu as pltpu
from jax.sharding import PartitionSpec as P

NORM_EPS = 1e-05
MAX_NORM = 512.0
RATE = 0.05
BETA_ONE = 0.9
BETA_TWO = 0.95
ADAM_EPS = 1e-08
WEIGHT_DECAY = 0.1
AVERAGE_DECAY = 0.999

LANES = 128
TINY = 1e-20
STEPS = 18
LOG_TWO = 0.6931471805599453
TILE = 2048
PART = 512
B16 = jnp.bfloat16
F32 = jnp.float32
I32 = jnp.int32
I16 = jnp.int16
PARAMS = pltpu.CompilerParams(vmem_limit_bytes=20 * 1024 * 1024)


def dot(left, right):
    return jnp.dot(left, right, preferred_element_type=F32)


def dot_rows(left, right):
    return lax.dot_general(left, right, (((0,), (0,)), ((), ())), preferred_element_type=F32)


def dot_back(left, right):
    return lax.dot_general(left, right, (((1,), (1,)), ((), ())), preferred_element_type=F32)


def vectors_of(w_ref, width):
    return w_ref[7 * width : 7 * width + 8, :].astype(F32)


def split(values):
    high = values.astype(B16)
    return high, (values - high.astype(F32)).astype(B16)


def whole(shape):
    return pl.BlockSpec(shape, lambda i: (0,) * len(shape))


def tiled(rows, cols):
    return pl.BlockSpec((rows, cols), lambda i: (i, 0))


def column(row):
    return jnp.broadcast_to(row, (LANES, LANES)).T


def chosen_columns(index_ref, tile, rows, first, last):
    lane = lax.broadcasted_iota(I32, (LANES, LANES), 1)
    groups = []
    for g in range(rows // LANES):
        col = column(index_ref[pl.ds(tile * (rows // LANES) + g, 1), :])
        groups.append(
            jnp.concatenate(
                [jnp.where(col == lane + base, 1.0, 0.0).astype(B16) for base in range(first, last, LANES)],
                axis=1,
            )
        )
    return jnp.concatenate(groups, axis=0)


def chosen_rows(index_row, first, count):
    node = lax.broadcasted_iota(I32, (count, index_row.shape[1]), 0) + first
    return jnp.where(index_row == node, 1.0, 0.0).astype(B16)


def core_of(e):
    return e % 2


def odd_core():
    return core_of(lax.axis_index("edge")) == 1


def prologue_kernel(
    params_hbm, send_hbm, recv_hbm, latents_hbm, half_ref, send_ref, recv_ref, latents_ref, wide_ref, in_ref, sem,
    *, nodes,
):
    copies = [
        pltpu.make_async_copy(params_hbm, wide_ref, sem.at[0]),
        pltpu.make_async_copy(send_hbm, in_ref.at[0], sem.at[1]),
        pltpu.make_async_copy(recv_hbm, in_ref.at[1], sem.at[2]),
        pltpu.make_async_copy(latents_hbm, latents_ref, sem.at[3]),
    ]
    for copy in copies:
        copy.start()
    e = lax.axis_index("edge")
    core = core_of(e)
    for i, out_ref in ((0, send_ref), (1, recv_ref)):
        copies[1 + i].wait()
        index = in_ref[i]
        block = lax.div(index, nodes)
        slot = jnp.where(block == e, 0, jnp.where(block == e + 1 - 2 * core, 1, 2))
        out_ref[...] = (slot - block) * nodes + index
    copies[0].wait()
    half_ref[...] = jnp.where(core == 1, wide_ref[:, LANES : 2 * LANES], wide_ref[:, 0:LANES]).astype(B16)
    copies[3].wait()


def prologue(params, senders, receivers, latents):
    shape = (senders.size // LANES, LANES)
    out = jax.ShapeDtypeStruct(shape, I32)
    vmem, hbm = pl.BlockSpec(memory_space=pltpu.VMEM), pl.BlockSpec(memory_space=pltpu.HBM)
    operands = (params, senders.reshape(shape), receivers.reshape(shape), latents)
    half, send, recv, own = pl.pallas_call(
        functools.partial(prologue_kernel, nodes=latents.shape[0]),
        in_specs=[hbm] * 4,
        out_specs=[vmem] * 4,
        out_shape=[
            jax.ShapeDtypeStruct((params.shape[0], LANES), B16), out, out,
            jax.ShapeDtypeStruct(latents.shape, latents.dtype),
        ],
        scratch_shapes=[
            pltpu.VMEM(params.shape, F32), pltpu.VMEM((2, *shape), I32), pltpu.SemaphoreType.DMA((4,)),
        ],
        compiler_params=PARAMS,
        name="prologue",
    )(*(pltpu.with_memory_space_constraint(a, pltpu.HBM) for a in operands))
    return half, send.reshape(-1), recv.reshape(-1), own


def gather_near_kernel(index_ref, own_ref, pair_ref, out_ref):
    tile = pl.program_id(0)
    rows = out_ref.shape[0]
    nodes = own_ref.shape[0]
    total = dot(chosen_columns(index_ref, tile, rows, 0, nodes), own_ref[...])
    total = total + dot(chosen_columns(index_ref, tile, rows, nodes, 2 * nodes), pair_ref[...])
    out_ref[...] = total.astype(B16)


def gather_near(index, own, pair):
    nodes, width = own.shape
    edges = index.size
    return pl.pallas_call(
        gather_near_kernel,
        grid=(1,),
        in_specs=[whole((edges // LANES, LANES))] + [whole((nodes, width))] * 2,
        out_specs=tiled(edges, width),
        out_shape=jax.ShapeDtypeStruct((edges, width), B16),
        compiler_params=PARAMS,
        name="gather_near",
        cost_estimate=pl.CostEstimate(
            flops=2 * edges * 2 * nodes * width, transcendentals=0, bytes_accessed=edges * width * 2
        ),
    )(index.reshape(-1, LANES), own, pair)


def gather_off_kernel(index_ref, off_ref, near_ref, out_ref):
    tile = pl.program_id(0)
    rows = out_ref.shape[0]
    nodes = off_ref.shape[0]
    total = dot(chosen_columns(index_ref, tile, rows, 2 * nodes, 3 * nodes), off_ref[...])
    out_ref[...] = (total + near_ref[...].astype(F32)).astype(B16)


def gather_off(index, off, near):
    nodes, width = off.shape
    edges = index.size
    return pl.pallas_call(
        gather_off_kernel,
        grid=(1,),
        in_specs=[whole((edges // LANES, LANES)), whole((nodes, width)), tiled(edges, width)],
        out_specs=tiled(edges, width),
        out_shape=jax.ShapeDtypeStruct((edges, width), B16),
        compiler_params=PARAMS,
        name="gather_off",
        cost_estimate=pl.CostEstimate(
            flops=2 * edges * nodes * width, transcendentals=0, bytes_accessed=edges * width * 4
        ),
    )(index.reshape(-1, LANES), off, near)


def before_silu(region_ref, tile, hs_ref, hr_ref, x_ref, w_ref):
    rows, width = x_ref.shape
    vector_row = 7 * width
    regions = w_ref.shape[0] - vector_row - 8
    table = jnp.concatenate(
        [w_ref[vector_row + 8 :, :].astype(F32), jnp.zeros((LANES - regions, width), F32)], axis=0
    ).astype(B16)
    pre = dot(hs_ref[...], w_ref[0:width, :])
    pre = pre + dot(hr_ref[...], w_ref[width : 2 * width, :])
    pre = pre + dot(x_ref[...], w_ref[2 * width : 3 * width, :])
    pre = pre + dot(chosen_columns(region_ref, tile, rows, 0, LANES), table)
    return pre + vectors_of(w_ref, width)[0:1, :]


def normalized(hidden, w_ref, vec):
    width = hidden.shape[1]
    inner = dot(hidden, w_ref[3 * width : 4 * width, :]) + vec[1:2, :]
    center = inner - jnp.mean(inner, axis=-1, keepdims=True)
    inverse = lax.rsqrt(jnp.mean(center * center, axis=-1, keepdims=True) + NORM_EPS)
    return center * inverse, inverse


def power_of_two(exponents):
    return jnp.exp(exponents * LOG_TWO)


def encoded(values):
    rows, width = values.shape
    quarter = rows // 4
    largest = jnp.maximum(jnp.max(jnp.abs(values), axis=-1, keepdims=True), TINY)
    exponents = jnp.ceil(jnp.log(largest) * (1.0 / LOG_TWO))
    codes = jnp.round(values * power_of_two(STEPS - exponents)).astype(I32)
    upper = lax.shift_right_arithmetic(codes, 4)
    words = jnp.full((quarter, width), -32768, I32)
    for i in range(4):
        words = words + lax.shift_left(jnp.bitwise_and(codes[i * quarter : (i + 1) * quarter, :], 15), 4 * i)
    marks = [
        jnp.broadcast_to(exponents[g * LANES : (g + 1) * LANES, :], (LANES, LANES)).T[0:1, :]
        for g in range(rows // LANES)
    ]
    marks = jnp.concatenate([*marks, jnp.zeros((16 - len(marks), LANES), F32)], axis=0).astype(I32)
    marks = jnp.concatenate([marks, jnp.zeros((16, width - LANES), I32)], axis=1)
    return jnp.concatenate([upper, words, marks], axis=0).astype(I16)


def decoded(wire):
    width = wire.shape[1]
    quarter = (wire.shape[0] - 16) // 5
    rows = 4 * quarter
    wire = wire.astype(I32)
    words = wire[rows : rows + quarter, :] + 32768
    lower = jnp.concatenate([jnp.bitwise_and(lax.shift_right_arithmetic(words, 4 * i), 15) for i in range(4)], axis=0)
    codes = (wire[:rows, :] * 16 + lower).astype(F32)
    exponents = wire[rows + quarter :, :LANES].astype(F32)
    scale = [power_of_two(column(exponents[g : g + 1, :]) - STEPS) for g in range(rows // LANES)]
    return codes * jnp.concatenate([jnp.concatenate(scale, axis=0)] * (width // LANES), axis=1)


def ways(count):
    return sorted(range(1, count), key=lambda k: (k < count // 2, k))


def edge_forward_kernel(
    region_ref, recv_row_ref, hs_ref, hr_ref, x_ref, *refs,
):
    pieces, refs = refs[:-5], refs[-5:]
    w_ref, high_ref, low_ref, halo_ref, wide_ref = refs
    rows, width = x_ref.shape
    nodes = (halo_ref.shape[0] - 16) // 5 * 4

    @pl.when(pl.program_id(0) == 0)
    def _():
        odd, f = odd_core(), lax.axis_index("feat")
        share = pieces[0].shape[0]
        shares = w_ref.shape[0] // share
        for k in range(shares):
            at = ways(shares).index(k) if k else 0
            rows = slice(at * share, (at + 1) * share)
            mine, other = (pieces[i][...] if k == 0 else pieces[i + 1][rows, :] for i in (0, 2))
            mine, other = mine.astype(F32), other.astype(F32)
            base = pl.multiple_of(jnp.bitwise_xor(f, k) * share, 8)
            wide_ref[pl.ds(base, share), 0:LANES] = jnp.where(odd, other, mine)
            wide_ref[pl.ds(base, share), LANES : 2 * LANES] = jnp.where(odd, mine, other)
        w_ref[...] = wide_ref[...].astype(B16)

    vec = vectors_of(w_ref, width)
    total = None
    for i in range(rows // PART + 1):
        if i < rows // PART:
            here = slice(i * PART, (i + 1) * PART)
            pre = before_silu(region_ref, i, hs_ref.at[here, :], hr_ref.at[here, :], x_ref.at[here, :], w_ref)
            hidden = (pre / (1.0 + jnp.exp(-pre))).astype(B16)
            unit, _ = normalized(hidden, w_ref, vec)
            high, low = split(unit * vec[2:3, :] + vec[3:4, :])
            high_ref[here, :] = high
            low_ref[here, :] = low
        if i > 0:
            last = slice((i - 1) * PART, i * PART)
            onehot = chosen_rows(recv_row_ref[:, last], 2 * nodes, nodes)
            more = dot(onehot, high_ref[last, :]) + dot(onehot, low_ref[last, :])
            total = more if total is None else total + more
    halo_ref[...] = encoded(total)


def edge_forward(regions, recv, hs, hr, edges, pieces, total, nodes):
    count, width = edges.shape
    tile = tiled(count, width)
    return pl.pallas_call(
        edge_forward_kernel,
        grid=(1,),
        in_specs=[
            whole((count // LANES, LANES)), whole((1, count)), tile, tile, tile,
            *[whole(piece.shape) for piece in pieces],
        ],
        out_specs=[
            whole((total, width)), whole((count, width)), whole((count, width)),
            whole((nodes + nodes // 4 + 16, width)),
        ],
        out_shape=[
            jax.ShapeDtypeStruct((total, width), B16),
            jax.ShapeDtypeStruct((count, width), B16),
            jax.ShapeDtypeStruct((count, width), B16),
            jax.ShapeDtypeStruct((nodes + nodes // 4 + 16, width), I16),
        ],
        scratch_shapes=[pltpu.VMEM((total, width), F32)],
        compiler_params=PARAMS,
        name="edge_forward",
        cost_estimate=pl.CostEstimate(
            flops=2 * count * width * (5 * width + 2 * nodes), transcendentals=2 * count * width,
            bytes_accessed=count * width * 10,
        ),
    )(regions.reshape(-1, LANES), recv.reshape(1, -1), hs, hr, edges, *pieces)


def edge_slope_kernel(region_ref, hs_ref, hr_ref, x_ref, w_ref, hidden_ref, slope_ref):
    pre = before_silu(region_ref, pl.program_id(0), hs_ref, hr_ref, x_ref, w_ref)
    sigma = 1.0 / (1.0 + jnp.exp(-pre))
    hidden_ref[...] = (pre / (1.0 + jnp.exp(-pre))).astype(B16)
    slope_ref[...] = sigma * (1.0 + pre * (1.0 - sigma))


def edge_slope(regions, hs, hr, edges, weights):
    count, width = edges.shape
    tile = tiled(TILE, width)
    return pl.pallas_call(
        edge_slope_kernel,
        grid=(count // TILE,),
        in_specs=[whole((count // LANES, LANES)), tile, tile, tile, whole(weights.shape)],
        out_specs=[tile, tile],
        out_shape=[jax.ShapeDtypeStruct((count, width), B16), jax.ShapeDtypeStruct((count, width), F32)],
        compiler_params=PARAMS,
        name="edge_slope",
        cost_estimate=pl.CostEstimate(
            flops=2 * count * width * 4 * width, transcendentals=2 * count * width, bytes_accessed=count * width * 12
        ),
    )(regions.reshape(-1, LANES), hs, hr, edges, weights)


def edge_unit_kernel(hidden_ref, w_ref, unit_ref, inverse_ref):
    unit, inverse = normalized(hidden_ref[...], w_ref, vectors_of(w_ref, hidden_ref.shape[1]))
    unit_ref[...] = unit
    inverse_ref[...] = jnp.broadcast_to(inverse, inverse_ref.shape)


def edge_unit(hidden, weights):
    count, width = hidden.shape
    tile = tiled(TILE, width)
    return pl.pallas_call(
        edge_unit_kernel,
        grid=(count // TILE,),
        in_specs=[tile, whole(weights.shape)],
        out_specs=[tile, tiled(TILE, LANES)],
        out_shape=[jax.ShapeDtypeStruct((count, width), F32), jax.ShapeDtypeStruct((count, LANES), F32)],
        compiler_params=PARAMS,
        name="edge_unit",
        cost_estimate=pl.CostEstimate(
            flops=2 * count * width * width, transcendentals=count, bytes_accessed=count * width * 8
        ),
    )(hidden, weights)


def near_sum_kernel(recv_row_ref, high_ref, low_ref, pair_ref, more_ref, own_ref):
    nodes = own_ref.shape[0]
    half = nodes // 2
    for first, out_ref in ((nodes, pair_ref), (nodes + half, more_ref), (0, own_ref)):
        onehot = chosen_rows(recv_row_ref[...], first, out_ref.shape[0])
        out_ref[...] = dot(onehot, high_ref[...]) + dot(onehot, low_ref[...])


def near_sum(recv, high, low, nodes):
    count, width = high.shape
    half = jax.ShapeDtypeStruct((nodes // 2, width), F32)
    return pl.pallas_call(
        near_sum_kernel,
        out_shape=[half, half, jax.ShapeDtypeStruct((nodes, width), F32)],
        compiler_params=PARAMS,
        name="near_sum",
        cost_estimate=pl.CostEstimate(
            flops=8 * count * width * nodes, transcendentals=0, bytes_accessed=count * width * 4
        ),
    )(recv.reshape(1, -1), high, low)


def kept_nodes(forced_ref, width):
    keep = [column(forced_ref[g : g + 1, :]) for g in range(forced_ref.shape[0])]
    keep = 1.0 - jnp.concatenate(keep, axis=0).astype(F32)
    return jnp.concatenate([keep] * (width // LANES), axis=1)


def node_kernel(
    h_ref, own_ref, pair_ref, more_ref, off_ref, w_ref, forced_ref, up_ref,
    d_agg_ref, agg_ref, hidden_ref, d_inner_ref, d_pre_ref, unit_ref,
):
    width = h_ref.shape[1]
    pair = jnp.concatenate([pair_ref[...], more_ref[...]], axis=0)
    agg_ref[...] = (own_ref[...] + pair + decoded(off_ref[...])).astype(B16)
    vec = vectors_of(w_ref, width)
    latent, aggregate = w_ref[4 * width : 5 * width, :], w_ref[5 * width : 6 * width, :]
    second = w_ref[6 * width : 7 * width, :]
    pre = dot(h_ref[...], latent) + dot(agg_ref[...], aggregate) + vec[4:5, :]
    sigma = 1.0 / (1.0 + jnp.exp(-pre))
    hidden = (pre / (1.0 + jnp.exp(-pre))).astype(B16)
    hidden_ref[...] = hidden
    inner = dot(hidden, second) + vec[5:6, :]
    center = inner - jnp.mean(inner, axis=-1, keepdims=True)
    inverse = lax.rsqrt(jnp.mean(center * center, axis=-1, keepdims=True) + NORM_EPS)
    unit = center * inverse
    unit_ref[...] = unit
    scaled = kept_nodes(forced_ref, width) * up_ref[...] * vec[6:7, :]
    d_inner = inverse * (
        scaled
        - jnp.mean(scaled, axis=-1, keepdims=True)
        - unit * jnp.mean(scaled * unit, axis=-1, keepdims=True)
    )
    d_inner = d_inner.astype(B16)
    d_inner_ref[...] = d_inner
    slope = sigma * (1.0 + pre * (1.0 - sigma))
    d_pre = (dot_back(d_inner, second) * slope).astype(B16)
    d_pre_ref[...] = d_pre
    d_agg_ref[...] = dot_back(d_pre, aggregate).astype(B16)


def node_update(h, own, pair, more, off, weights, forced, upstream):
    nodes, width = h.shape
    half = jax.ShapeDtypeStruct((nodes, width), B16)
    return pl.pallas_call(
        node_kernel,
        out_shape=[half, half, half, half, half, jax.ShapeDtypeStruct((nodes, width), F32)],
        compiler_params=PARAMS,
        name="node_update",
        cost_estimate=pl.CostEstimate(
            flops=2 * nodes * width * width * 5, transcendentals=2 * nodes * width, bytes_accessed=nodes * width * 20
        ),
    )(h, own, pair, more, off, weights, forced.reshape(-1, LANES), upstream)


def node_grads_kernel(
    h_ref, agg_ref, hidden_ref, d_inner_ref, d_pre_ref, unit_ref, w_ref, forced_ref, up_ref,
    new_ref, grad_ref, sums_ref, back_ref,
):
    width = h_ref.shape[1]
    vec = vectors_of(w_ref, width)
    keep = kept_nodes(forced_ref, width)
    unit, upstream = unit_ref[...], up_ref[...]
    new_ref[...] = h_ref[...].astype(F32) + keep * (unit * vec[6:7, :] + vec[7:8, :])
    d_pre, d_inner, d_update = d_pre_ref[...], d_inner_ref[...], keep * upstream
    grad_ref[0:width, :] = dot_rows(h_ref[...], d_pre)
    grad_ref[width : 2 * width, :] = dot_rows(agg_ref[...], d_pre)
    grad_ref[2 * width : 3 * width, :] = dot_rows(hidden_ref[...], d_inner)
    back_ref[...] = upstream + dot_back(d_pre, w_ref[4 * width : 5 * width, :])
    sums_ref[...] = jnp.concatenate(
        [
            jnp.sum(d_pre.astype(F32), axis=0, keepdims=True),
            jnp.sum(d_inner.astype(F32), axis=0, keepdims=True),
            jnp.sum(d_update * unit, axis=0, keepdims=True),
            jnp.sum(d_update, axis=0, keepdims=True),
        ],
        axis=0,
    )


def node_grads(h, agg, hidden, d_inner, d_pre, unit, weights, forced, upstream):
    nodes, width = h.shape
    full = jax.ShapeDtypeStruct((nodes, width), F32)
    return pl.pallas_call(
        node_grads_kernel,
        out_shape=[full, jax.ShapeDtypeStruct((3 * width, width), F32), jax.ShapeDtypeStruct((4, width), F32), full],
        compiler_params=PARAMS,
        name="node_grads",
        cost_estimate=pl.CostEstimate(
            flops=2 * nodes * width * width * 4, transcendentals=0, bytes_accessed=nodes * width * 18
        ),
    )(h, agg, hidden, d_inner, d_pre, unit, weights, forced.reshape(-1, LANES), upstream)


def edge_backward_kernel(
    recv_ref, region_row_ref, off_ref, near_ref, hs_ref, hr_ref, x_ref, hidden_ref, slope_ref, unit_ref,
    inverse_ref, w_ref, node_grad_ref, node_sum_ref,
    d_pre_ref, kept_ref, sent_ref,
    d_inner_ref, vec_acc_ref,
):
    step = pl.program_id(0)
    steps = pl.num_programs(0)
    rows = slope_ref.shape[0]
    width = x_ref.shape[1]
    nodes = off_ref.shape[0]
    regions = w_ref.shape[0] - 7 * width - 8
    vec = vectors_of(w_ref, width)

    @pl.when(step == 0)
    def _():
        vec_acc_ref[...] = jnp.zeros_like(vec_acc_ref)

    d_message = dot(chosen_columns(recv_ref, step, rows, 2 * nodes, 3 * nodes), off_ref[...])
    d_message = d_message + near_ref[...].astype(F32)
    unit = unit_ref[...]
    scaled = d_message * vec[2:3, :]
    inverse = inverse_ref[:, 0:1]
    d_inner = inverse * (
        scaled
        - jnp.mean(scaled, axis=-1, keepdims=True)
        - unit * jnp.mean(scaled * unit, axis=-1, keepdims=True)
    )
    vec_acc_ref[0:8, :] += jnp.sum((d_message * unit).reshape(rows // 8, 8, width), axis=0)
    vec_acc_ref[8:16, :] += jnp.sum(d_message.reshape(rows // 8, 8, width), axis=0)
    d_inner = d_inner.astype(B16)
    d_pre = (dot_back(d_inner, w_ref[3 * width : 4 * width, :]) * slope_ref[...]).astype(B16)
    base = pl.multiple_of(step * rows, rows)
    d_inner_ref[pl.ds(base, rows), :] = d_inner
    d_pre_ref[pl.ds(base, rows), :] = d_pre

    @pl.when(step == steps - 1)
    def _():
        odd = odd_core()

        def put(start, piece):
            left, right = piece[:, 0:LANES], piece[:, LANES:]
            kept_ref[start : start + piece.shape[0], :] = jnp.where(odd, right, left)
            sent_ref[start : start + piece.shape[0], :] = jnp.where(odd, left, right)

        table_rows = node_grad_ref.shape[0] + 4 * width
        d_inner, d_pre = d_inner_ref[...], d_pre_ref[...]
        second_sum = dot(jnp.ones((16, d_inner.shape[0]), B16), d_inner)[0:1, :]
        table_grad = dot(chosen_rows(region_row_ref[...], 0, regions), d_pre)
        put(3 * width, dot_rows(hidden_ref[...], d_inner))
        put(0, dot_rows(hs_ref[...], d_pre))
        put(width, dot_rows(hr_ref[...], d_pre))
        put(2 * width, dot_rows(x_ref[...], d_pre))
        put(4 * width, node_grad_ref[...])
        vector_rows = jnp.concatenate(
            [
                jnp.sum(table_grad, axis=0, keepdims=True),
                second_sum,
                jnp.sum(vec_acc_ref[0:8, :], axis=0, keepdims=True),
                jnp.sum(vec_acc_ref[8:16, :], axis=0, keepdims=True),
                node_sum_ref[...],
            ],
            axis=0,
        )
        put(table_rows, vector_rows)
        put(table_rows + 8, table_grad)


def edge_backward(
    recv, regions, off, near, hs, hr, edges, hidden, slope, unit, inverse, weights, node_grad, node_sum,
):
    count, width = edges.shape
    tile, full = tiled(TILE, width), whole((count, width))
    grad_rows = weights.shape[0]
    half = whole((grad_rows, LANES))
    return pl.pallas_call(
        edge_backward_kernel,
        grid=(count // TILE,),
        in_specs=[
            whole((count // LANES, LANES)), whole((1, count)),
            whole(off.shape), tile, full, full, full, full, tile, tile, tiled(TILE, LANES),
            whole(weights.shape), whole(node_grad.shape), whole(node_sum.shape),
        ],
        out_specs=[full, half, half],
        out_shape=[
            jax.ShapeDtypeStruct((count, width), B16),
            jax.ShapeDtypeStruct((grad_rows, LANES), F32),
            jax.ShapeDtypeStruct((grad_rows, LANES), F32),
        ],
        scratch_shapes=[pltpu.VMEM((count, width), B16), pltpu.VMEM((16, width), F32)],
        compiler_params=PARAMS,
        name="edge_backward",
        cost_estimate=pl.CostEstimate(
            flops=2 * count * width * (6 * width + off.shape[0]), transcendentals=0, bytes_accessed=count * width * 20
        ),
    )(
        recv.reshape(-1, LANES), regions.reshape(1, -1), off, near, hs, hr, edges, hidden, slope, unit, inverse,
        weights, node_grad, node_sum,
    )


def node_part_of(index_row_ref, d_pre_ref, weight, slot, nodes):
    high, low = split(dot(chosen_rows(index_row_ref[...], slot * nodes, nodes), d_pre_ref[...]))
    return dot_back(high, weight) + dot_back(low, weight)


def sender_part_kernel(index_row_ref, d_pre_ref, w_ref, out_ref):
    nodes, width = out_ref.shape
    out_ref[...] = node_part_of(index_row_ref, d_pre_ref, w_ref[0:width, :], pl.program_id(0), nodes)


def sender_part(index, d_pre, weights, nodes):
    count, width = d_pre.shape
    return pl.pallas_call(
        sender_part_kernel,
        grid=(3,),
        in_specs=[whole((1, count)), whole((count, width)), whole(weights.shape)],
        out_specs=tiled(nodes, width),
        out_shape=jax.ShapeDtypeStruct((3 * nodes, width), F32),
        compiler_params=PARAMS,
        name="sender_part",
        cost_estimate=pl.CostEstimate(
            flops=6 * count * width * nodes, transcendentals=0, bytes_accessed=count * width * 2
        ),
    )(index.reshape(1, -1), d_pre, weights)


def receiver_part_kernel(index_row_ref, d_pre_ref, w_ref, part_ref, back_ref, own_ref, pair_ref, off_ref):
    nodes, width = back_ref.shape
    slot = pl.program_id(0)
    part = node_part_of(index_row_ref, d_pre_ref, w_ref[width : 2 * width, :], slot, nodes) + part_ref[...]

    @pl.when(slot == 0)
    def _():
        own_ref[...] = part + back_ref[...]

    @pl.when(slot == 1)
    def _():
        pair_ref[...] = part.astype(B16)

    @pl.when(slot == 2)
    def _():
        off_ref[...] = part.astype(B16)


def receiver_part(index, d_pre, weights, part, back):
    count, width = d_pre.shape
    nodes = back.shape[0]
    half = jax.ShapeDtypeStruct(back.shape, B16)
    return pl.pallas_call(
        receiver_part_kernel,
        grid=(3,),
        in_specs=[
            whole((1, count)), whole((count, width)), whole(weights.shape), tiled(nodes, width), whole(back.shape),
        ],
        out_specs=[whole(back.shape)] * 3,
        out_shape=[jax.ShapeDtypeStruct(back.shape, F32), half, half],
        compiler_params=PARAMS,
        name="receiver_part",
        cost_estimate=pl.CostEstimate(
            flops=6 * count * width * nodes, transcendentals=0, bytes_accessed=count * width * 2
        ),
    )(index.reshape(1, -1), d_pre, weights, part, back)


def edge_grads_kernel(d_pre_ref, w_ref, out_ref):
    width = d_pre_ref.shape[1]
    out_ref[...] = dot_back(d_pre_ref[...], w_ref[2 * width : 3 * width, :]).astype(B16)


def edge_grads(d_pre, weights):
    count, width = d_pre.shape
    return pl.pallas_call(
        edge_grads_kernel,
        grid=(count // TILE,),
        in_specs=[tiled(TILE, width), whole(weights.shape)],
        out_specs=tiled(TILE, width),
        out_shape=jax.ShapeDtypeStruct((count, width), B16),
        compiler_params=PARAMS,
        name="edge_grads",
        cost_estimate=pl.CostEstimate(
            flops=2 * count * width * width, transcendentals=0, bytes_accessed=count * width * 4
        ),
    )(d_pre, weights)


def packed(values, first):
    rows = values[first : first + 8, :]
    return jnp.concatenate([values, rows - rows.astype(B16).astype(F32)], axis=0).astype(B16)


def unpacked(wire, first):
    values = wire.astype(F32)
    share = values.shape[0] - 8
    exact = values[first : first + 8, :] + values[share:, :]
    return jnp.concatenate([values[:first, :], exact, values[first + 8 : share, :]], axis=0)


def parted_kernel(mine_ref, other_ref, kept_ref, *sent_refs, share, first):
    for k, out_ref in enumerate((kept_ref, *sent_refs)):
        rows = pl.ds(pl.multiple_of(jnp.bitwise_xor(lax.axis_index("feat"), k) * share, 8), share)
        total = mine_ref[rows, :] + other_ref[rows, :]
        out_ref[...] = packed(total, first) if k else total


def parted(mine, other, share, first):
    sent = jax.ShapeDtypeStruct((share + 8, LANES), B16)
    return pl.pallas_call(
        functools.partial(parted_kernel, share=share, first=first),
        out_shape=[jax.ShapeDtypeStruct((share, LANES), F32)] + [sent] * (mine.shape[0] // share - 1),
        compiler_params=PARAMS,
        name="parted",
    )(mine, other)


def gathered_kernel(mine_ref, *refs, first):
    total = mine_ref[...]
    for ref in refs[:-1]:
        total = total + unpacked(ref[...], first)
    refs[-1][...] = packed(total, first)


def gathered(mine, others, first):
    return pl.pallas_call(
        functools.partial(gathered_kernel, first=first),
        out_shape=jax.ShapeDtypeStruct(others[0].shape, B16),
        compiler_params=PARAMS,
        name="gathered",
    )(mine, *others)


def add_kernel(mine_ref, other_ref, out_ref, *, first):
    out_ref[...] = packed(unpacked(mine_ref[...], first) + unpacked(other_ref[...], first), first)


def add(mine, other, first):
    return pl.pallas_call(
        functools.partial(add_kernel, first=first),
        out_shape=jax.ShapeDtypeStruct(other.shape, B16),
        compiler_params=PARAMS,
        name="add",
    )(mine, other)


def finish_kernel(mine_ref, other_ref, out_ref, *, first, owner):
    share = out_ref.shape[0] - 16
    part = unpacked(mine_ref[...], first) + unpacked(other_ref[...], first)
    out_ref[0:share, :] = part
    out_ref[share : share + 8, :] = jnp.where(lax.axis_index("feat") == owner, part[first : first + 8, :], 0.0)
    squares = jnp.sum(jnp.sum(part * part, axis=0, keepdims=True), axis=1, keepdims=True)
    out_ref[share + 8 : share + 16, :] = jnp.broadcast_to(squares, (8, LANES))


def finish(mine, other, share, first, owner):
    return pl.pallas_call(
        functools.partial(finish_kernel, first=first, owner=owner),
        out_shape=jax.ShapeDtypeStruct((share + 16, LANES), F32),
        compiler_params=PARAMS,
        name="finish",
    )(mine, other)


def adam_kernel(
    step_ref, stats_ref, more_ref, mine_ref, other_ref, params_ref, first_ref, second_ref, averaged_ref,
    own_ref, pair_ref, off_ref,
    new_first_hbm, new_second_hbm, new_params_hbm, new_average_hbm, norm_ref, vector_ref, latents_hbm,
    new_first_ref, new_second_ref, new_params_ref, new_average_ref, latents_ref, sem,
):
    share = params_ref.shape[0]
    odd = odd_core()
    latents_ref[...] = own_ref[...] + pair_ref[...].astype(F32) + off_ref[...].astype(F32)
    copies = [pltpu.make_async_copy(latents_ref, latents_hbm, sem.at[0])]
    copies[0].start()
    stats = stats_ref[...] + more_ref[...]
    norm = jnp.sqrt(stats[8:9, 0:1] + stats[24:25, 0:1])
    norm_ref[...] = norm
    factor = jnp.minimum(1.0, MAX_NORM / (norm + 1e-06))
    count = step_ref[0:1, 0:1]
    first_scale = 1.0 - jnp.exp(count * jnp.log(jnp.full((1, 1), BETA_ONE, F32)))
    second_scale = 1.0 - jnp.exp(count * jnp.log(jnp.full((1, 1), BETA_TWO, F32)))
    decay = jnp.minimum(AVERAGE_DECAY, (1.0 + count) / (10.0 + count))
    vector_ref[:, 0:LANES] = jnp.where(odd, stats[16:24, :], stats[0:8, :]) * factor
    vector_ref[:, LANES : 2 * LANES] = jnp.where(odd, stats[0:8, :], stats[16:24, :]) * factor
    chunk = share // 3 if share % 24 == 0 else share
    for i in range(share // chunk):
        rows = slice(i * chunk, (i + 1) * chunk)
        mine, other = mine_ref[rows, :], other_ref[rows, :]
        both = jnp.concatenate([jnp.where(odd, other, mine), jnp.where(odd, mine, other)], axis=1)
        clipped = both * factor
        params = params_ref[rows, :]
        new_first = BETA_ONE * first_ref[rows, :] + (1.0 - BETA_ONE) * clipped
        new_second = BETA_TWO * second_ref[rows, :] + (1.0 - BETA_TWO) * clipped * clipped
        first_hat = new_first / first_scale
        second_hat = new_second / second_scale
        new_params = params - RATE * (first_hat / (jnp.sqrt(second_hat) + ADAM_EPS) + WEIGHT_DECAY * params)
        new_first_ref[rows, :] = new_first
        new_second_ref[rows, :] = new_second
        new_params_ref[rows, :] = new_params
        new_average_ref[rows, :] = decay * averaged_ref[rows, :] + (1.0 - decay) * new_params
        for k, (src, dst) in enumerate(
            (
                (new_first_ref, new_first_hbm), (new_second_ref, new_second_hbm), (new_params_ref, new_params_hbm),
                (new_average_ref, new_average_hbm),
            )
        ):
            copies.append(pltpu.make_async_copy(src.at[rows, :], dst.at[rows, :], sem.at[1 + 4 * i + k]))
            copies[-1].start()
    for copy in copies:
        copy.wait()


def adam(step, stats, more, mine, other, params, first_moment, second_moment, averaged, own, pair, off):
    rows = jax.ShapeDtypeStruct(params.shape, F32)
    vmem, hbm = (pl.BlockSpec(memory_space=m) for m in (pltpu.VMEM, pltpu.HBM))
    return pl.pallas_call(
        adam_kernel,
        in_specs=[vmem] * 12,
        out_specs=[hbm] * 4 + [vmem] * 2 + [hbm],
        out_shape=[
            rows, rows, rows, rows, jax.ShapeDtypeStruct((1, 1), F32), jax.ShapeDtypeStruct((8, params.shape[1]), F32),
            jax.ShapeDtypeStruct(own.shape, F32),
        ],
        scratch_shapes=[pltpu.VMEM(params.shape, F32)] * 4
        + [pltpu.VMEM(own.shape, F32), pltpu.SemaphoreType.DMA((13,))],
        compiler_params=PARAMS,
        name="adam",
        cost_estimate=pl.CostEstimate(
            flops=20 * params.size, transcendentals=2 * params.size, bytes_accessed=params.size * 32
        ),
    )(jnp.broadcast_to(step.astype(F32), (8, LANES)), stats, more, mine, other, params, first_moment, second_moment, averaged, own, pair, off)


def flipped(value, axis, bit):
    return lax.ppermute(value, axis, [(i, i ^ bit) for i in range(lax.axis_size(axis))])


def across(value, axis):
    count = lax.axis_size(axis)
    return lax.ppermute(value, axis, [(i, (i + 1 if i % 2 else i - 1) % count) for i in range(count)])


def neighbours(value):
    off = across(value, "edge")
    return flipped(value, "edge", 1), off


def on_device(
    node_latents, edge_latents, senders, receivers, regions, forced, params, first_moment, second_moment,
    averaged, step, cotangent,
):
    latents = node_latents[0]
    edges = edge_latents[0]
    upstream = cotangent[0]
    nodes, width = latents.shape
    share = params.shape[0]
    blocks, feats = lax.axis_size("edge"), lax.axis_size("feat")
    total = share * feats
    vector_row = 7 * width

    pair, off = neighbours(latents)

    mine, send, recv, latents = prologue(params, senders, receivers, latents)
    far = [flipped(mine, "feat", k) for k in ways(feats)]

    near_send = gather_near(send, latents, pair)
    near_recv = gather_near(recv, latents, pair)
    others = jnp.concatenate(lax.optimization_barrier((near_send, near_recv, *far))[2:])
    pieces = [mine, others, flipped(mine, "edge", 1), flipped(others, "edge", 1)]
    hs = gather_off(send, off, near_send)
    hr = gather_off(recv, off, near_recv)
    weights, high, low, to_off = edge_forward(regions, recv, hs, hr, edges, pieces, total, nodes)
    from_off = across(to_off, "edge")
    to_pair, more, own = near_sum(recv, high, low, nodes)
    from_pair, more = flipped(to_pair, "edge", 1), flipped(more, "edge", 1)
    hidden, slope = edge_slope(regions, hs, hr, edges, weights)
    own, hidden, slope = lax.optimization_barrier((own, hidden, slope))
    d_agg, agg, node_hidden, d_inner, d_pre, node_unit = node_update(
        latents, own, from_pair, more, from_off, weights, forced, upstream
    )
    back_pair, back_off = neighbours(d_agg)
    new_latents, node_grad, node_sum, back = node_grads(
        latents, agg, node_hidden, d_inner, d_pre, node_unit, weights, forced, upstream
    )
    near = gather_near(recv, d_agg, back_pair)
    unit, inverse = edge_unit(lax.optimization_barrier((hidden, d_agg))[0], weights)

    d_pre, kept, sent = edge_backward(
        recv, regions, back_off, near, hs, hr, edges, hidden, slope, unit, inverse, weights, node_grad, node_sum,
    )

    low_rows = vector_row % share
    part, *sent = parted(kept, flipped(sent, "edge", 1), share, low_rows)
    came = [flipped(sent[k - 1], "feat", k) for k in ways(feats)]
    d_pre, part = lax.optimization_barrier((d_pre, part))
    send_part = sender_part(send, d_pre, weights, nodes)
    part_own, part_pair, part_off = receiver_part(recv, d_pre, weights, send_part, back)
    part, part_own, part_pair, part_off = lax.optimization_barrier((part, part_own, part_pair, part_off))
    wire = gathered(part, came, low_rows)
    bit = 2
    while 2 * bit < blocks:
        wire = add(wire, flipped(wire, "edge", bit), low_rows)
        bit *= 2
    grad_edges = edge_grads(d_pre, weights)
    wire, part_pair, part_off, grad_edges = lax.optimization_barrier((wire, part_pair, part_off, grad_edges))
    mine = finish(wire, flipped(wire, "edge", bit), share, low_rows, vector_row // share)
    grads_off = across(part_off, "edge")
    grads_pair = flipped(part_pair, "edge", 1)

    other = flipped(mine, "edge", 1)
    stats = jnp.concatenate([mine[share:], other[share:]], axis=0)
    bit = 1
    while 2 * bit < feats:
        stats = stats + flipped(stats, "feat", bit)
        bit *= 2
    more = flipped(stats, "feat", bit)
    new_first, new_second, new_params, new_average, grad_norm, vector_grads, grad_latents = adam(
        step, stats, more, mine, other, params, first_moment, second_moment, averaged,
        part_own, grads_pair, grads_off,
    )
    return (
        new_latents[None],
        grad_latents[None],
        grad_edges[None],
        new_first,
        new_second,
        new_params,
        new_average,
        grad_norm.reshape(1),
        vector_grads,
    )


def solution(mesh):
    nodes, rows = P("feat", "edge", None), P("feat", None)
    return jax.shard_map(
        on_device,
        mesh=mesh,
        in_specs=(nodes, nodes, P("edge"), P("edge"), P("edge"), P("edge"), rows, rows, rows, rows, P(), nodes),
        out_specs=(nodes, nodes, nodes, rows, rows, rows, rows, P(), P()),
        check_vma=False,
    )
```

```python
import functools

import jax
import jax.numpy as jnp
from jax import lax
from jax.experimental import pallas as pl
from jax.experimental.pallas import tpu as pltpu
from jax.sharding import PartitionSpec as P

NORM_EPS = 1e-05
MAX_NORM = 512.0
RATE = 0.05
BETA_ONE = 0.9
BETA_TWO = 0.95
ADAM_EPS = 1e-08
WEIGHT_DECAY = 0.1
AVERAGE_DECAY = 0.999

LANES = 128
TINY = 1e-20
STEPS = 18
LOG_TWO = 0.6931471805599453
TILE = 2048
PART = 512
B16 = jnp.bfloat16
F32 = jnp.float32
I32 = jnp.int32
I16 = jnp.int16
PARAMS = pltpu.CompilerParams(vmem_limit_bytes=20 * 1024 * 1024)


def dot(left, right):
    return jnp.dot(left, right, preferred_element_type=F32)


def dot_rows(left, right):
    return lax.dot_general(left, right, (((0,), (0,)), ((), ())), preferred_element_type=F32)


def dot_back(left, right):
    return lax.dot_general(left, right, (((1,), (1,)), ((), ())), preferred_element_type=F32)


def vectors_of(w_ref, width):
    return w_ref[7 * width : 7 * width + 8, :].astype(F32)


def split(values):
    high = values.astype(B16)
    return high, (values - high.astype(F32)).astype(B16)


def whole(shape):
    return pl.BlockSpec(shape, lambda i: (0,) * len(shape))


def tiled(rows, cols):
    return pl.BlockSpec((rows, cols), lambda i: (i, 0))


def column(row):
    return jnp.broadcast_to(row, (LANES, LANES)).T


def chosen_columns(index_ref, tile, rows, first, last):
    lane = lax.broadcasted_iota(I32, (LANES, LANES), 1)
    groups = []
    for g in range(rows // LANES):
        col = column(index_ref[pl.ds(tile * (rows // LANES) + g, 1), :])
        groups.append(
            jnp.concatenate(
                [jnp.where(col == lane + base, 1.0, 0.0).astype(B16) for base in range(first, last, LANES)],
                axis=1,
            )
        )
    return jnp.concatenate(groups, axis=0)


def chosen_rows(index_row, first, count):
    node = lax.broadcasted_iota(I32, (count, index_row.shape[1]), 0) + first
    return jnp.where(index_row == node, 1.0, 0.0).astype(B16)


def core_of(e):
    return e % 2


def odd_core():
    return core_of(lax.axis_index("edge")) == 1


def prologue_kernel(
    params_hbm, send_hbm, recv_hbm, latents_hbm, half_ref, send_ref, recv_ref, latents_ref, wide_ref, in_ref, sem,
    *, nodes,
):
    copies = [
        pltpu.make_async_copy(params_hbm, wide_ref, sem.at[0]),
        pltpu.make_async_copy(send_hbm, in_ref.at[0], sem.at[1]),
        pltpu.make_async_copy(recv_hbm, in_ref.at[1], sem.at[2]),
        pltpu.make_async_copy(latents_hbm, latents_ref, sem.at[3]),
    ]
    for copy in copies:
        copy.start()
    e = lax.axis_index("edge")
    core = core_of(e)
    for i, out_ref in ((0, send_ref), (1, recv_ref)):
        copies[1 + i].wait()
        index = in_ref[i]
        block = lax.div(index, nodes)
        slot = jnp.where(block == e, 0, jnp.where(block == e + 1 - 2 * core, 1, 2))
        out_ref[...] = (slot - block) * nodes + index
    copies[0].wait()
    half_ref[...] = jnp.where(core == 1, wide_ref[:, LANES : 2 * LANES], wide_ref[:, 0:LANES]).astype(B16)
    copies[3].wait()


def prologue(params, senders, receivers, latents):
    shape = (senders.size // LANES, LANES)
    out = jax.ShapeDtypeStruct(shape, I32)
    vmem, hbm = pl.BlockSpec(memory_space=pltpu.VMEM), pl.BlockSpec(memory_space=pltpu.HBM)
    operands = (params, senders.reshape(shape), receivers.reshape(shape), latents)
    half, send, recv, own = pl.pallas_call(
        functools.partial(prologue_kernel, nodes=latents.shape[0]),
        in_specs=[hbm] * 4,
        out_specs=[vmem] * 4,
        out_shape=[
            jax.ShapeDtypeStruct((params.shape[0], LANES), B16), out, out,
            jax.ShapeDtypeStruct(latents.shape, latents.dtype),
        ],
        scratch_shapes=[
            pltpu.VMEM(params.shape, F32), pltpu.VMEM((2, *shape), I32), pltpu.SemaphoreType.DMA((4,)),
        ],
        compiler_params=PARAMS,
        name="prologue",
    )(*(pltpu.with_memory_space_constraint(a, pltpu.HBM) for a in operands))
    return half, send.reshape(-1), recv.reshape(-1), own


def gather_near_kernel(index_ref, own_ref, pair_ref, out_ref):
    tile = pl.program_id(0)
    rows = out_ref.shape[0]
    nodes = own_ref.shape[0]
    total = dot(chosen_columns(index_ref, tile, rows, 0, nodes), own_ref[...])
    total = total + dot(chosen_columns(index_ref, tile, rows, nodes, 2 * nodes), pair_ref[...])
    out_ref[...] = total.astype(B16)


def gather_near(index, own, pair):
    nodes, width = own.shape
    edges = index.size
    return pl.pallas_call(
        gather_near_kernel,
        grid=(1,),
        in_specs=[whole((edges // LANES, LANES))] + [whole((nodes, width))] * 2,
        out_specs=tiled(edges, width),
        out_shape=jax.ShapeDtypeStruct((edges, width), B16),
        compiler_params=PARAMS,
        name="gather_near",
        cost_estimate=pl.CostEstimate(
            flops=2 * edges * 2 * nodes * width, transcendentals=0, bytes_accessed=edges * width * 2
        ),
    )(index.reshape(-1, LANES), own, pair)


def gather_off_kernel(index_ref, off_ref, near_ref, out_ref):
    tile = pl.program_id(0)
    rows = out_ref.shape[0]
    nodes = off_ref.shape[0]
    total = dot(chosen_columns(index_ref, tile, rows, 2 * nodes, 3 * nodes), off_ref[...])
    out_ref[...] = (total + near_ref[...].astype(F32)).astype(B16)


def gather_off(index, off, near):
    nodes, width = off.shape
    edges = index.size
    return pl.pallas_call(
        gather_off_kernel,
        grid=(1,),
        in_specs=[whole((edges // LANES, LANES)), whole((nodes, width)), tiled(edges, width)],
        out_specs=tiled(edges, width),
        out_shape=jax.ShapeDtypeStruct((edges, width), B16),
        compiler_params=PARAMS,
        name="gather_off",
        cost_estimate=pl.CostEstimate(
            flops=2 * edges * nodes * width, transcendentals=0, bytes_accessed=edges * width * 4
        ),
    )(index.reshape(-1, LANES), off, near)


def before_silu(region_ref, tile, hs_ref, hr_ref, x_ref, w_ref):
    rows, width = x_ref.shape
    vector_row = 7 * width
    regions = w_ref.shape[0] - vector_row - 8
    table = jnp.concatenate(
        [w_ref[vector_row + 8 :, :].astype(F32), jnp.zeros((LANES - regions, width), F32)], axis=0
    ).astype(B16)
    pre = dot(hs_ref[...], w_ref[0:width, :])
    pre = pre + dot(hr_ref[...], w_ref[width : 2 * width, :])
    pre = pre + dot(x_ref[...], w_ref[2 * width : 3 * width, :])
    pre = pre + dot(chosen_columns(region_ref, tile, rows, 0, LANES), table)
    return pre + vectors_of(w_ref, width)[0:1, :]


def normalized(hidden, w_ref, vec):
    width = hidden.shape[1]
    inner = dot(hidden, w_ref[3 * width : 4 * width, :]) + vec[1:2, :]
    center = inner - jnp.mean(inner, axis=-1, keepdims=True)
    inverse = lax.rsqrt(jnp.mean(center * center, axis=-1, keepdims=True) + NORM_EPS)
    return center * inverse, inverse


def power_of_two(exponents):
    return jnp.exp(exponents * LOG_TWO)


def encoded(values):
    rows, width = values.shape
    quarter = rows // 4
    largest = jnp.maximum(jnp.max(jnp.abs(values), axis=-1, keepdims=True), TINY)
    exponents = jnp.ceil(jnp.log(largest) * (1.0 / LOG_TWO))
    codes = jnp.round(values * power_of_two(STEPS - exponents)).astype(I32)
    upper = lax.shift_right_arithmetic(codes, 4)
    words = jnp.full((quarter, width), -32768, I32)
    for i in range(4):
        words = words + lax.shift_left(jnp.bitwise_and(codes[i * quarter : (i + 1) * quarter, :], 15), 4 * i)
    marks = [
        jnp.broadcast_to(exponents[g * LANES : (g + 1) * LANES, :], (LANES, LANES)).T[0:1, :]
        for g in range(rows // LANES)
    ]
    marks = jnp.concatenate([*marks, jnp.zeros((16 - len(marks), LANES), F32)], axis=0).astype(I32)
    marks = jnp.concatenate([marks, jnp.zeros((16, width - LANES), I32)], axis=1)
    return jnp.concatenate([upper, words, marks], axis=0).astype(I16)


def decoded(wire):
    width = wire.shape[1]
    quarter = (wire.shape[0] - 16) // 5
    rows = 4 * quarter
    wire = wire.astype(I32)
    words = wire[rows : rows + quarter, :] + 32768
    lower = jnp.concatenate([jnp.bitwise_and(lax.shift_right_arithmetic(words, 4 * i), 15) for i in range(4)], axis=0)
    codes = (wire[:rows, :] * 16 + lower).astype(F32)
    exponents = wire[rows + quarter :, :LANES].astype(F32)
    scale = [power_of_two(column(exponents[g : g + 1, :]) - STEPS) for g in range(rows // LANES)]
    return codes * jnp.concatenate([jnp.concatenate(scale, axis=0)] * (width // LANES), axis=1)


def ways(count):
    return sorted(range(1, count), key=lambda k: (k < count // 2, k))


def edge_forward_kernel(
    region_ref, recv_row_ref, hs_ref, hr_ref, x_ref, *refs,
):
    pieces, refs = refs[:-5], refs[-5:]
    w_ref, high_ref, low_ref, halo_ref, wide_ref = refs
    rows, width = x_ref.shape
    nodes = (halo_ref.shape[0] - 16) // 5 * 4

    @pl.when(pl.program_id(0) == 0)
    def _():
        odd, f = odd_core(), lax.axis_index("feat")
        share = pieces[0].shape[0]
        shares = w_ref.shape[0] // share
        for k in range(shares):
            at = ways(shares).index(k) if k else 0
            rows = slice(at * share, (at + 1) * share)
            mine, other = (pieces[i][...] if k == 0 else pieces[i + 1][rows, :] for i in (0, 2))
            mine, other = mine.astype(F32), other.astype(F32)
            base = pl.multiple_of(jnp.bitwise_xor(f, k) * share, 8)
            wide_ref[pl.ds(base, share), 0:LANES] = jnp.where(odd, other, mine)
            wide_ref[pl.ds(base, share), LANES : 2 * LANES] = jnp.where(odd, mine, other)
        w_ref[...] = wide_ref[...].astype(B16)

    vec = vectors_of(w_ref, width)
    total = None
    for i in range(rows // PART + 1):
        if i < rows // PART:
            here = slice(i * PART, (i + 1) * PART)
            pre = before_silu(region_ref, i, hs_ref.at[here, :], hr_ref.at[here, :], x_ref.at[here, :], w_ref)
            hidden = (pre / (1.0 + jnp.exp(-pre))).astype(B16)
            unit, _ = normalized(hidden, w_ref, vec)
            high, low = split(unit * vec[2:3, :] + vec[3:4, :])
            high_ref[here, :] = high
            low_ref[here, :] = low
        if i > 0:
            last = slice((i - 1) * PART, i * PART)
            onehot = chosen_rows(recv_row_ref[:, last], 2 * nodes, nodes)
            more = dot(onehot, high_ref[last, :]) + dot(onehot, low_ref[last, :])
            total = more if total is None else total + more
    halo_ref[...] = encoded(total)


def edge_forward(regions, recv, hs, hr, edges, pieces, total, nodes):
    count, width = edges.shape
    tile = tiled(count, width)
    return pl.pallas_call(
        edge_forward_kernel,
        grid=(1,),
        in_specs=[
            whole((count // LANES, LANES)), whole((1, count)), tile, tile, tile,
            *[whole(piece.shape) for piece in pieces],
        ],
        out_specs=[
            whole((total, width)), whole((count, width)), whole((count, width)),
            whole((nodes + nodes // 4 + 16, width)),
        ],
        out_shape=[
            jax.ShapeDtypeStruct((total, width), B16),
            jax.ShapeDtypeStruct((count, width), B16),
            jax.ShapeDtypeStruct((count, width), B16),
            jax.ShapeDtypeStruct((nodes + nodes // 4 + 16, width), I16),
        ],
        scratch_shapes=[pltpu.VMEM((total, width), F32)],
        compiler_params=PARAMS,
        name="edge_forward",
        cost_estimate=pl.CostEstimate(
            flops=2 * count * width * (5 * width + 2 * nodes), transcendentals=2 * count * width,
            bytes_accessed=count * width * 10,
        ),
    )(regions.reshape(-1, LANES), recv.reshape(1, -1), hs, hr, edges, *pieces)


def edge_slope_kernel(region_ref, hs_ref, hr_ref, x_ref, w_ref, hidden_ref, slope_ref):
    pre = before_silu(region_ref, pl.program_id(0), hs_ref, hr_ref, x_ref, w_ref)
    sigma = 1.0 / (1.0 + jnp.exp(-pre))
    hidden_ref[...] = (pre / (1.0 + jnp.exp(-pre))).astype(B16)
    slope_ref[...] = sigma * (1.0 + pre * (1.0 - sigma))


def edge_slope(regions, hs, hr, edges, weights):
    count, width = edges.shape
    tile = tiled(TILE, width)
    return pl.pallas_call(
        edge_slope_kernel,
        grid=(count // TILE,),
        in_specs=[whole((count // LANES, LANES)), tile, tile, tile, whole(weights.shape)],
        out_specs=[tile, tile],
        out_shape=[jax.ShapeDtypeStruct((count, width), B16), jax.ShapeDtypeStruct((count, width), F32)],
        compiler_params=PARAMS,
        name="edge_slope",
        cost_estimate=pl.CostEstimate(
            flops=2 * count * width * 4 * width, transcendentals=2 * count * width, bytes_accessed=count * width * 12
        ),
    )(regions.reshape(-1, LANES), hs, hr, edges, weights)


def edge_unit_kernel(hidden_ref, w_ref, unit_ref, inverse_ref):
    unit, inverse = normalized(hidden_ref[...], w_ref, vectors_of(w_ref, hidden_ref.shape[1]))
    unit_ref[...] = unit
    inverse_ref[...] = jnp.broadcast_to(inverse, inverse_ref.shape)


def edge_unit(hidden, weights):
    count, width = hidden.shape
    tile = tiled(TILE, width)
    return pl.pallas_call(
        edge_unit_kernel,
        grid=(count // TILE,),
        in_specs=[tile, whole(weights.shape)],
        out_specs=[tile, tiled(TILE, LANES)],
        out_shape=[jax.ShapeDtypeStruct((count, width), F32), jax.ShapeDtypeStruct((count, LANES), F32)],
        compiler_params=PARAMS,
        name="edge_unit",
        cost_estimate=pl.CostEstimate(
            flops=2 * count * width * width, transcendentals=count, bytes_accessed=count * width * 8
        ),
    )(hidden, weights)


def near_sum_kernel(recv_row_ref, high_ref, low_ref, pair_ref, more_ref, own_ref):
    nodes = own_ref.shape[0]
    half = nodes // 2
    for first, out_ref in ((nodes, pair_ref), (nodes + half, more_ref), (0, own_ref)):
        onehot = chosen_rows(recv_row_ref[...], first, out_ref.shape[0])
        out_ref[...] = dot(onehot, high_ref[...]) + dot(onehot, low_ref[...])


def near_sum(recv, high, low, nodes):
    count, width = high.shape
    half = jax.ShapeDtypeStruct((nodes // 2, width), F32)
    return pl.pallas_call(
        near_sum_kernel,
        out_shape=[half, half, jax.ShapeDtypeStruct((nodes, width), F32)],
        compiler_params=PARAMS,
        name="near_sum",
        cost_estimate=pl.CostEstimate(
            flops=8 * count * width * nodes, transcendentals=0, bytes_accessed=count * width * 4
        ),
    )(recv.reshape(1, -1), high, low)


def kept_nodes(forced_ref, width):
    keep = [column(forced_ref[g : g + 1, :]) for g in range(forced_ref.shape[0])]
    keep = 1.0 - jnp.concatenate(keep, axis=0).astype(F32)
    return jnp.concatenate([keep] * (width // LANES), axis=1)


def node_kernel(
    h_ref, own_ref, pair_ref, more_ref, off_ref, w_ref, forced_ref, up_ref,
    d_agg_ref, agg_ref, hidden_ref, d_inner_ref, d_pre_ref, unit_ref,
):
    width = h_ref.shape[1]
    pair = jnp.concatenate([pair_ref[...], more_ref[...]], axis=0)
    agg_ref[...] = (own_ref[...] + pair + decoded(off_ref[...])).astype(B16)
    vec = vectors_of(w_ref, width)
    latent, aggregate = w_ref[4 * width : 5 * width, :], w_ref[5 * width : 6 * width, :]
    second = w_ref[6 * width : 7 * width, :]
    pre = dot(h_ref[...], latent) + dot(agg_ref[...], aggregate) + vec[4:5, :]
    sigma = 1.0 / (1.0 + jnp.exp(-pre))
    hidden = (pre / (1.0 + jnp.exp(-pre))).astype(B16)
    hidden_ref[...] = hidden
    inner = dot(hidden, second) + vec[5:6, :]
    center = inner - jnp.mean(inner, axis=-1, keepdims=True)
    inverse = lax.rsqrt(jnp.mean(center * center, axis=-1, keepdims=True) + NORM_EPS)
    unit = center * inverse
    unit_ref[...] = unit
    scaled = kept_nodes(forced_ref, width) * up_ref[...] * vec[6:7, :]
    d_inner = inverse * (
        scaled
        - jnp.mean(scaled, axis=-1, keepdims=True)
        - unit * jnp.mean(scaled * unit, axis=-1, keepdims=True)
    )
    d_inner = d_inner.astype(B16)
    d_inner_ref[...] = d_inner
    slope = sigma * (1.0 + pre * (1.0 - sigma))
    d_pre = (dot_back(d_inner, second) * slope).astype(B16)
    d_pre_ref[...] = d_pre
    d_agg_ref[...] = dot_back(d_pre, aggregate).astype(B16)


def node_update(h, own, pair, more, off, weights, forced, upstream):
    nodes, width = h.shape
    half = jax.ShapeDtypeStruct((nodes, width), B16)
    return pl.pallas_call(
        node_kernel,
        out_shape=[half, half, half, half, half, jax.ShapeDtypeStruct((nodes, width), F32)],
        compiler_params=PARAMS,
        name="node_update",
        cost_estimate=pl.CostEstimate(
            flops=2 * nodes * width * width * 5, transcendentals=2 * nodes * width, bytes_accessed=nodes * width * 20
        ),
    )(h, own, pair, more, off, weights, forced.reshape(-1, LANES), upstream)


def node_grads_kernel(
    h_ref, agg_ref, hidden_ref, d_inner_ref, d_pre_ref, unit_ref, w_ref, forced_ref, up_ref,
    new_ref, grad_ref, sums_ref, back_ref,
):
    width = h_ref.shape[1]
    vec = vectors_of(w_ref, width)
    keep = kept_nodes(forced_ref, width)
    unit, upstream = unit_ref[...], up_ref[...]
    new_ref[...] = h_ref[...].astype(F32) + keep * (unit * vec[6:7, :] + vec[7:8, :])
    d_pre, d_inner, d_update = d_pre_ref[...], d_inner_ref[...], keep * upstream
    grad_ref[0:width, :] = dot_rows(h_ref[...], d_pre)
    grad_ref[width : 2 * width, :] = dot_rows(agg_ref[...], d_pre)
    grad_ref[2 * width : 3 * width, :] = dot_rows(hidden_ref[...], d_inner)
    back_ref[...] = upstream + dot_back(d_pre, w_ref[4 * width : 5 * width, :])
    sums_ref[...] = jnp.concatenate(
        [
            jnp.sum(d_pre.astype(F32), axis=0, keepdims=True),
            jnp.sum(d_inner.astype(F32), axis=0, keepdims=True),
            jnp.sum(d_update * unit, axis=0, keepdims=True),
            jnp.sum(d_update, axis=0, keepdims=True),
        ],
        axis=0,
    )


def node_grads(h, agg, hidden, d_inner, d_pre, unit, weights, forced, upstream):
    nodes, width = h.shape
    full = jax.ShapeDtypeStruct((nodes, width), F32)
    return pl.pallas_call(
        node_grads_kernel,
        out_shape=[full, jax.ShapeDtypeStruct((3 * width, width), F32), jax.ShapeDtypeStruct((4, width), F32), full],
        compiler_params=PARAMS,
        name="node_grads",
        cost_estimate=pl.CostEstimate(
            flops=2 * nodes * width * width * 4, transcendentals=0, bytes_accessed=nodes * width * 18
        ),
    )(h, agg, hidden, d_inner, d_pre, unit, weights, forced.reshape(-1, LANES), upstream)


def edge_backward_kernel(
    recv_ref, region_row_ref, off_ref, near_ref, hs_ref, hr_ref, x_ref, hidden_ref, slope_ref, unit_ref,
    inverse_ref, w_ref, node_grad_ref, node_sum_ref,
    d_pre_ref, kept_ref, sent_ref,
    d_inner_ref, vec_acc_ref,
):
    step = pl.program_id(0)
    steps = pl.num_programs(0)
    rows = slope_ref.shape[0]
    width = x_ref.shape[1]
    nodes = off_ref.shape[0]
    regions = w_ref.shape[0] - 7 * width - 8
    vec = vectors_of(w_ref, width)

    @pl.when(step == 0)
    def _():
        vec_acc_ref[...] = jnp.zeros_like(vec_acc_ref)

    d_message = dot(chosen_columns(recv_ref, step, rows, 2 * nodes, 3 * nodes), off_ref[...])
    d_message = d_message + near_ref[...].astype(F32)
    unit = unit_ref[...]
    scaled = d_message * vec[2:3, :]
    inverse = inverse_ref[:, 0:1]
    d_inner = inverse * (
        scaled
        - jnp.mean(scaled, axis=-1, keepdims=True)
        - unit * jnp.mean(scaled * unit, axis=-1, keepdims=True)
    )
    vec_acc_ref[0:8, :] += jnp.sum((d_message * unit).reshape(rows // 8, 8, width), axis=0)
    vec_acc_ref[8:16, :] += jnp.sum(d_message.reshape(rows // 8, 8, width), axis=0)
    d_inner = d_inner.astype(B16)
    d_pre = (dot_back(d_inner, w_ref[3 * width : 4 * width, :]) * slope_ref[...]).astype(B16)
    base = pl.multiple_of(step * rows, rows)
    d_inner_ref[pl.ds(base, rows), :] = d_inner
    d_pre_ref[pl.ds(base, rows), :] = d_pre

    @pl.when(step == steps - 1)
    def _():
        odd = odd_core()

        def put(start, piece):
            left, right = piece[:, 0:LANES], piece[:, LANES:]
            kept_ref[start : start + piece.shape[0], :] = jnp.where(odd, right, left)
            sent_ref[start : start + piece.shape[0], :] = jnp.where(odd, left, right)

        table_rows = node_grad_ref.shape[0] + 4 * width
        d_inner, d_pre = d_inner_ref[...], d_pre_ref[...]
        left = jnp.concatenate([hidden_ref[...].T, jnp.ones((16, d_inner.shape[0]), B16)], axis=0)
        both = dot(left, d_inner)
        second_sum = both[width : width + 1, :]
        put(3 * width, both[0:width, :])
        left = jnp.concatenate([hs_ref[...].T, chosen_rows(region_row_ref[...], 0, -(-regions // 16) * 16)], axis=0)
        both = dot(left, d_pre)
        table_grad = both[width : width + regions, :]
        put(0, both[0:width, :])
        put(width, dot_rows(hr_ref[...], d_pre))
        put(2 * width, dot_rows(x_ref[...], d_pre))
        put(4 * width, node_grad_ref[...])
        vector_rows = jnp.concatenate(
            [
                jnp.sum(table_grad, axis=0, keepdims=True),
                second_sum,
                jnp.sum(vec_acc_ref[0:8, :], axis=0, keepdims=True),
                jnp.sum(vec_acc_ref[8:16, :], axis=0, keepdims=True),
                node_sum_ref[...],
            ],
            axis=0,
        )
        put(table_rows, vector_rows)
        put(table_rows + 8, table_grad)


def edge_backward(
    recv, regions, off, near, hs, hr, edges, hidden, slope, unit, inverse, weights, node_grad, node_sum,
):
    count, width = edges.shape
    tile, full = tiled(TILE, width), whole((count, width))
    grad_rows = weights.shape[0]
    half = whole((grad_rows, LANES))
    return pl.pallas_call(
        edge_backward_kernel,
        grid=(count // TILE,),
        in_specs=[
            whole((count // LANES, LANES)), whole((1, count)),
            whole(off.shape), tile, full, full, full, full, tile, tile, tiled(TILE, LANES),
            whole(weights.shape), whole(node_grad.shape), whole(node_sum.shape),
        ],
        out_specs=[full, half, half],
        out_shape=[
            jax.ShapeDtypeStruct((count, width), B16),
            jax.ShapeDtypeStruct((grad_rows, LANES), F32),
            jax.ShapeDtypeStruct((grad_rows, LANES), F32),
        ],
        scratch_shapes=[pltpu.VMEM((count, width), B16), pltpu.VMEM((16, width), F32)],
        compiler_params=PARAMS,
        name="edge_backward",
        cost_estimate=pl.CostEstimate(
            flops=2 * count * width * (6 * width + off.shape[0]), transcendentals=0, bytes_accessed=count * width * 20
        ),
    )(
        recv.reshape(-1, LANES), regions.reshape(1, -1), off, near, hs, hr, edges, hidden, slope, unit, inverse,
        weights, node_grad, node_sum,
    )


def node_part_of(index_row_ref, d_pre_ref, weight, slot, nodes):
    high, low = split(dot(chosen_rows(index_row_ref[...], slot * nodes, nodes), d_pre_ref[...]))
    return dot_back(high, weight) + dot_back(low, weight)


def sender_part_kernel(index_row_ref, d_pre_ref, w_ref, out_ref):
    nodes, width = out_ref.shape
    out_ref[...] = node_part_of(index_row_ref, d_pre_ref, w_ref[0:width, :], pl.program_id(0), nodes)


def sender_part(index, d_pre, weights, nodes):
    count, width = d_pre.shape
    return pl.pallas_call(
        sender_part_kernel,
        grid=(3,),
        in_specs=[whole((1, count)), whole((count, width)), whole(weights.shape)],
        out_specs=tiled(nodes, width),
        out_shape=jax.ShapeDtypeStruct((3 * nodes, width), F32),
        compiler_params=PARAMS,
        name="sender_part",
        cost_estimate=pl.CostEstimate(
            flops=6 * count * width * nodes, transcendentals=0, bytes_accessed=count * width * 2
        ),
    )(index.reshape(1, -1), d_pre, weights)


def receiver_part_kernel(index_row_ref, d_pre_ref, w_ref, part_ref, pair_ref, off_ref):
    nodes, width = pair_ref.shape
    slot = pl.program_id(0) + 1
    part = node_part_of(index_row_ref, d_pre_ref, w_ref[width : 2 * width, :], slot, nodes) + part_ref[...]

    @pl.when(slot == 1)
    def _():
        pair_ref[...] = part.astype(B16)

    @pl.when(slot == 2)
    def _():
        off_ref[...] = part.astype(B16)


def receiver_part(index, d_pre, weights, part, nodes):
    count, width = d_pre.shape
    half = jax.ShapeDtypeStruct((nodes, width), B16)
    return pl.pallas_call(
        receiver_part_kernel,
        grid=(2,),
        in_specs=[
            whole((1, count)), whole((count, width)), whole(weights.shape),
            pl.BlockSpec((nodes, width), lambda i: (i + 1, 0)),
        ],
        out_specs=[whole((nodes, width))] * 2,
        out_shape=[half, half],
        compiler_params=PARAMS,
        name="receiver_part",
        cost_estimate=pl.CostEstimate(
            flops=4 * count * width * nodes, transcendentals=0, bytes_accessed=count * width * 2
        ),
    )(index.reshape(1, -1), d_pre, weights, part)


def own_part_kernel(index_row_ref, d_pre_ref, w_ref, part_ref, back_ref, own_ref):
    nodes, width = own_ref.shape
    part = node_part_of(index_row_ref, d_pre_ref, w_ref[width : 2 * width, :], 0, nodes)
    own_ref[...] = part + (part_ref[...] + back_ref[...])


def own_part(index, d_pre, weights, part, back):
    count, width = d_pre.shape
    return pl.pallas_call(
        own_part_kernel,
        grid=(1,),
        in_specs=[whole((1, count)), whole((count, width)), whole(weights.shape), whole(back.shape), whole(back.shape)],
        out_specs=whole(back.shape),
        out_shape=jax.ShapeDtypeStruct(back.shape, F32),
        compiler_params=PARAMS,
        name="own_part",
        cost_estimate=pl.CostEstimate(
            flops=2 * count * width * back.shape[0], transcendentals=0, bytes_accessed=count * width * 2
        ),
    )(index.reshape(1, -1), d_pre, weights, part, back)


def edge_grads_kernel(d_pre_ref, w_ref, out_ref):
    width = d_pre_ref.shape[1]
    out_ref[...] = dot_back(d_pre_ref[...], w_ref[2 * width : 3 * width, :]).astype(B16)


def edge_grads(d_pre, weights):
    count, width = d_pre.shape
    return pl.pallas_call(
        edge_grads_kernel,
        grid=(count // TILE,),
        in_specs=[tiled(TILE, width), whole(weights.shape)],
        out_specs=tiled(TILE, width),
        out_shape=jax.ShapeDtypeStruct((count, width), B16),
        compiler_params=PARAMS,
        name="edge_grads",
        cost_estimate=pl.CostEstimate(
            flops=2 * count * width * width, transcendentals=0, bytes_accessed=count * width * 4
        ),
    )(d_pre, weights)


def packed(values, first):
    rows = values[first : first + 8, :]
    return jnp.concatenate([values, rows - rows.astype(B16).astype(F32)], axis=0).astype(B16)


def unpacked(wire, first):
    values = wire.astype(F32)
    share = values.shape[0] - 8
    exact = values[first : first + 8, :] + values[share:, :]
    return jnp.concatenate([values[:first, :], exact, values[first + 8 : share, :]], axis=0)


def parted_kernel(mine_ref, other_ref, kept_ref, *sent_refs, share, first):
    for k, out_ref in enumerate((kept_ref, *sent_refs)):
        rows = pl.ds(pl.multiple_of(jnp.bitwise_xor(lax.axis_index("feat"), k) * share, 8), share)
        total = mine_ref[rows, :] + other_ref[rows, :]
        out_ref[...] = packed(total, first) if k else total


def parted(mine, other, share, first):
    sent = jax.ShapeDtypeStruct((share + 8, LANES), B16)
    return pl.pallas_call(
        functools.partial(parted_kernel, share=share, first=first),
        out_shape=[jax.ShapeDtypeStruct((share, LANES), F32)] + [sent] * (mine.shape[0] // share - 1),
        compiler_params=PARAMS,
        name="parted",
    )(mine, other)


def gathered_kernel(mine_ref, *refs, first):
    total = mine_ref[...]
    for ref in refs[:-1]:
        total = total + unpacked(ref[...], first)
    refs[-1][...] = packed(total, first)


def gathered(mine, others, first):
    return pl.pallas_call(
        functools.partial(gathered_kernel, first=first),
        out_shape=jax.ShapeDtypeStruct(others[0].shape, B16),
        compiler_params=PARAMS,
        name="gathered",
    )(mine, *others)


def add_kernel(mine_ref, other_ref, out_ref, *, first):
    out_ref[...] = packed(unpacked(mine_ref[...], first) + unpacked(other_ref[...], first), first)


def add(mine, other, first):
    return pl.pallas_call(
        functools.partial(add_kernel, first=first),
        out_shape=jax.ShapeDtypeStruct(other.shape, B16),
        compiler_params=PARAMS,
        name="add",
    )(mine, other)


def finish_kernel(mine_ref, other_ref, out_ref, *, first, owner):
    share = out_ref.shape[0] - 16
    part = unpacked(mine_ref[...], first) + unpacked(other_ref[...], first)
    out_ref[0:share, :] = part
    out_ref[share : share + 8, :] = jnp.where(lax.axis_index("feat") == owner, part[first : first + 8, :], 0.0)
    squares = jnp.sum(jnp.sum(part * part, axis=0, keepdims=True), axis=1, keepdims=True)
    out_ref[share + 8 : share + 16, :] = jnp.broadcast_to(squares, (8, LANES))


def finish(mine, other, share, first, owner):
    return pl.pallas_call(
        functools.partial(finish_kernel, first=first, owner=owner),
        out_shape=jax.ShapeDtypeStruct((share + 16, LANES), F32),
        compiler_params=PARAMS,
        name="finish",
    )(mine, other)


def adam_kernel(
    step_ref, stats_ref, more_ref, mine_ref, other_ref, params_ref, first_ref, second_ref, averaged_ref,
    own_ref, pair_ref, off_ref,
    new_first_hbm, new_second_hbm, new_params_hbm, new_average_hbm, norm_ref, vector_ref, latents_hbm,
    new_first_ref, new_second_ref, new_params_ref, new_average_ref, latents_ref, sem,
):
    share = params_ref.shape[0]
    odd = odd_core()
    latents_ref[...] = own_ref[...] + pair_ref[...].astype(F32) + off_ref[...].astype(F32)
    copies = [pltpu.make_async_copy(latents_ref, latents_hbm, sem.at[0])]
    copies[0].start()
    stats = stats_ref[...] + more_ref[...]
    norm = jnp.sqrt(stats[8:9, 0:1] + stats[24:25, 0:1])
    norm_ref[...] = norm
    factor = jnp.minimum(1.0, MAX_NORM / (norm + 1e-06))
    count = step_ref[0:1, 0:1]
    first_scale = 1.0 - jnp.exp(count * jnp.log(jnp.full((1, 1), BETA_ONE, F32)))
    second_scale = 1.0 - jnp.exp(count * jnp.log(jnp.full((1, 1), BETA_TWO, F32)))
    decay = jnp.minimum(AVERAGE_DECAY, (1.0 + count) / (10.0 + count))
    vector_ref[:, 0:LANES] = jnp.where(odd, stats[16:24, :], stats[0:8, :]) * factor
    vector_ref[:, LANES : 2 * LANES] = jnp.where(odd, stats[0:8, :], stats[16:24, :]) * factor
    chunk = share // 3 if share % 24 == 0 else share
    for i in range(share // chunk):
        rows = slice(i * chunk, (i + 1) * chunk)
        mine, other = mine_ref[rows, :], other_ref[rows, :]
        both = jnp.concatenate([jnp.where(odd, other, mine), jnp.where(odd, mine, other)], axis=1)
        clipped = both * factor
        params = params_ref[rows, :]
        new_first = BETA_ONE * first_ref[rows, :] + (1.0 - BETA_ONE) * clipped
        new_second = BETA_TWO * second_ref[rows, :] + (1.0 - BETA_TWO) * clipped * clipped
        first_hat = new_first / first_scale
        second_hat = new_second / second_scale
        new_params = params - RATE * (first_hat / (jnp.sqrt(second_hat) + ADAM_EPS) + WEIGHT_DECAY * params)
        new_first_ref[rows, :] = new_first
        new_second_ref[rows, :] = new_second
        new_params_ref[rows, :] = new_params
        new_average_ref[rows, :] = decay * averaged_ref[rows, :] + (1.0 - decay) * new_params
        for k, (src, dst) in enumerate(
            (
                (new_first_ref, new_first_hbm), (new_second_ref, new_second_hbm), (new_params_ref, new_params_hbm),
                (new_average_ref, new_average_hbm),
            )
        ):
            copies.append(pltpu.make_async_copy(src.at[rows, :], dst.at[rows, :], sem.at[1 + 4 * i + k]))
            copies[-1].start()
    for copy in copies:
        copy.wait()


def adam(step, stats, more, mine, other, params, first_moment, second_moment, averaged, own, pair, off):
    rows = jax.ShapeDtypeStruct(params.shape, F32)
    vmem, hbm = (pl.BlockSpec(memory_space=m) for m in (pltpu.VMEM, pltpu.HBM))
    return pl.pallas_call(
        adam_kernel,
        in_specs=[vmem] * 12,
        out_specs=[hbm] * 4 + [vmem] * 2 + [hbm],
        out_shape=[
            rows, rows, rows, rows, jax.ShapeDtypeStruct((1, 1), F32), jax.ShapeDtypeStruct((8, params.shape[1]), F32),
            jax.ShapeDtypeStruct(own.shape, F32),
        ],
        scratch_shapes=[pltpu.VMEM(params.shape, F32)] * 4
        + [pltpu.VMEM(own.shape, F32), pltpu.SemaphoreType.DMA((13,))],
        compiler_params=PARAMS,
        name="adam",
        cost_estimate=pl.CostEstimate(
            flops=20 * params.size, transcendentals=2 * params.size, bytes_accessed=params.size * 32
        ),
    )(jnp.broadcast_to(step.astype(F32), (8, LANES)), stats, more, mine, other, params, first_moment, second_moment, averaged, own, pair, off)


def flipped(value, axis, bit):
    return lax.ppermute(value, axis, [(i, i ^ bit) for i in range(lax.axis_size(axis))])


def across(value, axis):
    count = lax.axis_size(axis)
    return lax.ppermute(value, axis, [(i, (i + 1 if i % 2 else i - 1) % count) for i in range(count)])


def neighbours(value):
    off = across(value, "edge")
    return flipped(value, "edge", 1), off


def on_device(
    node_latents, edge_latents, senders, receivers, regions, forced, params, first_moment, second_moment,
    averaged, step, cotangent,
):
    latents = node_latents[0]
    edges = edge_latents[0]
    upstream = cotangent[0]
    nodes, width = latents.shape
    share = params.shape[0]
    blocks, feats = lax.axis_size("edge"), lax.axis_size("feat")
    total = share * feats
    vector_row = 7 * width

    pair, off = neighbours(latents)

    mine, send, recv, latents = prologue(params, senders, receivers, latents)
    far = [flipped(mine, "feat", k) for k in ways(feats)]

    near_send = gather_near(send, latents, pair)
    near_recv = gather_near(recv, latents, pair)
    others = jnp.concatenate(lax.optimization_barrier((near_send, near_recv, *far))[2:])
    pieces = [mine, others, flipped(mine, "edge", 1), flipped(others, "edge", 1)]
    hs = gather_off(send, off, near_send)
    hr = gather_off(recv, off, near_recv)
    weights, high, low, to_off = edge_forward(regions, recv, hs, hr, edges, pieces, total, nodes)
    from_off = across(to_off, "edge")
    to_pair, more, own = near_sum(recv, high, low, nodes)
    from_pair, more = flipped(to_pair, "edge", 1), flipped(more, "edge", 1)
    hidden, slope = edge_slope(regions, hs, hr, edges, weights)
    own, hidden, slope = lax.optimization_barrier((own, hidden, slope))
    d_agg, agg, node_hidden, d_inner, d_pre, node_unit = node_update(
        latents, own, from_pair, more, from_off, weights, forced, upstream
    )
    back_pair, back_off = neighbours(d_agg)
    new_latents, node_grad, node_sum, back = node_grads(
        latents, agg, node_hidden, d_inner, d_pre, node_unit, weights, forced, upstream
    )
    near = gather_near(recv, d_agg, back_pair)
    unit, inverse = edge_unit(lax.optimization_barrier((hidden, d_agg))[0], weights)

    d_pre, kept, sent = edge_backward(
        recv, regions, back_off, near, hs, hr, edges, hidden, slope, unit, inverse, weights, node_grad, node_sum,
    )

    low_rows = vector_row % share
    grad_edges = edge_grads(d_pre, weights)
    other, grad_edges = lax.optimization_barrier((flipped(sent, "edge", 1), grad_edges))
    part, *sent = parted(kept, other, share, low_rows)
    came = [flipped(sent[k - 1], "feat", k) for k in ways(feats)]
    d_pre, part = lax.optimization_barrier((d_pre, part))
    send_part = sender_part(send, d_pre, weights, nodes)
    part_pair, part_off = receiver_part(recv, d_pre, weights, send_part, nodes)
    part, part_pair, part_off = lax.optimization_barrier((part, part_pair, part_off))
    wire = gathered(part, came, low_rows)
    bit = 2
    while 2 * bit < blocks:
        wire = add(wire, flipped(wire, "edge", bit), low_rows)
        bit *= 2
    part_own = own_part(recv, d_pre, weights, send_part, back)
    wire, part_pair, part_off, part_own = lax.optimization_barrier((wire, part_pair, part_off, part_own))
    mine = finish(wire, flipped(wire, "edge", bit), share, low_rows, vector_row // share)
    grads_off = across(part_off, "edge")
    grads_pair = flipped(part_pair, "edge", 1)

    other = flipped(mine, "edge", 1)
    stats = jnp.concatenate([mine[share:], other[share:]], axis=0)
    bit = 1
    while 2 * bit < feats:
        stats = stats + flipped(stats, "feat", bit)
        bit *= 2
    more = flipped(stats, "feat", bit)
    new_first, new_second, new_params, new_average, grad_norm, vector_grads, grad_latents = adam(
        step, stats, more, mine, other, params, first_moment, second_moment, averaged,
        part_own, grads_pair, grads_off,
    )
    return (
        new_latents[None],
        grad_latents[None],
        grad_edges[None],
        new_first,
        new_second,
        new_params,
        new_average,
        grad_norm.reshape(1),
        vector_grads,
    )


def solution(mesh):
    nodes, rows = P("feat", "edge", None), P("feat", None)
    return jax.shard_map(
        on_device,
        mesh=mesh,
        in_specs=(nodes, nodes, P("edge"), P("edge"), P("edge"), P("edge"), rows, rows, rows, rows, P(), nodes),
        out_specs=(nodes, nodes, nodes, rows, rows, rows, rows, P(), P()),
        check_vma=False,
    )
```

```python
import functools

import jax
import jax.numpy as jnp
from jax import lax
from jax.experimental import pallas as pl
from jax.experimental.pallas import tpu as pltpu
from jax.sharding import PartitionSpec as P

NORM_EPS = 1e-05
MAX_NORM = 512.0
RATE = 0.05
BETA_ONE = 0.9
BETA_TWO = 0.95
ADAM_EPS = 1e-08
WEIGHT_DECAY = 0.1
AVERAGE_DECAY = 0.999

LANES = 128
TINY = 1e-20
STEPS = 18
LOG_TWO = 0.6931471805599453
TILE = 2048
PART = 512
B16 = jnp.bfloat16
F32 = jnp.float32
I32 = jnp.int32
I16 = jnp.int16
PARAMS = pltpu.CompilerParams(vmem_limit_bytes=20 * 1024 * 1024)


def dot(left, right):
    return jnp.dot(left, right, preferred_element_type=F32)


def dot_rows(left, right):
    return lax.dot_general(left, right, (((0,), (0,)), ((), ())), preferred_element_type=F32)


def dot_back(left, right):
    return lax.dot_general(left, right, (((1,), (1,)), ((), ())), preferred_element_type=F32)


def vectors_of(w_ref, width):
    return w_ref[7 * width : 7 * width + 8, :].astype(F32)


def split(values):
    high = values.astype(B16)
    return high, (values - high.astype(F32)).astype(B16)


def whole(shape):
    return pl.BlockSpec(shape, lambda i: (0,) * len(shape))


def tiled(rows, cols):
    return pl.BlockSpec((rows, cols), lambda i: (i, 0))


def column(row):
    return jnp.broadcast_to(row, (LANES, LANES)).T


def chosen_columns(index_ref, tile, rows, first, last):
    lane = lax.broadcasted_iota(I32, (LANES, LANES), 1)
    groups = []
    for g in range(rows // LANES):
        col = column(index_ref[pl.ds(tile * (rows // LANES) + g, 1), :])
        groups.append(
            jnp.concatenate(
                [jnp.where(col == lane + base, 1.0, 0.0).astype(B16) for base in range(first, last, LANES)],
                axis=1,
            )
        )
    return jnp.concatenate(groups, axis=0)


def chosen_rows(index_row, first, count):
    node = lax.broadcasted_iota(I32, (count, index_row.shape[1]), 0) + first
    return jnp.where(index_row == node, 1.0, 0.0).astype(B16)


def core_of(e):
    return e % 2


def odd_core():
    return core_of(lax.axis_index("edge")) == 1


def prologue_kernel(
    params_hbm, send_hbm, recv_hbm, latents_hbm, half_ref, send_ref, recv_ref, latents_ref, wide_ref, in_ref, sem,
    *, nodes,
):
    copies = [
        pltpu.make_async_copy(params_hbm, wide_ref, sem.at[0]),
        pltpu.make_async_copy(send_hbm, in_ref.at[0], sem.at[1]),
        pltpu.make_async_copy(recv_hbm, in_ref.at[1], sem.at[2]),
        pltpu.make_async_copy(latents_hbm, latents_ref, sem.at[3]),
    ]
    for copy in copies:
        copy.start()
    e = lax.axis_index("edge")
    core = core_of(e)
    for i, out_ref in ((0, send_ref), (1, recv_ref)):
        copies[1 + i].wait()
        index = in_ref[i]
        block = lax.div(index, nodes)
        slot = jnp.where(block == e, 0, jnp.where(block == e + 1 - 2 * core, 1, 2))
        out_ref[...] = (slot - block) * nodes + index
    copies[0].wait()
    half_ref[...] = jnp.where(core == 1, wide_ref[:, LANES : 2 * LANES], wide_ref[:, 0:LANES]).astype(B16)
    copies[3].wait()


def prologue(params, senders, receivers, latents):
    shape = (senders.size // LANES, LANES)
    out = jax.ShapeDtypeStruct(shape, I32)
    vmem, hbm = pl.BlockSpec(memory_space=pltpu.VMEM), pl.BlockSpec(memory_space=pltpu.HBM)
    operands = (params, senders.reshape(shape), receivers.reshape(shape), latents)
    half, send, recv, own = pl.pallas_call(
        functools.partial(prologue_kernel, nodes=latents.shape[0]),
        in_specs=[hbm] * 4,
        out_specs=[vmem] * 4,
        out_shape=[
            jax.ShapeDtypeStruct((params.shape[0], LANES), B16), out, out,
            jax.ShapeDtypeStruct(latents.shape, latents.dtype),
        ],
        scratch_shapes=[
            pltpu.VMEM(params.shape, F32), pltpu.VMEM((2, *shape), I32), pltpu.SemaphoreType.DMA((4,)),
        ],
        compiler_params=PARAMS,
        name="prologue",
    )(*(pltpu.with_memory_space_constraint(a, pltpu.HBM) for a in operands))
    return half, send.reshape(-1), recv.reshape(-1), own


def gather_near_kernel(index_ref, own_ref, pair_ref, out_ref):
    tile = pl.program_id(0)
    rows = out_ref.shape[0]
    nodes = own_ref.shape[0]
    total = dot(chosen_columns(index_ref, tile, rows, 0, nodes), own_ref[...])
    total = total + dot(chosen_columns(index_ref, tile, rows, nodes, 2 * nodes), pair_ref[...])
    out_ref[...] = total.astype(B16)


def gather_near(index, own, pair):
    nodes, width = own.shape
    edges = index.size
    return pl.pallas_call(
        gather_near_kernel,
        grid=(1,),
        in_specs=[whole((edges // LANES, LANES))] + [whole((nodes, width))] * 2,
        out_specs=tiled(edges, width),
        out_shape=jax.ShapeDtypeStruct((edges, width), B16),
        compiler_params=PARAMS,
        name="gather_near",
        cost_estimate=pl.CostEstimate(
            flops=2 * edges * 2 * nodes * width, transcendentals=0, bytes_accessed=edges * width * 2
        ),
    )(index.reshape(-1, LANES), own, pair)


def gather_off_kernel(index_ref, off_ref, near_ref, out_ref):
    tile = pl.program_id(0)
    rows = out_ref.shape[0]
    nodes = off_ref.shape[0]
    total = dot(chosen_columns(index_ref, tile, rows, 2 * nodes, 3 * nodes), off_ref[...])
    out_ref[...] = (total + near_ref[...].astype(F32)).astype(B16)


def gather_off(index, off, near):
    nodes, width = off.shape
    edges = index.size
    return pl.pallas_call(
        gather_off_kernel,
        grid=(1,),
        in_specs=[whole((edges // LANES, LANES)), whole((nodes, width)), tiled(edges, width)],
        out_specs=tiled(edges, width),
        out_shape=jax.ShapeDtypeStruct((edges, width), B16),
        compiler_params=PARAMS,
        name="gather_off",
        cost_estimate=pl.CostEstimate(
            flops=2 * edges * nodes * width, transcendentals=0, bytes_accessed=edges * width * 4
        ),
    )(index.reshape(-1, LANES), off, near)


def off_choice_kernel(index_ref, out_ref):
    rows, nodes = out_ref.shape
    out_ref[...] = chosen_columns(index_ref, pl.program_id(0), rows, 2 * nodes, 3 * nodes)


def off_choice(index, nodes):
    edges = index.size
    return pl.pallas_call(
        off_choice_kernel,
        grid=(edges // TILE,),
        in_specs=[whole((edges // LANES, LANES))],
        out_specs=tiled(TILE, nodes),
        out_shape=jax.ShapeDtypeStruct((edges, nodes), B16),
        compiler_params=PARAMS,
        name="off_choice",
        cost_estimate=pl.CostEstimate(flops=edges * nodes, transcendentals=0, bytes_accessed=edges * nodes * 2),
    )(index.reshape(-1, LANES))


def before_silu(region_ref, tile, hs_ref, hr_ref, x_ref, w_ref):
    rows, width = x_ref.shape
    vector_row = 7 * width
    regions = w_ref.shape[0] - vector_row - 8
    table = jnp.concatenate(
        [w_ref[vector_row + 8 :, :].astype(F32), jnp.zeros((LANES - regions, width), F32)], axis=0
    ).astype(B16)
    pre = dot(hs_ref[...], w_ref[0:width, :])
    pre = pre + dot(hr_ref[...], w_ref[width : 2 * width, :])
    pre = pre + dot(x_ref[...], w_ref[2 * width : 3 * width, :])
    pre = pre + dot(chosen_columns(region_ref, tile, rows, 0, LANES), table)
    return pre + vectors_of(w_ref, width)[0:1, :]


def normalized(hidden, w_ref, vec):
    width = hidden.shape[1]
    inner = dot(hidden, w_ref[3 * width : 4 * width, :]) + vec[1:2, :]
    center = inner - jnp.mean(inner, axis=-1, keepdims=True)
    inverse = lax.rsqrt(jnp.mean(center * center, axis=-1, keepdims=True) + NORM_EPS)
    return center * inverse, inverse


def power_of_two(exponents):
    return jnp.exp(exponents * LOG_TWO)


def encoded(values):
    rows, width = values.shape
    quarter = rows // 4
    largest = jnp.maximum(jnp.max(jnp.abs(values), axis=-1, keepdims=True), TINY)
    exponents = jnp.ceil(jnp.log(largest) * (1.0 / LOG_TWO))
    codes = jnp.round(values * power_of_two(STEPS - exponents)).astype(I32)
    upper = lax.shift_right_arithmetic(codes, 4)
    words = jnp.full((quarter, width), -32768, I32)
    for i in range(4):
        words = words + lax.shift_left(jnp.bitwise_and(codes[i * quarter : (i + 1) * quarter, :], 15), 4 * i)
    marks = [
        jnp.broadcast_to(exponents[g * LANES : (g + 1) * LANES, :], (LANES, LANES)).T[0:1, :]
        for g in range(rows // LANES)
    ]
    marks = jnp.concatenate([*marks, jnp.zeros((16 - len(marks), LANES), F32)], axis=0).astype(I32)
    marks = jnp.concatenate([marks, jnp.zeros((16, width - LANES), I32)], axis=1)
    return jnp.concatenate([upper, words, marks], axis=0).astype(I16)


def decoded(wire):
    width = wire.shape[1]
    quarter = (wire.shape[0] - 16) // 5
    rows = 4 * quarter
    wire = wire.astype(I32)
    words = wire[rows : rows + quarter, :] + 32768
    lower = jnp.concatenate([jnp.bitwise_and(lax.shift_right_arithmetic(words, 4 * i), 15) for i in range(4)], axis=0)
    codes = (wire[:rows, :] * 16 + lower).astype(F32)
    exponents = wire[rows + quarter :, :LANES].astype(F32)
    scale = [power_of_two(column(exponents[g : g + 1, :]) - STEPS) for g in range(rows // LANES)]
    return codes * jnp.concatenate([jnp.concatenate(scale, axis=0)] * (width // LANES), axis=1)


def ways(count):
    return sorted(range(1, count), key=lambda k: (k < count // 2, k))


def edge_forward_kernel(
    region_ref, recv_row_ref, hs_ref, hr_ref, x_ref, *refs,
):
    pieces, refs = refs[:-5], refs[-5:]
    w_ref, high_ref, low_ref, halo_ref, wide_ref = refs
    rows, width = x_ref.shape
    nodes = (halo_ref.shape[0] - 16) // 5 * 4

    @pl.when(pl.program_id(0) == 0)
    def _():
        odd, f = odd_core(), lax.axis_index("feat")
        share = pieces[0].shape[0]
        shares = w_ref.shape[0] // share
        for k in range(shares):
            at = ways(shares).index(k) if k else 0
            rows = slice(at * share, (at + 1) * share)
            mine, other = (pieces[i][...] if k == 0 else pieces[i + 1][rows, :] for i in (0, 2))
            mine, other = mine.astype(F32), other.astype(F32)
            base = pl.multiple_of(jnp.bitwise_xor(f, k) * share, 8)
            wide_ref[pl.ds(base, share), 0:LANES] = jnp.where(odd, other, mine)
            wide_ref[pl.ds(base, share), LANES : 2 * LANES] = jnp.where(odd, mine, other)
        w_ref[...] = wide_ref[...].astype(B16)

    vec = vectors_of(w_ref, width)
    total = None
    for i in range(rows // PART + 1):
        if i < rows // PART:
            here = slice(i * PART, (i + 1) * PART)
            pre = before_silu(region_ref, i, hs_ref.at[here, :], hr_ref.at[here, :], x_ref.at[here, :], w_ref)
            hidden = (pre / (1.0 + jnp.exp(-pre))).astype(B16)
            unit, _ = normalized(hidden, w_ref, vec)
            high, low = split(unit * vec[2:3, :] + vec[3:4, :])
            high_ref[here, :] = high
            low_ref[here, :] = low
        if i > 0:
            last = slice((i - 1) * PART, i * PART)
            onehot = chosen_rows(recv_row_ref[:, last], 2 * nodes, nodes)
            more = dot(onehot, high_ref[last, :]) + dot(onehot, low_ref[last, :])
            total = more if total is None else total + more
    halo_ref[...] = encoded(total)


def edge_forward(regions, recv, hs, hr, edges, pieces, total, nodes):
    count, width = edges.shape
    tile = tiled(count, width)
    return pl.pallas_call(
        edge_forward_kernel,
        grid=(1,),
        in_specs=[
            whole((count // LANES, LANES)), whole((1, count)), tile, tile, tile,
            *[whole(piece.shape) for piece in pieces],
        ],
        out_specs=[
            whole((total, width)), whole((count, width)), whole((count, width)),
            whole((nodes + nodes // 4 + 16, width)),
        ],
        out_shape=[
            jax.ShapeDtypeStruct((total, width), B16),
            jax.ShapeDtypeStruct((count, width), B16),
            jax.ShapeDtypeStruct((count, width), B16),
            jax.ShapeDtypeStruct((nodes + nodes // 4 + 16, width), I16),
        ],
        scratch_shapes=[pltpu.VMEM((total, width), F32)],
        compiler_params=PARAMS,
        name="edge_forward",
        cost_estimate=pl.CostEstimate(
            flops=2 * count * width * (5 * width + 2 * nodes), transcendentals=2 * count * width,
            bytes_accessed=count * width * 10,
        ),
    )(regions.reshape(-1, LANES), recv.reshape(1, -1), hs, hr, edges, *pieces)


def edge_slope_kernel(region_ref, hs_ref, hr_ref, x_ref, w_ref, hidden_ref, slope_ref):
    pre = before_silu(region_ref, pl.program_id(0), hs_ref, hr_ref, x_ref, w_ref)
    sigma = 1.0 / (1.0 + jnp.exp(-pre))
    hidden_ref[...] = (pre / (1.0 + jnp.exp(-pre))).astype(B16)
    slope_ref[...] = sigma * (1.0 + pre * (1.0 - sigma))


def edge_slope(regions, hs, hr, edges, weights):
    count, width = edges.shape
    tile = tiled(TILE, width)
    return pl.pallas_call(
        edge_slope_kernel,
        grid=(count // TILE,),
        in_specs=[whole((count // LANES, LANES)), tile, tile, tile, whole(weights.shape)],
        out_specs=[tile, tile],
        out_shape=[jax.ShapeDtypeStruct((count, width), B16), jax.ShapeDtypeStruct((count, width), F32)],
        compiler_params=PARAMS,
        name="edge_slope",
        cost_estimate=pl.CostEstimate(
            flops=2 * count * width * 4 * width, transcendentals=2 * count * width, bytes_accessed=count * width * 12
        ),
    )(regions.reshape(-1, LANES), hs, hr, edges, weights)


def edge_unit_kernel(hidden_ref, w_ref, unit_ref, inverse_ref):
    unit, inverse = normalized(hidden_ref[...], w_ref, vectors_of(w_ref, hidden_ref.shape[1]))
    unit_ref[...] = unit
    inverse_ref[...] = jnp.broadcast_to(inverse, inverse_ref.shape)


def edge_unit(hidden, weights):
    count, width = hidden.shape
    tile = tiled(TILE, width)
    return pl.pallas_call(
        edge_unit_kernel,
        grid=(count // TILE,),
        in_specs=[tile, whole(weights.shape)],
        out_specs=[tile, tiled(TILE, LANES)],
        out_shape=[jax.ShapeDtypeStruct((count, width), F32), jax.ShapeDtypeStruct((count, LANES), F32)],
        compiler_params=PARAMS,
        name="edge_unit",
        cost_estimate=pl.CostEstimate(
            flops=2 * count * width * width, transcendentals=count, bytes_accessed=count * width * 8
        ),
    )(hidden, weights)


def near_sum_kernel(recv_row_ref, high_ref, low_ref, pair_ref, more_ref, own_ref):
    nodes = own_ref.shape[0]
    half = nodes // 2
    for first, out_ref in ((nodes, pair_ref), (nodes + half, more_ref), (0, own_ref)):
        onehot = chosen_rows(recv_row_ref[...], first, out_ref.shape[0])
        out_ref[...] = dot(onehot, high_ref[...]) + dot(onehot, low_ref[...])


def near_sum(recv, high, low, nodes):
    count, width = high.shape
    half = jax.ShapeDtypeStruct((nodes // 2, width), F32)
    return pl.pallas_call(
        near_sum_kernel,
        out_shape=[half, half, jax.ShapeDtypeStruct((nodes, width), F32)],
        compiler_params=PARAMS,
        name="near_sum",
        cost_estimate=pl.CostEstimate(
            flops=8 * count * width * nodes, transcendentals=0, bytes_accessed=count * width * 4
        ),
    )(recv.reshape(1, -1), high, low)


def kept_nodes(forced_ref, width):
    keep = [column(forced_ref[g : g + 1, :]) for g in range(forced_ref.shape[0])]
    keep = 1.0 - jnp.concatenate(keep, axis=0).astype(F32)
    return jnp.concatenate([keep] * (width // LANES), axis=1)


def node_kernel(
    h_ref, own_ref, pair_ref, more_ref, off_ref, w_ref, forced_ref, up_ref,
    d_agg_ref, agg_ref, hidden_ref, d_inner_ref, d_pre_ref, unit_ref,
):
    width = h_ref.shape[1]
    pair = jnp.concatenate([pair_ref[...], more_ref[...]], axis=0)
    agg_ref[...] = (own_ref[...] + pair + decoded(off_ref[...])).astype(B16)
    vec = vectors_of(w_ref, width)
    latent, aggregate = w_ref[4 * width : 5 * width, :], w_ref[5 * width : 6 * width, :]
    second = w_ref[6 * width : 7 * width, :]
    pre = dot(h_ref[...], latent) + dot(agg_ref[...], aggregate) + vec[4:5, :]
    sigma = 1.0 / (1.0 + jnp.exp(-pre))
    hidden = (pre / (1.0 + jnp.exp(-pre))).astype(B16)
    hidden_ref[...] = hidden
    inner = dot(hidden, second) + vec[5:6, :]
    center = inner - jnp.mean(inner, axis=-1, keepdims=True)
    inverse = lax.rsqrt(jnp.mean(center * center, axis=-1, keepdims=True) + NORM_EPS)
    unit = center * inverse
    unit_ref[...] = unit
    scaled = kept_nodes(forced_ref, width) * up_ref[...] * vec[6:7, :]
    d_inner = inverse * (
        scaled
        - jnp.mean(scaled, axis=-1, keepdims=True)
        - unit * jnp.mean(scaled * unit, axis=-1, keepdims=True)
    )
    d_inner = d_inner.astype(B16)
    d_inner_ref[...] = d_inner
    slope = sigma * (1.0 + pre * (1.0 - sigma))
    d_pre = (dot_back(d_inner, second) * slope).astype(B16)
    d_pre_ref[...] = d_pre
    d_agg_ref[...] = dot_back(d_pre, aggregate).astype(B16)


def node_update(h, own, pair, more, off, weights, forced, upstream):
    nodes, width = h.shape
    half = jax.ShapeDtypeStruct((nodes, width), B16)
    return pl.pallas_call(
        node_kernel,
        out_shape=[half, half, half, half, half, jax.ShapeDtypeStruct((nodes, width), F32)],
        compiler_params=PARAMS,
        name="node_update",
        cost_estimate=pl.CostEstimate(
            flops=2 * nodes * width * width * 5, transcendentals=2 * nodes * width, bytes_accessed=nodes * width * 20
        ),
    )(h, own, pair, more, off, weights, forced.reshape(-1, LANES), upstream)


def node_grads_kernel(
    h_ref, agg_ref, hidden_ref, d_inner_ref, d_pre_ref, unit_ref, w_ref, forced_ref, up_ref,
    new_ref, grad_ref, sums_ref, back_ref,
):
    width = h_ref.shape[1]
    vec = vectors_of(w_ref, width)
    keep = kept_nodes(forced_ref, width)
    unit, upstream = unit_ref[...], up_ref[...]
    new_ref[...] = h_ref[...].astype(F32) + keep * (unit * vec[6:7, :] + vec[7:8, :])
    d_pre, d_inner, d_update = d_pre_ref[...], d_inner_ref[...], keep * upstream
    grad_ref[0:width, :] = dot_rows(h_ref[...], d_pre)
    grad_ref[width : 2 * width, :] = dot_rows(agg_ref[...], d_pre)
    grad_ref[2 * width : 3 * width, :] = dot_rows(hidden_ref[...], d_inner)
    back_ref[...] = upstream + dot_back(d_pre, w_ref[4 * width : 5 * width, :])
    sums_ref[...] = jnp.concatenate(
        [
            jnp.sum(d_pre.astype(F32), axis=0, keepdims=True),
            jnp.sum(d_inner.astype(F32), axis=0, keepdims=True),
            jnp.sum(d_update * unit, axis=0, keepdims=True),
            jnp.sum(d_update, axis=0, keepdims=True),
        ],
        axis=0,
    )


def node_grads(h, agg, hidden, d_inner, d_pre, unit, weights, forced, upstream):
    nodes, width = h.shape
    full = jax.ShapeDtypeStruct((nodes, width), F32)
    return pl.pallas_call(
        node_grads_kernel,
        out_shape=[full, jax.ShapeDtypeStruct((3 * width, width), F32), jax.ShapeDtypeStruct((4, width), F32), full],
        compiler_params=PARAMS,
        name="node_grads",
        cost_estimate=pl.CostEstimate(
            flops=2 * nodes * width * width * 4, transcendentals=0, bytes_accessed=nodes * width * 18
        ),
    )(h, agg, hidden, d_inner, d_pre, unit, weights, forced.reshape(-1, LANES), upstream)


def edge_backward_kernel(
    choice_ref, region_row_ref, off_ref, near_ref, hs_ref, hr_ref, x_ref, hidden_ref, slope_ref, unit_ref,
    inverse_ref, w_ref, node_grad_ref, node_sum_ref,
    d_pre_ref, kept_ref, sent_ref,
    d_inner_ref, vec_acc_ref,
):
    step = pl.program_id(0)
    steps = pl.num_programs(0)
    rows = slope_ref.shape[0]
    width = x_ref.shape[1]
    regions = w_ref.shape[0] - 7 * width - 8
    vec = vectors_of(w_ref, width)

    @pl.when(step == 0)
    def _():
        vec_acc_ref[...] = jnp.zeros_like(vec_acc_ref)

    d_message = dot(choice_ref[...], off_ref[...])
    d_message = d_message + near_ref[...].astype(F32)
    unit = unit_ref[...]
    scaled = d_message * vec[2:3, :]
    inverse = jnp.concatenate([inverse_ref[...]] * (width // LANES), axis=1)
    d_inner = inverse * (
        scaled
        - jnp.mean(scaled, axis=-1, keepdims=True)
        - unit * jnp.mean(scaled * unit, axis=-1, keepdims=True)
    )
    vec_acc_ref[0:8, :] += jnp.sum((d_message * unit).reshape(rows // 8, 8, width), axis=0)
    vec_acc_ref[8:16, :] += jnp.sum(d_message.reshape(rows // 8, 8, width), axis=0)
    d_inner = d_inner.astype(B16)
    d_pre = (dot_back(d_inner, w_ref[3 * width : 4 * width, :]) * slope_ref[...]).astype(B16)
    base = pl.multiple_of(step * rows, rows)
    d_inner_ref[pl.ds(base, rows), :] = d_inner
    d_pre_ref[pl.ds(base, rows), :] = d_pre

    @pl.when(step == steps - 1)
    def _():
        odd = odd_core()

        def put(start, piece):
            left, right = piece[:, 0:LANES], piece[:, LANES:]
            kept_ref[start : start + piece.shape[0], :] = jnp.where(odd, right, left)
            sent_ref[start : start + piece.shape[0], :] = jnp.where(odd, left, right)

        table_rows = node_grad_ref.shape[0] + 4 * width
        d_inner, d_pre = d_inner_ref[...], d_pre_ref[...]
        left = jnp.concatenate([hidden_ref[...].T, jnp.ones((16, d_inner.shape[0]), B16)], axis=0)
        both = dot(left, d_inner)
        second_sum = both[width : width + 1, :]
        put(3 * width, both[0:width, :])
        left = jnp.concatenate([hs_ref[...].T, chosen_rows(region_row_ref[...], 0, -(-regions // 16) * 16)], axis=0)
        both = dot(left, d_pre)
        table_grad = both[width : width + regions, :]
        put(0, both[0:width, :])
        put(width, dot_rows(hr_ref[...], d_pre))
        put(2 * width, dot_rows(x_ref[...], d_pre))
        put(4 * width, node_grad_ref[...])
        vector_rows = jnp.concatenate(
            [
                jnp.sum(table_grad, axis=0, keepdims=True),
                second_sum,
                jnp.sum(vec_acc_ref[0:8, :], axis=0, keepdims=True),
                jnp.sum(vec_acc_ref[8:16, :], axis=0, keepdims=True),
                node_sum_ref[...],
            ],
            axis=0,
        )
        put(table_rows, vector_rows)
        put(table_rows + 8, table_grad)


def edge_backward(
    choice, regions, off, near, hs, hr, edges, hidden, slope, unit, inverse, weights, node_grad, node_sum,
):
    count, width = edges.shape
    tile, full = tiled(TILE, width), whole((count, width))
    grad_rows = weights.shape[0]
    half = whole((grad_rows, LANES))
    return pl.pallas_call(
        edge_backward_kernel,
        grid=(count // TILE,),
        in_specs=[
            tiled(TILE, off.shape[0]), whole((1, count)),
            whole(off.shape), tile, full, full, full, full, tile, tile, tiled(TILE, LANES),
            whole(weights.shape), whole(node_grad.shape), whole(node_sum.shape),
        ],
        out_specs=[full, half, half],
        out_shape=[
            jax.ShapeDtypeStruct((count, width), B16),
            jax.ShapeDtypeStruct((grad_rows, LANES), F32),
            jax.ShapeDtypeStruct((grad_rows, LANES), F32),
        ],
        scratch_shapes=[pltpu.VMEM((count, width), B16), pltpu.VMEM((16, width), F32)],
        compiler_params=PARAMS,
        name="edge_backward",
        cost_estimate=pl.CostEstimate(
            flops=2 * count * width * (6 * width + off.shape[0]), transcendentals=0, bytes_accessed=count * width * 20
        ),
    )(
        choice, regions.reshape(1, -1), off, near, hs, hr, edges, hidden, slope, unit, inverse,
        weights, node_grad, node_sum,
    )


def node_part_of(index_row_ref, d_pre_ref, weight, slot, nodes):
    high, low = split(dot(chosen_rows(index_row_ref[...], slot * nodes, nodes), d_pre_ref[...]))
    return dot_back(high, weight) + dot_back(low, weight)


def sender_part_kernel(index_row_ref, d_pre_ref, w_ref, out_ref):
    nodes, width = out_ref.shape
    out_ref[...] = node_part_of(index_row_ref, d_pre_ref, w_ref[0:width, :], pl.program_id(0), nodes)


def sender_part(index, d_pre, weights, nodes):
    count, width = d_pre.shape
    return pl.pallas_call(
        sender_part_kernel,
        grid=(3,),
        in_specs=[whole((1, count)), whole((count, width)), whole(weights.shape)],
        out_specs=tiled(nodes, width),
        out_shape=jax.ShapeDtypeStruct((3 * nodes, width), F32),
        compiler_params=PARAMS,
        name="sender_part",
        cost_estimate=pl.CostEstimate(
            flops=6 * count * width * nodes, transcendentals=0, bytes_accessed=count * width * 2
        ),
    )(index.reshape(1, -1), d_pre, weights)


def receiver_part_kernel(index_row_ref, d_pre_ref, w_ref, part_ref, pair_ref, off_ref):
    nodes, width = pair_ref.shape
    slot = pl.program_id(0) + 1
    part = node_part_of(index_row_ref, d_pre_ref, w_ref[width : 2 * width, :], slot, nodes) + part_ref[...]

    @pl.when(slot == 1)
    def _():
        pair_ref[...] = part.astype(B16)

    @pl.when(slot == 2)
    def _():
        off_ref[...] = part.astype(B16)


def receiver_part(index, d_pre, weights, part, nodes):
    count, width = d_pre.shape
    half = jax.ShapeDtypeStruct((nodes, width), B16)
    return pl.pallas_call(
        receiver_part_kernel,
        grid=(2,),
        in_specs=[
            whole((1, count)), whole((count, width)), whole(weights.shape),
            pl.BlockSpec((nodes, width), lambda i: (i + 1, 0)),
        ],
        out_specs=[whole((nodes, width))] * 2,
        out_shape=[half, half],
        compiler_params=PARAMS,
        name="receiver_part",
        cost_estimate=pl.CostEstimate(
            flops=4 * count * width * nodes, transcendentals=0, bytes_accessed=count * width * 2
        ),
    )(index.reshape(1, -1), d_pre, weights, part)


def own_part_kernel(index_row_ref, d_pre_ref, w_ref, part_ref, back_ref, own_ref):
    nodes, width = own_ref.shape
    part = node_part_of(index_row_ref, d_pre_ref, w_ref[width : 2 * width, :], 0, nodes)
    own_ref[...] = part + (part_ref[...] + back_ref[...])


def own_part(index, d_pre, weights, part, back):
    count, width = d_pre.shape
    return pl.pallas_call(
        own_part_kernel,
        grid=(1,),
        in_specs=[whole((1, count)), whole((count, width)), whole(weights.shape), whole(back.shape), whole(back.shape)],
        out_specs=whole(back.shape),
        out_shape=jax.ShapeDtypeStruct(back.shape, F32),
        compiler_params=PARAMS,
        name="own_part",
        cost_estimate=pl.CostEstimate(
            flops=2 * count * width * back.shape[0], transcendentals=0, bytes_accessed=count * width * 2
        ),
    )(index.reshape(1, -1), d_pre, weights, part, back)


def edge_grads_kernel(d_pre_ref, w_ref, out_ref):
    width = d_pre_ref.shape[1]
    out_ref[...] = dot_back(d_pre_ref[...], w_ref[2 * width : 3 * width, :]).astype(B16)


def edge_grads(d_pre, weights):
    count, width = d_pre.shape
    return pl.pallas_call(
        edge_grads_kernel,
        grid=(count // TILE,),
        in_specs=[tiled(TILE, width), whole(weights.shape)],
        out_specs=tiled(TILE, width),
        out_shape=jax.ShapeDtypeStruct((count, width), B16),
        compiler_params=PARAMS,
        name="edge_grads",
        cost_estimate=pl.CostEstimate(
            flops=2 * count * width * width, transcendentals=0, bytes_accessed=count * width * 4
        ),
    )(d_pre, weights)


def packed(values, first):
    rows = values[first : first + 8, :]
    return jnp.concatenate([values, rows - rows.astype(B16).astype(F32)], axis=0).astype(B16)


def unpacked(wire, first):
    values = wire.astype(F32)
    share = values.shape[0] - 8
    exact = values[first : first + 8, :] + values[share:, :]
    return jnp.concatenate([values[:first, :], exact, values[first + 8 : share, :]], axis=0)


def parted_kernel(mine_ref, other_ref, kept_ref, *sent_refs, share, first):
    for k, out_ref in enumerate((kept_ref, *sent_refs)):
        rows = pl.ds(pl.multiple_of(jnp.bitwise_xor(lax.axis_index("feat"), k) * share, 8), share)
        total = mine_ref[rows, :] + other_ref[rows, :]
        out_ref[...] = packed(total, first) if k else total


def parted(mine, other, share, first):
    sent = jax.ShapeDtypeStruct((share + 8, LANES), B16)
    return pl.pallas_call(
        functools.partial(parted_kernel, share=share, first=first),
        out_shape=[jax.ShapeDtypeStruct((share, LANES), F32)] + [sent] * (mine.shape[0] // share - 1),
        compiler_params=PARAMS,
        name="parted",
    )(mine, other)


def gathered_kernel(mine_ref, *refs, first):
    total = mine_ref[...]
    for ref in refs[:-1]:
        total = total + unpacked(ref[...], first)
    refs[-1][...] = packed(total, first)


def gathered(mine, others, first):
    return pl.pallas_call(
        functools.partial(gathered_kernel, first=first),
        out_shape=jax.ShapeDtypeStruct(others[0].shape, B16),
        compiler_params=PARAMS,
        name="gathered",
    )(mine, *others)


def add_kernel(mine_ref, other_ref, out_ref, *, first):
    out_ref[...] = packed(unpacked(mine_ref[...], first) + unpacked(other_ref[...], first), first)


def add(mine, other, first):
    return pl.pallas_call(
        functools.partial(add_kernel, first=first),
        out_shape=jax.ShapeDtypeStruct(other.shape, B16),
        compiler_params=PARAMS,
        name="add",
    )(mine, other)


def finish_kernel(mine_ref, other_ref, out_ref, *, first, owner):
    share = out_ref.shape[0] - 16
    part = unpacked(mine_ref[...], first) + unpacked(other_ref[...], first)
    out_ref[0:share, :] = part
    out_ref[share : share + 8, :] = jnp.where(lax.axis_index("feat") == owner, part[first : first + 8, :], 0.0)
    squares = jnp.sum(jnp.sum(part * part, axis=0, keepdims=True), axis=1, keepdims=True)
    out_ref[share + 8 : share + 16, :] = jnp.broadcast_to(squares, (8, LANES))


def finish(mine, other, share, first, owner):
    return pl.pallas_call(
        functools.partial(finish_kernel, first=first, owner=owner),
        out_shape=jax.ShapeDtypeStruct((share + 16, LANES), F32),
        compiler_params=PARAMS,
        name="finish",
    )(mine, other)


def adam_kernel(
    step_ref, stats_ref, more_ref, mine_ref, other_ref, params_ref, first_ref, second_ref, averaged_ref,
    own_ref, pair_ref, off_ref,
    new_first_hbm, new_second_hbm, new_params_hbm, new_average_hbm, norm_ref, vector_ref, latents_hbm,
    new_first_ref, new_second_ref, new_params_ref, new_average_ref, latents_ref, sem,
):
    share = params_ref.shape[0]
    odd = odd_core()
    latents_ref[...] = own_ref[...] + pair_ref[...].astype(F32) + off_ref[...].astype(F32)
    copies = [pltpu.make_async_copy(latents_ref, latents_hbm, sem.at[0])]
    copies[0].start()
    stats = stats_ref[...] + more_ref[...]
    norm = jnp.sqrt(stats[8:9, 0:1] + stats[24:25, 0:1])
    norm_ref[...] = norm
    factor = jnp.minimum(1.0, MAX_NORM / (norm + 1e-06))
    count = step_ref[0:1, 0:1]
    first_scale = 1.0 - jnp.exp(count * jnp.log(jnp.full((1, 1), BETA_ONE, F32)))
    second_scale = 1.0 - jnp.exp(count * jnp.log(jnp.full((1, 1), BETA_TWO, F32)))
    decay = jnp.minimum(AVERAGE_DECAY, (1.0 + count) / (10.0 + count))
    vector_ref[:, 0:LANES] = jnp.where(odd, stats[16:24, :], stats[0:8, :]) * factor
    vector_ref[:, LANES : 2 * LANES] = jnp.where(odd, stats[0:8, :], stats[16:24, :]) * factor
    chunk = share // 3 if share % 24 == 0 else share
    for i in range(share // chunk):
        rows = slice(i * chunk, (i + 1) * chunk)
        mine, other = mine_ref[rows, :], other_ref[rows, :]
        both = jnp.concatenate([jnp.where(odd, other, mine), jnp.where(odd, mine, other)], axis=1)
        clipped = both * factor
        params = params_ref[rows, :]
        new_first = BETA_ONE * first_ref[rows, :] + (1.0 - BETA_ONE) * clipped
        new_second = BETA_TWO * second_ref[rows, :] + (1.0 - BETA_TWO) * clipped * clipped
        first_hat = new_first / first_scale
        second_hat = new_second / second_scale
        new_params = params - RATE * (first_hat / (jnp.sqrt(second_hat) + ADAM_EPS) + WEIGHT_DECAY * params)
        new_first_ref[rows, :] = new_first
        new_second_ref[rows, :] = new_second
        new_params_ref[rows, :] = new_params
        new_average_ref[rows, :] = decay * averaged_ref[rows, :] + (1.0 - decay) * new_params
        for k, (src, dst) in enumerate(
            (
                (new_first_ref, new_first_hbm), (new_second_ref, new_second_hbm), (new_params_ref, new_params_hbm),
                (new_average_ref, new_average_hbm),
            )
        ):
            copies.append(pltpu.make_async_copy(src.at[rows, :], dst.at[rows, :], sem.at[1 + 4 * i + k]))
            copies[-1].start()
    for copy in copies:
        copy.wait()


def adam(step, stats, more, mine, other, params, first_moment, second_moment, averaged, own, pair, off):
    rows = jax.ShapeDtypeStruct(params.shape, F32)
    vmem, hbm = (pl.BlockSpec(memory_space=m) for m in (pltpu.VMEM, pltpu.HBM))
    return pl.pallas_call(
        adam_kernel,
        in_specs=[vmem] * 12,
        out_specs=[hbm] * 4 + [vmem] * 2 + [hbm],
        out_shape=[
            rows, rows, rows, rows, jax.ShapeDtypeStruct((1, 1), F32), jax.ShapeDtypeStruct((8, params.shape[1]), F32),
            jax.ShapeDtypeStruct(own.shape, F32),
        ],
        scratch_shapes=[pltpu.VMEM(params.shape, F32)] * 4
        + [pltpu.VMEM(own.shape, F32), pltpu.SemaphoreType.DMA((13,))],
        compiler_params=PARAMS,
        name="adam",
        cost_estimate=pl.CostEstimate(
            flops=20 * params.size, transcendentals=2 * params.size, bytes_accessed=params.size * 32
        ),
    )(jnp.broadcast_to(step.astype(F32), (8, LANES)), stats, more, mine, other, params, first_moment, second_moment, averaged, own, pair, off)


def flipped(value, axis, bit):
    return lax.ppermute(value, axis, [(i, i ^ bit) for i in range(lax.axis_size(axis))])


def across(value, axis):
    count = lax.axis_size(axis)
    return lax.ppermute(value, axis, [(i, (i + 1 if i % 2 else i - 1) % count) for i in range(count)])


def neighbours(value):
    off = across(value, "edge")
    return flipped(value, "edge", 1), off


def on_device(
    node_latents, edge_latents, senders, receivers, regions, forced, params, first_moment, second_moment,
    averaged, step, cotangent,
):
    latents = node_latents[0]
    edges = edge_latents[0]
    upstream = cotangent[0]
    nodes, width = latents.shape
    share = params.shape[0]
    blocks, feats = lax.axis_size("edge"), lax.axis_size("feat")
    total = share * feats
    vector_row = 7 * width

    pair, off = neighbours(latents)

    mine, send, recv, latents = prologue(params, senders, receivers, latents)
    far = [flipped(mine, "feat", k) for k in ways(feats)]

    near_send = gather_near(send, latents, pair)
    near_recv = gather_near(recv, latents, pair)
    others = jnp.concatenate(lax.optimization_barrier((near_send, near_recv, *far))[2:])
    pieces = [mine, others, flipped(mine, "edge", 1), flipped(others, "edge", 1)]
    hs = gather_off(send, off, near_send)
    hr = gather_off(recv, off, near_recv)
    weights, high, low, to_off = edge_forward(regions, recv, hs, hr, edges, pieces, total, nodes)
    from_off = across(to_off, "edge")
    to_pair, more, own = near_sum(recv, high, low, nodes)
    from_pair, more = flipped(to_pair, "edge", 1), flipped(more, "edge", 1)
    hidden, slope = edge_slope(regions, hs, hr, edges, weights)
    own, hidden, slope = lax.optimization_barrier((own, hidden, slope))
    d_agg, agg, node_hidden, d_inner, d_pre, node_unit = node_update(
        latents, own, from_pair, more, from_off, weights, forced, upstream
    )
    back_pair, back_off = neighbours(d_agg)
    new_latents, node_grad, node_sum, back = node_grads(
        latents, agg, node_hidden, d_inner, d_pre, node_unit, weights, forced, upstream
    )
    near = gather_near(recv, d_agg, back_pair)
    hidden, index = lax.optimization_barrier((hidden, recv, d_agg))[:2]
    unit, inverse = edge_unit(hidden, weights)
    choice = off_choice(index, nodes)

    d_pre, kept, sent = edge_backward(
        choice, regions, back_off, near, hs, hr, edges, hidden, slope, unit, inverse, weights, node_grad, node_sum,
    )

    low_rows = vector_row % share
    grad_edges = edge_grads(d_pre, weights)
    other, grad_edges = lax.optimization_barrier((flipped(sent, "edge", 1), grad_edges))
    part, *sent = parted(kept, other, share, low_rows)
    came = [flipped(sent[k - 1], "feat", k) for k in ways(feats)]
    d_pre, part = lax.optimization_barrier((d_pre, part))
    send_part = sender_part(send, d_pre, weights, nodes)
    part_pair, part_off = receiver_part(recv, d_pre, weights, send_part, nodes)
    part, part_pair, part_off = lax.optimization_barrier((part, part_pair, part_off))
    wire = gathered(part, came, low_rows)
    bit = 2
    while 2 * bit < blocks:
        wire = add(wire, flipped(wire, "edge", bit), low_rows)
        bit *= 2
    part_own = own_part(recv, d_pre, weights, send_part, back)
    wire, part_pair, part_off, part_own = lax.optimization_barrier((wire, part_pair, part_off, part_own))
    mine = finish(wire, flipped(wire, "edge", bit), share, low_rows, vector_row // share)
    grads_off = across(part_off, "edge")
    grads_pair = flipped(part_pair, "edge", 1)

    other = flipped(mine, "edge", 1)
    stats = jnp.concatenate([mine[share:], other[share:]], axis=0)
    bit = 1
    while 2 * bit < feats:
        stats = stats + flipped(stats, "feat", bit)
        bit *= 2
    more = flipped(stats, "feat", bit)
    new_first, new_second, new_params, new_average, grad_norm, vector_grads, grad_latents = adam(
        step, stats, more, mine, other, params, first_moment, second_moment, averaged,
        part_own, grads_pair, grads_off,
    )
    return (
        new_latents[None],
        grad_latents[None],
        grad_edges[None],
        new_first,
        new_second,
        new_params,
        new_average,
        grad_norm.reshape(1),
        vector_grads,
    )


def solution(mesh):
    nodes, rows = P("feat", "edge", None), P("feat", None)
    return jax.shard_map(
        on_device,
        mesh=mesh,
        in_specs=(nodes, nodes, P("edge"), P("edge"), P("edge"), P("edge"), rows, rows, rows, rows, P(), nodes),
        out_specs=(nodes, nodes, nodes, rows, rows, rows, rows, P(), P()),
        check_vma=False,
    )
```

```python
import functools

import jax
import jax.numpy as jnp
from jax import lax
from jax.experimental import pallas as pl
from jax.experimental.pallas import tpu as pltpu
from jax.sharding import PartitionSpec as P

NORM_EPS = 1e-05
MAX_NORM = 512.0
RATE = 0.05
BETA_ONE = 0.9
BETA_TWO = 0.95
ADAM_EPS = 1e-08
WEIGHT_DECAY = 0.1
AVERAGE_DECAY = 0.999

LANES = 128
TINY = 1e-20
STEPS = 18
LOG_TWO = 0.6931471805599453
TILE = 2048
PART = 512
B16 = jnp.bfloat16
F32 = jnp.float32
I32 = jnp.int32
I16 = jnp.int16
PARAMS = pltpu.CompilerParams(vmem_limit_bytes=20 * 1024 * 1024)


def dot(left, right):
    return jnp.dot(left, right, preferred_element_type=F32)


def dot_rows(left, right):
    return lax.dot_general(left, right, (((0,), (0,)), ((), ())), preferred_element_type=F32)


def dot_back(left, right):
    return lax.dot_general(left, right, (((1,), (1,)), ((), ())), preferred_element_type=F32)


def vectors_of(w_ref, width):
    return w_ref[7 * width : 7 * width + 8, :].astype(F32)


def split(values):
    high = values.astype(B16)
    return high, (values - high.astype(F32)).astype(B16)


def whole(shape):
    return pl.BlockSpec(shape, lambda i: (0,) * len(shape))


def tiled(rows, cols):
    return pl.BlockSpec((rows, cols), lambda i: (i, 0))


def column(row):
    return jnp.broadcast_to(row, (LANES, LANES)).T


def chosen_columns(index_ref, tile, rows, first, last):
    lane = lax.broadcasted_iota(I32, (LANES, LANES), 1)
    groups = []
    for g in range(rows // LANES):
        col = column(index_ref[pl.ds(tile * (rows // LANES) + g, 1), :])
        groups.append(
            jnp.concatenate(
                [jnp.where(col == lane + base, 1.0, 0.0).astype(B16) for base in range(first, last, LANES)],
                axis=1,
            )
        )
    return jnp.concatenate(groups, axis=0)


def chosen_rows(index_row, first, count):
    node = lax.broadcasted_iota(I32, (count, index_row.shape[1]), 0) + first
    return jnp.where(index_row == node, 1.0, 0.0).astype(B16)


def core_of(e):
    return e % 2


def odd_core():
    return core_of(lax.axis_index("edge")) == 1


def prologue_kernel(
    params_hbm, send_hbm, recv_hbm, latents_hbm, half_ref, send_ref, recv_ref, latents_ref, wide_ref, in_ref, sem,
    *, nodes,
):
    copies = [
        pltpu.make_async_copy(params_hbm, wide_ref, sem.at[0]),
        pltpu.make_async_copy(send_hbm, in_ref.at[0], sem.at[1]),
        pltpu.make_async_copy(recv_hbm, in_ref.at[1], sem.at[2]),
        pltpu.make_async_copy(latents_hbm, latents_ref, sem.at[3]),
    ]
    for copy in copies:
        copy.start()
    e = lax.axis_index("edge")
    core = core_of(e)
    for i, out_ref in ((0, send_ref), (1, recv_ref)):
        copies[1 + i].wait()
        index = in_ref[i]
        block = lax.div(index, nodes)
        slot = jnp.where(block == e, 0, jnp.where(block == e + 1 - 2 * core, 1, 2))
        out_ref[...] = (slot - block) * nodes + index
    copies[0].wait()
    half_ref[...] = jnp.where(core == 1, wide_ref[:, LANES : 2 * LANES], wide_ref[:, 0:LANES]).astype(B16)
    copies[3].wait()


def prologue(params, senders, receivers, latents):
    shape = (senders.size // LANES, LANES)
    out = jax.ShapeDtypeStruct(shape, I32)
    vmem, hbm = pl.BlockSpec(memory_space=pltpu.VMEM), pl.BlockSpec(memory_space=pltpu.HBM)
    operands = (params, senders.reshape(shape), receivers.reshape(shape), latents)
    half, send, recv, own = pl.pallas_call(
        functools.partial(prologue_kernel, nodes=latents.shape[0]),
        in_specs=[hbm] * 4,
        out_specs=[vmem] * 4,
        out_shape=[
            jax.ShapeDtypeStruct((params.shape[0], LANES), B16), out, out,
            jax.ShapeDtypeStruct(latents.shape, latents.dtype),
        ],
        scratch_shapes=[
            pltpu.VMEM(params.shape, F32), pltpu.VMEM((2, *shape), I32), pltpu.SemaphoreType.DMA((4,)),
        ],
        compiler_params=PARAMS,
        name="prologue",
    )(*(pltpu.with_memory_space_constraint(a, pltpu.HBM) for a in operands))
    return half, send.reshape(-1), recv.reshape(-1), own


def gather_near_kernel(index_ref, own_ref, pair_ref, out_ref):
    tile = pl.program_id(0)
    rows = out_ref.shape[0]
    nodes = own_ref.shape[0]
    total = dot(chosen_columns(index_ref, tile, rows, 0, nodes), own_ref[...])
    total = total + dot(chosen_columns(index_ref, tile, rows, nodes, 2 * nodes), pair_ref[...])
    out_ref[...] = total.astype(B16)


def gather_near(index, own, pair):
    nodes, width = own.shape
    edges = index.size
    return pl.pallas_call(
        gather_near_kernel,
        grid=(1,),
        in_specs=[whole((edges // LANES, LANES))] + [whole((nodes, width))] * 2,
        out_specs=tiled(edges, width),
        out_shape=jax.ShapeDtypeStruct((edges, width), B16),
        compiler_params=PARAMS,
        name="gather_near",
        cost_estimate=pl.CostEstimate(
            flops=2 * edges * 2 * nodes * width, transcendentals=0, bytes_accessed=edges * width * 2
        ),
    )(index.reshape(-1, LANES), own, pair)


def gather_off_kernel(index_ref, off_ref, near_ref, out_ref):
    tile = pl.program_id(0)
    rows = out_ref.shape[0]
    nodes = off_ref.shape[0]
    total = dot(chosen_columns(index_ref, tile, rows, 2 * nodes, 3 * nodes), off_ref[...])
    out_ref[...] = (total + near_ref[...].astype(F32)).astype(B16)


def gather_off(index, off, near):
    nodes, width = off.shape
    edges = index.size
    return pl.pallas_call(
        gather_off_kernel,
        grid=(1,),
        in_specs=[whole((edges // LANES, LANES)), whole((nodes, width)), tiled(edges, width)],
        out_specs=tiled(edges, width),
        out_shape=jax.ShapeDtypeStruct((edges, width), B16),
        compiler_params=PARAMS,
        name="gather_off",
        cost_estimate=pl.CostEstimate(
            flops=2 * edges * nodes * width, transcendentals=0, bytes_accessed=edges * width * 4
        ),
    )(index.reshape(-1, LANES), off, near)


def off_choice_kernel(index_ref, out_ref):
    rows, nodes = out_ref.shape
    out_ref[...] = chosen_columns(index_ref, pl.program_id(0), rows, 2 * nodes, 3 * nodes)


def off_choice(index, nodes):
    edges = index.size
    return pl.pallas_call(
        off_choice_kernel,
        grid=(edges // TILE,),
        in_specs=[whole((edges // LANES, LANES))],
        out_specs=tiled(TILE, nodes),
        out_shape=jax.ShapeDtypeStruct((edges, nodes), B16),
        compiler_params=PARAMS,
        name="off_choice",
        cost_estimate=pl.CostEstimate(flops=edges * nodes, transcendentals=0, bytes_accessed=edges * nodes * 2),
    )(index.reshape(-1, LANES))


def before_silu(region_ref, tile, hs_ref, hr_ref, x_ref, w_ref):
    rows, width = x_ref.shape
    vector_row = 7 * width
    regions = w_ref.shape[0] - vector_row - 8
    table = jnp.concatenate(
        [w_ref[vector_row + 8 :, :].astype(F32), jnp.zeros((LANES - regions, width), F32)], axis=0
    ).astype(B16)
    pre = dot(hs_ref[...], w_ref[0:width, :])
    pre = pre + dot(hr_ref[...], w_ref[width : 2 * width, :])
    pre = pre + dot(x_ref[...], w_ref[2 * width : 3 * width, :])
    pre = pre + dot(chosen_columns(region_ref, tile, rows, 0, LANES), table)
    return pre + vectors_of(w_ref, width)[0:1, :]


def normalized(hidden, w_ref, vec):
    width = hidden.shape[1]
    inner = dot(hidden, w_ref[3 * width : 4 * width, :]) + vec[1:2, :]
    center = inner - jnp.mean(inner, axis=-1, keepdims=True)
    inverse = lax.rsqrt(jnp.mean(center * center, axis=-1, keepdims=True) + NORM_EPS)
    return center * inverse, inverse


def power_of_two(exponents):
    return jnp.exp(exponents * LOG_TWO)


def encoded(values):
    rows, width = values.shape
    quarter = rows // 4
    largest = jnp.maximum(jnp.max(jnp.abs(values), axis=-1, keepdims=True), TINY)
    exponents = jnp.ceil(jnp.log(largest) * (1.0 / LOG_TWO))
    codes = jnp.round(values * power_of_two(STEPS - exponents)).astype(I32)
    upper = lax.shift_right_arithmetic(codes, 4)
    words = jnp.full((quarter, width), -32768, I32)
    for i in range(4):
        words = words + lax.shift_left(jnp.bitwise_and(codes[i * quarter : (i + 1) * quarter, :], 15), 4 * i)
    marks = [
        jnp.broadcast_to(exponents[g * LANES : (g + 1) * LANES, :], (LANES, LANES)).T[0:1, :]
        for g in range(rows // LANES)
    ]
    marks = jnp.concatenate([*marks, jnp.zeros((16 - len(marks), LANES), F32)], axis=0).astype(I32)
    marks = jnp.concatenate([marks, jnp.zeros((16, width - LANES), I32)], axis=1)
    return jnp.concatenate([upper, words, marks], axis=0).astype(I16)


def decoded(wire):
    width = wire.shape[1]
    quarter = (wire.shape[0] - 16) // 5
    rows = 4 * quarter
    wire = wire.astype(I32)
    words = wire[rows : rows + quarter, :] + 32768
    lower = jnp.concatenate([jnp.bitwise_and(lax.shift_right_arithmetic(words, 4 * i), 15) for i in range(4)], axis=0)
    codes = (wire[:rows, :] * 16 + lower).astype(F32)
    exponents = wire[rows + quarter :, :LANES].astype(F32)
    scale = [power_of_two(column(exponents[g : g + 1, :]) - STEPS) for g in range(rows // LANES)]
    return codes * jnp.concatenate([jnp.concatenate(scale, axis=0)] * (width // LANES), axis=1)


def ways(count):
    return sorted(range(1, count), key=lambda k: (k < count // 2, k))


def edge_forward_kernel(
    region_ref, recv_row_ref, hs_ref, hr_ref, x_ref, *refs,
):
    pieces, refs = refs[:-5], refs[-5:]
    w_ref, high_ref, low_ref, halo_ref, wide_ref = refs
    rows, width = x_ref.shape
    nodes = (halo_ref.shape[0] - 16) // 5 * 4

    @pl.when(pl.program_id(0) == 0)
    def _():
        odd, f = odd_core(), lax.axis_index("feat")
        share = pieces[0].shape[0]
        shares = w_ref.shape[0] // share
        for k in range(shares):
            at = ways(shares).index(k) if k else 0
            rows = slice(at * share, (at + 1) * share)
            mine, other = (pieces[i][...] if k == 0 else pieces[i + 1][rows, :] for i in (0, 2))
            mine, other = mine.astype(F32), other.astype(F32)
            base = pl.multiple_of(jnp.bitwise_xor(f, k) * share, 8)
            wide_ref[pl.ds(base, share), 0:LANES] = jnp.where(odd, other, mine)
            wide_ref[pl.ds(base, share), LANES : 2 * LANES] = jnp.where(odd, mine, other)
        w_ref[...] = wide_ref[...].astype(B16)

    vec = vectors_of(w_ref, width)
    total = None
    for i in range(rows // PART + 1):
        if i < rows // PART:
            here = slice(i * PART, (i + 1) * PART)
            pre = before_silu(region_ref, i, hs_ref.at[here, :], hr_ref.at[here, :], x_ref.at[here, :], w_ref)
            hidden = (pre / (1.0 + jnp.exp(-pre))).astype(B16)
            unit, _ = normalized(hidden, w_ref, vec)
            high, low = split(unit * vec[2:3, :] + vec[3:4, :])
            high_ref[here, :] = high
            low_ref[here, :] = low
        if i > 0:
            last = slice((i - 1) * PART, i * PART)
            onehot = chosen_rows(recv_row_ref[:, last], 2 * nodes, nodes)
            more = dot(onehot, high_ref[last, :]) + dot(onehot, low_ref[last, :])
            total = more if total is None else total + more
    halo_ref[...] = encoded(total)


def edge_forward(regions, recv, hs, hr, edges, pieces, total, nodes):
    count, width = edges.shape
    tile = tiled(count, width)
    return pl.pallas_call(
        edge_forward_kernel,
        grid=(1,),
        in_specs=[
            whole((count // LANES, LANES)), whole((1, count)), tile, tile, tile,
            *[whole(piece.shape) for piece in pieces],
        ],
        out_specs=[
            whole((total, width)), whole((count, width)), whole((count, width)),
            whole((nodes + nodes // 4 + 16, width)),
        ],
        out_shape=[
            jax.ShapeDtypeStruct((total, width), B16),
            jax.ShapeDtypeStruct((count, width), B16),
            jax.ShapeDtypeStruct((count, width), B16),
            jax.ShapeDtypeStruct((nodes + nodes // 4 + 16, width), I16),
        ],
        scratch_shapes=[pltpu.VMEM((total, width), F32)],
        compiler_params=PARAMS,
        name="edge_forward",
        cost_estimate=pl.CostEstimate(
            flops=2 * count * width * (5 * width + 2 * nodes), transcendentals=2 * count * width,
            bytes_accessed=count * width * 10,
        ),
    )(regions.reshape(-1, LANES), recv.reshape(1, -1), hs, hr, edges, *pieces)


def edge_slope_kernel(region_ref, hs_ref, hr_ref, x_ref, w_ref, hidden_ref, slope_ref):
    pre = before_silu(region_ref, pl.program_id(0), hs_ref, hr_ref, x_ref, w_ref)
    sigma = 1.0 / (1.0 + jnp.exp(-pre))
    hidden_ref[...] = (pre / (1.0 + jnp.exp(-pre))).astype(B16)
    slope_ref[...] = sigma * (1.0 + pre * (1.0 - sigma))


def edge_slope(regions, hs, hr, edges, weights):
    count, width = edges.shape
    tile = tiled(TILE, width)
    return pl.pallas_call(
        edge_slope_kernel,
        grid=(count // TILE,),
        in_specs=[whole((count // LANES, LANES)), tile, tile, tile, whole(weights.shape)],
        out_specs=[tile, tile],
        out_shape=[jax.ShapeDtypeStruct((count, width), B16), jax.ShapeDtypeStruct((count, width), F32)],
        compiler_params=PARAMS,
        name="edge_slope",
        cost_estimate=pl.CostEstimate(
            flops=2 * count * width * 4 * width, transcendentals=2 * count * width, bytes_accessed=count * width * 12
        ),
    )(regions.reshape(-1, LANES), hs, hr, edges, weights)


def edge_unit_kernel(hidden_ref, w_ref, unit_ref, inverse_ref):
    unit, inverse = normalized(hidden_ref[...], w_ref, vectors_of(w_ref, hidden_ref.shape[1]))
    unit_ref[...] = unit
    inverse_ref[...] = jnp.broadcast_to(inverse, inverse_ref.shape)


def edge_unit(hidden, weights):
    count, width = hidden.shape
    tile = tiled(TILE, width)
    return pl.pallas_call(
        edge_unit_kernel,
        grid=(count // TILE,),
        in_specs=[tile, whole(weights.shape)],
        out_specs=[tile, tiled(TILE, LANES)],
        out_shape=[jax.ShapeDtypeStruct((count, width), F32), jax.ShapeDtypeStruct((count, LANES), F32)],
        compiler_params=PARAMS,
        name="edge_unit",
        cost_estimate=pl.CostEstimate(
            flops=2 * count * width * width, transcendentals=count, bytes_accessed=count * width * 8
        ),
    )(hidden, weights)


def near_sum_kernel(recv_row_ref, high_ref, low_ref, pair_ref, more_ref, own_ref):
    nodes = own_ref.shape[0]
    half = nodes // 2
    for first, out_ref in ((nodes, pair_ref), (nodes + half, more_ref), (0, own_ref)):
        onehot = chosen_rows(recv_row_ref[...], first, out_ref.shape[0])
        out_ref[...] = dot(onehot, high_ref[...]) + dot(onehot, low_ref[...])


def near_sum(recv, high, low, nodes):
    count, width = high.shape
    half = jax.ShapeDtypeStruct((nodes // 2, width), F32)
    return pl.pallas_call(
        near_sum_kernel,
        out_shape=[half, half, jax.ShapeDtypeStruct((nodes, width), F32)],
        compiler_params=PARAMS,
        name="near_sum",
        cost_estimate=pl.CostEstimate(
            flops=8 * count * width * nodes, transcendentals=0, bytes_accessed=count * width * 4
        ),
    )(recv.reshape(1, -1), high, low)


def kept_nodes(forced_ref, width):
    keep = [column(forced_ref[g : g + 1, :]) for g in range(forced_ref.shape[0])]
    keep = 1.0 - jnp.concatenate(keep, axis=0).astype(F32)
    return jnp.concatenate([keep] * (width // LANES), axis=1)


def node_kernel(
    h_ref, own_ref, pair_ref, more_ref, off_ref, w_ref, forced_ref, up_ref,
    d_agg_ref, agg_ref, hidden_ref, d_inner_ref, d_pre_ref, unit_ref,
):
    width = h_ref.shape[1]
    pair = jnp.concatenate([pair_ref[...], more_ref[...]], axis=0)
    agg_ref[...] = (own_ref[...] + pair + decoded(off_ref[...])).astype(B16)
    vec = vectors_of(w_ref, width)
    latent, aggregate = w_ref[4 * width : 5 * width, :], w_ref[5 * width : 6 * width, :]
    second = w_ref[6 * width : 7 * width, :]
    pre = dot(h_ref[...], latent) + dot(agg_ref[...], aggregate) + vec[4:5, :]
    sigma = 1.0 / (1.0 + jnp.exp(-pre))
    hidden = (pre / (1.0 + jnp.exp(-pre))).astype(B16)
    hidden_ref[...] = hidden
    inner = dot(hidden, second) + vec[5:6, :]
    center = inner - jnp.mean(inner, axis=-1, keepdims=True)
    inverse = lax.rsqrt(jnp.mean(center * center, axis=-1, keepdims=True) + NORM_EPS)
    unit = center * inverse
    unit_ref[...] = unit
    scaled = kept_nodes(forced_ref, width) * up_ref[...] * vec[6:7, :]
    d_inner = inverse * (
        scaled
        - jnp.mean(scaled, axis=-1, keepdims=True)
        - unit * jnp.mean(scaled * unit, axis=-1, keepdims=True)
    )
    d_inner = d_inner.astype(B16)
    d_inner_ref[...] = d_inner
    slope = sigma * (1.0 + pre * (1.0 - sigma))
    d_pre = (dot_back(d_inner, second) * slope).astype(B16)
    d_pre_ref[...] = d_pre
    d_agg_ref[...] = dot_back(d_pre, aggregate).astype(B16)


def node_update(h, own, pair, more, off, weights, forced, upstream):
    nodes, width = h.shape
    half = jax.ShapeDtypeStruct((nodes, width), B16)
    return pl.pallas_call(
        node_kernel,
        out_shape=[half, half, half, half, half, jax.ShapeDtypeStruct((nodes, width), F32)],
        compiler_params=PARAMS,
        name="node_update",
        cost_estimate=pl.CostEstimate(
            flops=2 * nodes * width * width * 5, transcendentals=2 * nodes * width, bytes_accessed=nodes * width * 20
        ),
    )(h, own, pair, more, off, weights, forced.reshape(-1, LANES), upstream)


def node_grads_kernel(
    h_ref, agg_ref, hidden_ref, d_inner_ref, d_pre_ref, unit_ref, w_ref, forced_ref, up_ref,
    new_ref, grad_ref, sums_ref, back_ref,
):
    width = h_ref.shape[1]
    vec = vectors_of(w_ref, width)
    keep = kept_nodes(forced_ref, width)
    unit, upstream = unit_ref[...], up_ref[...]
    new_ref[...] = h_ref[...].astype(F32) + keep * (unit * vec[6:7, :] + vec[7:8, :])
    d_pre, d_inner, d_update = d_pre_ref[...], d_inner_ref[...], keep * upstream
    grad_ref[0:width, :] = dot_rows(h_ref[...], d_pre)
    grad_ref[width : 2 * width, :] = dot_rows(agg_ref[...], d_pre)
    grad_ref[2 * width : 3 * width, :] = dot_rows(hidden_ref[...], d_inner)
    back_ref[...] = upstream + dot_back(d_pre, w_ref[4 * width : 5 * width, :])
    sums_ref[...] = jnp.concatenate(
        [
            jnp.sum(d_pre.astype(F32), axis=0, keepdims=True),
            jnp.sum(d_inner.astype(F32), axis=0, keepdims=True),
            jnp.sum(d_update * unit, axis=0, keepdims=True),
            jnp.sum(d_update, axis=0, keepdims=True),
        ],
        axis=0,
    )


def node_grads(h, agg, hidden, d_inner, d_pre, unit, weights, forced, upstream):
    nodes, width = h.shape
    full = jax.ShapeDtypeStruct((nodes, width), F32)
    return pl.pallas_call(
        node_grads_kernel,
        out_shape=[full, jax.ShapeDtypeStruct((3 * width, width), F32), jax.ShapeDtypeStruct((4, width), F32), full],
        compiler_params=PARAMS,
        name="node_grads",
        cost_estimate=pl.CostEstimate(
            flops=2 * nodes * width * width * 4, transcendentals=0, bytes_accessed=nodes * width * 18
        ),
    )(h, agg, hidden, d_inner, d_pre, unit, weights, forced.reshape(-1, LANES), upstream)


def edge_backward_kernel(
    choice_ref, region_row_ref, off_ref, near_ref, hs_ref, hr_ref, x_ref, hidden_ref, slope_ref, unit_ref,
    inverse_ref, w_ref, node_grad_ref, node_sum_ref,
    d_pre_ref, kept_ref, sent_ref,
    d_inner_ref, vec_acc_ref,
):
    step = pl.program_id(0)
    steps = pl.num_programs(0)
    rows = slope_ref.shape[0]
    width = x_ref.shape[1]
    regions = w_ref.shape[0] - 7 * width - 8
    vec = vectors_of(w_ref, width)

    @pl.when(step == 0)
    def _():
        vec_acc_ref[...] = jnp.zeros_like(vec_acc_ref)

    d_message = dot(choice_ref[...], off_ref[...])
    d_message = d_message + near_ref[...].astype(F32)
    unit = unit_ref[...]
    scaled = d_message * vec[2:3, :]
    inverse = jnp.concatenate([inverse_ref[...]] * (width // LANES), axis=1)
    d_inner = inverse * (
        scaled
        - jnp.mean(scaled, axis=-1, keepdims=True)
        - unit * jnp.mean(scaled * unit, axis=-1, keepdims=True)
    )
    vec_acc_ref[0:8, :] += jnp.sum((d_message * unit).reshape(rows // 8, 8, width), axis=0)
    vec_acc_ref[8:16, :] += jnp.sum(d_message.reshape(rows // 8, 8, width), axis=0)
    d_inner = d_inner.astype(B16)
    d_pre = (dot_back(d_inner, w_ref[3 * width : 4 * width, :]) * slope_ref[...]).astype(B16)
    base = pl.multiple_of(step * rows, rows)
    d_inner_ref[pl.ds(base, rows), :] = d_inner
    d_pre_ref[pl.ds(base, rows), :] = d_pre

    @pl.when(step == steps - 1)
    def _():
        odd = odd_core()

        def put(start, piece):
            left, right = piece[:, 0:LANES], piece[:, LANES:]
            kept_ref[start : start + piece.shape[0], :] = jnp.where(odd, right, left)
            sent_ref[start : start + piece.shape[0], :] = jnp.where(odd, left, right)

        table_rows = node_grad_ref.shape[0] + 4 * width
        d_inner, d_pre = d_inner_ref[...], d_pre_ref[...]
        left = jnp.concatenate([hidden_ref[...].T, jnp.ones((16, d_inner.shape[0]), B16)], axis=0)
        both = dot(left, d_inner)
        second_sum = both[width : width + 1, :]
        put(3 * width, both[0:width, :])
        left = jnp.concatenate([hs_ref[...].T, chosen_rows(region_row_ref[...], 0, -(-regions // 16) * 16)], axis=0)
        both = dot(left, d_pre)
        table_grad = both[width : width + regions, :]
        put(0, both[0:width, :])
        put(width, dot_rows(hr_ref[...], d_pre))
        put(2 * width, dot_rows(x_ref[...], d_pre))
        put(4 * width, node_grad_ref[...])
        vector_rows = jnp.concatenate(
            [
                jnp.sum(table_grad, axis=0, keepdims=True),
                second_sum,
                jnp.sum(vec_acc_ref[0:8, :], axis=0, keepdims=True),
                jnp.sum(vec_acc_ref[8:16, :], axis=0, keepdims=True),
                node_sum_ref[...],
            ],
            axis=0,
        )
        put(table_rows, vector_rows)
        put(table_rows + 8, table_grad)


def edge_backward(
    choice, regions, off, near, hs, hr, edges, hidden, slope, unit, inverse, weights, node_grad, node_sum,
):
    count, width = edges.shape
    tile, full = tiled(TILE, width), whole((count, width))
    grad_rows = weights.shape[0]
    half = whole((grad_rows, LANES))
    return pl.pallas_call(
        edge_backward_kernel,
        grid=(count // TILE,),
        in_specs=[
            tiled(TILE, off.shape[0]), whole((1, count)),
            whole(off.shape), tile, full, full, full, full, tile, tile, tiled(TILE, LANES),
            whole(weights.shape), whole(node_grad.shape), whole(node_sum.shape),
        ],
        out_specs=[full, half, half],
        out_shape=[
            jax.ShapeDtypeStruct((count, width), B16),
            jax.ShapeDtypeStruct((grad_rows, LANES), F32),
            jax.ShapeDtypeStruct((grad_rows, LANES), F32),
        ],
        scratch_shapes=[pltpu.VMEM((count, width), B16), pltpu.VMEM((16, width), F32)],
        compiler_params=PARAMS,
        name="edge_backward",
        cost_estimate=pl.CostEstimate(
            flops=2 * count * width * (6 * width + off.shape[0]), transcendentals=0, bytes_accessed=count * width * 20
        ),
    )(
        choice, regions.reshape(1, -1), off, near, hs, hr, edges, hidden, slope, unit, inverse,
        weights, node_grad, node_sum,
    )


def node_part_of(index_row_ref, d_pre_ref, weight, slot, nodes):
    high, low = split(dot(chosen_rows(index_row_ref[...], slot * nodes, nodes), d_pre_ref[...]))
    return dot_back(high, weight) + dot_back(low, weight)


def sender_part_kernel(index_row_ref, d_pre_ref, w_ref, out_ref):
    nodes, width = out_ref.shape
    out_ref[...] = node_part_of(index_row_ref, d_pre_ref, w_ref[0:width, :], pl.program_id(0), nodes)


def sender_part(index, d_pre, weights, nodes):
    count, width = d_pre.shape
    return pl.pallas_call(
        sender_part_kernel,
        grid=(3,),
        in_specs=[whole((1, count)), whole((count, width)), whole(weights.shape)],
        out_specs=tiled(nodes, width),
        out_shape=jax.ShapeDtypeStruct((3 * nodes, width), F32),
        compiler_params=PARAMS,
        name="sender_part",
        cost_estimate=pl.CostEstimate(
            flops=6 * count * width * nodes, transcendentals=0, bytes_accessed=count * width * 2
        ),
    )(index.reshape(1, -1), d_pre, weights)


def receiver_part_kernel(index_row_ref, d_pre_ref, w_ref, part_ref, pair_ref, off_ref):
    nodes, width = pair_ref.shape
    slot = pl.program_id(0) + 1
    part = node_part_of(index_row_ref, d_pre_ref, w_ref[width : 2 * width, :], slot, nodes) + part_ref[...]

    @pl.when(slot == 1)
    def _():
        pair_ref[...] = part.astype(B16)

    @pl.when(slot == 2)
    def _():
        off_ref[...] = part.astype(B16)


def receiver_part(index, d_pre, weights, part, nodes):
    count, width = d_pre.shape
    half = jax.ShapeDtypeStruct((nodes, width), B16)
    return pl.pallas_call(
        receiver_part_kernel,
        grid=(2,),
        in_specs=[
            whole((1, count)), whole((count, width)), whole(weights.shape),
            pl.BlockSpec((nodes, width), lambda i: (i + 1, 0)),
        ],
        out_specs=[whole((nodes, width))] * 2,
        out_shape=[half, half],
        compiler_params=PARAMS,
        name="receiver_part",
        cost_estimate=pl.CostEstimate(
            flops=4 * count * width * nodes, transcendentals=0, bytes_accessed=count * width * 2
        ),
    )(index.reshape(1, -1), d_pre, weights, part)


def own_part_kernel(index_row_ref, d_pre_ref, w_ref, part_ref, back_ref, own_ref):
    nodes, width = own_ref.shape
    part = node_part_of(index_row_ref, d_pre_ref, w_ref[width : 2 * width, :], 0, nodes)
    own_ref[...] = part + (part_ref[...] + back_ref[...])


def own_part(index, d_pre, weights, part, back):
    count, width = d_pre.shape
    return pl.pallas_call(
        own_part_kernel,
        grid=(1,),
        in_specs=[whole((1, count)), whole((count, width)), whole(weights.shape), whole(back.shape), whole(back.shape)],
        out_specs=whole(back.shape),
        out_shape=jax.ShapeDtypeStruct(back.shape, F32),
        compiler_params=PARAMS,
        name="own_part",
        cost_estimate=pl.CostEstimate(
            flops=2 * count * width * back.shape[0], transcendentals=0, bytes_accessed=count * width * 2
        ),
    )(index.reshape(1, -1), d_pre, weights, part, back)


def edge_grads_kernel(d_pre_ref, w_ref, out_ref):
    width = d_pre_ref.shape[1]
    out_ref[...] = dot_back(d_pre_ref[...], w_ref[2 * width : 3 * width, :]).astype(B16)


def edge_grads(d_pre, weights):
    count, width = d_pre.shape
    return pl.pallas_call(
        edge_grads_kernel,
        grid=(count // TILE,),
        in_specs=[tiled(TILE, width), whole(weights.shape)],
        out_specs=tiled(TILE, width),
        out_shape=jax.ShapeDtypeStruct((count, width), B16),
        compiler_params=PARAMS,
        name="edge_grads",
        cost_estimate=pl.CostEstimate(
            flops=2 * count * width * width, transcendentals=0, bytes_accessed=count * width * 4
        ),
    )(d_pre, weights)


def packed(values, first):
    rows = values[first : first + 8, :]
    return jnp.concatenate([values, rows - rows.astype(B16).astype(F32)], axis=0).astype(B16)


def unpacked(wire, first):
    values = wire.astype(F32)
    share = values.shape[0] - 8
    exact = values[first : first + 8, :] + values[share:, :]
    return jnp.concatenate([values[:first, :], exact, values[first + 8 : share, :]], axis=0)


def parted_kernel(mine_ref, other_ref, kept_ref, *sent_refs, share, first):
    for k, out_ref in enumerate((kept_ref, *sent_refs)):
        rows = pl.ds(pl.multiple_of(jnp.bitwise_xor(lax.axis_index("feat"), k) * share, 8), share)
        total = mine_ref[rows, :] + other_ref[rows, :]
        out_ref[...] = packed(total, first) if k else total


def parted(mine, other, share, first):
    sent = jax.ShapeDtypeStruct((share + 8, LANES), B16)
    return pl.pallas_call(
        functools.partial(parted_kernel, share=share, first=first),
        out_shape=[jax.ShapeDtypeStruct((share, LANES), F32)] + [sent] * (mine.shape[0] // share - 1),
        compiler_params=PARAMS,
        name="parted",
    )(mine, other)


def gathered_kernel(mine_ref, *refs, first):
    total = mine_ref[...]
    for ref in refs[:-1]:
        total = total + unpacked(ref[...], first)
    refs[-1][...] = packed(total, first)


def gathered(mine, others, first):
    return pl.pallas_call(
        functools.partial(gathered_kernel, first=first),
        out_shape=jax.ShapeDtypeStruct(others[0].shape, B16),
        compiler_params=PARAMS,
        name="gathered",
    )(mine, *others)


def add_kernel(mine_ref, other_ref, out_ref, *, first):
    out_ref[...] = packed(unpacked(mine_ref[...], first) + unpacked(other_ref[...], first), first)


def add(mine, other, first):
    return pl.pallas_call(
        functools.partial(add_kernel, first=first),
        out_shape=jax.ShapeDtypeStruct(other.shape, B16),
        compiler_params=PARAMS,
        name="add",
    )(mine, other)


def finish_kernel(mine_ref, other_ref, out_ref, *, first, owner):
    share = out_ref.shape[0] - 16
    part = unpacked(mine_ref[...], first) + unpacked(other_ref[...], first)
    out_ref[0:share, :] = part
    out_ref[share : share + 8, :] = jnp.where(lax.axis_index("feat") == owner, part[first : first + 8, :], 0.0)
    squares = jnp.sum(jnp.sum(part * part, axis=0, keepdims=True), axis=1, keepdims=True)
    out_ref[share + 8 : share + 16, :] = jnp.broadcast_to(squares, (8, LANES))


def finish(mine, other, share, first, owner):
    return pl.pallas_call(
        functools.partial(finish_kernel, first=first, owner=owner),
        out_shape=jax.ShapeDtypeStruct((share + 16, LANES), F32),
        compiler_params=PARAMS,
        name="finish",
    )(mine, other)


def adam_kernel(
    step_ref, stats_ref, more_ref, mine_ref, other_ref, params_ref, first_ref, second_ref, averaged_ref,
    own_ref, pair_ref, off_ref,
    new_first_hbm, new_second_hbm, new_params_hbm, new_average_hbm, norm_ref, vector_ref, latents_hbm,
    new_first_ref, new_second_ref, new_params_ref, new_average_ref, latents_ref, sem,
):
    share = params_ref.shape[0]
    odd = odd_core()
    latents_ref[...] = own_ref[...] + pair_ref[...].astype(F32) + off_ref[...].astype(F32)
    copies = [pltpu.make_async_copy(latents_ref, latents_hbm, sem.at[0])]
    copies[0].start()
    stats, more = stats_ref[...], more_ref[...]
    norm = jnp.sqrt(stats[8:9, 0:1] + more[8:9, 0:1])
    norm_ref[...] = norm
    factor = jnp.minimum(1.0, MAX_NORM / (norm + 1e-06))
    count = step_ref[0:1, 0:1]
    first_scale = 1.0 - jnp.exp(count * jnp.log(jnp.full((1, 1), BETA_ONE, F32)))
    second_scale = 1.0 - jnp.exp(count * jnp.log(jnp.full((1, 1), BETA_TWO, F32)))
    decay = jnp.minimum(AVERAGE_DECAY, (1.0 + count) / (10.0 + count))
    vector_ref[:, 0:LANES] = jnp.where(odd, more[0:8, :], stats[0:8, :]) * factor
    vector_ref[:, LANES : 2 * LANES] = jnp.where(odd, stats[0:8, :], more[0:8, :]) * factor
    chunk = share // 3 if share % 24 == 0 else share
    for i in range(share // chunk):
        rows = slice(i * chunk, (i + 1) * chunk)
        mine, other = mine_ref[rows, :], other_ref[rows, :]
        both = jnp.concatenate([jnp.where(odd, other, mine), jnp.where(odd, mine, other)], axis=1)
        clipped = both * factor
        params = params_ref[rows, :]
        new_first = BETA_ONE * first_ref[rows, :] + (1.0 - BETA_ONE) * clipped
        new_second = BETA_TWO * second_ref[rows, :] + (1.0 - BETA_TWO) * clipped * clipped
        first_hat = new_first / first_scale
        second_hat = new_second / second_scale
        new_params = params - RATE * (first_hat / (jnp.sqrt(second_hat) + ADAM_EPS) + WEIGHT_DECAY * params)
        new_first_ref[rows, :] = new_first
        new_second_ref[rows, :] = new_second
        new_params_ref[rows, :] = new_params
        new_average_ref[rows, :] = decay * averaged_ref[rows, :] + (1.0 - decay) * new_params
        for k, (src, dst) in enumerate(
            (
                (new_first_ref, new_first_hbm), (new_second_ref, new_second_hbm), (new_params_ref, new_params_hbm),
                (new_average_ref, new_average_hbm),
            )
        ):
            copies.append(pltpu.make_async_copy(src.at[rows, :], dst.at[rows, :], sem.at[1 + 4 * i + k]))
            copies[-1].start()
    for copy in copies:
        copy.wait()


def adam(step, stats, more, mine, other, params, first_moment, second_moment, averaged, own, pair, off):
    rows = jax.ShapeDtypeStruct(params.shape, F32)
    vmem, hbm = (pl.BlockSpec(memory_space=m) for m in (pltpu.VMEM, pltpu.HBM))
    return pl.pallas_call(
        adam_kernel,
        in_specs=[vmem] * 12,
        out_specs=[hbm] * 4 + [vmem] * 2 + [hbm],
        out_shape=[
            rows, rows, rows, rows, jax.ShapeDtypeStruct((1, 1), F32), jax.ShapeDtypeStruct((8, params.shape[1]), F32),
            jax.ShapeDtypeStruct(own.shape, F32),
        ],
        scratch_shapes=[pltpu.VMEM(params.shape, F32)] * 4
        + [pltpu.VMEM(own.shape, F32), pltpu.SemaphoreType.DMA((13,))],
        compiler_params=PARAMS,
        name="adam",
        cost_estimate=pl.CostEstimate(
            flops=20 * params.size, transcendentals=2 * params.size, bytes_accessed=params.size * 32
        ),
    )(jnp.broadcast_to(step.astype(F32), (8, LANES)), stats, more, mine, other, params, first_moment, second_moment, averaged, own, pair, off)


def flipped(value, axis, bit):
    return lax.ppermute(value, axis, [(i, i ^ bit) for i in range(lax.axis_size(axis))])


def across(value, axis):
    count = lax.axis_size(axis)
    return lax.ppermute(value, axis, [(i, (i + 1 if i % 2 else i - 1) % count) for i in range(count)])


def neighbours(value):
    off = across(value, "edge")
    return flipped(value, "edge", 1), off


def on_device(
    node_latents, edge_latents, senders, receivers, regions, forced, params, first_moment, second_moment,
    averaged, step, cotangent,
):
    latents = node_latents[0]
    edges = edge_latents[0]
    upstream = cotangent[0]
    nodes, width = latents.shape
    share = params.shape[0]
    blocks, feats = lax.axis_size("edge"), lax.axis_size("feat")
    total = share * feats
    vector_row = 7 * width

    pair, off = neighbours(latents)

    mine, send, recv, latents = prologue(params, senders, receivers, latents)
    far = [flipped(mine, "feat", k) for k in ways(feats)]

    near_send = gather_near(send, latents, pair)
    near_recv = gather_near(recv, latents, pair)
    others = jnp.concatenate(lax.optimization_barrier((near_send, near_recv, *far))[2:])
    pieces = [mine, others, flipped(mine, "edge", 1), flipped(others, "edge", 1)]
    hs = gather_off(send, off, near_send)
    hr = gather_off(recv, off, near_recv)
    weights, high, low, to_off = edge_forward(regions, recv, hs, hr, edges, pieces, total, nodes)
    from_off = across(to_off, "edge")
    to_pair, more, own = near_sum(recv, high, low, nodes)
    from_pair, more = flipped(to_pair, "edge", 1), flipped(more, "edge", 1)
    hidden, slope = edge_slope(regions, hs, hr, edges, weights)
    own, hidden, slope = lax.optimization_barrier((own, hidden, slope))
    d_agg, agg, node_hidden, d_inner, d_pre, node_unit = node_update(
        latents, own, from_pair, more, from_off, weights, forced, upstream
    )
    back_pair, back_off = neighbours(d_agg)
    new_latents, node_grad, node_sum, back = node_grads(
        latents, agg, node_hidden, d_inner, d_pre, node_unit, weights, forced, upstream
    )
    near = gather_near(recv, d_agg, back_pair)
    hidden, index = lax.optimization_barrier((hidden, recv, d_agg))[:2]
    unit, inverse = edge_unit(hidden, weights)
    choice = off_choice(index, nodes)

    d_pre, kept, sent = edge_backward(
        choice, regions, back_off, near, hs, hr, edges, hidden, slope, unit, inverse, weights, node_grad, node_sum,
    )

    low_rows = vector_row % share
    grad_edges = edge_grads(d_pre, weights)
    other, grad_edges = lax.optimization_barrier((flipped(sent, "edge", 1), grad_edges))
    part, *sent = parted(kept, other, share, low_rows)
    came = [flipped(sent[k - 1], "feat", k) for k in ways(feats)]
    d_pre, part = lax.optimization_barrier((d_pre, part))
    send_part = sender_part(send, d_pre, weights, nodes)
    part_pair, part_off = receiver_part(recv, d_pre, weights, send_part, nodes)
    part, part_pair, part_off = lax.optimization_barrier((part, part_pair, part_off))
    wire = gathered(part, came, low_rows)
    bit = 2
    while 2 * bit < blocks:
        wire = add(wire, flipped(wire, "edge", bit), low_rows)
        bit *= 2
    part_own = own_part(recv, d_pre, weights, send_part, back)
    wire, part_pair, part_off, part_own = lax.optimization_barrier((wire, part_pair, part_off, part_own))
    mine = finish(wire, flipped(wire, "edge", bit), share, low_rows, vector_row // share)
    grads_off = across(part_off, "edge")
    grads_pair = flipped(part_pair, "edge", 1)

    other = flipped(mine[:share], "edge", 1)
    held = {0: mine[share:], **{k: flipped(mine[share:], "feat", k) for k in ways(feats)}}
    held = [held[k] for k in range(feats)]
    while len(held) > 1:
        held = [held[i] + held[i + 1] for i in range(0, len(held), 2)]
    stats = held[0]
    more = flipped(stats, "edge", 1)
    new_first, new_second, new_params, new_average, grad_norm, vector_grads, grad_latents = adam(
        step, stats, more, mine, other, params, first_moment, second_moment, averaged,
        part_own, grads_pair, grads_off,
    )
    return (
        new_latents[None],
        grad_latents[None],
        grad_edges[None],
        new_first,
        new_second,
        new_params,
        new_average,
        grad_norm.reshape(1),
        vector_grads,
    )


def solution(mesh):
    nodes, rows = P("feat", "edge", None), P("feat", None)
    return jax.shard_map(
        on_device,
        mesh=mesh,
        in_specs=(nodes, nodes, P("edge"), P("edge"), P("edge"), P("edge"), rows, rows, rows, rows, P(), nodes),
        out_specs=(nodes, nodes, nodes, rows, rows, rows, rows, P(), P()),
        check_vma=False,
    )
```

```python
import functools

import jax
import jax.numpy as jnp
from jax import lax
from jax.experimental import pallas as pl
from jax.experimental.pallas import tpu as pltpu
from jax.sharding import PartitionSpec as P

NORM_EPS = 1e-05
MAX_NORM = 512.0
RATE = 0.05
BETA_ONE = 0.9
BETA_TWO = 0.95
ADAM_EPS = 1e-08
WEIGHT_DECAY = 0.1
AVERAGE_DECAY = 0.999

LANES = 128
TINY = 1e-20
STEPS = 18
LOG_TWO = 0.6931471805599453
TILE = 2048
PART = 512
B16 = jnp.bfloat16
F32 = jnp.float32
I32 = jnp.int32
I16 = jnp.int16
PARAMS = pltpu.CompilerParams(vmem_limit_bytes=20 * 1024 * 1024)


def dot(left, right):
    return jnp.dot(left, right, preferred_element_type=F32)


def dot_rows(left, right):
    return lax.dot_general(left, right, (((0,), (0,)), ((), ())), preferred_element_type=F32)


def dot_back(left, right):
    return lax.dot_general(left, right, (((1,), (1,)), ((), ())), preferred_element_type=F32)


def vectors_of(w_ref, width):
    return w_ref[7 * width : 7 * width + 8, :].astype(F32)


def split(values):
    high = values.astype(B16)
    return high, (values - high.astype(F32)).astype(B16)


def whole(shape):
    return pl.BlockSpec(shape, lambda i: (0,) * len(shape))


def tiled(rows, cols):
    return pl.BlockSpec((rows, cols), lambda i: (i, 0))


def column(row):
    return jnp.broadcast_to(row, (LANES, LANES)).T


def chosen_columns(index_ref, tile, rows, first, last):
    lane = lax.broadcasted_iota(I32, (LANES, LANES), 1)
    groups = []
    for g in range(rows // LANES):
        col = column(index_ref[pl.ds(tile * (rows // LANES) + g, 1), :])
        groups.append(
            jnp.concatenate(
                [jnp.where(col == lane + base, 1.0, 0.0).astype(B16) for base in range(first, last, LANES)],
                axis=1,
            )
        )
    return jnp.concatenate(groups, axis=0)


def chosen_rows(index_row, first, count):
    node = lax.broadcasted_iota(I32, (count, index_row.shape[1]), 0) + first
    return jnp.where(index_row == node, 1.0, 0.0).astype(B16)


def core_of(e):
    return e % 2


def odd_core():
    return core_of(lax.axis_index("edge")) == 1


def prologue_kernel(
    params_hbm, send_hbm, recv_hbm, latents_hbm, half_ref, send_ref, recv_ref, latents_ref, wide_ref, in_ref, sem,
    *, nodes,
):
    copies = [
        pltpu.make_async_copy(params_hbm, wide_ref, sem.at[0]),
        pltpu.make_async_copy(send_hbm, in_ref.at[0], sem.at[1]),
        pltpu.make_async_copy(recv_hbm, in_ref.at[1], sem.at[2]),
        pltpu.make_async_copy(latents_hbm, latents_ref, sem.at[3]),
    ]
    for copy in copies:
        copy.start()
    e = lax.axis_index("edge")
    core = core_of(e)
    for i, out_ref in ((0, send_ref), (1, recv_ref)):
        copies[1 + i].wait()
        index = in_ref[i]
        block = lax.div(index, nodes)
        slot = jnp.where(block == e, 0, jnp.where(block == e + 1 - 2 * core, 1, 2))
        out_ref[...] = (slot - block) * nodes + index
    copies[0].wait()
    half_ref[...] = jnp.where(core == 1, wide_ref[:, LANES : 2 * LANES], wide_ref[:, 0:LANES]).astype(B16)
    copies[3].wait()


def prologue(params, senders, receivers, latents):
    shape = (senders.size // LANES, LANES)
    out = jax.ShapeDtypeStruct(shape, I32)
    vmem, hbm = pl.BlockSpec(memory_space=pltpu.VMEM), pl.BlockSpec(memory_space=pltpu.HBM)
    operands = (params, senders.reshape(shape), receivers.reshape(shape), latents)
    half, send, recv, own = pl.pallas_call(
        functools.partial(prologue_kernel, nodes=latents.shape[0]),
        in_specs=[hbm] * 4,
        out_specs=[vmem] * 4,
        out_shape=[
            jax.ShapeDtypeStruct((params.shape[0], LANES), B16), out, out,
            jax.ShapeDtypeStruct(latents.shape, latents.dtype),
        ],
        scratch_shapes=[
            pltpu.VMEM(params.shape, F32), pltpu.VMEM((2, *shape), I32), pltpu.SemaphoreType.DMA((4,)),
        ],
        compiler_params=PARAMS,
        name="prologue",
    )(*(pltpu.with_memory_space_constraint(a, pltpu.HBM) for a in operands))
    return half, send.reshape(-1), recv.reshape(-1), own


def gather_near_kernel(index_ref, own_ref, pair_ref, out_ref):
    tile = pl.program_id(0)
    rows = out_ref.shape[0]
    nodes = own_ref.shape[0]
    total = dot(chosen_columns(index_ref, tile, rows, 0, nodes), own_ref[...])
    total = total + dot(chosen_columns(index_ref, tile, rows, nodes, 2 * nodes), pair_ref[...])
    out_ref[...] = total.astype(B16)


def gather_near(index, own, pair):
    nodes, width = own.shape
    edges = index.size
    return pl.pallas_call(
        gather_near_kernel,
        grid=(1,),
        in_specs=[whole((edges // LANES, LANES))] + [whole((nodes, width))] * 2,
        out_specs=tiled(edges, width),
        out_shape=jax.ShapeDtypeStruct((edges, width), B16),
        compiler_params=PARAMS,
        name="gather_near",
        cost_estimate=pl.CostEstimate(
            flops=2 * edges * 2 * nodes * width, transcendentals=0, bytes_accessed=edges * width * 2
        ),
    )(index.reshape(-1, LANES), own, pair)


def gather_off_kernel(index_ref, off_ref, near_ref, out_ref):
    tile = pl.program_id(0)
    rows = out_ref.shape[0]
    nodes = off_ref.shape[0]
    total = dot(chosen_columns(index_ref, tile, rows, 2 * nodes, 3 * nodes), off_ref[...])
    out_ref[...] = (total + near_ref[...].astype(F32)).astype(B16)


def gather_off(index, off, near):
    nodes, width = off.shape
    edges = index.size
    return pl.pallas_call(
        gather_off_kernel,
        grid=(1,),
        in_specs=[whole((edges // LANES, LANES)), whole((nodes, width)), tiled(edges, width)],
        out_specs=tiled(edges, width),
        out_shape=jax.ShapeDtypeStruct((edges, width), B16),
        compiler_params=PARAMS,
        name="gather_off",
        cost_estimate=pl.CostEstimate(
            flops=2 * edges * nodes * width, transcendentals=0, bytes_accessed=edges * width * 4
        ),
    )(index.reshape(-1, LANES), off, near)


def off_rows_kernel(index_row_ref, out_ref):
    nodes = out_ref.shape[0]
    out_ref[...] = chosen_rows(index_row_ref[...], 2 * nodes, nodes)


def off_rows(index, nodes):
    edges = index.size
    return pl.pallas_call(
        off_rows_kernel,
        grid=(edges // TILE,),
        in_specs=[pl.BlockSpec((1, TILE), lambda i: (0, i))],
        out_specs=pl.BlockSpec((nodes, TILE), lambda i: (0, i)),
        out_shape=jax.ShapeDtypeStruct((nodes, edges), B16),
        compiler_params=PARAMS,
        name="off_rows",
        cost_estimate=pl.CostEstimate(flops=edges * nodes, transcendentals=0, bytes_accessed=edges * nodes * 2),
    )(index.reshape(1, -1))


def off_choice_kernel(index_ref, out_ref):
    rows, nodes = out_ref.shape
    out_ref[...] = chosen_columns(index_ref, pl.program_id(0), rows, 2 * nodes, 3 * nodes)


def off_choice(index, nodes):
    edges = index.size
    return pl.pallas_call(
        off_choice_kernel,
        grid=(edges // TILE,),
        in_specs=[whole((edges // LANES, LANES))],
        out_specs=tiled(TILE, nodes),
        out_shape=jax.ShapeDtypeStruct((edges, nodes), B16),
        compiler_params=PARAMS,
        name="off_choice",
        cost_estimate=pl.CostEstimate(flops=edges * nodes, transcendentals=0, bytes_accessed=edges * nodes * 2),
    )(index.reshape(-1, LANES))


def before_silu(region_ref, tile, hs_ref, hr_ref, x_ref, w_ref):
    rows, width = x_ref.shape
    vector_row = 7 * width
    regions = w_ref.shape[0] - vector_row - 8
    table = jnp.concatenate(
        [w_ref[vector_row + 8 :, :].astype(F32), jnp.zeros((LANES - regions, width), F32)], axis=0
    ).astype(B16)
    pre = dot(hs_ref[...], w_ref[0:width, :])
    pre = pre + dot(hr_ref[...], w_ref[width : 2 * width, :])
    pre = pre + dot(x_ref[...], w_ref[2 * width : 3 * width, :])
    pre = pre + dot(chosen_columns(region_ref, tile, rows, 0, LANES), table)
    return pre + vectors_of(w_ref, width)[0:1, :]


def normalized(hidden, w_ref, vec):
    width = hidden.shape[1]
    inner = dot(hidden, w_ref[3 * width : 4 * width, :]) + vec[1:2, :]
    center = inner - jnp.mean(inner, axis=-1, keepdims=True)
    inverse = lax.rsqrt(jnp.mean(center * center, axis=-1, keepdims=True) + NORM_EPS)
    return center * inverse, inverse


def power_of_two(exponents):
    return jnp.exp(exponents * LOG_TWO)


def encoded(values):
    rows, width = values.shape
    quarter = rows // 4
    largest = jnp.maximum(jnp.max(jnp.abs(values), axis=-1, keepdims=True), TINY)
    exponents = jnp.ceil(jnp.log(largest) * (1.0 / LOG_TWO))
    codes = jnp.round(values * power_of_two(STEPS - exponents)).astype(I32)
    upper = lax.shift_right_arithmetic(codes, 4)
    words = jnp.full((quarter, width), -32768, I32)
    for i in range(4):
        words = words + lax.shift_left(jnp.bitwise_and(codes[i * quarter : (i + 1) * quarter, :], 15), 4 * i)
    marks = [
        jnp.broadcast_to(exponents[g * LANES : (g + 1) * LANES, :], (LANES, LANES)).T[0:1, :]
        for g in range(rows // LANES)
    ]
    marks = jnp.concatenate([*marks, jnp.zeros((16 - len(marks), LANES), F32)], axis=0).astype(I32)
    marks = jnp.concatenate([marks, jnp.zeros((16, width - LANES), I32)], axis=1)
    return jnp.concatenate([upper, words, marks], axis=0).astype(I16)


def decoded(wire):
    width = wire.shape[1]
    quarter = (wire.shape[0] - 16) // 5
    rows = 4 * quarter
    wire = wire.astype(I32)
    words = wire[rows : rows + quarter, :] + 32768
    lower = jnp.concatenate([jnp.bitwise_and(lax.shift_right_arithmetic(words, 4 * i), 15) for i in range(4)], axis=0)
    codes = (wire[:rows, :] * 16 + lower).astype(F32)
    exponents = wire[rows + quarter :, :LANES].astype(F32)
    scale = [power_of_two(column(exponents[g : g + 1, :]) - STEPS) for g in range(rows // LANES)]
    return codes * jnp.concatenate([jnp.concatenate(scale, axis=0)] * (width // LANES), axis=1)


def ways(count):
    return sorted(range(1, count), key=lambda k: (k < count // 2, k))


def edge_forward_kernel(
    region_ref, choice_ref, hs_ref, hr_ref, x_ref, *refs,
):
    pieces, refs = refs[:-5], refs[-5:]
    w_ref, high_ref, low_ref, halo_ref, wide_ref = refs
    rows, width = x_ref.shape
    nodes = (halo_ref.shape[0] - 16) // 5 * 4

    @pl.when(pl.program_id(0) == 0)
    def _():
        odd, f = odd_core(), lax.axis_index("feat")
        share = pieces[0].shape[0]
        shares = w_ref.shape[0] // share
        for k in range(shares):
            at = ways(shares).index(k) if k else 0
            rows = slice(at * share, (at + 1) * share)
            mine, other = (pieces[i][...] if k == 0 else pieces[i + 1][rows, :] for i in (0, 2))
            mine, other = mine.astype(F32), other.astype(F32)
            base = pl.multiple_of(jnp.bitwise_xor(f, k) * share, 8)
            wide_ref[pl.ds(base, share), 0:LANES] = jnp.where(odd, other, mine)
            wide_ref[pl.ds(base, share), LANES : 2 * LANES] = jnp.where(odd, mine, other)
        w_ref[...] = wide_ref[...].astype(B16)

    vec = vectors_of(w_ref, width)
    total = None
    for i in range(rows // PART + 1):
        if i < rows // PART:
            here = slice(i * PART, (i + 1) * PART)
            pre = before_silu(region_ref, i, hs_ref.at[here, :], hr_ref.at[here, :], x_ref.at[here, :], w_ref)
            hidden = (pre / (1.0 + jnp.exp(-pre))).astype(B16)
            unit, _ = normalized(hidden, w_ref, vec)
            high, low = split(unit * vec[2:3, :] + vec[3:4, :])
            high_ref[here, :] = high
            low_ref[here, :] = low
        if i > 0:
            last = slice((i - 1) * PART, i * PART)
            onehot = choice_ref[:, last]
            more = dot(onehot, high_ref[last, :]) + dot(onehot, low_ref[last, :])
            total = more if total is None else total + more
    halo_ref[...] = encoded(total)


def edge_forward(regions, choice, hs, hr, edges, pieces, total, nodes):
    count, width = edges.shape
    tile = tiled(count, width)
    return pl.pallas_call(
        edge_forward_kernel,
        grid=(1,),
        in_specs=[
            whole((count // LANES, LANES)), whole(choice.shape), tile, tile, tile,
            *[whole(piece.shape) for piece in pieces],
        ],
        out_specs=[
            whole((total, width)), whole((count, width)), whole((count, width)),
            whole((nodes + nodes // 4 + 16, width)),
        ],
        out_shape=[
            jax.ShapeDtypeStruct((total, width), B16),
            jax.ShapeDtypeStruct((count, width), B16),
            jax.ShapeDtypeStruct((count, width), B16),
            jax.ShapeDtypeStruct((nodes + nodes // 4 + 16, width), I16),
        ],
        scratch_shapes=[pltpu.VMEM((total, width), F32)],
        compiler_params=PARAMS,
        name="edge_forward",
        cost_estimate=pl.CostEstimate(
            flops=2 * count * width * (5 * width + 2 * nodes), transcendentals=2 * count * width,
            bytes_accessed=count * width * 10,
        ),
    )(regions.reshape(-1, LANES), choice, hs, hr, edges, *pieces)


def edge_slope_kernel(region_ref, hs_ref, hr_ref, x_ref, w_ref, hidden_ref, slope_ref):
    pre = before_silu(region_ref, pl.program_id(0), hs_ref, hr_ref, x_ref, w_ref)
    sigma = 1.0 / (1.0 + jnp.exp(-pre))
    hidden_ref[...] = (pre / (1.0 + jnp.exp(-pre))).astype(B16)
    slope_ref[...] = sigma * (1.0 + pre * (1.0 - sigma))


def edge_slope(regions, hs, hr, edges, weights):
    count, width = edges.shape
    tile = tiled(TILE, width)
    return pl.pallas_call(
        edge_slope_kernel,
        grid=(count // TILE,),
        in_specs=[whole((count // LANES, LANES)), tile, tile, tile, whole(weights.shape)],
        out_specs=[tile, tile],
        out_shape=[jax.ShapeDtypeStruct((count, width), B16), jax.ShapeDtypeStruct((count, width), F32)],
        compiler_params=PARAMS,
        name="edge_slope",
        cost_estimate=pl.CostEstimate(
            flops=2 * count * width * 4 * width, transcendentals=2 * count * width, bytes_accessed=count * width * 12
        ),
    )(regions.reshape(-1, LANES), hs, hr, edges, weights)


def edge_unit_kernel(hidden_ref, w_ref, unit_ref, inverse_ref):
    unit, inverse = normalized(hidden_ref[...], w_ref, vectors_of(w_ref, hidden_ref.shape[1]))
    unit_ref[...] = unit
    inverse_ref[...] = jnp.broadcast_to(inverse, inverse_ref.shape)


def edge_unit(hidden, weights):
    count, width = hidden.shape
    tile = tiled(TILE, width)
    return pl.pallas_call(
        edge_unit_kernel,
        grid=(count // TILE,),
        in_specs=[tile, whole(weights.shape)],
        out_specs=[tile, tiled(TILE, LANES)],
        out_shape=[jax.ShapeDtypeStruct((count, width), F32), jax.ShapeDtypeStruct((count, LANES), F32)],
        compiler_params=PARAMS,
        name="edge_unit",
        cost_estimate=pl.CostEstimate(
            flops=2 * count * width * width, transcendentals=count, bytes_accessed=count * width * 8
        ),
    )(hidden, weights)


def near_sum_kernel(recv_row_ref, high_ref, low_ref, pair_ref, more_ref, own_ref):
    nodes = own_ref.shape[0]
    half = nodes // 2
    for first, out_ref in ((nodes, pair_ref), (nodes + half, more_ref), (0, own_ref)):
        onehot = chosen_rows(recv_row_ref[...], first, out_ref.shape[0])
        out_ref[...] = dot(onehot, high_ref[...]) + dot(onehot, low_ref[...])


def near_sum(recv, high, low, nodes):
    count, width = high.shape
    half = jax.ShapeDtypeStruct((nodes // 2, width), F32)
    return pl.pallas_call(
        near_sum_kernel,
        out_shape=[half, half, jax.ShapeDtypeStruct((nodes, width), F32)],
        compiler_params=PARAMS,
        name="near_sum",
        cost_estimate=pl.CostEstimate(
            flops=8 * count * width * nodes, transcendentals=0, bytes_accessed=count * width * 4
        ),
    )(recv.reshape(1, -1), high, low)


def kept_nodes(forced_ref, width):
    keep = [column(forced_ref[g : g + 1, :]) for g in range(forced_ref.shape[0])]
    keep = 1.0 - jnp.concatenate(keep, axis=0).astype(F32)
    return jnp.concatenate([keep] * (width // LANES), axis=1)


def node_kernel(
    h_ref, own_ref, pair_ref, more_ref, off_ref, w_ref, forced_ref, up_ref,
    d_agg_ref, agg_ref, hidden_ref, d_inner_ref, d_pre_ref, unit_ref,
):
    width = h_ref.shape[1]
    pair = jnp.concatenate([pair_ref[...], more_ref[...]], axis=0)
    agg_ref[...] = (own_ref[...] + pair + decoded(off_ref[...])).astype(B16)
    vec = vectors_of(w_ref, width)
    latent, aggregate = w_ref[4 * width : 5 * width, :], w_ref[5 * width : 6 * width, :]
    second = w_ref[6 * width : 7 * width, :]
    pre = dot(h_ref[...], latent) + dot(agg_ref[...], aggregate) + vec[4:5, :]
    sigma = 1.0 / (1.0 + jnp.exp(-pre))
    hidden = (pre / (1.0 + jnp.exp(-pre))).astype(B16)
    hidden_ref[...] = hidden
    inner = dot(hidden, second) + vec[5:6, :]
    center = inner - jnp.mean(inner, axis=-1, keepdims=True)
    inverse = lax.rsqrt(jnp.mean(center * center, axis=-1, keepdims=True) + NORM_EPS)
    unit = center * inverse
    unit_ref[...] = unit
    scaled = kept_nodes(forced_ref, width) * up_ref[...] * vec[6:7, :]
    d_inner = inverse * (
        scaled
        - jnp.mean(scaled, axis=-1, keepdims=True)
        - unit * jnp.mean(scaled * unit, axis=-1, keepdims=True)
    )
    d_inner = d_inner.astype(B16)
    d_inner_ref[...] = d_inner
    slope = sigma * (1.0 + pre * (1.0 - sigma))
    d_pre = (dot_back(d_inner, second) * slope).astype(B16)
    d_pre_ref[...] = d_pre
    d_agg_ref[...] = dot_back(d_pre, aggregate).astype(B16)


def node_update(h, own, pair, more, off, weights, forced, upstream):
    nodes, width = h.shape
    half = jax.ShapeDtypeStruct((nodes, width), B16)
    return pl.pallas_call(
        node_kernel,
        out_shape=[half, half, half, half, half, jax.ShapeDtypeStruct((nodes, width), F32)],
        compiler_params=PARAMS,
        name="node_update",
        cost_estimate=pl.CostEstimate(
            flops=2 * nodes * width * width * 5, transcendentals=2 * nodes * width, bytes_accessed=nodes * width * 20
        ),
    )(h, own, pair, more, off, weights, forced.reshape(-1, LANES), upstream)


def node_grads_kernel(
    h_ref, agg_ref, hidden_ref, d_inner_ref, d_pre_ref, unit_ref, w_ref, forced_ref, up_ref,
    new_ref, grad_ref, sums_ref, back_ref,
):
    width = h_ref.shape[1]
    vec = vectors_of(w_ref, width)
    keep = kept_nodes(forced_ref, width)
    unit, upstream = unit_ref[...], up_ref[...]
    new_ref[...] = h_ref[...].astype(F32) + keep * (unit * vec[6:7, :] + vec[7:8, :])
    d_pre, d_inner, d_update = d_pre_ref[...], d_inner_ref[...], keep * upstream
    grad_ref[0:width, :] = dot_rows(h_ref[...], d_pre)
    grad_ref[width : 2 * width, :] = dot_rows(agg_ref[...], d_pre)
    grad_ref[2 * width : 3 * width, :] = dot_rows(hidden_ref[...], d_inner)
    back_ref[...] = upstream + dot_back(d_pre, w_ref[4 * width : 5 * width, :])
    sums_ref[...] = jnp.concatenate(
        [
            jnp.sum(d_pre.astype(F32), axis=0, keepdims=True),
            jnp.sum(d_inner.astype(F32), axis=0, keepdims=True),
            jnp.sum(d_update * unit, axis=0, keepdims=True),
            jnp.sum(d_update, axis=0, keepdims=True),
        ],
        axis=0,
    )


def node_grads(h, agg, hidden, d_inner, d_pre, unit, weights, forced, upstream):
    nodes, width = h.shape
    full = jax.ShapeDtypeStruct((nodes, width), F32)
    return pl.pallas_call(
        node_grads_kernel,
        out_shape=[full, jax.ShapeDtypeStruct((3 * width, width), F32), jax.ShapeDtypeStruct((4, width), F32), full],
        compiler_params=PARAMS,
        name="node_grads",
        cost_estimate=pl.CostEstimate(
            flops=2 * nodes * width * width * 4, transcendentals=0, bytes_accessed=nodes * width * 18
        ),
    )(h, agg, hidden, d_inner, d_pre, unit, weights, forced.reshape(-1, LANES), upstream)


def edge_backward_kernel(
    choice_ref, region_row_ref, off_ref, near_ref, hs_ref, hr_ref, x_ref, hidden_ref, slope_ref, unit_ref,
    inverse_ref, w_ref, node_grad_ref, node_sum_ref,
    d_pre_ref, kept_ref, sent_ref,
    d_inner_ref, vec_acc_ref,
):
    step = pl.program_id(0)
    steps = pl.num_programs(0)
    rows = slope_ref.shape[0]
    width = x_ref.shape[1]
    regions = w_ref.shape[0] - 7 * width - 8
    vec = vectors_of(w_ref, width)

    @pl.when(step == 0)
    def _():
        vec_acc_ref[...] = jnp.zeros_like(vec_acc_ref)

    d_message = dot(choice_ref[...], off_ref[...])
    d_message = d_message + near_ref[...].astype(F32)
    unit = unit_ref[...]
    scaled = d_message * vec[2:3, :]
    inverse = jnp.concatenate([inverse_ref[...]] * (width // LANES), axis=1)
    d_inner = inverse * (
        scaled
        - jnp.mean(scaled, axis=-1, keepdims=True)
        - unit * jnp.mean(scaled * unit, axis=-1, keepdims=True)
    )
    vec_acc_ref[0:8, :] += jnp.sum((d_message * unit).reshape(rows // 8, 8, width), axis=0)
    vec_acc_ref[8:16, :] += jnp.sum(d_message.reshape(rows // 8, 8, width), axis=0)
    d_inner = d_inner.astype(B16)
    d_pre = (dot_back(d_inner, w_ref[3 * width : 4 * width, :]) * slope_ref[...]).astype(B16)
    base = pl.multiple_of(step * rows, rows)
    d_inner_ref[pl.ds(base, rows), :] = d_inner
    d_pre_ref[pl.ds(base, rows), :] = d_pre

    @pl.when(step == steps - 1)
    def _():
        odd = odd_core()

        def put(start, piece):
            left, right = piece[:, 0:LANES], piece[:, LANES:]
            kept_ref[start : start + piece.shape[0], :] = jnp.where(odd, right, left)
            sent_ref[start : start + piece.shape[0], :] = jnp.where(odd, left, right)

        table_rows = node_grad_ref.shape[0] + 4 * width
        d_inner, d_pre = d_inner_ref[...], d_pre_ref[...]
        left = jnp.concatenate([hidden_ref[...].T, jnp.ones((16, d_inner.shape[0]), B16)], axis=0)
        both = dot(left, d_inner)
        second_sum = both[width : width + 1, :]
        put(3 * width, both[0:width, :])
        left = jnp.concatenate([hs_ref[...].T, chosen_rows(region_row_ref[...], 0, -(-regions // 16) * 16)], axis=0)
        both = dot(left, d_pre)
        table_grad = both[width : width + regions, :]
        put(0, both[0:width, :])
        put(width, dot_rows(hr_ref[...], d_pre))
        put(2 * width, dot_rows(x_ref[...], d_pre))
        put(4 * width, node_grad_ref[...])
        vector_rows = jnp.concatenate(
            [
                jnp.sum(table_grad, axis=0, keepdims=True),
                second_sum,
                jnp.sum(vec_acc_ref[0:8, :], axis=0, keepdims=True),
                jnp.sum(vec_acc_ref[8:16, :], axis=0, keepdims=True),
                node_sum_ref[...],
            ],
            axis=0,
        )
        put(table_rows, vector_rows)
        put(table_rows + 8, table_grad)


def edge_backward(
    choice, regions, off, near, hs, hr, edges, hidden, slope, unit, inverse, weights, node_grad, node_sum,
):
    count, width = edges.shape
    tile, full = tiled(TILE, width), whole((count, width))
    grad_rows = weights.shape[0]
    half = whole((grad_rows, LANES))
    return pl.pallas_call(
        edge_backward_kernel,
        grid=(count // TILE,),
        in_specs=[
            tiled(TILE, off.shape[0]), whole((1, count)),
            whole(off.shape), tile, full, full, full, full, tile, tile, tiled(TILE, LANES),
            whole(weights.shape), whole(node_grad.shape), whole(node_sum.shape),
        ],
        out_specs=[full, half, half],
        out_shape=[
            jax.ShapeDtypeStruct((count, width), B16),
            jax.ShapeDtypeStruct((grad_rows, LANES), F32),
            jax.ShapeDtypeStruct((grad_rows, LANES), F32),
        ],
        scratch_shapes=[pltpu.VMEM((count, width), B16), pltpu.VMEM((16, width), F32)],
        compiler_params=PARAMS,
        name="edge_backward",
        cost_estimate=pl.CostEstimate(
            flops=2 * count * width * (6 * width + off.shape[0]), transcendentals=0, bytes_accessed=count * width * 20
        ),
    )(
        choice, regions.reshape(1, -1), off, near, hs, hr, edges, hidden, slope, unit, inverse,
        weights, node_grad, node_sum,
    )


def node_part_of(index_row_ref, d_pre_ref, weight, slot, nodes):
    high, low = split(dot(chosen_rows(index_row_ref[...], slot * nodes, nodes), d_pre_ref[...]))
    return dot_back(high, weight) + dot_back(low, weight)


def sender_part_kernel(index_row_ref, d_pre_ref, w_ref, out_ref):
    nodes, width = out_ref.shape
    out_ref[...] = node_part_of(index_row_ref, d_pre_ref, w_ref[0:width, :], pl.program_id(0), nodes)


def sender_part(index, d_pre, weights, nodes):
    count, width = d_pre.shape
    return pl.pallas_call(
        sender_part_kernel,
        grid=(3,),
        in_specs=[whole((1, count)), whole((count, width)), whole(weights.shape)],
        out_specs=tiled(nodes, width),
        out_shape=jax.ShapeDtypeStruct((3 * nodes, width), F32),
        compiler_params=PARAMS,
        name="sender_part",
        cost_estimate=pl.CostEstimate(
            flops=6 * count * width * nodes, transcendentals=0, bytes_accessed=count * width * 2
        ),
    )(index.reshape(1, -1), d_pre, weights)


def receiver_part_kernel(index_row_ref, d_pre_ref, w_ref, part_ref, pair_ref, off_ref):
    nodes, width = pair_ref.shape
    slot = pl.program_id(0) + 1
    part = node_part_of(index_row_ref, d_pre_ref, w_ref[width : 2 * width, :], slot, nodes) + part_ref[...]

    @pl.when(slot == 1)
    def _():
        pair_ref[...] = part.astype(B16)

    @pl.when(slot == 2)
    def _():
        off_ref[...] = part.astype(B16)


def receiver_part(index, d_pre, weights, part, nodes):
    count, width = d_pre.shape
    half = jax.ShapeDtypeStruct((nodes, width), B16)
    return pl.pallas_call(
        receiver_part_kernel,
        grid=(2,),
        in_specs=[
            whole((1, count)), whole((count, width)), whole(weights.shape),
            pl.BlockSpec((nodes, width), lambda i: (i + 1, 0)),
        ],
        out_specs=[whole((nodes, width))] * 2,
        out_shape=[half, half],
        compiler_params=PARAMS,
        name="receiver_part",
        cost_estimate=pl.CostEstimate(
            flops=4 * count * width * nodes, transcendentals=0, bytes_accessed=count * width * 2
        ),
    )(index.reshape(1, -1), d_pre, weights, part)


def own_part_kernel(index_row_ref, d_pre_ref, w_ref, part_ref, back_ref, own_ref):
    nodes, width = own_ref.shape
    part = node_part_of(index_row_ref, d_pre_ref, w_ref[width : 2 * width, :], 0, nodes)
    own_ref[...] = part + (part_ref[...] + back_ref[...])


def own_part(index, d_pre, weights, part, back):
    count, width = d_pre.shape
    return pl.pallas_call(
        own_part_kernel,
        grid=(1,),
        in_specs=[whole((1, count)), whole((count, width)), whole(weights.shape), whole(back.shape), whole(back.shape)],
        out_specs=whole(back.shape),
        out_shape=jax.ShapeDtypeStruct(back.shape, F32),
        compiler_params=PARAMS,
        name="own_part",
        cost_estimate=pl.CostEstimate(
            flops=2 * count * width * back.shape[0], transcendentals=0, bytes_accessed=count * width * 2
        ),
    )(index.reshape(1, -1), d_pre, weights, part, back)


def edge_grads_kernel(d_pre_ref, w_ref, out_ref):
    width = d_pre_ref.shape[1]
    out_ref[...] = dot_back(d_pre_ref[...], w_ref[2 * width : 3 * width, :]).astype(B16)


def edge_grads(d_pre, weights):
    count, width = d_pre.shape
    return pl.pallas_call(
        edge_grads_kernel,
        grid=(count // TILE,),
        in_specs=[tiled(TILE, width), whole(weights.shape)],
        out_specs=tiled(TILE, width),
        out_shape=jax.ShapeDtypeStruct((count, width), B16),
        compiler_params=PARAMS,
        name="edge_grads",
        cost_estimate=pl.CostEstimate(
            flops=2 * count * width * width, transcendentals=0, bytes_accessed=count * width * 4
        ),
    )(d_pre, weights)


def packed(values, first):
    rows = values[first : first + 8, :]
    return jnp.concatenate([values, rows - rows.astype(B16).astype(F32)], axis=0).astype(B16)


def unpacked(wire, first):
    values = wire.astype(F32)
    share = values.shape[0] - 8
    exact = values[first : first + 8, :] + values[share:, :]
    return jnp.concatenate([values[:first, :], exact, values[first + 8 : share, :]], axis=0)


def parted_kernel(mine_ref, other_ref, kept_ref, *sent_refs, share, first):
    for k, out_ref in enumerate((kept_ref, *sent_refs)):
        rows = pl.ds(pl.multiple_of(jnp.bitwise_xor(lax.axis_index("feat"), k) * share, 8), share)
        total = mine_ref[rows, :] + other_ref[rows, :]
        out_ref[...] = packed(total, first) if k else total


def parted(mine, other, share, first):
    sent = jax.ShapeDtypeStruct((share + 8, LANES), B16)
    return pl.pallas_call(
        functools.partial(parted_kernel, share=share, first=first),
        out_shape=[jax.ShapeDtypeStruct((share, LANES), F32)] + [sent] * (mine.shape[0] // share - 1),
        compiler_params=PARAMS,
        name="parted",
    )(mine, other)


def gathered_kernel(mine_ref, *refs, first):
    total = mine_ref[...]
    for ref in refs[:-1]:
        total = total + unpacked(ref[...], first)
    refs[-1][...] = packed(total, first)


def gathered(mine, others, first):
    return pl.pallas_call(
        functools.partial(gathered_kernel, first=first),
        out_shape=jax.ShapeDtypeStruct(others[0].shape, B16),
        compiler_params=PARAMS,
        name="gathered",
    )(mine, *others)


def add_kernel(mine_ref, other_ref, out_ref, *, first):
    out_ref[...] = packed(unpacked(mine_ref[...], first) + unpacked(other_ref[...], first), first)


def add(mine, other, first):
    return pl.pallas_call(
        functools.partial(add_kernel, first=first),
        out_shape=jax.ShapeDtypeStruct(other.shape, B16),
        compiler_params=PARAMS,
        name="add",
    )(mine, other)


def finish_kernel(mine_ref, other_ref, out_ref, *, first, owner):
    share = out_ref.shape[0] - 16
    part = unpacked(mine_ref[...], first) + unpacked(other_ref[...], first)
    out_ref[0:share, :] = part
    out_ref[share : share + 8, :] = jnp.where(lax.axis_index("feat") == owner, part[first : first + 8, :], 0.0)
    squares = jnp.sum(jnp.sum(part * part, axis=0, keepdims=True), axis=1, keepdims=True)
    out_ref[share + 8 : share + 16, :] = jnp.broadcast_to(squares, (8, LANES))


def finish(mine, other, share, first, owner):
    return pl.pallas_call(
        functools.partial(finish_kernel, first=first, owner=owner),
        out_shape=jax.ShapeDtypeStruct((share + 16, LANES), F32),
        compiler_params=PARAMS,
        name="finish",
    )(mine, other)


def adam_kernel(
    step_ref, stats_ref, more_ref, mine_ref, other_ref, params_ref, first_ref, second_ref, averaged_ref,
    own_ref, pair_ref, off_ref,
    new_first_hbm, new_second_hbm, new_params_hbm, new_average_hbm, norm_ref, vector_ref, latents_hbm,
    new_first_ref, new_second_ref, new_params_ref, new_average_ref, latents_ref, sem,
):
    share = params_ref.shape[0]
    odd = odd_core()
    latents_ref[...] = own_ref[...] + pair_ref[...].astype(F32) + off_ref[...].astype(F32)
    copies = [pltpu.make_async_copy(latents_ref, latents_hbm, sem.at[0])]
    copies[0].start()
    stats, more = stats_ref[...], more_ref[...]
    norm = jnp.sqrt(stats[8:9, 0:1] + more[8:9, 0:1])
    norm_ref[...] = norm
    factor = jnp.minimum(1.0, MAX_NORM / (norm + 1e-06))
    count = step_ref[0:1, 0:1]
    first_scale = 1.0 - jnp.exp(count * jnp.log(jnp.full((1, 1), BETA_ONE, F32)))
    second_scale = 1.0 - jnp.exp(count * jnp.log(jnp.full((1, 1), BETA_TWO, F32)))
    decay = jnp.minimum(AVERAGE_DECAY, (1.0 + count) / (10.0 + count))
    vector_ref[:, 0:LANES] = jnp.where(odd, more[0:8, :], stats[0:8, :]) * factor
    vector_ref[:, LANES : 2 * LANES] = jnp.where(odd, stats[0:8, :], more[0:8, :]) * factor
    chunk = share // 3 if share % 24 == 0 else share
    for i in range(share // chunk):
        rows = slice(i * chunk, (i + 1) * chunk)
        mine, other = mine_ref[rows, :], other_ref[rows, :]
        both = jnp.concatenate([jnp.where(odd, other, mine), jnp.where(odd, mine, other)], axis=1)
        clipped = both * factor
        params = params_ref[rows, :]
        new_first = BETA_ONE * first_ref[rows, :] + (1.0 - BETA_ONE) * clipped
        new_second = BETA_TWO * second_ref[rows, :] + (1.0 - BETA_TWO) * clipped * clipped
        first_hat = new_first / first_scale
        second_hat = new_second / second_scale
        new_params = params - RATE * (first_hat / (jnp.sqrt(second_hat) + ADAM_EPS) + WEIGHT_DECAY * params)
        new_first_ref[rows, :] = new_first
        new_second_ref[rows, :] = new_second
        new_params_ref[rows, :] = new_params
        new_average_ref[rows, :] = decay * averaged_ref[rows, :] + (1.0 - decay) * new_params
        for k, (src, dst) in enumerate(
            (
                (new_first_ref, new_first_hbm), (new_second_ref, new_second_hbm), (new_params_ref, new_params_hbm),
                (new_average_ref, new_average_hbm),
            )
        ):
            copies.append(pltpu.make_async_copy(src.at[rows, :], dst.at[rows, :], sem.at[1 + 4 * i + k]))
            copies[-1].start()
    for copy in copies:
        copy.wait()


def adam(step, stats, more, mine, other, params, first_moment, second_moment, averaged, own, pair, off):
    rows = jax.ShapeDtypeStruct(params.shape, F32)
    vmem, hbm = (pl.BlockSpec(memory_space=m) for m in (pltpu.VMEM, pltpu.HBM))
    return pl.pallas_call(
        adam_kernel,
        in_specs=[vmem] * 12,
        out_specs=[hbm] * 4 + [vmem] * 2 + [hbm],
        out_shape=[
            rows, rows, rows, rows, jax.ShapeDtypeStruct((1, 1), F32), jax.ShapeDtypeStruct((8, params.shape[1]), F32),
            jax.ShapeDtypeStruct(own.shape, F32),
        ],
        scratch_shapes=[pltpu.VMEM(params.shape, F32)] * 4
        + [pltpu.VMEM(own.shape, F32), pltpu.SemaphoreType.DMA((13,))],
        compiler_params=PARAMS,
        name="adam",
        cost_estimate=pl.CostEstimate(
            flops=20 * params.size, transcendentals=2 * params.size, bytes_accessed=params.size * 32
        ),
    )(jnp.broadcast_to(step.astype(F32), (8, LANES)), stats, more, mine, other, params, first_moment, second_moment, averaged, own, pair, off)


def flipped(value, axis, bit):
    return lax.ppermute(value, axis, [(i, i ^ bit) for i in range(lax.axis_size(axis))])


def across(value, axis):
    count = lax.axis_size(axis)
    return lax.ppermute(value, axis, [(i, (i + 1 if i % 2 else i - 1) % count) for i in range(count)])


def neighbours(value):
    off = across(value, "edge")
    return flipped(value, "edge", 1), off


def on_device(
    node_latents, edge_latents, senders, receivers, regions, forced, params, first_moment, second_moment,
    averaged, step, cotangent,
):
    latents = node_latents[0]
    edges = edge_latents[0]
    upstream = cotangent[0]
    nodes, width = latents.shape
    share = params.shape[0]
    blocks, feats = lax.axis_size("edge"), lax.axis_size("feat")
    total = share * feats
    vector_row = 7 * width

    pair, off = neighbours(latents)

    mine, send, recv, latents = prologue(params, senders, receivers, latents)
    far = [flipped(mine, "feat", k) for k in ways(feats)]

    near_send = gather_near(send, latents, pair)
    near_recv = gather_near(recv, latents, pair)
    off_sums = off_rows(recv, nodes)
    others = jnp.concatenate(lax.optimization_barrier((near_send, near_recv, off_sums, *far))[3:])
    pieces = [mine, others, flipped(mine, "edge", 1), flipped(others, "edge", 1)]
    hs = gather_off(send, off, near_send)
    hr = gather_off(recv, off, near_recv)
    weights, high, low, to_off = edge_forward(regions, off_sums, hs, hr, edges, pieces, total, nodes)
    from_off = across(to_off, "edge")
    to_pair, more, own = near_sum(recv, high, low, nodes)
    from_pair, more = flipped(to_pair, "edge", 1), flipped(more, "edge", 1)
    hidden, slope = edge_slope(regions, hs, hr, edges, weights)
    own, hidden, slope = lax.optimization_barrier((own, hidden, slope))
    d_agg, agg, node_hidden, d_inner, d_pre, node_unit = node_update(
        latents, own, from_pair, more, from_off, weights, forced, upstream
    )
    back_pair, back_off = neighbours(d_agg)
    new_latents, node_grad, node_sum, back = node_grads(
        latents, agg, node_hidden, d_inner, d_pre, node_unit, weights, forced, upstream
    )
    near = gather_near(recv, d_agg, back_pair)
    hidden, index = lax.optimization_barrier((hidden, recv, d_agg))[:2]
    unit, inverse = edge_unit(hidden, weights)
    choice = off_choice(index, nodes)

    d_pre, kept, sent = edge_backward(
        choice, regions, back_off, near, hs, hr, edges, hidden, slope, unit, inverse, weights, node_grad, node_sum,
    )

    low_rows = vector_row % share
    grad_edges = edge_grads(d_pre, weights)
    other, grad_edges = lax.optimization_barrier((flipped(sent, "edge", 1), grad_edges))
    part, *sent = parted(kept, other, share, low_rows)
    came = [flipped(sent[k - 1], "feat", k) for k in ways(feats)]
    d_pre, part = lax.optimization_barrier((d_pre, part))
    send_part = sender_part(send, d_pre, weights, nodes)
    part_pair, part_off = receiver_part(recv, d_pre, weights, send_part, nodes)
    part, part_pair, part_off = lax.optimization_barrier((part, part_pair, part_off))
    wire = gathered(part, came, low_rows)
    bit = 2
    while 2 * bit < blocks:
        wire = add(wire, flipped(wire, "edge", bit), low_rows)
        bit *= 2
    part_own = own_part(recv, d_pre, weights, send_part, back)
    wire, part_pair, part_off, part_own = lax.optimization_barrier((wire, part_pair, part_off, part_own))
    mine = finish(wire, flipped(wire, "edge", bit), share, low_rows, vector_row // share)
    grads_off = across(part_off, "edge")
    grads_pair = flipped(part_pair, "edge", 1)

    other = flipped(mine[:share], "edge", 1)
    held = {0: mine[share:], **{k: flipped(mine[share:], "feat", k) for k in ways(feats)}}
    held = [held[k] for k in range(feats)]
    while len(held) > 1:
        held = [held[i] + held[i + 1] for i in range(0, len(held), 2)]
    stats = held[0]
    more = flipped(stats, "edge", 1)
    new_first, new_second, new_params, new_average, grad_norm, vector_grads, grad_latents = adam(
        step, stats, more, mine, other, params, first_moment, second_moment, averaged,
        part_own, grads_pair, grads_off,
    )
    return (
        new_latents[None],
        grad_latents[None],
        grad_edges[None],
        new_first,
        new_second,
        new_params,
        new_average,
        grad_norm.reshape(1),
        vector_grads,
    )


def solution(mesh):
    nodes, rows = P("feat", "edge", None), P("feat", None)
    return jax.shard_map(
        on_device,
        mesh=mesh,
        in_specs=(nodes, nodes, P("edge"), P("edge"), P("edge"), P("edge"), rows, rows, rows, rows, P(), nodes),
        out_specs=(nodes, nodes, nodes, rows, rows, rows, rows, P(), P()),
        check_vma=False,
    )
```
